32 devices in a mesh: dp: 2 (over y), seq: 16 (over z, x, core).
Axes of the slice: x: 2, y: 2, z: 4, core: 2. Of those that a mesh axis runs over, the one named last changes fastest.
Arguments:
- tokens: bfloat16 [2, 4096, 1024], P('dp', 'seq'), may hold values from -6 to 6
- segment_ids: int32 [2, 4096], P('dp', 'seq'), may hold values from 0 to 7, never falling along the last dimension, each value on 1 to 2048 neighbouring positions
- second_doc: int32 [2, 8], P('dp'), may hold values from 0 to 7, as said below
- memory_index: int32 [2, 32, 8, 128], P('dp', 'seq'), may hold values from 0 to 511
- cache_keys: bfloat16 [2, 8, 256, 1024], P('dp'), may hold values from -6 to 6
- cache_values: bfloat16 [2, 8, 256, 1024], P('dp'), may hold values from -6 to 6
- first_gain: bfloat16 [1024], P(('dp', 'seq')), may hold values from 0.099609375 to 1.8984375
- query_weight: bfloat16 [1024, 1024], P(('dp', 'seq')), may hold values from -0.1875 to 0.1875
- key_weight: bfloat16 [1024, 1024], P(('dp', 'seq')), may hold values from -0.1875 to 0.1875
- value_weight: bfloat16 [1024, 1024], P(('dp', 'seq')), may hold values from -0.1875 to 0.1875
- out_weight: bfloat16 [1024, 1024], P(('dp', 'seq')), may hold values from -1.5 to 1.5
- second_gain: bfloat16 [1024], P(('dp', 'seq')), may hold values from 0.099609375 to 1.8984375
- gate_weight: bfloat16 [1024, 2816], P(('dp', 'seq')), may hold values from -0.1875 to 0.1875
- up_weight: bfloat16 [1024, 2816], P(('dp', 'seq')), may hold values from -0.1875 to 0.1875
- down_weight: bfloat16 [2816, 1024], P(('dp', 'seq')), may hold values from -0.109375 to 0.109375
- cotangent: bfloat16 [2, 4096, 1024], P('dp', 'seq'), may hold values from -6 to 6
Outputs:
- output: bfloat16 [2, 4096, 1024], P('dp', 'seq')
- input_grad: float32 [2, 4096, 1024], P('dp', 'seq')
- first_gain_grad: float32 [1024], P(('dp', 'seq'))
- query_weight_grad: float32 [1024, 1024], P(('dp', 'seq'))
- key_weight_grad: float32 [1024, 1024], P(('dp', 'seq'))
- value_weight_grad: float32 [1024, 1024], P(('dp', 'seq'))
- out_weight_grad: float32 [1024, 1024], P(('dp', 'seq'))
- second_gain_grad: float32 [1024], P(('dp', 'seq'))
- gate_weight_grad: float32 [1024, 2816], P(('dp', 'seq'))
- up_weight_grad: float32 [1024, 2816], P(('dp', 'seq'))
- down_weight_grad: float32 [2816, 1024], P(('dp', 'seq'))
The draws below stay inside these ranges and needn't reach their ends.
Inputs may be any that keep to these rules, and one draw needn't show every extreme that they name: `segment_ids`: within each sequence the numbers never fall; every document spans at most 2048 positions and one spans exactly 2048. `second_doc`: never the document's own number.
All inputs are finite; a program needn't handle non-finite values.
Results may differ from the reference program's by a relative error of at most 0.018.
Values may be sent and summed in bfloat16 or wider, within the bound.
No kernel may reach another device: no remote copies, remote signals or barrier semaphores. Data moves between devices by JAX's collectives and lax.ppermute only.
A program may use at most 320 MiB of HBM per device.

```python
import math
import jax
import jax.numpy as jnp
import numpy as np
from jax import lax

D = 1024
FF = 2816
HEADS = 8
HEAD_DIM = 128
QUERY_BLOCK = 128
RETRIEVED = 128
MEM_ROWS = 256
DOC_MAX = 2048
SEQS = 2
SEQ_LEN = 4096
DOCS = 8
BLOCKS = 32


def draw_second_doc(key, part):
    offsets = jax.random.randint(key, (SEQS, DOCS), 1, DOCS)
    return ((jnp.arange(DOCS, dtype=jnp.int32)[None, :] + offsets) % DOCS).astype(jnp.int32)


def set_ends(entries, key, least, largest):
    spot = [jax.random.randint(jax.random.fold_in(key, axis), (), 0, length) for axis, length in enumerate(entries.shape)]
    longest = entries.shape.index(max(entries.shape))
    beside = spot[:longest] + [(spot[longest] + 1) % entries.shape[longest]] + spot[longest + 1:]
    return entries.at[tuple(spot)].set(least).at[tuple(beside)].set(largest)


def block_levels(key, extent, cuts, smallest, largest):
    loudness, own = 1.0, jax.random.fold_in(key, 6)
    for axis_at, blocks in cuts:
        heights = jnp.exp(jax.random.uniform(jax.random.fold_in(own, axis_at), (blocks,), jnp.float32, smallest / len(cuts), largest / len(cuts)))
        loudness = loudness * jnp.repeat(heights, extent[axis_at] // blocks).reshape([-1 if axis == axis_at else 1 for axis in range(len(extent))])
    return loudness


def profile(number_of, total, limit, skew):
    portions = [(1 << 20) // math.isqrt(standing ** skew) + 1 for standing in range(2, number_of + 1)]
    rest, counts = total - limit - (number_of - 1), [1] * (number_of - 1)
    while rest > 0:
        free = [i for i in range(number_of - 1) if counts[i] < limit]
        whole, left = sum([portions[i] for i in free]), rest
        for i in free:
            more = min(limit - counts[i], max(1, left * portions[i] // whole), rest)
            counts[i] = counts[i] + more
            rest = rest - more
    return np.array([limit] + counts)


def uneven_parts(own_key, number_of, total, limit, lean):
    if number_of == 2:
        one = jax.random.randint(own_key, (), max(1, total - limit), min(limit, total - 1) + 1)
        return jnp.stack([one, total - one])
    sizes = jnp.asarray(profile(number_of, total, limit, lean), jnp.int32)
    pairs = (number_of - 1) // 2
    giver, receiver = sizes[1:1 + 2 * pairs:2], sizes[2:2 + 2 * pairs:2]
    margin = jnp.minimum(giver - 1, limit - receiver)
    passed = jax.random.randint(jax.random.fold_in(own_key, 1), (pairs,), 0, 1 << 20) % (margin + 1)
    sizes = sizes.at[1:1 + 2 * pairs:2].set(giver - passed).at[2:2 + 2 * pairs:2].set(receiver + passed)
    return sizes[jax.random.permutation(jax.random.fold_in(own_key, 2), number_of)]


def noise(key, shape, spread, limit, pieces=(), kind=jnp.bfloat16):
    result = spread * jax.random.normal(key, shape, jnp.float32)
    if pieces:
        result = result * block_levels(key, shape, pieces, -0.22, 0.18)
    return jnp.clip(result, -limit, limit).astype(kind)


def setup_inputs(seed: int = 0) -> dict:
    arg_keys = jax.random.split(jax.random.key(seed), 17)
    tokens = noise(arg_keys[0], (SEQS, SEQ_LEN, D), 1.0, 6.0, ((0, 2), (1, 16)))
    segment_ids = jax.vmap(lambda own: jnp.searchsorted(jnp.cumsum(uneven_parts(own, DOCS, SEQ_LEN, DOC_MAX, 0)), jnp.arange(SEQ_LEN), side="right"))(jax.random.split(arg_keys[1], SEQS)).reshape((SEQS, SEQ_LEN)).astype(jnp.int32)
    second_doc = draw_second_doc(jax.random.fold_in(arg_keys[16], 71), 0)
    memory_index = set_ends(jax.random.randint(arg_keys[3], (SEQS, BLOCKS, HEADS, RETRIEVED), 0, 2 * MEM_ROWS), jax.random.fold_in(arg_keys[3], 1), 0, (2 * MEM_ROWS) - 1).astype(jnp.int32)
    cache_keys = noise(arg_keys[4], (SEQS, DOCS, MEM_ROWS, D), 1.0, 6.0, ((0, 2),))
    cache_values = noise(arg_keys[5], (SEQS, DOCS, MEM_ROWS, D), 1.0, 6.0, ((0, 2),))
    first_gain = jnp.clip(1.0 + 0.18 * jax.random.normal(arg_keys[6], (D,), jnp.float32), 0.099609375, 1.8984375).astype(jnp.bfloat16)
    query_weight = noise(arg_keys[7], (D, D), D ** -0.5, 0.1875, ((0, 32),))
    key_weight = noise(arg_keys[8], (D, D), D ** -0.5, 0.1875, ((0, 32),))
    value_weight = noise(arg_keys[9], (D, D), D ** -0.5, 0.1875, ((0, 32),))
    out_weight = noise(arg_keys[10], (D, D), (D // 64) ** -0.5, 1.5, ((0, 32),))
    second_gain = jnp.clip(1.0 + 0.18 * jax.random.normal(arg_keys[11], (D,), jnp.float32), 0.099609375, 1.8984375).astype(jnp.bfloat16)
    gate_weight = noise(arg_keys[12], (D, FF), D ** -0.5, 0.1875, ((0, 32),))
    up_weight = noise(arg_keys[13], (D, FF), D ** -0.5, 0.1875, ((0, 32),))
    down_weight = noise(arg_keys[14], (FF, D), FF ** -0.5, 0.109375, ((0, 32),))
    cotangent = noise(arg_keys[15], (SEQS, SEQ_LEN, D), 1.0, 6.0, ((0, 2), (1, 16)))
    return dict(tokens=tokens, segment_ids=segment_ids, second_doc=second_doc, memory_index=memory_index, cache_keys=cache_keys, cache_values=cache_values, first_gain=first_gain, query_weight=query_weight, key_weight=key_weight, value_weight=value_weight, out_weight=out_weight, second_gain=second_gain, gate_weight=gate_weight, up_weight=up_weight, down_weight=down_weight, cotangent=cotangent)


EPSILON = 1e-05
NEGATIVE = -1e+30

@jax.custom_vjp
def low(v):
    return lax.optimization_barrier(v.astype(jnp.bfloat16)).astype(jnp.float32)

@jax.custom_vjp
def low_back(v):
    return v

def low_keep(v):
    return (low(v), None)

def low_pass(kept, grad):
    return (grad,)

def back_keep(v):
    return (v, None)

def back_low(kept, grad):
    return (low(grad),)
low.defvjp(low_keep, low_pass)
low_back.defvjp(back_keep, back_low)

def normalize(values, gain):
    scale_rows = lax.rsqrt(lax.optimization_barrier(jnp.mean(values * values, axis=-1, keepdims=True)) + EPSILON)
    return values * scale_rows * gain

def angles(positions, half):
    freqs = 10000.0 ** (-jnp.arange(half, dtype=jnp.float32) * 2.0 / (2 * half))
    turned = positions.astype(jnp.float32)[:, None] * freqs[None, :]
    return (jnp.cos(turned)[:, None, :], jnp.sin(turned)[:, None, :])

def rotate(values, cosine, sine):
    half = values.shape[-1] // 2
    first = values[..., :half]
    second = values[..., half:]
    return jnp.concatenate([first * cosine - second * sine, second * cosine + first * sine], axis=-1)

def layer(inputs, segs, partner, pick, cache_k, cache_v, params):
    gain_one, query_w, key_w, value_w, out_w, gain_two, gate_w, up_w, down_w = params
    length = inputs.shape[0]
    highest = lax.Precision.HIGHEST
    positions = jnp.arange(length, dtype=jnp.int32)
    cosine, sine = angles(positions, HEAD_DIM // 2)
    normed_one = low(normalize(inputs, gain_one))

    def project(weight):
        return jnp.dot(normed_one, weight, precision=highest).reshape(length, HEADS, HEAD_DIM)
    queries = low(rotate(low_back(project(query_w)), cosine, sine))
    keys = low(rotate(low_back(project(key_w)), cosine, sine))
    values = low(low_back(project(value_w)))
    block_docs = segs[::QUERY_BLOCK]
    docs = partner.shape[0]
    partner_blocks = partner[block_docs]
    from_own = pick < MEM_ROWS
    owner = jnp.where(from_own, block_docs[:, None, None], partner_blocks[:, None, None])
    row = jnp.where(from_own, pick, pick - MEM_ROWS)
    head_ids = jnp.arange(HEADS, dtype=jnp.int32)[None, :, None]
    memory_keys = cache_k.reshape(docs, MEM_ROWS, HEADS, HEAD_DIM)[owner, row, head_ids]
    memory_values = cache_v.reshape(docs, MEM_ROWS, HEADS, HEAD_DIM)[owner, row, head_ids]
    rows = math.gcd(length, 512)
    per = rows // QUERY_BLOCK
    scale = 1.0 / math.sqrt(HEAD_DIM)

    def attend(start):
        query_part = lax.dynamic_slice_in_dim(queries, start, rows, 0)
        query_segs = lax.dynamic_slice_in_dim(segs, start, rows, 0)
        query_pos = start + jnp.arange(rows, dtype=jnp.int32)
        local = low_back(jnp.einsum('qhd,khd->hqk', query_part, keys, precision=highest) * scale)
        allowed = (segs[None, :] == query_segs[:, None]) & (positions[None, :] <= query_pos[:, None])
        local = jnp.where(allowed[None], local, NEGATIVE)
        first = (start // QUERY_BLOCK).astype(jnp.int32)
        block_keys = lax.dynamic_slice_in_dim(memory_keys, first, per, 0)
        block_values = lax.dynamic_slice_in_dim(memory_values, first, per, 0)
        docs_here = lax.dynamic_slice_in_dim(block_docs, first, per, 0)
        remote = low_back(jnp.einsum('bqhd,bhrd->hbqr', query_part.reshape(per, QUERY_BLOCK, HEADS, HEAD_DIM), block_keys, precision=highest) * scale)
        remote_allowed = query_segs.reshape(per, QUERY_BLOCK) == docs_here[:, None]
        remote = jnp.where(remote_allowed[None, :, :, None], remote, NEGATIVE).reshape(HEADS, rows, RETRIEVED)
        joined = jnp.concatenate([local, remote], axis=-1)
        probs = low(jax.nn.softmax(joined, axis=-1))
        out_local = jnp.einsum('hqk,khd->qhd', probs[:, :, :length], values, precision=highest)
        out_memory = jnp.einsum('hbqr,bhrd->bqhd', probs[:, :, length:].reshape(HEADS, per, QUERY_BLOCK, RETRIEVED), block_values, precision=highest)
        return out_local + out_memory.reshape(rows, HEADS, HEAD_DIM)
    starts = jnp.arange(length // rows, dtype=jnp.int32) * rows
    attention = lax.map(jax.checkpoint(attend), starts).reshape(length, HEADS * HEAD_DIM)
    attention = low(low_back(attention))
    branch = low_back(jnp.dot(attention, out_w, precision=highest))
    mid = inputs + branch
    normed_two = low(normalize(mid, gain_two))
    gate = low_back(jnp.dot(normed_two, gate_w, precision=highest))
    upper = low_back(jnp.dot(normed_two, up_w, precision=highest))
    hidden = low(jax.nn.silu(gate) * upper)
    return mid + jnp.dot(hidden, down_w, precision=highest)

def reference(tokens, segment_ids, second_doc, memory_index, cache_keys, cache_values, first_gain, query_weight, key_weight, value_weight, out_weight, second_gain, gate_weight, up_weight, down_weight, cotangent):
    params = (first_gain.astype(jnp.float32), query_weight.astype(jnp.float32), key_weight.astype(jnp.float32), value_weight.astype(jnp.float32), out_weight.astype(jnp.float32), second_gain.astype(jnp.float32), gate_weight.astype(jnp.float32), up_weight.astype(jnp.float32), down_weight.astype(jnp.float32))
    inputs = tokens.astype(jnp.float32)

    def forward(inputs, params):

        def single(item):
            seq_inputs, segs, partner, pick, cache_k, cache_v = item
            return layer(seq_inputs, segs, partner, pick, cache_k.astype(jnp.float32), cache_v.astype(jnp.float32), params)
        return lax.map(single, (inputs, segment_ids, second_doc, memory_index, cache_keys, cache_values))
    output, pullback = jax.vjp(forward, inputs, params)
    input_grad, grads = pullback(cotangent.astype(jnp.float32))
    return (output.astype(jnp.bfloat16), input_grad, grads[0], grads[1], grads[2], grads[3], grads[4], grads[5], grads[6], grads[7], grads[8])
```

```python
import functools
import math

import jax
import jax.numpy as jnp
from jax import lax
from jax.experimental import pallas as pl
from jax.experimental.pallas import tpu as pltpu
from jax.sharding import Mesh
from jax.sharding import PartitionSpec as P

D = 1024
FF = 2816
HEADS = 8
HEAD_DIM = 128
QUERY_BLOCK = 128
MEM_ROWS = 256
EPSILON = 1e-05
NEGATIVE = -1e30
SCALE = 1.0 / math.sqrt(HEAD_DIM)
LOG2 = SCALE * math.log2(math.e)
LOW = jnp.bfloat16
WIDE = jnp.float32

RING = [2 * i for i in range(HEADS // 2)] + [2 * i + 1 for i in reversed(range(HEADS // 2))]
PLACE = [RING.index(i) for i in range(HEADS)]


def dot_nn(a, b):
    return lax.dot_general(a, b, (((1,), (0,)), ((), ())), preferred_element_type=WIDE)


def dot_nt(a, b):
    return lax.dot_general(a, b, (((1,), (1,)), ((), ())), preferred_element_type=WIDE)


def dot_tn(a, b):
    return lax.dot_general(a, b, (((0,), (0,)), ((), ())), preferred_element_type=WIDE)


def swap(block, axis):
    return lax.ppermute(block, axis, [(0, 1), (1, 0)])


def turn(block, distance):
    route = [(RING[i], RING[(i + distance) % HEADS]) for i in range(HEADS)]
    return lax.ppermute(block, "h", route)


def at_place(place):
    place = lax.rem(place + 2 * HEADS, HEADS)
    return jnp.where(place < HEADS // 2, 2 * place, 2 * (HEADS - 1 - place) + 1)


def rolled(blocks, start):
    return lax.dynamic_slice_in_dim(
        jnp.concatenate([blocks, blocks], axis=0), start, HEADS, axis=0
    )


def reverse(blocks):
    return jnp.concatenate([blocks[:1], jnp.flip(blocks[1:], axis=0)], axis=0)


def to_ahead(blocks, mine):
    return rolled(jnp.stack([blocks[i] for i in RING]), mine)


def from_behind(blocks, mine):
    placed = rolled(reverse(blocks), lax.rem(HEADS - mine, HEADS))
    return jnp.stack([placed[i] for i in PLACE])


def pick(flag, first, second):
    return jnp.where(flag == 0, first, second)


def smem():
    return pl.BlockSpec(memory_space=pltpu.SMEM)


def vmem():
    return pl.BlockSpec(memory_space=pltpu.VMEM)


def qkv_kernel(slot_ref, x_ref, gain_ref, w_ref, cos_ref, sin_ref, *rest):
    q_ref, kv_ref, n_ref = rest[-3:]
    x = x_ref[...].astype(WIDE)
    r = lax.rsqrt(jnp.mean(x * x, axis=-1, keepdims=True) + EPSILON)
    normed = (x * r * gain_ref[...].astype(WIDE)).astype(LOW)
    n_ref[0] = normed
    out = dot_nn(normed, w_ref[...])
    c, s = cos_ref[0], sin_ref[0]

    def rot(v):
        return v * c + pltpu.roll(v, HEAD_DIM // 2, 1) * s

    q_ref[0] = rot(out[:, :HEAD_DIM]).astype(LOW)
    kv_ref[0, 0] = rot(out[:, HEAD_DIM : 2 * HEAD_DIM]).astype(LOW)
    kv_ref[1, 0] = out[:, 2 * HEAD_DIM :].astype(LOW)


def qkv_block(slot, x, gain, w, cos, sin, held):
    count = x.shape[0]
    spec = pltpu.PrefetchScalarGridSpec(
        num_scalar_prefetch=1,
        grid=(1,),
        in_specs=[
            pl.BlockSpec((count, D), lambda i, s: (0, 0)),
            pl.BlockSpec((1, D), lambda i, s: (0, 0)),
            pl.BlockSpec((D, 3 * HEAD_DIM), lambda i, s: (0, 0)),
            pl.BlockSpec((1, count, HEAD_DIM), lambda i, s: (slot, 0, 0)),
            pl.BlockSpec((1, count, HEAD_DIM), lambda i, s: (slot, 0, 0)),
        ]
        + [pl.BlockSpec(memory_space=pl.ANY)] * len(held),
        out_specs=[
            pl.BlockSpec((1, count, HEAD_DIM), lambda i, s: (slot, 0, 0)),
            pl.BlockSpec((2, 1, count, HEAD_DIM), lambda i, s: (0, slot, 0, 0)),
            pl.BlockSpec((1, count, D), lambda i, s: (slot, 0, 0)),
        ],
    )
    return pl.pallas_call(
        qkv_kernel,
        grid_spec=spec,
        out_shape=[
            jax.ShapeDtypeStruct((HEADS, count, HEAD_DIM), LOW),
            jax.ShapeDtypeStruct((2, HEADS, count, HEAD_DIM), LOW),
            jax.ShapeDtypeStruct((HEADS, count, D), LOW),
        ],
        input_output_aliases={6 + i: i for i in range(len(held))},
        cost_estimate=pl.CostEstimate(
            flops=2 * count * D * 3 * HEAD_DIM, bytes_accessed=4 * count * D, transcendentals=0
        ),
        name=f"qkv{slot}",
    )(jnp.zeros((1,), jnp.int32), x, gain, w, cos, sin, *held)


def allowed_keys(segq, segk, qpos, kstart, shape):
    kpos = kstart + lax.broadcasted_iota(jnp.int32, shape, 1)
    return (segk == segq) & (kpos <= qpos)


def attend_kernel(
    tab, q_ref, own_ref, oth_ref, segq_ref, sego_ref, segt_ref, idx_ref, ck_ref, cv_ref,
    o_ref, low_ref, lse_ref, mem_ref,
):
    i = pl.program_id(0)
    chip = tab[i]
    parity = tab[48]
    count = q_ref.shape[1]
    for b in range(count // QUERY_BLOCK):
        rows = pl.ds(b * QUERY_BLOCK, QUERY_BLOCK)
        q = q_ref[0, rows, :]
        segq = segq_ref[0, rows, :]
        doc = tab[16 + 2 * i + b]
        mate = tab[32 + 2 * i + b]
        idx = idx_ref[0, rows, :]
        lane = lax.broadcasted_iota(jnp.int32, (QUERY_BLOCK, MEM_ROWS), 1)
        first = jnp.where(idx == lane, 1.0, 0.0).astype(LOW)
        second = jnp.where(idx == lane + MEM_ROWS, 1.0, 0.0).astype(LOW)
        here = pl.ds(pl.multiple_of(doc * MEM_ROWS, MEM_ROWS), MEM_ROWS)
        there = pl.ds(pl.multiple_of(mate * MEM_ROWS, MEM_ROWS), MEM_ROWS)
        mk = (dot_nn(first, ck_ref[here, :]) + dot_nn(second, ck_ref[there, :])).astype(LOW)
        mv = (dot_nn(first, cv_ref[here, :]) + dot_nn(second, cv_ref[there, :])).astype(LOW)
        mem_ref[0, 0, rows, :] = mk
        mem_ref[1, 0, rows, :] = mv
        s = dot_nt(q, mk) * LOG2
        mask = segq == doc
        top = jnp.where(mask, jnp.max(s, axis=-1, keepdims=True), NEGATIVE)
        p = jnp.where(mask, jnp.exp2(s - top), 0.0)
        total = jnp.sum(p, axis=-1, keepdims=True)
        acc = dot_nn(p.astype(LOW), mv)
        shape = (QUERY_BLOCK, count)
        qpos = (2 * chip + parity) * count + b * QUERY_BLOCK + lax.broadcasted_iota(
            jnp.int32, shape, 0
        )

        def body(j, state):
            top, total, acc = state
            slot = tab[8 + j]
            s1 = dot_nt(q, own_ref[0, slot]) * LOG2
            s2 = dot_nt(q, oth_ref[0, slot]) * LOG2
            ok1 = allowed_keys(segq, sego_ref[j], qpos, (2 * j + parity) * count, shape)
            ok2 = allowed_keys(segq, segt_ref[j], qpos, (2 * j + 1 - parity) * count, shape)
            s1 = jnp.where(ok1, s1, NEGATIVE)
            s2 = jnp.where(ok2, s2, NEGATIVE)
            fresh = jnp.maximum(
                top, jnp.max(jnp.maximum(s1, s2), axis=-1, keepdims=True)
            )
            p1 = jnp.where(ok1, jnp.exp2(s1 - fresh), 0.0)
            p2 = jnp.where(ok2, jnp.exp2(s2 - fresh), 0.0)
            decay = jnp.exp2(top - fresh)
            total = total * decay + jnp.sum(p1 + p2, axis=-1, keepdims=True)
            acc = (
                acc * decay
                + dot_nn(p1.astype(LOW), own_ref[1, slot])
                + dot_nn(p2.astype(LOW), oth_ref[1, slot])
            )
            return fresh, total, acc

        top, total, acc = lax.fori_loop(tab[64 + i], chip + 1, body, (top, total, acc))
        out = acc / total
        o_ref[0, rows, :] = out
        low_ref[0, rows, :] = out.astype(LOW)
        lse_ref[0, rows, :] = top + jnp.log2(total)


def attend(tab, q, own, oth, segq, sego, segt, idx, ck, cv):
    count = q.shape[1]
    block = pl.BlockSpec((1, count, HEAD_DIM), lambda i, t: (i, 0, 0))
    thin = pl.BlockSpec((1, count, 1), lambda i, t: (i, 0, 0))
    whole = pl.BlockSpec((2, HEADS, count, HEAD_DIM), lambda i, t: (0, 0, 0, 0))
    segs = pl.BlockSpec((HEADS, 1, count), lambda i, t: (0, 0, 0))
    cache = pl.BlockSpec((ck.shape[0], HEAD_DIM), lambda i, t: (0, t[49]))
    mem = pl.BlockSpec((2, 1, count, HEAD_DIM), lambda i, t: (0, i, 0, 0))
    return pl.pallas_call(
        attend_kernel,
        grid_spec=pltpu.PrefetchScalarGridSpec(
            num_scalar_prefetch=1,
            grid=(HEADS,),
            in_specs=[block, whole, whole, thin, segs, segs, thin, cache, cache],
            out_specs=[block, block, thin, mem],
        ),
        out_shape=[
            jax.ShapeDtypeStruct((HEADS, count, HEAD_DIM), WIDE),
            jax.ShapeDtypeStruct((HEADS, count, HEAD_DIM), LOW),
            jax.ShapeDtypeStruct((HEADS, count, 1), WIDE),
            jax.ShapeDtypeStruct((2, HEADS, count, HEAD_DIM), LOW),
        ],
        cost_estimate=pl.CostEstimate(
            flops=4 * 10**9, bytes_accessed=6 * 2**20, transcendentals=3 * 10**6
        ),
        name="attend",
    )(tab, q, own, oth, segq, sego, segt, idx, ck, cv)


def attend_back_kernel(
    tab, q_ref, up_ref, o_ref, lse_ref, own_ref, oth_ref, mem_ref, segq_ref, sego_ref, segt_ref,
    dq_ref, down_ref, doth_ref, sum_ref,
):
    i = pl.program_id(0)

    @pl.when(i == 0)
    def _():
        sum_ref[...] = jnp.zeros_like(sum_ref)

    chip = tab[i]
    parity = tab[48]
    count = q_ref.shape[1]
    for b in range(count // QUERY_BLOCK):
        rows = pl.ds(b * QUERY_BLOCK, QUERY_BLOCK)
        q = q_ref[0, rows, :]
        up = up_ref[0, rows, :]
        lse = lse_ref[0, rows, :]
        segq = segq_ref[0, rows, :]
        delta = jnp.sum(up.astype(WIDE) * o_ref[0, rows, :], axis=-1, keepdims=True)
        doc = tab[16 + 2 * i + b]
        mk = mem_ref[0, 0, rows, :]
        mv = mem_ref[1, 0, rows, :]
        p = jnp.where(segq == doc, jnp.exp2(dot_nt(q, mk) * LOG2 - lse), 0.0)
        ds = (p * (dot_nt(up, mv) - delta)).astype(LOW)
        dq = dot_nn(ds, mk)
        shape = (QUERY_BLOCK, count)
        qpos = (2 * chip + parity) * count + b * QUERY_BLOCK + lax.broadcasted_iota(
            jnp.int32, shape, 0
        )

        def body(j, dq):
            slot = tab[8 + j]
            for side, ref, seg_ref, start in (
                (0, own_ref, sego_ref, (2 * j + parity) * count),
                (1, oth_ref, segt_ref, (2 * j + 1 - parity) * count),
            ):
                k = ref[0, slot]
                v = ref[1, slot]
                ok = allowed_keys(segq, seg_ref[j], qpos, start, shape)
                p = jnp.where(ok, jnp.exp2(dot_nt(q, k) * LOG2 - lse), 0.0)
                ds = (p * (dot_nt(up, v) - delta)).astype(LOW)
                sum_ref[side, 0, slot] += dot_tn(ds, q)
                sum_ref[side, 1, slot] += dot_tn(p.astype(LOW), up)
                dq = dq + dot_nn(ds, k)
            return dq

        dq_ref[0, rows, :] = lax.fori_loop(tab[64 + i], chip + 1, body, dq)

    @pl.when(i == HEADS - 1)
    def _():
        down_ref[...] = sum_ref[0]
        doth_ref[...] = sum_ref[1].astype(LOW)


def attend_back(tab, q, up, o, lse, own, oth, mem, segq, sego, segt):
    count = q.shape[1]
    block = pl.BlockSpec((1, count, HEAD_DIM), lambda i, t: (i, 0, 0))
    thin = pl.BlockSpec((1, count, 1), lambda i, t: (i, 0, 0))
    whole = pl.BlockSpec((2, HEADS, count, HEAD_DIM), lambda i, t: (0, 0, 0, 0))
    segs = pl.BlockSpec((HEADS, 1, count), lambda i, t: (0, 0, 0))
    memory = pl.BlockSpec((2, 1, count, HEAD_DIM), lambda i, t: (0, i, 0, 0))
    return pl.pallas_call(
        attend_back_kernel,
        grid_spec=pltpu.PrefetchScalarGridSpec(
            num_scalar_prefetch=1,
            grid=(HEADS,),
            in_specs=[block, block, block, thin, whole, whole, memory, thin, segs, segs],
            out_specs=[block, whole, whole],
            scratch_shapes=[pltpu.VMEM((2, 2, HEADS, count, HEAD_DIM), WIDE)],
        ),
        out_shape=[
            jax.ShapeDtypeStruct((HEADS, count, HEAD_DIM), WIDE),
            jax.ShapeDtypeStruct((2, HEADS, count, HEAD_DIM), WIDE),
            jax.ShapeDtypeStruct((2, HEADS, count, HEAD_DIM), LOW),
        ],
        cost_estimate=pl.CostEstimate(
            flops=10 * 10**9, bytes_accessed=10 * 2**20, transcendentals=3 * 10**6
        ),
        name="attend_back",
    )(tab, q, up, o, lse, own, oth, mem, segq, sego, segt)


def out_kernel(tab, heads_ref, w_ref, x_ref, gain_ref, att_ref, mid_ref, n_ref):
    for h in range(HEADS):
        att_ref[:, h * HEAD_DIM : (h + 1) * HEAD_DIM] = heads_ref[tab[h]]
    mid = x_ref[...].astype(WIDE) + dot_nn(att_ref[...], w_ref[...])
    mid_ref[...] = mid
    r = lax.rsqrt(jnp.mean(mid * mid, axis=-1, keepdims=True) + EPSILON)
    n_ref[...] = (mid * r * gain_ref[...].astype(WIDE)).astype(LOW)


def out_block(tab, heads, w, x, gain):
    count = x.shape[0]
    return pl.pallas_call(
        out_kernel,
        in_specs=[smem()] + [vmem()] * 4,
        out_specs=[vmem()] * 3,
        out_shape=[
            jax.ShapeDtypeStruct((count, D), LOW),
            jax.ShapeDtypeStruct((count, D), WIDE),
            jax.ShapeDtypeStruct((count, D), LOW),
        ],
        cost_estimate=pl.CostEstimate(
            flops=2 * count * D * D, bytes_accessed=4 * 2**20, transcendentals=0
        ),
        name="out_block",
    )(tab, heads, w, x, gain)


def ffn_kernel(na, nb, ga, gb, g_ref, u_ref, d_ref, hid_ref, gg_ref, ug_ref, dn_ref):
    for t, (n_ref, c_ref) in enumerate(((na, ga), (nb, gb))):
        n = n_ref[...]
        gate = dot_nn(n, g_ref[...])
        upper = dot_nn(n, u_ref[...])
        sigma = jax.nn.sigmoid(gate)
        silu = gate * sigma
        hid_ref[t] = (silu * upper).astype(LOW)
        hg = dot_nt(c_ref[...], d_ref[...])
        gg = (hg * upper * sigma * (1.0 + gate * (1.0 - sigma))).astype(LOW)
        ug = (hg * silu).astype(LOW)
        gg_ref[t] = gg
        ug_ref[t] = ug
        dn_ref[t] = (dot_nt(gg, g_ref[...]) + dot_nt(ug, u_ref[...])).astype(LOW)


def ffn(na, nb, ga, gb, g, u, d):
    count = na.shape[0]
    units = g.shape[1]
    return pl.pallas_call(
        ffn_kernel,
        in_specs=[vmem()] * 7,
        out_specs=[vmem()] * 4,
        out_shape=[jax.ShapeDtypeStruct((2, count, units), LOW)] * 3
        + [jax.ShapeDtypeStruct((2, count, D), LOW)],
        cost_estimate=pl.CostEstimate(
            flops=20 * count * D * units,
            bytes_accessed=6 * D * units + 16 * count * D,
            transcendentals=2 * count * units,
        ),
        name="ffn",
    )(na, nb, ga, gb, g, u, d)


def mid_kernel(tab, mid_ref, pa, pb, pc, up_ref, gain_ref, w_ref, mg_ref, bg_ref, ag_ref):
    mid = mid_ref[...]
    scaled = (pa[...].astype(WIDE) + pb[...].astype(WIDE) + pc[...].astype(WIDE)) * gain_ref[
        ...
    ].astype(WIDE)
    r = lax.rsqrt(jnp.mean(mid * mid, axis=-1, keepdims=True) + EPSILON)
    inner = jnp.mean(scaled * mid, axis=-1, keepdims=True)
    mid_grad = up_ref[...].astype(WIDE) + r * scaled - mid * (r * r * r * inner)
    mg_ref[...] = mid_grad
    branch = mid_grad.astype(LOW)
    bg_ref[...] = branch
    att = dot_nt(branch, w_ref[...]).astype(LOW)
    for h in range(HEADS):
        ag_ref[tab[h]] = att[:, h * HEAD_DIM : (h + 1) * HEAD_DIM]


def mid_block(tab, mid, pa, pb, pc, up, gain, w):
    count = mid.shape[0]
    return pl.pallas_call(
        mid_kernel,
        in_specs=[smem()] + [vmem()] * 7,
        out_specs=[vmem()] * 3,
        out_shape=[
            jax.ShapeDtypeStruct((count, D), WIDE),
            jax.ShapeDtypeStruct((count, D), LOW),
            jax.ShapeDtypeStruct((HEADS, count, HEAD_DIM), LOW),
        ],
        cost_estimate=pl.CostEstimate(
            flops=2 * count * D * D, bytes_accessed=6 * 2**20, transcendentals=0
        ),
        name="mid_block",
    )(tab, mid, pa, pb, pc, up, gain, w)


def qkv_back_kernel(dq_ref, own_ref, got_ref, cos_ref, sin_ref, n_ref, w_ref, dx_ref, dw_ref, sum_ref):
    i = pl.program_id(0)

    @pl.when(i == 0)
    def _():
        sum_ref[...] = jnp.zeros_like(sum_ref)

    c, s = cos_ref[0], sin_ref[0]

    def rot(v):
        return v * c - pltpu.roll(v, HEAD_DIM // 2, 1) * s

    dq = rot(dq_ref[0] * SCALE).astype(LOW)
    dk = rot((own_ref[0, 0] + got_ref[0, 0].astype(WIDE)) * SCALE).astype(LOW)
    dv = (own_ref[1, 0] + got_ref[1, 0].astype(WIDE)).astype(LOW)
    grads = jnp.concatenate([dq, dk, dv], axis=1)
    dx_ref[0] = dot_nt(grads, w_ref[...]).astype(LOW)
    sum_ref[...] += dot_tn(n_ref[0], grads)

    @pl.when(i == HEADS - 1)
    def _():
        dw_ref[...] = sum_ref[...].astype(LOW)


def qkv_back(dq, own, got, cos, sin, normed, w):
    count = dq.shape[1]
    block = pl.BlockSpec((1, count, HEAD_DIM), lambda i: (i, 0, 0))
    pair = pl.BlockSpec((2, 1, count, HEAD_DIM), lambda i: (0, i, 0, 0))
    wide = pl.BlockSpec((1, count, D), lambda i: (i, 0, 0))
    weight = pl.BlockSpec((D, 3 * HEAD_DIM), lambda i: (0, 0))
    return pl.pallas_call(
        qkv_back_kernel,
        grid=(HEADS,),
        in_specs=[block, pair, pair, block, block, wide, weight],
        out_specs=[wide, weight],
        scratch_shapes=[pltpu.VMEM((D, 3 * HEAD_DIM), WIDE)],
        out_shape=[
            jax.ShapeDtypeStruct((HEADS, count, D), LOW),
            jax.ShapeDtypeStruct((D, 3 * HEAD_DIM), LOW),
        ],
        cost_estimate=pl.CostEstimate(
            flops=4 * HEADS * count * D * 3 * HEAD_DIM,
            bytes_accessed=4 * HEADS * count * D,
            transcendentals=0,
        ),
        name="qkv_back",
    )(dq, own, got, cos, sin, normed, w)


def local(
    far,
    tokens,
    segment_ids,
    second_doc,
    memory_index,
    cache_keys,
    cache_values,
    first_gain,
    query_weight,
    key_weight,
    value_weight,
    out_weight,
    second_gain,
    gate_weight,
    up_weight,
    down_weight,
    cotangent,
):
    x = tokens[0]
    upstream = cotangent[0]
    count = x.shape[0]
    blocks = count // QUERY_BLOCK
    rows = query_weight.shape[0]
    share = down_weight.shape[0]
    units = far * HEADS * share
    chip, core, pair = lax.axis_index("h"), lax.axis_index("c"), lax.axis_index("dl")
    mine = jnp.where(chip % 2 == 0, chip // 2, HEADS - 1 - chip // 2)
    slots = jnp.arange(HEADS, dtype=jnp.int32)
    chips = at_place(mine - slots)
    group = ("dh", "h") if far > 1 else "h"

    forth, back = [x], [x]
    for step in range(HEADS // 2):
        forth.append(turn(forth[-1], 1))
        if step < HEADS // 2 - 1:
            back.append(turn(back[-1], -1))
    x_slots = forth + back[:0:-1]

    def by_head(w):
        return w.reshape(rows, HEADS, HEAD_DIM).transpose(1, 0, 2)

    picked = memory_index[0].transpose(1, 0, 2)
    seg_rows = jnp.broadcast_to(
        segment_ids[0].astype(LOW).reshape(1, blocks, QUERY_BLOCK), (HEADS, blocks, QUERY_BLOCK)
    )
    gains = jnp.concatenate([first_gain, second_gain])
    gain_rows = jnp.broadcast_to(
        jnp.pad(gains, (0, HEAD_DIM - 2 * rows)).reshape(1, 1, HEAD_DIM), (HEADS, 1, HEAD_DIM)
    )
    pack = jnp.concatenate(
        [
            by_head(query_weight),
            by_head(key_weight),
            by_head(value_weight),
            seg_rows,
            (picked // MEM_ROWS).astype(LOW),
            (picked % MEM_ROWS).astype(LOW),
            gain_rows,
        ],
        axis=1,
    )
    height = pack.shape[1]
    pack = jnp.pad(pack, ((0, 0), (0, -height % 16), (0, 0)))
    pack = to_ahead(pack, mine)
    got = jnp.stack([pack[0]] + [turn(pack[d], d) for d in range(1, HEADS)])
    got_c = swap(got, "c")
    got_y = swap(got, "dl")
    got_yc = swap(got_y, "c")
    near = pick(core, jnp.stack([got, got_c]), jnp.stack([got_c, got]))
    away = pick(core, jnp.stack([got_y, got_yc]), jnp.stack([got_yc, got_y]))
    every = pick(pair, jnp.stack([near, away]), jnp.stack([away, near]))
    every = every.transpose(2, 0, 1, 3, 4)
    every = from_behind(every, mine)
    if far > 1:
        every = lax.all_gather(every, "dh", axis=0)
    else:
        every = every[None]
    every = every.transpose(0, 2, 1, 3, 4, 5)
    w_qkv = jnp.concatenate(
        [every[..., i * rows : (i + 1) * rows, :].reshape(D, HEAD_DIM) for i in range(3)], axis=1
    )
    gain_all = every[..., 3 * rows + 3 * blocks, : 2 * rows].reshape(-1, 2, rows)
    gain_one = gain_all[:, 0].reshape(1, D)
    gain_two = gain_all[:, 1].reshape(1, D)

    def seg_of(blocks_of):
        return (
            blocks_of[:, 3 * rows : 3 * rows + blocks]
            .astype(WIDE)
            .astype(jnp.int32)
            .reshape(HEADS, count)
        )

    seg_own_slots = seg_of(got)
    seg_own = from_behind(seg_own_slots, mine)
    seg_oth = from_behind(seg_of(got_c), mine)
    seg_all = pick(core, jnp.stack([seg_own, seg_oth], 1), jnp.stack([seg_oth, seg_own], 1))
    idx = (
        got[:, 3 * rows + blocks : 3 * rows + 2 * blocks].astype(WIDE) * MEM_ROWS
        + got[:, 3 * rows + 2 * blocks : 3 * rows + 3 * blocks].astype(WIDE)
    ).astype(jnp.int32)
    idx = idx.reshape(HEADS, count, 1)

    block_docs = seg_own_slots[:, ::QUERY_BLOCK]
    docs = second_doc.shape[1]
    doc_ids = jnp.arange(docs, dtype=jnp.int32)
    mates = jnp.sum(
        jnp.where(block_docs[:, :, None] == doc_ids, second_doc[0][None, None, :], 0), axis=-1
    )
    before = jnp.sum(
        (seg_all.reshape(1, -1) < block_docs[:, :1]).astype(jnp.int32), axis=1
    )
    places = jnp.asarray(PLACE, jnp.int32)
    tab = jnp.concatenate(
        [
            chips,
            lax.rem(mine - places + HEADS, HEADS),
            block_docs.reshape(-1),
            mates.reshape(-1),
            jnp.stack([core, chip]),
            jnp.zeros((14,), jnp.int32),
            before // (2 * count),
        ]
    ).astype(jnp.int32)
    ahead_of = lax.rem(places - mine + HEADS, HEADS).astype(jnp.int32)

    half = HEAD_DIM // 2
    freqs = 10000.0 ** (-jnp.arange(half, dtype=WIDE) * 2.0 / (2 * half))
    positions = ((2 * chips + core) * count)[:, None] + jnp.arange(count, dtype=jnp.int32)[None]
    turned = positions.astype(WIDE)[:, :, None] * freqs
    cosine, sine = jnp.cos(turned), jnp.sin(turned)
    cosine = jnp.concatenate([cosine, cosine], axis=-1)
    sine = jnp.concatenate([-sine, sine], axis=-1)

    def by_owner(w):
        return w.reshape(rows, far, 2, HEADS, 2, share).transpose(2, 4, 0, 1, 3, 5).reshape(
            2, 2, rows, units
        )

    gu = jnp.concatenate([by_owner(gate_weight), by_owner(up_weight)], axis=-1)
    kept = pick(core, gu[:, 0], gu[:, 1])
    came = swap(pick(core, gu[:, 1], gu[:, 0]), "c")
    gu = pick(core, jnp.stack([kept, came], 1), jnp.stack([came, kept], 1))
    kept = pick(pair, gu[0], gu[1])
    came = swap(pick(pair, gu[1], gu[0]), "dl")
    gu = pick(pair, jnp.stack([kept, came]), jnp.stack([came, kept])).reshape(4 * rows, 2 * units)
    wide = 2 * units
    third = wide - D
    pieces = [out_weight[:, i * third : (i + 1) * third] for i in range(-(-D // third))]
    pieces[-1] = jnp.pad(pieces[-1], ((0, 0), (0, third - pieces[-1].shape[1])))
    pieces = jnp.concatenate(pieces, axis=0)
    deep = max(share, pieces.shape[0])
    lower = jnp.concatenate(
        [
            jnp.pad(down_weight, ((0, deep - share), (0, 0))),
            jnp.pad(pieces, ((0, deep - pieces.shape[0]), (0, 0))),
        ],
        axis=1,
    )
    gathered = lax.all_gather(jnp.concatenate([gu, lower], axis=0), group, axis=0)
    gathered = gathered.reshape(far, HEADS, 4 * rows + deep, wide)
    gu_w = (
        gathered[:, :, : 4 * rows]
        .reshape(far, HEADS, 2, 2 * rows, wide)
        .transpose(0, 2, 1, 3, 4)
        .reshape(D, wide)
    )
    gate_w, up_w = gu_w[:, :units], gu_w[:, units:]
    down_w = gathered[:, :, 4 * rows : 4 * rows + share, :D].reshape(units, D)
    outs = gathered[:, :, 4 * rows :, D:]
    outs = jnp.concatenate(
        [outs[:, :, i * rows : (i + 1) * rows] for i in range(pieces.shape[0] // rows)], axis=-1
    )[..., :D]
    outs_c = swap(outs, "c")
    outs_y = swap(outs, "dl")
    outs_yc = swap(outs_y, "c")
    near = pick(core, jnp.stack([outs, outs_c], 2), jnp.stack([outs_c, outs], 2))
    away = pick(core, jnp.stack([outs_y, outs_yc], 2), jnp.stack([outs_yc, outs_y], 2))
    out_w = pick(pair, jnp.stack([near, away], 1), jnp.stack([away, near], 1)).reshape(D, D)

    up_c = swap(upstream, "c")
    up_y = swap(upstream, "dl")
    up_yc = swap(up_y, "c")

    order = [0]
    for step in range(1, HEADS // 2 + 1):
        order += [step] if step == HEADS // 2 else [step, HEADS - step]
    held = ()
    for slot in order:
        held = qkv_block(slot, x_slots[slot], gain_one, w_qkv, cosine, sine, held)
    queries, own, normed_one = held
    other = swap(own, "c")

    seg_thin = seg_own_slots.reshape(HEADS, count, 1)
    seg_own_row = seg_own.reshape(HEADS, 1, count)
    seg_oth_row = seg_oth.reshape(HEADS, 1, count)
    attention, attention_low, lse, memory = attend(
        tab,
        queries,
        own,
        other,
        seg_thin,
        seg_own_row,
        seg_oth_row,
        idx,
        cache_keys[0].reshape(-1, D),
        cache_values[0].reshape(-1, D),
    )

    heads = jnp.stack(
        [attention_low[0]] + [turn(attention_low[d], -d) for d in range(1, HEADS)]
    )
    attended, mid, normed_two = out_block(ahead_of, heads, out_w, x, gain_two)

    n_c = swap(normed_two, "c")
    n_y = swap(normed_two, "dl")
    n_yc = swap(n_y, "c")
    hid_l, gg_l, ug_l, dn_l = ffn(normed_two, n_c, upstream, up_c, gate_w, up_w, down_w)
    hid_r, gg_r, ug_r, dn_r = ffn(n_y, n_yc, up_y, up_yc, gate_w, up_w, down_w)

    def sum_back(near, away):
        there = (away[0].astype(WIDE) + swap(away[1], "c").astype(WIDE)).astype(LOW)
        return near[0], swap(near[1], "c"), swap(there, "dl")

    parts = sum_back(dn_l, dn_r)
    mid_grad, branch, att_grad = mid_block(
        ahead_of, mid, *parts, upstream, gain_two, out_w
    )

    def over_tokens(a, b):
        return jnp.einsum("gtd,gtf->df", a, b, preferred_element_type=WIDE)

    n_l, n_r = jnp.stack([normed_two, n_c]), jnp.stack([n_y, n_yc])
    u_l, u_r = jnp.stack([upstream, up_c]), jnp.stack([up_y, up_yc])
    gate_part = (over_tokens(n_l, gg_l) + over_tokens(n_r, gg_r)).astype(LOW)
    up_part = (over_tokens(n_l, ug_l) + over_tokens(n_r, ug_r)).astype(LOW)
    down_part = (over_tokens(hid_l, u_l) + over_tokens(hid_r, u_r)).astype(LOW)

    def by_rows(w):
        return (
            w.reshape(far, 2, HEADS, 2 * rows, units)
            .transpose(0, 2, 1, 3, 4)
            .reshape(far * HEADS, 4 * rows, units)
        )

    height = 4 * rows + share
    height += -height % 16
    parts = jnp.concatenate(
        [
            jnp.concatenate([by_rows(gate_part), by_rows(up_part)], axis=-1),
            jnp.pad(
                down_part.reshape(far * HEADS, share, D),
                ((0, 0), (0, height - 4 * rows - share), (0, wide - D)),
            ),
        ],
        axis=1,
    )
    summed = lax.psum_scatter(
        parts.reshape(far * HEADS * height, wide), group, scatter_dimension=0, tiled=True
    )
    down_w_grad = summed[4 * rows : 4 * rows + share, :D].astype(WIDE)
    gu = summed[: 4 * rows].reshape(2, 2, rows, wide)
    kept = pick(core, gu[:, 0], gu[:, 1])
    came = swap(pick(core, gu[:, 1], gu[:, 0]), "c")
    gu = pick(core, jnp.stack([kept, came], 1), jnp.stack([came, kept], 1))
    kept = pick(pair, gu[0], gu[1])
    came = swap(pick(pair, gu[1], gu[0]), "dl")
    gu = pick(pair, jnp.stack([kept, came]), jnp.stack([came, kept]))
    gu = (
        gu.reshape(2, 2, rows, 2, far, HEADS, share)
        .transpose(3, 2, 4, 0, 5, 1, 6)
        .reshape(2, rows, FF)
        .astype(WIDE)
    )
    gate_w_grad, up_w_grad = gu[0], gu[1]

    out_l = jnp.einsum("gtf,fd->gtd", hid_l, down_w, preferred_element_type=WIDE).astype(LOW)
    out_r = jnp.einsum("gtf,fd->gtd", hid_r, down_w, preferred_element_type=WIDE).astype(LOW)
    output = mid
    for part in sum_back(out_l, out_r):
        output = output + part.astype(WIDE)
    output = output.astype(LOW)

    def to_owners(w, width):
        w = w.reshape(far, 2, HEADS, 2, rows, width)
        kept = pick(core, w[:, :, :, 0], w[:, :, :, 1])
        came = swap(pick(core, w[:, :, :, 1], w[:, :, :, 0]), "c")
        w = kept.astype(WIDE) + came.astype(WIDE)
        kept = pick(pair, w[:, 0], w[:, 1])
        came = swap(pick(pair, w[:, 1], w[:, 0]).astype(LOW), "dl")
        w = (kept + came.astype(WIDE)).astype(LOW)
        if far > 1:
            w = lax.psum_scatter(w, "dh", scatter_dimension=0, tiled=True)
        w = to_ahead(w[0], mine)
        return [w[0]] + [turn(w[d], d) for d in range(1, HEADS)]

    out_part = jnp.einsum("td,te->de", attended, branch, preferred_element_type=WIDE).astype(LOW)
    out_w_grad = functools.reduce(
        lambda a, b: a + b, [w.astype(WIDE) for w in to_owners(out_part, D)]
    )

    ups = jnp.stack([att_grad[0]] + [turn(att_grad[d], d) for d in range(1, HEADS)])
    dq, d_own, d_oth = attend_back(
        tab, queries, ups, attention, lse, own, other, memory, seg_thin, seg_own_row, seg_oth_row
    )
    d_got = swap(d_oth, "c")
    dx, dw = qkv_back(dq, d_own, d_got, cosine, sine, normed_one, w_qkv)

    forth = dx[HEADS // 2]
    for slot in range(HEADS // 2 + 1, HEADS):
        forth = (turn(forth, 1).astype(WIDE) + dx[slot].astype(WIDE)).astype(LOW)
    forth = turn(forth, 1)
    back = dx[HEADS // 2 - 1]
    for slot in range(HEADS // 2 - 2, 0, -1):
        back = (turn(back, -1).astype(WIDE) + dx[slot].astype(WIDE)).astype(LOW)
    back = turn(back, -1)
    normed_one_grad = dx[0].astype(WIDE) + forth.astype(WIDE) + back.astype(WIDE)

    wide_x = x.astype(WIDE)
    r = lax.rsqrt(jnp.mean(wide_x * wide_x, axis=-1, keepdims=True) + EPSILON)
    scaled = normed_one_grad * gain_one.astype(WIDE)
    inner = jnp.mean(scaled * wide_x, axis=-1, keepdims=True)
    input_grad = mid_grad + r * scaled - wide_x * (r * r * r * inner)

    qkv_grads = from_behind(jnp.stack(to_owners(dw, 3 * HEAD_DIM)), mine).astype(WIDE)
    q_w_grad, k_w_grad, v_w_grad = (
        qkv_grads[:, :, i * HEAD_DIM : (i + 1) * HEAD_DIM].transpose(1, 0, 2).reshape(rows, D)
        for i in range(3)
    )

    def gain_grad(gain, pairs):
        total = 0.0
        for grad, weight in pairs:
            total = total + jnp.sum(grad * weight.astype(WIDE), axis=1)
        return total / gain.astype(WIDE)

    first_gain_grad = gain_grad(
        first_gain,
        ((q_w_grad, query_weight), (k_w_grad, key_weight), (v_w_grad, value_weight)),
    )
    second_gain_grad = gain_grad(
        second_gain, ((gate_w_grad, gate_weight), (up_w_grad, up_weight))
    )
    return (
        output[None],
        input_grad[None],
        first_gain_grad,
        q_w_grad,
        k_w_grad,
        v_w_grad,
        out_w_grad,
        second_gain_grad,
        gate_w_grad,
        up_w_grad,
        down_w_grad,
    )


def solution(mesh):
    far = mesh.shape["dp"] // 2
    cores = mesh.shape["seq"] // HEADS
    fine = Mesh(mesh.devices.reshape(far, 2, HEADS, cores), ("dh", "dl", "h", "c"))
    dp, seq, every = ("dh", "dl"), ("h", "c"), ("dh", "dl", "h", "c")
    rows = P(every, None)
    return jax.shard_map(
        functools.partial(local, far),
        mesh=fine,
        in_specs=(
            P(dp, seq, None),
            P(dp, seq),
            P(dp, None),
            P(dp, seq, None, None),
            P(dp, None, None, None),
            P(dp, None, None, None),
            P(every),
            rows,
            rows,
            rows,
            rows,
            P(every),
            rows,
            rows,
            rows,
            P(dp, seq, None),
        ),
        out_specs=(
            P(dp, seq, None),
            P(dp, seq, None),
            P(every),
            rows,
            rows,
            rows,
            rows,
            P(every),
            rows,
            rows,
            rows,
        ),
        check_vma=False,
    )
```

```python
import functools
import math

import jax
import jax.numpy as jnp
from jax import lax
from jax.experimental import pallas as pl
from jax.experimental.pallas import tpu as pltpu
from jax.sharding import Mesh
from jax.sharding import PartitionSpec as P

D = 1024
FF = 2816
HEADS = 8
HEAD_DIM = 128
QUERY_BLOCK = 128
MEM_ROWS = 256
EPSILON = 1e-05
NEGATIVE = -1e30
SCALE = 1.0 / math.sqrt(HEAD_DIM)
LOG2 = SCALE * math.log2(math.e)
LOW = jnp.bfloat16
WIDE = jnp.float32

RING = [2 * i for i in range(HEADS // 2)] + [2 * i + 1 for i in reversed(range(HEADS // 2))]


def dot_nn(a, b):
    return lax.dot_general(a, b, (((1,), (0,)), ((), ())), preferred_element_type=WIDE)


def dot_nt(a, b):
    return lax.dot_general(a, b, (((1,), (1,)), ((), ())), preferred_element_type=WIDE)


def dot_tn(a, b):
    return lax.dot_general(a, b, (((0,), (0,)), ((), ())), preferred_element_type=WIDE)


def swap(block, axis):
    return lax.ppermute(block, axis, [(0, 1), (1, 0)])


def turn(block, distance):
    route = [(RING[i], RING[(i + distance) % HEADS]) for i in range(HEADS)]
    return lax.ppermute(block, "h", route)


def at_place(place):
    place = lax.rem(place + 2 * HEADS, HEADS)
    return jnp.where(place < HEADS // 2, 2 * place, 2 * (HEADS - 1 - place) + 1)


def exchange(blocks):
    return lax.all_to_all(blocks, "h", 0, 0)


def pick(flag, first, second):
    return jnp.where(flag == 0, first, second)


def vmem():
    return pl.BlockSpec(memory_space=pltpu.VMEM)


def qkv_kernel(parts, tab, *refs):
    xs, (gain_ref, w_ref, cos_ref, sin_ref) = refs[: sum(parts)], refs[sum(parts) : sum(parts) + 4]
    q_ref, kv_ref, n_ref, x_ref = refs[-4:]
    i = pl.program_id(0)
    first = 0
    for step, number in enumerate(parts):

        @pl.when(i == step)
        def _(blocks=xs[first : first + number]):
            row = 0
            for block in blocks:
                x_ref[row : row + block.shape[0], :] = block[...]
                row += block.shape[0]

        first += number
    x = x_ref[...].astype(WIDE)
    r = lax.rsqrt(jnp.mean(x * x, axis=-1, keepdims=True) + EPSILON)
    normed = (x * r * gain_ref[...].astype(WIDE)).astype(LOW)
    n_ref[0] = normed
    out = dot_nn(normed, w_ref[...])
    c, s = cos_ref[0], sin_ref[0]

    def rot(v):
        return v * c + pltpu.roll(v, HEAD_DIM // 2, 1) * s

    q_ref[0] = rot(out[:, :HEAD_DIM]).astype(LOW)
    kv_ref[0, 0] = rot(out[:, HEAD_DIM : 2 * HEAD_DIM]).astype(LOW)
    kv_ref[1, 0] = out[:, 2 * HEAD_DIM :].astype(LOW)


def qkv_blocks(chips, xs, gain, w, cos, sin, held):
    count = cos.shape[1]
    flat = [piece for block in xs for piece in block]

    def whole(shape):
        return pl.BlockSpec(shape, lambda i, t: (0, 0))

    def block(*shape):
        return pl.BlockSpec((1, *shape), lambda i, t: (t[i], 0, 0))

    spec = pltpu.PrefetchScalarGridSpec(
        num_scalar_prefetch=1,
        grid=(len(xs),),
        in_specs=[whole(piece.shape) for piece in flat]
        + [whole((1, D)), whole((D, 3 * HEAD_DIM)), block(count, HEAD_DIM), block(count, HEAD_DIM)]
        + [pl.BlockSpec(memory_space=pl.ANY)] * len(held),
        out_specs=[
            block(count, HEAD_DIM),
            pl.BlockSpec((2, 1, count, HEAD_DIM), lambda i, t: (0, t[i], 0, 0)),
            block(count, D),
        ],
        scratch_shapes=[pltpu.VMEM((count, D), LOW)],
    )
    return pl.pallas_call(
        functools.partial(qkv_kernel, [len(block) for block in xs]),
        grid_spec=spec,
        out_shape=[
            jax.ShapeDtypeStruct((HEADS, count, HEAD_DIM), LOW),
            jax.ShapeDtypeStruct((2, HEADS, count, HEAD_DIM), LOW),
            jax.ShapeDtypeStruct((HEADS, count, D), LOW),
        ],
        input_output_aliases={len(flat) + 5 + i: i for i in range(len(held))},
        cost_estimate=pl.CostEstimate(
            flops=2 * len(xs) * count * D * 3 * HEAD_DIM,
            bytes_accessed=5 * len(xs) * count * D,
            transcendentals=0,
        ),
        name=f"qkv{len(xs)}",
    )(chips, *flat, gain, w, cos, sin, *held)


def causal(count):
    rows = lax.broadcasted_iota(jnp.int32, (count, count), 0)
    return lax.broadcasted_iota(jnp.int32, (count, count), 1) <= rows


def attend_kernel(
    tab, q_ref, own_ref, oth_ref, segq_ref, sego_ref, segt_ref, idx_ref, ck_ref, cv_ref,
    o_ref, low_ref, lse_ref, mem_ref,
):
    i = pl.program_id(0)
    parity = tab[40]
    count = q_ref.shape[1]
    q = q_ref[0]
    segq = segq_ref[0]

    s1 = dot_nt(q, own_ref[0, i]) * LOG2
    s2 = dot_nt(q, oth_ref[0, i]) * LOG2
    s1 = jnp.where((sego_ref[i] == segq) & causal(count), s1, NEGATIVE)
    s2 = jnp.where(segt_ref[i] == segq + 64 * (1 - parity), s2, NEGATIVE)
    memory = []
    for b in range(count // QUERY_BLOCK):
        rows = slice(b * QUERY_BLOCK, (b + 1) * QUERY_BLOCK)
        doc = tab[2 * i + b]
        mate = tab[16 + 2 * i + b]
        idx = idx_ref[0, rows, :]
        lane = lax.broadcasted_iota(jnp.int32, (QUERY_BLOCK, MEM_ROWS), 1)
        first = jnp.where(idx == lane, 1.0, 0.0).astype(LOW)
        second = jnp.where(idx == lane + MEM_ROWS, 1.0, 0.0).astype(LOW)
        here = pl.ds(pl.multiple_of(doc * MEM_ROWS, MEM_ROWS), MEM_ROWS)
        there = pl.ds(pl.multiple_of(mate * MEM_ROWS, MEM_ROWS), MEM_ROWS)
        mk = (dot_nn(first, ck_ref[here, :]) + dot_nn(second, ck_ref[there, :])).astype(LOW)
        mv = (dot_nn(first, cv_ref[here, :]) + dot_nn(second, cv_ref[there, :])).astype(LOW)
        mem_ref[0, 0, rows, :] = mk
        mem_ref[1, 0, rows, :] = mv
        s = jnp.where(segq[rows] == doc, dot_nt(q[rows], mk) * LOG2, NEGATIVE)
        memory.append((s, mv))
    sm = jnp.concatenate([s for s, _ in memory], axis=0)
    top = jnp.maximum(
        jnp.max(jnp.maximum(s1, s2), axis=-1, keepdims=True), jnp.max(sm, axis=-1, keepdims=True)
    )
    p1 = jnp.exp2(s1 - top)
    p2 = jnp.exp2(s2 - top)
    pm = jnp.exp2(sm - top)
    total = jnp.sum(p1 + p2, axis=-1, keepdims=True) + jnp.sum(pm, axis=-1, keepdims=True)
    pm = pm.astype(LOW)
    acc = jnp.concatenate(
        [
            dot_nn(pm[b * QUERY_BLOCK : (b + 1) * QUERY_BLOCK], mv)
            for b, (_, mv) in enumerate(memory)
        ],
        axis=0,
    )
    acc = acc + dot_nn(p1.astype(LOW), own_ref[1, i]) + dot_nn(p2.astype(LOW), oth_ref[1, i])

    def body(j, state):
        top, total, acc = state
        s1 = dot_nt(q, own_ref[0, j]) * LOG2
        s2 = dot_nt(q, oth_ref[0, j]) * LOG2
        s1 = jnp.where(sego_ref[j] == segq, s1, NEGATIVE)
        s2 = jnp.where(segt_ref[j] == segq, s2, NEGATIVE)
        fresh = jnp.maximum(top, jnp.max(jnp.maximum(s1, s2), axis=-1, keepdims=True))
        p1 = jnp.exp2(s1 - fresh)
        p2 = jnp.exp2(s2 - fresh)
        decay = jnp.exp2(top - fresh)
        total = total * decay + jnp.sum(p1 + p2, axis=-1, keepdims=True)
        acc = (
            acc * decay
            + dot_nn(p1.astype(LOW), own_ref[1, j])
            + dot_nn(p2.astype(LOW), oth_ref[1, j])
        )
        return fresh, total, acc

    top, total, acc = lax.fori_loop(tab[32 + i], i, body, (top, total, acc))
    out = acc / total
    o_ref[0] = out
    low_ref[0] = out.astype(LOW)
    lse_ref[0] = top + jnp.log2(total)


def attend(tab, q, own, oth, segq, sego, segt, idx, ck, cv):
    count = q.shape[1]
    block = pl.BlockSpec((1, count, HEAD_DIM), lambda i, t: (i, 0, 0))
    thin = pl.BlockSpec((1, count, 1), lambda i, t: (i, 0, 0))
    whole = pl.BlockSpec((2, HEADS, count, HEAD_DIM), lambda i, t: (0, 0, 0, 0))
    segs = pl.BlockSpec((HEADS, 1, count), lambda i, t: (0, 0, 0))
    cache = pl.BlockSpec((ck.shape[0], HEAD_DIM), lambda i, t: (0, t[41]))
    mem = pl.BlockSpec((2, 1, count, HEAD_DIM), lambda i, t: (0, i, 0, 0))
    return pl.pallas_call(
        attend_kernel,
        grid_spec=pltpu.PrefetchScalarGridSpec(
            num_scalar_prefetch=1,
            grid=(HEADS,),
            in_specs=[block, whole, whole, thin, segs, segs, thin, cache, cache],
            out_specs=[block, block, thin, mem],
        ),
        out_shape=[
            jax.ShapeDtypeStruct((HEADS, count, HEAD_DIM), WIDE),
            jax.ShapeDtypeStruct((HEADS, count, HEAD_DIM), LOW),
            jax.ShapeDtypeStruct((HEADS, count, 1), WIDE),
            jax.ShapeDtypeStruct((2, HEADS, count, HEAD_DIM), LOW),
        ],
        cost_estimate=pl.CostEstimate(
            flops=25 * 10**9, bytes_accessed=6 * 2**20, transcendentals=3 * 10**6
        ),
        name="attend",
    )(tab, q, own, oth, segq, sego, segt, idx, ck, cv)


def attend_back_kernel(
    tab, q_ref, up_ref, o_ref, lse_ref, own_ref, oth_ref, mem_ref, segq_ref, sego_ref, segt_ref,
    dq_ref, down_ref, doth_ref, sum_ref,
):
    i = pl.program_id(0)

    @pl.when(i == 0)
    def _():
        sum_ref[...] = jnp.zeros_like(sum_ref)

    parity = tab[40]
    count = q_ref.shape[1]
    q = q_ref[0]
    up = up_ref[0]
    lse = lse_ref[0]
    segq = segq_ref[0]
    delta = jnp.sum(up.astype(WIDE) * o_ref[0], axis=-1, keepdims=True)
    partial = []
    for b in range(count // QUERY_BLOCK):
        rows = slice(b * QUERY_BLOCK, (b + 1) * QUERY_BLOCK)
        mk = mem_ref[0, 0, rows, :]
        mv = mem_ref[1, 0, rows, :]
        ok = segq[rows] == tab[2 * i + b]
        p = jnp.exp2(jnp.where(ok, dot_nt(q[rows], mk) * LOG2 - lse[rows], NEGATIVE))
        ds = (p * (dot_nt(up[rows], mv) - delta[rows])).astype(LOW)
        partial.append(dot_nn(ds, mk))

    def tile(side, ref, j, ok, dq):
        k = ref[0, j]
        v = ref[1, j]
        p = jnp.exp2(jnp.where(ok, dot_nt(q, k) * LOG2 - lse, NEGATIVE))
        ds = (p * (dot_nt(up, v) - delta)).astype(LOW)
        sum_ref[side, 0, j] += dot_tn(ds, q)
        sum_ref[side, 1, j] += dot_tn(p.astype(LOW), up)
        return dq + dot_nn(ds, k)

    dq = jnp.concatenate(partial, axis=0)
    dq = tile(0, own_ref, i, (sego_ref[i] == segq) & causal(count), dq)
    dq = tile(1, oth_ref, i, segt_ref[i] == segq + 64 * (1 - parity), dq)

    def body(j, dq):
        dq = tile(0, own_ref, j, sego_ref[j] == segq, dq)
        return tile(1, oth_ref, j, segt_ref[j] == segq, dq)

    dq_ref[0] = lax.fori_loop(tab[32 + i], i, body, dq)

    @pl.when(i == HEADS - 1)
    def _():
        down_ref[...] = sum_ref[0]
        doth_ref[...] = sum_ref[1].astype(LOW)


def attend_back(tab, q, up, o, lse, own, oth, mem, segq, sego, segt):
    count = q.shape[1]
    block = pl.BlockSpec((1, count, HEAD_DIM), lambda i, t: (i, 0, 0))
    thin = pl.BlockSpec((1, count, 1), lambda i, t: (i, 0, 0))
    whole = pl.BlockSpec((2, HEADS, count, HEAD_DIM), lambda i, t: (0, 0, 0, 0))
    segs = pl.BlockSpec((HEADS, 1, count), lambda i, t: (0, 0, 0))
    memory = pl.BlockSpec((2, 1, count, HEAD_DIM), lambda i, t: (0, i, 0, 0))
    return pl.pallas_call(
        attend_back_kernel,
        grid_spec=pltpu.PrefetchScalarGridSpec(
            num_scalar_prefetch=1,
            grid=(HEADS,),
            in_specs=[block, block, block, thin, whole, whole, memory, thin, segs, segs],
            out_specs=[block, whole, whole],
            scratch_shapes=[pltpu.VMEM((2, 2, HEADS, count, HEAD_DIM), WIDE)],
        ),
        out_shape=[
            jax.ShapeDtypeStruct((HEADS, count, HEAD_DIM), WIDE),
            jax.ShapeDtypeStruct((2, HEADS, count, HEAD_DIM), WIDE),
            jax.ShapeDtypeStruct((2, HEADS, count, HEAD_DIM), LOW),
        ],
        cost_estimate=pl.CostEstimate(
            flops=30 * 10**9, bytes_accessed=10 * 2**20, transcendentals=3 * 10**6
        ),
        name="attend_back",
    )(tab, q, up, o, lse, own, oth, mem, segq, sego, segt)


def out_kernel(heads_ref, w_ref, x_ref, gain_ref, att_ref, mid_ref, n_ref):
    for h in range(HEADS):
        att_ref[:, h * HEAD_DIM : (h + 1) * HEAD_DIM] = heads_ref[h]
    mid = x_ref[...].astype(WIDE) + dot_nn(att_ref[...], w_ref[...])
    mid_ref[...] = mid
    r = lax.rsqrt(jnp.mean(mid * mid, axis=-1, keepdims=True) + EPSILON)
    n_ref[...] = (mid * r * gain_ref[...].astype(WIDE)).astype(LOW)


def out_block(heads, w, x, gain):
    count = x.shape[0]
    return pl.pallas_call(
        out_kernel,
        in_specs=[vmem()] * 4,
        out_specs=[vmem()] * 3,
        out_shape=[
            jax.ShapeDtypeStruct((count, D), LOW),
            jax.ShapeDtypeStruct((count, D), WIDE),
            jax.ShapeDtypeStruct((count, D), LOW),
        ],
        cost_estimate=pl.CostEstimate(
            flops=2 * count * D * D, bytes_accessed=4 * 2**20, transcendentals=0
        ),
        name="out_block",
    )(heads, w, x, gain)


def ffn_kernel(na, nb, ga, gb, g_ref, u_ref, d_ref, hid_ref, gg_ref, ug_ref, dn_ref):
    for t, (n_ref, c_ref) in enumerate(((na, ga), (nb, gb))):
        n = n_ref[...]
        gate = dot_nn(n, g_ref[...])
        upper = dot_nn(n, u_ref[...])
        sigma = jax.nn.sigmoid(gate)
        silu = gate * sigma
        hid_ref[t] = (silu * upper).astype(LOW)
        hg = dot_nt(c_ref[...], d_ref[...])
        gg = (hg * upper * sigma * (1.0 + gate * (1.0 - sigma))).astype(LOW)
        ug = (hg * silu).astype(LOW)
        gg_ref[t] = gg
        ug_ref[t] = ug
        dn_ref[t] = (dot_nt(gg, g_ref[...]) + dot_nt(ug, u_ref[...])).astype(LOW)


def ffn(na, nb, ga, gb, g, u, d):
    count = na.shape[0]
    units = g.shape[1]
    return pl.pallas_call(
        ffn_kernel,
        in_specs=[vmem()] * 7,
        out_specs=[vmem()] * 4,
        out_shape=[jax.ShapeDtypeStruct((2, count, units), LOW)] * 3
        + [jax.ShapeDtypeStruct((2, count, D), LOW)],
        cost_estimate=pl.CostEstimate(
            flops=20 * count * D * units,
            bytes_accessed=6 * D * units + 16 * count * D,
            transcendentals=2 * count * units,
        ),
        name="ffn",
    )(na, nb, ga, gb, g, u, d)


def mid_kernel(mid_ref, pa, pb, pc, up_ref, gain_ref, w_ref, mg_ref, bg_ref, ag_ref):
    mid = mid_ref[...]
    scaled = (pa[...].astype(WIDE) + pb[...].astype(WIDE) + pc[...].astype(WIDE)) * gain_ref[
        ...
    ].astype(WIDE)
    r = lax.rsqrt(jnp.mean(mid * mid, axis=-1, keepdims=True) + EPSILON)
    inner = jnp.mean(scaled * mid, axis=-1, keepdims=True)
    mid_grad = up_ref[...].astype(WIDE) + r * scaled - mid * (r * r * r * inner)
    mg_ref[...] = mid_grad
    branch = mid_grad.astype(LOW)
    bg_ref[...] = branch
    att = dot_nt(branch, w_ref[...]).astype(LOW)
    for h in range(HEADS):
        ag_ref[h] = att[:, h * HEAD_DIM : (h + 1) * HEAD_DIM]


def mid_block(mid, pa, pb, pc, up, gain, w):
    count = mid.shape[0]
    return pl.pallas_call(
        mid_kernel,
        in_specs=[vmem()] * 7,
        out_specs=[vmem()] * 3,
        out_shape=[
            jax.ShapeDtypeStruct((count, D), WIDE),
            jax.ShapeDtypeStruct((count, D), LOW),
            jax.ShapeDtypeStruct((HEADS, count, HEAD_DIM), LOW),
        ],
        cost_estimate=pl.CostEstimate(
            flops=2 * count * D * D, bytes_accessed=6 * 2**20, transcendentals=0
        ),
        name="mid_block",
    )(mid, pa, pb, pc, up, gain, w)


def qkv_back_kernel(tab, dq_ref, own_ref, got_ref, cos_ref, sin_ref, w_ref, dx_ref, g_ref):
    c, s = cos_ref[0], sin_ref[0]

    def rot(v):
        return v * c - pltpu.roll(v, HEAD_DIM // 2, 1) * s

    dq = rot(dq_ref[0] * SCALE).astype(LOW)
    dk = rot((own_ref[0, 0] + got_ref[0, 0].astype(WIDE)) * SCALE).astype(LOW)
    dv = (own_ref[1, 0] + got_ref[1, 0].astype(WIDE)).astype(LOW)
    grads = jnp.concatenate([dq, dk, dv], axis=1)
    g_ref[0] = grads
    dx_ref[0] = dot_nt(grads, w_ref[...]).astype(LOW)


def qkv_back(chips, dq, own, got, cos, sin, w):
    count = dq.shape[1]
    block = pl.BlockSpec((1, count, HEAD_DIM), lambda i, t: (t[i], 0, 0))
    pair = pl.BlockSpec((2, 1, count, HEAD_DIM), lambda i, t: (0, t[i], 0, 0))
    return pl.pallas_call(
        qkv_back_kernel,
        grid_spec=pltpu.PrefetchScalarGridSpec(
            num_scalar_prefetch=1,
            grid=(HEADS,),
            in_specs=[
                block, pair, pair, block, block,
                pl.BlockSpec((D, 3 * HEAD_DIM), lambda i, t: (0, 0)),
            ],
            out_specs=[
                pl.BlockSpec((1, count, D), lambda i, t: (i, 0, 0)),
                pl.BlockSpec((1, count, 3 * HEAD_DIM), lambda i, t: (t[i], 0, 0)),
            ],
        ),
        out_shape=[
            jax.ShapeDtypeStruct((HEADS, count, D), LOW),
            jax.ShapeDtypeStruct((HEADS, count, 3 * HEAD_DIM), LOW),
        ],
        cost_estimate=pl.CostEstimate(
            flops=2 * HEADS * count * D * 3 * HEAD_DIM,
            bytes_accessed=4 * HEADS * count * D,
            transcendentals=0,
        ),
        name="qkv_back",
    )(chips, dq, own, got, cos, sin, w)


def local(
    far,
    tokens,
    segment_ids,
    second_doc,
    memory_index,
    cache_keys,
    cache_values,
    first_gain,
    query_weight,
    key_weight,
    value_weight,
    out_weight,
    second_gain,
    gate_weight,
    up_weight,
    down_weight,
    cotangent,
):
    x = tokens[0]
    upstream = cotangent[0]
    count = x.shape[0]
    blocks = count // QUERY_BLOCK
    rows = query_weight.shape[0]
    share = down_weight.shape[0]
    units = far * HEADS * share
    chip, core, pair = lax.axis_index("h"), lax.axis_index("c"), lax.axis_index("dl")
    mine = jnp.where(chip % 2 == 0, chip // 2, HEADS - 1 - chip // 2)
    slots = jnp.arange(HEADS, dtype=jnp.int32)
    chips = at_place(mine - slots)
    group = ("dh", "h") if far > 1 else "h"

    def by_head(w):
        return w.reshape(rows, HEADS, HEAD_DIM).transpose(1, 0, 2)

    picked = memory_index[0].transpose(1, 0, 2)
    seg_rows = jnp.broadcast_to(
        segment_ids[0].astype(LOW).reshape(1, blocks, QUERY_BLOCK), (HEADS, blocks, QUERY_BLOCK)
    )
    gains = jnp.concatenate([first_gain, second_gain])
    gain_rows = jnp.broadcast_to(
        jnp.pad(gains, (0, HEAD_DIM - 2 * rows)).reshape(1, 1, HEAD_DIM), (HEADS, 1, HEAD_DIM)
    )
    pack = jnp.concatenate(
        [
            by_head(query_weight),
            by_head(key_weight),
            by_head(value_weight),
            seg_rows,
            (picked // MEM_ROWS).astype(LOW),
            (picked % MEM_ROWS).astype(LOW),
            gain_rows,
        ],
        axis=1,
    )
    height = pack.shape[1]
    pack = jnp.pad(pack, ((0, 0), (0, -height % 16), (0, 0)))

    forth, back = [x, turn(x, 1)], [x, turn(x, -1)]
    pack, forth[1], back[1] = lax.optimization_barrier((pack, forth[1], back[1]))
    got = exchange(pack)
    for step in range(HEADS // 2 - 2):
        forth.append(turn(forth[-1], 1))
        back.append(turn(back[-1], -1))
    got, forth[-1], back[-1] = lax.optimization_barrier((got, forth[-1], back[-1]))
    split = count // 2
    far_first, far_last = turn(forth[-1][:split], 1), turn(back[-1][split:], -1)
    x_slots = [(v,) for v in forth] + [(far_first, far_last)] + [(v,) for v in back[:0:-1]]
    got_c = swap(got, "c")
    got_y = swap(got, "dl")
    got_yc = swap(got_y, "c")
    near = pick(core, jnp.stack([got, got_c]), jnp.stack([got_c, got]))
    away = pick(core, jnp.stack([got_y, got_yc]), jnp.stack([got_yc, got_y]))
    every = pick(pair, jnp.stack([near, away]), jnp.stack([away, near]))
    every = every.transpose(2, 0, 1, 3, 4)
    if far > 1:
        every = lax.all_gather(every, "dh", axis=0)
    else:
        every = every[None]
    every = every.transpose(0, 2, 1, 3, 4, 5)
    w_qkv = jnp.concatenate(
        [every[..., i * rows : (i + 1) * rows, :].reshape(D, HEAD_DIM) for i in range(3)], axis=1
    )
    gain_all = every[..., 3 * rows + 3 * blocks, : 2 * rows].reshape(-1, 2, rows)
    gain_one = gain_all[:, 0].reshape(1, D)
    gain_two = gain_all[:, 1].reshape(1, D)

    def seg_of(blocks_of):
        return (
            blocks_of[:, 3 * rows : 3 * rows + blocks]
            .astype(WIDE)
            .astype(jnp.int32)
            .reshape(HEADS, count)
        )

    seg_own = seg_of(got)
    seg_oth = seg_of(got_c)
    idx = (
        got[:, 3 * rows + blocks : 3 * rows + 2 * blocks].astype(WIDE) * MEM_ROWS
        + got[:, 3 * rows + 2 * blocks : 3 * rows + 3 * blocks].astype(WIDE)
    ).astype(jnp.int32)
    idx = idx.reshape(HEADS, count, 1)

    block_docs = seg_own[:, ::QUERY_BLOCK]
    docs = second_doc.shape[1]
    doc_ids = jnp.arange(docs, dtype=jnp.int32)
    mates = jnp.sum(
        jnp.where(block_docs[:, :, None] == doc_ids, second_doc[0][None, None, :], 0), axis=-1
    )
    seg_all = jnp.concatenate([seg_own, seg_oth], axis=0)
    before = jnp.sum(
        (seg_all.reshape(1, -1) < block_docs[:, :1]).astype(jnp.int32), axis=1
    )
    tab = jnp.concatenate(
        [
            block_docs.reshape(-1),
            mates.reshape(-1),
            before // (2 * count),
            jnp.stack([core, chip]),
        ]
    ).astype(jnp.int32)

    half = HEAD_DIM // 2
    freqs = 10000.0 ** (-jnp.arange(half, dtype=WIDE) * 2.0 / (2 * half))
    positions = ((2 * slots + core) * count)[:, None] + jnp.arange(count, dtype=jnp.int32)[None]
    turned = positions.astype(WIDE)[:, :, None] * freqs
    cosine, sine = jnp.cos(turned), jnp.sin(turned)
    cosine = jnp.concatenate([cosine, cosine], axis=-1)
    sine = jnp.concatenate([-sine, sine], axis=-1)

    def by_owner(w):
        return w.reshape(rows, far, 2, HEADS, 2, share).transpose(2, 4, 0, 1, 3, 5).reshape(
            2, 2, rows, units
        )

    gu = jnp.concatenate([by_owner(gate_weight), by_owner(up_weight)], axis=-1)
    kept = pick(core, gu[:, 0], gu[:, 1])
    came = swap(pick(core, gu[:, 1], gu[:, 0]), "c")
    gu = pick(core, jnp.stack([kept, came], 1), jnp.stack([came, kept], 1))
    kept = pick(pair, gu[0], gu[1])
    came = swap(pick(pair, gu[1], gu[0]), "dl")
    gu = pick(pair, jnp.stack([kept, came]), jnp.stack([came, kept])).reshape(4 * rows, 2 * units)
    wide = 2 * units
    third = wide - D
    pieces = [out_weight[:, i * third : (i + 1) * third] for i in range(-(-D // third))]
    pieces[-1] = jnp.pad(pieces[-1], ((0, 0), (0, third - pieces[-1].shape[1])))
    pieces = jnp.concatenate(pieces, axis=0)
    deep = max(share, pieces.shape[0])
    lower = jnp.concatenate(
        [
            jnp.pad(down_weight, ((0, deep - share), (0, 0))),
            jnp.pad(pieces, ((0, deep - pieces.shape[0]), (0, 0))),
        ],
        axis=1,
    )
    bundle = jnp.concatenate([gu, lower], axis=0)
    bundle, *_ = lax.optimization_barrier((bundle, *x_slots[3], *x_slots[4], *x_slots[5]))
    gathered = lax.all_gather(bundle, group, axis=0)
    up_c = swap(upstream, "c")
    up_y = swap(upstream, "dl")
    up_yc = swap(up_y, "c")

    held = ()
    for order in ([0, 1, 7, 2, 6], [3, 5, 4]):
        held = qkv_blocks(
            at_place(mine - jnp.asarray(order, jnp.int32)).astype(jnp.int32),
            [x_slots[i] for i in order],
            gain_one,
            w_qkv,
            cosine,
            sine,
            held,
        )
    queries, own, normed_one = held
    other = swap(own, "c")

    seg_thin = seg_own.reshape(HEADS, count, 1)
    seg_own_row = seg_own.reshape(HEADS, 1, count)
    seg_oth_row = seg_oth.reshape(HEADS, 1, count)
    attention, attention_low, lse, memory = attend(
        tab,
        queries,
        own,
        other,
        seg_thin,
        seg_own_row,
        seg_oth_row,
        idx,
        cache_keys[0].reshape(-1, D),
        cache_values[0].reshape(-1, D),
    )

    heads = exchange(attention_low)
    gathered, heads = lax.optimization_barrier((gathered, heads))
    gathered = gathered.reshape(far, HEADS, 4 * rows + deep, wide)
    gu_w = (
        gathered[:, :, : 4 * rows]
        .reshape(far, HEADS, 2, 2 * rows, wide)
        .transpose(0, 2, 1, 3, 4)
        .reshape(D, wide)
    )
    gate_w, up_w = gu_w[:, :units], gu_w[:, units:]
    down_w = gathered[:, :, 4 * rows : 4 * rows + share, :D].reshape(units, D)
    outs = gathered[:, :, 4 * rows :, D:]
    outs = jnp.concatenate(
        [outs[:, :, i * rows : (i + 1) * rows] for i in range(pieces.shape[0] // rows)], axis=-1
    )[..., :D]
    outs_c = swap(outs, "c")
    outs_y = swap(outs, "dl")
    outs_yc = swap(outs_y, "c")
    near = pick(core, jnp.stack([outs, outs_c], 2), jnp.stack([outs_c, outs], 2))
    away = pick(core, jnp.stack([outs_y, outs_yc], 2), jnp.stack([outs_yc, outs_y], 2))
    out_w = pick(pair, jnp.stack([near, away], 1), jnp.stack([away, near], 1)).reshape(D, D)

    attended, mid, normed_two = out_block(heads, out_w, x, gain_two)

    n_c = swap(normed_two, "c")
    n_y = swap(normed_two, "dl")
    n_yc = swap(n_y, "c")
    hid_l, gg_l, ug_l, dn_l = ffn(normed_two, n_c, upstream, up_c, gate_w, up_w, down_w)
    hid_r, gg_r, ug_r, dn_r = ffn(n_y, n_yc, up_y, up_yc, gate_w, up_w, down_w)

    def sum_back(near, away):
        there = (away[0].astype(WIDE) + swap(away[1], "c").astype(WIDE)).astype(LOW)
        return near[0], swap(near[1], "c"), swap(there, "dl")

    parts = sum_back(dn_l, dn_r)
    mid_grad, branch, att_grad = mid_block(
        mid, *parts, upstream, gain_two, out_w
    )

    ups = exchange(att_grad)

    hid_l, gg_l, ug_l, hid_r, gg_r, ug_r, branch = lax.optimization_barrier(
        (hid_l, gg_l, ug_l, hid_r, gg_r, ug_r, branch)
    )

    def over_owner(w):
        w = w.reshape(far, 2, HEADS, 2, rows, D)
        kept = pick(core, w[:, :, :, 0], w[:, :, :, 1])
        came = swap(pick(core, w[:, :, :, 1], w[:, :, :, 0]), "c")
        w = kept.astype(WIDE) + came.astype(WIDE)
        kept = pick(pair, w[:, 0], w[:, 1])
        came = swap(pick(pair, w[:, 1], w[:, 0]).astype(LOW), "dl")
        return (kept + came.astype(WIDE)).astype(LOW).reshape(far * HEADS, rows, D)

    out_part = over_owner(
        jnp.einsum("td,te->de", attended, branch, preferred_element_type=WIDE).astype(LOW)
    )

    def over_tokens(a, b):
        return jnp.einsum("gtd,gtf->df", a, b, preferred_element_type=WIDE)

    n_l, n_r = jnp.stack([normed_two, n_c]), jnp.stack([n_y, n_yc])
    u_l, u_r = jnp.stack([upstream, up_c]), jnp.stack([up_y, up_yc])
    gate_part = (over_tokens(n_l, gg_l) + over_tokens(n_r, gg_r)).astype(LOW)
    up_part = (over_tokens(n_l, ug_l) + over_tokens(n_r, ug_r)).astype(LOW)
    down_part = (over_tokens(hid_l, u_l) + over_tokens(hid_r, u_r)).astype(LOW)

    def by_rows(w):
        return (
            w.reshape(far, 2, HEADS, 2 * rows, units)
            .transpose(0, 2, 1, 3, 4)
            .reshape(far * HEADS, 4 * rows, units)
        )

    strips = [out_part[:, :, i * third : (i + 1) * third] for i in range(-(-D // third))]
    strips[-1] = jnp.pad(strips[-1], ((0, 0), (0, 0), (0, third - strips[-1].shape[-1])))
    strips = jnp.concatenate(strips, axis=1)
    height = 4 * rows + deep
    parts = jnp.concatenate(
        [
            jnp.concatenate([by_rows(gate_part), by_rows(up_part)], axis=-1),
            jnp.concatenate(
                [
                    jnp.pad(
                        down_part.reshape(far * HEADS, share, D), ((0, 0), (0, deep - share), (0, 0))
                    ),
                    jnp.pad(strips, ((0, 0), (0, deep - strips.shape[1]), (0, 0))),
                ],
                axis=2,
            ),
        ],
        axis=1,
    )
    ups, parts = lax.optimization_barrier((ups, parts))
    summed = lax.psum_scatter(
        parts.reshape(far * HEADS * height, wide), group, scatter_dimension=0, tiled=True
    )
    down_w_grad = summed[4 * rows : 4 * rows + share, :D].astype(WIDE)
    out_w_grad = jnp.concatenate(
        [
            summed[4 * rows + i * rows : 4 * rows + (i + 1) * rows, D:]
            for i in range(-(-D // third))
        ],
        axis=1,
    )[:, :D].astype(WIDE)
    gu = summed[: 4 * rows].reshape(2, 2, rows, wide)
    kept = pick(core, gu[:, 0], gu[:, 1])
    came = swap(pick(core, gu[:, 1], gu[:, 0]), "c")
    gu = pick(core, jnp.stack([kept, came], 1), jnp.stack([came, kept], 1))
    kept = pick(pair, gu[0], gu[1])
    came = swap(pick(pair, gu[1], gu[0]), "dl")
    gu = pick(pair, jnp.stack([kept, came]), jnp.stack([came, kept]))
    gu = (
        gu.reshape(2, 2, rows, 2, far, HEADS, share)
        .transpose(3, 2, 4, 0, 5, 1, 6)
        .reshape(2, rows, FF)
        .astype(WIDE)
    )
    gate_w_grad, up_w_grad = gu[0], gu[1]

    out_l = jnp.einsum("gtf,fd->gtd", hid_l, down_w, preferred_element_type=WIDE).astype(LOW)
    out_r = jnp.einsum("gtf,fd->gtd", hid_r, down_w, preferred_element_type=WIDE).astype(LOW)
    output = mid
    for part in sum_back(out_l, out_r):
        output = output + part.astype(WIDE)
    output = output.astype(LOW)

    dq, d_own, d_oth = attend_back(
        tab, queries, ups, attention, lse, own, other, memory, seg_thin, seg_own_row, seg_oth_row
    )
    d_got = swap(d_oth, "c")
    dx, grads = qkv_back(chips.astype(jnp.int32), dq, d_own, d_got, cosine, sine, w_qkv)

    def plus(block, arrived, start):
        size = arrived.shape[0]
        total = block[start : start + size].astype(WIDE) + arrived.astype(WIDE)
        pieces = [block[:start], total.astype(LOW), block[start + size :]]
        return jnp.concatenate([piece for piece in pieces if piece.shape[0]], axis=0)

    middle = dx[HEADS // 2]
    forth, back = middle[:split], middle[split:]
    for step in range(1, HEADS // 2):
        forth = plus(dx[HEADS // 2 + step], turn(forth, 1), 0)
        back = plus(dx[HEADS // 2 - step], turn(back, -1), split if step == 1 else 0)
    forth, back = turn(forth, 1), turn(back, -1)
    normed_one_grad = dx[0].astype(WIDE) + forth.astype(WIDE) + back.astype(WIDE)

    dw = jnp.einsum("std,stg->dg", normed_one, grads, preferred_element_type=WIDE).astype(LOW)
    dw = dw.reshape(far, 2, HEADS, 2, rows, 3 * HEAD_DIM)
    kept = pick(core, dw[:, :, :, 0], dw[:, :, :, 1])
    came = swap(pick(core, dw[:, :, :, 1], dw[:, :, :, 0]), "c")
    dw = kept.astype(WIDE) + came.astype(WIDE)
    kept = pick(pair, dw[:, 0], dw[:, 1])
    came = swap(pick(pair, dw[:, 1], dw[:, 0]).astype(LOW), "dl")
    dw = (kept + came.astype(WIDE)).astype(LOW)
    if far > 1:
        dw = lax.psum_scatter(dw, "dh", scatter_dimension=0, tiled=True)
    qkv_grads = exchange(dw[0]).astype(WIDE)

    wide_x = x.astype(WIDE)
    r = lax.rsqrt(jnp.mean(wide_x * wide_x, axis=-1, keepdims=True) + EPSILON)
    scaled = normed_one_grad * gain_one.astype(WIDE)
    inner = jnp.mean(scaled * wide_x, axis=-1, keepdims=True)
    input_grad = mid_grad + r * scaled - wide_x * (r * r * r * inner)

    q_w_grad, k_w_grad, v_w_grad = (
        qkv_grads[:, :, i * HEAD_DIM : (i + 1) * HEAD_DIM].transpose(1, 0, 2).reshape(rows, D)
        for i in range(3)
    )

    def gain_grad(gain, pairs):
        total = 0.0
        for grad, weight in pairs:
            total = total + jnp.sum(grad * weight.astype(WIDE), axis=1)
        return total / gain.astype(WIDE)

    first_gain_grad = gain_grad(
        first_gain,
        ((q_w_grad, query_weight), (k_w_grad, key_weight), (v_w_grad, value_weight)),
    )
    second_gain_grad = gain_grad(
        second_gain, ((gate_w_grad, gate_weight), (up_w_grad, up_weight))
    )
    return (
        output[None],
        input_grad[None],
        first_gain_grad,
        q_w_grad,
        k_w_grad,
        v_w_grad,
        out_w_grad,
        second_gain_grad,
        gate_w_grad,
        up_w_grad,
        down_w_grad,
    )


def solution(mesh):
    far = mesh.shape["dp"] // 2
    cores = mesh.shape["seq"] // HEADS
    fine = Mesh(mesh.devices.reshape(far, 2, HEADS, cores), ("dh", "dl", "h", "c"))
    dp, seq, every = ("dh", "dl"), ("h", "c"), ("dh", "dl", "h", "c")
    rows = P(every, None)
    return jax.shard_map(
        functools.partial(local, far),
        mesh=fine,
        in_specs=(
            P(dp, seq, None),
            P(dp, seq),
            P(dp, None),
            P(dp, seq, None, None),
            P(dp, None, None, None),
            P(dp, None, None, None),
            P(every),
            rows,
            rows,
            rows,
            rows,
            P(every),
            rows,
            rows,
            rows,
            P(dp, seq, None),
        ),
        out_specs=(
            P(dp, seq, None),
            P(dp, seq, None),
            P(every),
            rows,
            rows,
            rows,
            rows,
            P(every),
            rows,
            rows,
            rows,
        ),
        check_vma=False,
    )
```

```python
import functools
import math

import jax
import jax.numpy as jnp
from jax import lax
from jax.experimental import pallas as pl
from jax.experimental.pallas import tpu as pltpu
from jax.sharding import Mesh
from jax.sharding import PartitionSpec as P

D = 1024
FF = 2816
HEADS = 8
HEAD_DIM = 128
QUERY_BLOCK = 128
MEM_ROWS = 256
EPSILON = 1e-05
NEGATIVE = -1e30
SCALE = 1.0 / math.sqrt(HEAD_DIM)
LOG2 = SCALE * math.log2(math.e)
LOW = jnp.bfloat16
WIDE = jnp.float32

RING = [2 * i for i in range(HEADS // 2)] + [2 * i + 1 for i in reversed(range(HEADS // 2))]
PLACE = [RING.index(i) for i in range(HEADS)]


def dot_nn(a, b):
    return lax.dot_general(a, b, (((1,), (0,)), ((), ())), preferred_element_type=WIDE)


def dot_nt(a, b):
    return lax.dot_general(a, b, (((1,), (1,)), ((), ())), preferred_element_type=WIDE)


def dot_tn(a, b):
    return lax.dot_general(a, b, (((0,), (0,)), ((), ())), preferred_element_type=WIDE)


def swap(block, axis):
    return lax.ppermute(block, axis, [(0, 1), (1, 0)])


def turn(block, distance):
    route = [(RING[i], RING[(i + distance) % HEADS]) for i in range(HEADS)]
    return lax.ppermute(block, "h", route)


def at_place(place):
    place = lax.rem(place + 2 * HEADS, HEADS)
    return jnp.where(place < HEADS // 2, 2 * place, 2 * (HEADS - 1 - place) + 1)


def exchange(blocks):
    return lax.all_to_all(blocks, "h", 0, 0)


def pick(flag, first, second):
    return jnp.where(flag == 0, first, second)


def smem():
    return pl.BlockSpec(memory_space=pltpu.SMEM)


def vmem():
    return pl.BlockSpec(memory_space=pltpu.VMEM)


def qkv_kernel(parts, tab, *refs):
    xs, (gain_ref, w_ref, cos_ref, sin_ref) = refs[: sum(parts)], refs[sum(parts) : sum(parts) + 4]
    q_ref, kv_ref, n_ref, x_ref = refs[-4:]
    i = pl.program_id(0)
    first = 0
    for step, number in enumerate(parts):

        @pl.when(i == step)
        def _(blocks=xs[first : first + number]):
            row = 0
            for block in blocks:
                size = block.shape[0]
                x_ref[row : row + size, :] = block[...]
                row += size

        first += number
    x = x_ref[...].astype(WIDE)
    r = lax.rsqrt(jnp.mean(x * x, axis=-1, keepdims=True) + EPSILON)
    normed = (x * r * gain_ref[...].astype(WIDE)).astype(LOW)
    n_ref[0] = normed
    out = dot_nn(normed, w_ref[...])
    c, s = cos_ref[0], sin_ref[0]

    def rot(v):
        return v * c + pltpu.roll(v, HEAD_DIM // 2, 1) * s

    q_ref[0] = rot(out[:, :HEAD_DIM]).astype(LOW)
    kv_ref[0, 0] = rot(out[:, HEAD_DIM : 2 * HEAD_DIM]).astype(LOW)
    kv_ref[1, 0] = out[:, 2 * HEAD_DIM :].astype(LOW)


def qkv_blocks(chips, xs, gain, w, cos, sin, held):
    count = cos.shape[1]
    flat = [piece for block in xs for piece, _ in block]
    read = [size for block in xs for _, size in block]

    def whole(shape):
        return pl.BlockSpec(shape, lambda i, t: (0, 0))

    def block(*shape):
        return pl.BlockSpec((1, *shape), lambda i, t: (t[i], 0, 0))

    spec = pltpu.PrefetchScalarGridSpec(
        num_scalar_prefetch=1,
        grid=(len(xs),),
        in_specs=[whole((size, D)) for size in read]
        + [whole((1, D)), whole((D, 3 * HEAD_DIM)), block(count, HEAD_DIM), block(count, HEAD_DIM)]
        + [pl.BlockSpec(memory_space=pl.ANY)] * len(held),
        out_specs=[
            block(count, HEAD_DIM),
            pl.BlockSpec((2, 1, count, HEAD_DIM), lambda i, t: (0, t[i], 0, 0)),
            block(count, D),
        ],
        scratch_shapes=[pltpu.VMEM((count, D), LOW)],
    )
    return pl.pallas_call(
        functools.partial(qkv_kernel, [len(block) for block in xs]),
        grid_spec=spec,
        out_shape=[
            jax.ShapeDtypeStruct((HEADS, count, HEAD_DIM), LOW),
            jax.ShapeDtypeStruct((2, HEADS, count, HEAD_DIM), LOW),
            jax.ShapeDtypeStruct((HEADS, count, D), LOW),
        ],
        input_output_aliases={len(flat) + 5 + i: i for i in range(len(held))},
        cost_estimate=pl.CostEstimate(
            flops=2 * len(xs) * count * D * 3 * HEAD_DIM,
            bytes_accessed=5 * len(xs) * count * D,
            transcendentals=0,
        ),
        name=f"qkv{len(xs)}",
    )(chips, *flat, gain, w, cos, sin, *held)


def causal(count):
    rows = lax.broadcasted_iota(jnp.int32, (count, count), 0)
    return lax.broadcasted_iota(jnp.int32, (count, count), 1) <= rows


def attend_kernel(
    tab, q_ref, own_ref, oth_ref, segq_ref, sego_ref, segt_ref, idx_ref, ck_ref, cv_ref,
    o_ref, low_ref, lse_ref, mem_ref,
):
    i = pl.program_id(0)
    parity = tab[40]
    count = q_ref.shape[1]
    q = q_ref[0]
    segq = segq_ref[0]

    s1 = dot_nt(q, own_ref[0, i]) * LOG2
    s2 = dot_nt(q, oth_ref[0, i]) * LOG2
    s1 = jnp.where((sego_ref[i] == segq) & causal(count), s1, NEGATIVE)
    s2 = jnp.where(segt_ref[i] == segq + 64 * (1 - parity), s2, NEGATIVE)
    memory = []
    for b in range(count // QUERY_BLOCK):
        rows = slice(b * QUERY_BLOCK, (b + 1) * QUERY_BLOCK)
        doc = tab[2 * i + b]
        mate = tab[16 + 2 * i + b]
        idx = idx_ref[0, rows, :]
        lane = lax.broadcasted_iota(jnp.int32, (QUERY_BLOCK, MEM_ROWS), 1)
        first = jnp.where(idx == lane, 1.0, 0.0).astype(LOW)
        second = jnp.where(idx == lane + MEM_ROWS, 1.0, 0.0).astype(LOW)
        here = pl.ds(pl.multiple_of(doc * MEM_ROWS, MEM_ROWS), MEM_ROWS)
        there = pl.ds(pl.multiple_of(mate * MEM_ROWS, MEM_ROWS), MEM_ROWS)
        mk = (dot_nn(first, ck_ref[here, :]) + dot_nn(second, ck_ref[there, :])).astype(LOW)
        mv = (dot_nn(first, cv_ref[here, :]) + dot_nn(second, cv_ref[there, :])).astype(LOW)
        mem_ref[0, 0, rows, :] = mk
        mem_ref[1, 0, rows, :] = mv
        s = jnp.where(segq[rows] == doc, dot_nt(q[rows], mk) * LOG2, NEGATIVE)
        memory.append((s, mv))
    sm = jnp.concatenate([s for s, _ in memory], axis=0)
    top = jnp.maximum(
        jnp.max(jnp.maximum(s1, s2), axis=-1, keepdims=True), jnp.max(sm, axis=-1, keepdims=True)
    )
    p1 = jnp.exp2(s1 - top)
    p2 = jnp.exp2(s2 - top)
    pm = jnp.exp2(sm - top)
    total = jnp.sum(p1 + p2, axis=-1, keepdims=True) + jnp.sum(pm, axis=-1, keepdims=True)
    pm = pm.astype(LOW)
    acc = jnp.concatenate(
        [
            dot_nn(pm[b * QUERY_BLOCK : (b + 1) * QUERY_BLOCK], mv)
            for b, (_, mv) in enumerate(memory)
        ],
        axis=0,
    )
    acc = acc + dot_nn(p1.astype(LOW), own_ref[1, i]) + dot_nn(p2.astype(LOW), oth_ref[1, i])

    def body(j, state):
        top, total, acc = state
        s1 = dot_nt(q, own_ref[0, j]) * LOG2
        s2 = dot_nt(q, oth_ref[0, j]) * LOG2
        s1 = jnp.where(sego_ref[j] == segq, s1, NEGATIVE)
        s2 = jnp.where(segt_ref[j] == segq, s2, NEGATIVE)
        fresh = jnp.maximum(top, jnp.max(jnp.maximum(s1, s2), axis=-1, keepdims=True))
        p1 = jnp.exp2(s1 - fresh)
        p2 = jnp.exp2(s2 - fresh)
        decay = jnp.exp2(top - fresh)
        total = total * decay + jnp.sum(p1 + p2, axis=-1, keepdims=True)
        acc = (
            acc * decay
            + dot_nn(p1.astype(LOW), own_ref[1, j])
            + dot_nn(p2.astype(LOW), oth_ref[1, j])
        )
        return fresh, total, acc

    top, total, acc = lax.fori_loop(tab[32 + i], i, body, (top, total, acc))
    out = acc / total
    o_ref[0] = out
    low_ref[0] = out.astype(LOW)
    lse_ref[0] = top + jnp.log2(total)


def attend(tab, q, own, oth, segq, sego, segt, idx, ck, cv):
    count = q.shape[1]
    block = pl.BlockSpec((1, count, HEAD_DIM), lambda i, t: (i, 0, 0))
    thin = pl.BlockSpec((1, count, 1), lambda i, t: (i, 0, 0))
    whole = pl.BlockSpec((2, HEADS, count, HEAD_DIM), lambda i, t: (0, 0, 0, 0))
    segs = pl.BlockSpec((HEADS, 1, count), lambda i, t: (0, 0, 0))
    cache = pl.BlockSpec((ck.shape[0], HEAD_DIM), lambda i, t: (0, t[41]))
    mem = pl.BlockSpec((2, 1, count, HEAD_DIM), lambda i, t: (0, i, 0, 0))
    return pl.pallas_call(
        attend_kernel,
        grid_spec=pltpu.PrefetchScalarGridSpec(
            num_scalar_prefetch=1,
            grid=(HEADS,),
            in_specs=[block, whole, whole, thin, segs, segs, thin, cache, cache],
            out_specs=[block, block, thin, mem],
        ),
        out_shape=[
            jax.ShapeDtypeStruct((HEADS, count, HEAD_DIM), WIDE),
            jax.ShapeDtypeStruct((HEADS, count, HEAD_DIM), LOW),
            jax.ShapeDtypeStruct((HEADS, count, 1), WIDE),
            jax.ShapeDtypeStruct((2, HEADS, count, HEAD_DIM), LOW),
        ],
        cost_estimate=pl.CostEstimate(
            flops=25 * 10**9, bytes_accessed=6 * 2**20, transcendentals=3 * 10**6
        ),
        name="attend",
    )(tab, q, own, oth, segq, sego, segt, idx, ck, cv)


def attend_back_kernel(
    tab, q_ref, up_ref, o_ref, lse_ref, own_ref, oth_ref, mem_ref, segq_ref, sego_ref, segt_ref,
    dq_ref, down_ref, doth_ref, sum_ref,
):
    i = pl.program_id(0)

    @pl.when(i == 0)
    def _():
        sum_ref[...] = jnp.zeros_like(sum_ref)

    parity = tab[40]
    count = q_ref.shape[1]
    q = q_ref[0]
    up = up_ref[0]
    lse = lse_ref[0]
    segq = segq_ref[0]
    delta = jnp.sum(up.astype(WIDE) * o_ref[0], axis=-1, keepdims=True)
    partial = []
    for b in range(count // QUERY_BLOCK):
        rows = slice(b * QUERY_BLOCK, (b + 1) * QUERY_BLOCK)
        mk = mem_ref[0, 0, rows, :]
        mv = mem_ref[1, 0, rows, :]
        ok = segq[rows] == tab[2 * i + b]
        p = jnp.exp2(jnp.where(ok, dot_nt(q[rows], mk) * LOG2 - lse[rows], NEGATIVE))
        ds = (p * (dot_nt(up[rows], mv) - delta[rows])).astype(LOW)
        partial.append(dot_nn(ds, mk))

    def tile(side, ref, j, ok, dq):
        k = ref[0, j]
        v = ref[1, j]
        p = jnp.exp2(jnp.where(ok, dot_nt(q, k) * LOG2 - lse, NEGATIVE))
        ds = (p * (dot_nt(up, v) - delta)).astype(LOW)
        sum_ref[side, 0, j] += dot_tn(ds, q)
        sum_ref[side, 1, j] += dot_tn(p.astype(LOW), up)
        return dq + dot_nn(ds, k)

    dq = jnp.concatenate(partial, axis=0)
    dq = tile(0, own_ref, i, (sego_ref[i] == segq) & causal(count), dq)
    dq = tile(1, oth_ref, i, segt_ref[i] == segq + 64 * (1 - parity), dq)

    def body(j, dq):
        dq = tile(0, own_ref, j, sego_ref[j] == segq, dq)
        return tile(1, oth_ref, j, segt_ref[j] == segq, dq)

    dq_ref[0] = lax.fori_loop(tab[32 + i], i, body, dq)

    @pl.when(i == HEADS - 1)
    def _():
        down_ref[...] = sum_ref[0]
        doth_ref[...] = sum_ref[1].astype(LOW)


def attend_back(tab, q, up, o, lse, own, oth, mem, segq, sego, segt):
    count = q.shape[1]
    block = pl.BlockSpec((1, count, HEAD_DIM), lambda i, t: (i, 0, 0))
    thin = pl.BlockSpec((1, count, 1), lambda i, t: (i, 0, 0))
    whole = pl.BlockSpec((2, HEADS, count, HEAD_DIM), lambda i, t: (0, 0, 0, 0))
    segs = pl.BlockSpec((HEADS, 1, count), lambda i, t: (0, 0, 0))
    memory = pl.BlockSpec((2, 1, count, HEAD_DIM), lambda i, t: (0, i, 0, 0))
    return pl.pallas_call(
        attend_back_kernel,
        grid_spec=pltpu.PrefetchScalarGridSpec(
            num_scalar_prefetch=1,
            grid=(HEADS,),
            in_specs=[block, block, block, thin, whole, whole, memory, thin, segs, segs],
            out_specs=[block, whole, whole],
            scratch_shapes=[pltpu.VMEM((2, 2, HEADS, count, HEAD_DIM), WIDE)],
        ),
        out_shape=[
            jax.ShapeDtypeStruct((HEADS, count, HEAD_DIM), WIDE),
            jax.ShapeDtypeStruct((2, HEADS, count, HEAD_DIM), WIDE),
            jax.ShapeDtypeStruct((2, HEADS, count, HEAD_DIM), LOW),
        ],
        cost_estimate=pl.CostEstimate(
            flops=30 * 10**9, bytes_accessed=10 * 2**20, transcendentals=3 * 10**6
        ),
        name="attend_back",
    )(tab, q, up, o, lse, own, oth, mem, segq, sego, segt)


def place_rows(tab, sources, w_ref):
    rows = sources[0].shape[1]
    for k, source in enumerate(sources):
        pair = tab[8] if k < 2 else 1 - tab[8]
        core = tab[9] if k % 2 == 0 else 1 - tab[9]
        for slot in range(HEADS):
            start = ((pair * HEADS + tab[slot]) * 2 + core) * rows
            w_ref[pl.ds(pl.multiple_of(start, rows), rows), :] = source[slot]


def out_kernel(tab, heads_ref, *refs):
    sources, (x_ref, gain_ref, att_ref, mid_ref, n_ref, w_ref) = refs[:-6], refs[-6:]
    if len(sources) == 1:
        w_ref[...] = sources[0][...]
    else:
        place_rows(tab, sources, w_ref)
    for h in range(HEADS):
        att_ref[:, h * HEAD_DIM : (h + 1) * HEAD_DIM] = heads_ref[h]
    mid = x_ref[...].astype(WIDE) + dot_nn(att_ref[...], w_ref[...])
    mid_ref[...] = mid
    r = lax.rsqrt(jnp.mean(mid * mid, axis=-1, keepdims=True) + EPSILON)
    n_ref[...] = (mid * r * gain_ref[...].astype(WIDE)).astype(LOW)


def out_block(tab, heads, sources, x, gain):
    count = x.shape[0]
    return pl.pallas_call(
        out_kernel,
        in_specs=[smem()] + [vmem()] * (3 + len(sources)),
        out_specs=[vmem()] * 4,
        out_shape=[
            jax.ShapeDtypeStruct((count, D), LOW),
            jax.ShapeDtypeStruct((count, D), WIDE),
            jax.ShapeDtypeStruct((count, D), LOW),
            jax.ShapeDtypeStruct((D, D), LOW),
        ],
        cost_estimate=pl.CostEstimate(
            flops=2 * count * D * D, bytes_accessed=6 * 2**20, transcendentals=0
        ),
        name="out_block",
    )(tab, heads, *sources, x, gain)


def weights_kernel(tab, *refs):
    blocks, (gate_ref, up_ref, down_ref, acc_ref) = refs[:-4], refs[-4:]
    units = gate_ref.shape[1]
    half = blocks[0].shape[1] // 2
    held = [(b, b) for b in blocks[: HEADS // 2]]
    held += [(blocks[HEADS // 2], blocks[HEADS // 2 + 1])]
    held += [(b, b) for b in blocks[HEADS // 2 + 2 :]]
    for slot, (upper, lower) in enumerate(held):
        chip = tab[slot]
        first = blocks[HEADS // 2].shape[0]
        rows = first // 2
        share = down_ref.shape[0] // HEADS
        for pair in range(2):
            here = pl.ds(pl.multiple_of((pair * HEADS + chip) * rows, rows), rows)
            gate_ref[here, :] = upper[pair * rows : (pair + 1) * rows, :units]
            up_ref[here, :] = upper[pair * rows : (pair + 1) * rows, half : half + units]
        start = 0 if lower is not upper else first
        here = pl.ds(pl.multiple_of(chip * share, 8), share)
        acc_ref[here, :] = lower[start : start + share, :D].astype(WIDE)
    down_ref[...] = acc_ref[...].astype(LOW)


def weights(chips, blocks, units):
    return pl.pallas_call(
        weights_kernel,
        in_specs=[smem()] + [vmem()] * len(blocks),
        out_specs=[vmem()] * 3,
        out_shape=[
            jax.ShapeDtypeStruct((D, units), LOW),
            jax.ShapeDtypeStruct((D, units), LOW),
            jax.ShapeDtypeStruct((units, D), LOW),
        ],
        scratch_shapes=[pltpu.VMEM((units, D), WIDE)],
        cost_estimate=pl.CostEstimate(
            flops=0, bytes_accessed=12 * D * units, transcendentals=0
        ),
        name="weights",
    )(chips, *blocks)


def ffn_kernel(na, nb, ga, gb, g_ref, u_ref, d_ref, hid_ref, gg_ref, ug_ref, dn_ref):
    for t, (n_ref, c_ref) in enumerate(((na, ga), (nb, gb))):
        n = n_ref[...]
        gate = dot_nn(n, g_ref[...])
        upper = dot_nn(n, u_ref[...])
        sigma = jax.nn.sigmoid(gate)
        silu = gate * sigma
        hid_ref[t] = (silu * upper).astype(LOW)
        hg = dot_nt(c_ref[...], d_ref[...])
        gg = (hg * upper * sigma * (1.0 + gate * (1.0 - sigma))).astype(LOW)
        ug = (hg * silu).astype(LOW)
        gg_ref[t] = gg
        ug_ref[t] = ug
        dn_ref[t] = (dot_nt(gg, g_ref[...]) + dot_nt(ug, u_ref[...])).astype(LOW)


def ffn(na, nb, ga, gb, g, u, d):
    count = na.shape[0]
    units = g.shape[1]
    return pl.pallas_call(
        ffn_kernel,
        in_specs=[vmem()] * 7,
        out_specs=[vmem()] * 4,
        out_shape=[jax.ShapeDtypeStruct((2, count, units), LOW)] * 3
        + [jax.ShapeDtypeStruct((2, count, D), LOW)],
        cost_estimate=pl.CostEstimate(
            flops=20 * count * D * units,
            bytes_accessed=6 * D * units + 16 * count * D,
            transcendentals=2 * count * units,
        ),
        name="ffn",
    )(na, nb, ga, gb, g, u, d)


def grads_kernel(tab, *refs):
    ns, ups, (hid_l, gg_l, ug_l, hid_r, gg_r, ug_r, out_ref, parts_ref) = (
        refs[:4], refs[4:8], refs[8:],
    )
    wide = parts_ref.shape[2]
    half = wide // 2
    units = hid_l.shape[2]
    share = units // HEADS
    own = out_ref.shape[1]
    rows = 2 * own
    edge = units - units % HEAD_DIM

    def tokens(near, away):
        return jnp.concatenate([near[0], near[1], away[0], away[1]], axis=0)

    n = jnp.concatenate([v[...] for v in ns], axis=0)
    up = jnp.concatenate([v[...] for v in ups], axis=0)
    for near, away, start in ((gg_l, gg_r, 0), (ug_l, ug_r, half)):
        total = dot_tn(n, tokens(near, away)).astype(LOW)
        for h in range(HEADS):
            slot = tab[h]
            for pair in range(2):
                first = (pair * HEADS + h) * rows
                here = slice(pair * rows, (pair + 1) * rows)
                parts_ref[slot, here, start + edge : start + half] = jnp.zeros(
                    (rows, half - edge), LOW
                )
                parts_ref[slot, here, start : start + units] = total[first : first + rows]
    total = dot_tn(tokens(hid_l, hid_r), up)
    strip = wide - D
    for h in range(HEADS):
        slot = tab[h]
        piece = total[h * share : (h + 1) * share].astype(LOW)
        parts_ref[slot, 2 * rows : 2 * rows + share, :D] = piece
        parts_ref[slot, 2 * rows : 2 * rows + share, D:] = jnp.zeros((share, strip), LOW)
        for i in range(D // strip):
            parts_ref[slot, 2 * rows + i * own : 2 * rows + (i + 1) * own, D:] = out_ref[
                h, :, i * strip : (i + 1) * strip
            ]


def weight_grads(slot_of, ns, ups, near, away, out, height, wide):
    count = ns[0].shape[0]
    units = near[0].shape[2]
    return pl.pallas_call(
        grads_kernel,
        in_specs=[smem()] + [vmem()] * 15,
        out_specs=vmem(),
        out_shape=jax.ShapeDtypeStruct((HEADS, height, wide), LOW),
        cost_estimate=pl.CostEstimate(
            flops=24 * count * D * units, bytes_accessed=14 * 2**20, transcendentals=0
        ),
        name="weight_grads",
    )(slot_of, *ns, *ups, *near, *away, out)


def mid_kernel(mid_ref, pa, pb, pc, up_ref, gain_ref, w_ref, mg_ref, bg_ref, ag_ref):
    mid = mid_ref[...]
    scaled = (pa[...].astype(WIDE) + pb[...].astype(WIDE) + pc[...].astype(WIDE)) * gain_ref[
        ...
    ].astype(WIDE)
    r = lax.rsqrt(jnp.mean(mid * mid, axis=-1, keepdims=True) + EPSILON)
    inner = jnp.mean(scaled * mid, axis=-1, keepdims=True)
    mid_grad = up_ref[...].astype(WIDE) + r * scaled - mid * (r * r * r * inner)
    mg_ref[...] = mid_grad
    branch = mid_grad.astype(LOW)
    bg_ref[...] = branch
    att = dot_nt(branch, w_ref[...]).astype(LOW)
    for h in range(HEADS):
        ag_ref[h] = att[:, h * HEAD_DIM : (h + 1) * HEAD_DIM]


def mid_block(mid, pa, pb, pc, up, gain, w):
    count = mid.shape[0]
    return pl.pallas_call(
        mid_kernel,
        in_specs=[vmem()] * 7,
        out_specs=[vmem()] * 3,
        out_shape=[
            jax.ShapeDtypeStruct((count, D), WIDE),
            jax.ShapeDtypeStruct((count, D), LOW),
            jax.ShapeDtypeStruct((HEADS, count, HEAD_DIM), LOW),
        ],
        cost_estimate=pl.CostEstimate(
            flops=2 * count * D * D, bytes_accessed=6 * 2**20, transcendentals=0
        ),
        name="mid_block",
    )(mid, pa, pb, pc, up, gain, w)


def qkv_back_kernel(tab, dq_ref, own_ref, got_ref, cos_ref, sin_ref, w_ref, dx_ref, g_ref):
    c, s = cos_ref[0], sin_ref[0]

    def rot(v):
        return v * c - pltpu.roll(v, HEAD_DIM // 2, 1) * s

    dq = rot(dq_ref[0] * SCALE).astype(LOW)
    dk = rot((own_ref[0, 0] + got_ref[0, 0].astype(WIDE)) * SCALE).astype(LOW)
    dv = (own_ref[1, 0] + got_ref[1, 0].astype(WIDE)).astype(LOW)
    grads = jnp.concatenate([dq, dk, dv], axis=1)
    g_ref[0] = grads
    dx_ref[0] = dot_nt(grads, w_ref[...]).astype(LOW)


def qkv_back(chips, dq, own, got, cos, sin, w):
    count = dq.shape[1]
    block = pl.BlockSpec((1, count, HEAD_DIM), lambda i, t: (t[i], 0, 0))
    pair = pl.BlockSpec((2, 1, count, HEAD_DIM), lambda i, t: (0, t[i], 0, 0))
    return pl.pallas_call(
        qkv_back_kernel,
        grid_spec=pltpu.PrefetchScalarGridSpec(
            num_scalar_prefetch=1,
            grid=(HEADS,),
            in_specs=[
                block, pair, pair, block, block,
                pl.BlockSpec((D, 3 * HEAD_DIM), lambda i, t: (0, 0)),
            ],
            out_specs=[
                pl.BlockSpec((1, count, D), lambda i, t: (i, 0, 0)),
                pl.BlockSpec((1, count, 3 * HEAD_DIM), lambda i, t: (t[i], 0, 0)),
            ],
        ),
        out_shape=[
            jax.ShapeDtypeStruct((HEADS, count, D), LOW),
            jax.ShapeDtypeStruct((HEADS, count, 3 * HEAD_DIM), LOW),
        ],
        cost_estimate=pl.CostEstimate(
            flops=2 * HEADS * count * D * 3 * HEAD_DIM,
            bytes_accessed=4 * HEADS * count * D,
            transcendentals=0,
        ),
        name="qkv_back",
    )(chips, dq, own, got, cos, sin, w)


def local(
    far,
    tokens,
    segment_ids,
    second_doc,
    memory_index,
    cache_keys,
    cache_values,
    first_gain,
    query_weight,
    key_weight,
    value_weight,
    out_weight,
    second_gain,
    gate_weight,
    up_weight,
    down_weight,
    cotangent,
):
    x = tokens[0]
    upstream = cotangent[0]
    count = x.shape[0]
    blocks = count // QUERY_BLOCK
    rows = query_weight.shape[0]
    share = down_weight.shape[0]
    units = far * HEADS * share
    chip, core, pair = lax.axis_index("h"), lax.axis_index("c"), lax.axis_index("dl")
    mine = jnp.where(chip % 2 == 0, chip // 2, HEADS - 1 - chip // 2)
    slots = jnp.arange(HEADS, dtype=jnp.int32)
    chips = at_place(mine - slots)

    def by_head(w):
        return w.reshape(rows, HEADS, HEAD_DIM).transpose(1, 0, 2)

    picked = memory_index[0].transpose(1, 0, 2)
    seg_rows = jnp.broadcast_to(
        segment_ids[0].astype(LOW).reshape(1, blocks, QUERY_BLOCK), (HEADS, blocks, QUERY_BLOCK)
    )
    gains = jnp.concatenate([first_gain, second_gain])
    gain_rows = jnp.broadcast_to(
        jnp.pad(gains, (0, HEAD_DIM - 2 * rows)).reshape(1, 1, HEAD_DIM), (HEADS, 1, HEAD_DIM)
    )
    pack = jnp.concatenate(
        [
            by_head(query_weight),
            by_head(key_weight),
            by_head(value_weight),
            seg_rows,
            (picked // MEM_ROWS).astype(LOW),
            (picked % MEM_ROWS).astype(LOW),
            gain_rows,
        ],
        axis=1,
    )
    height = pack.shape[1]
    pack = jnp.pad(pack, ((0, 0), (0, -height % 16), (0, 0)))

    block = jnp.concatenate([x, out_weight], axis=0)
    split = count // 2
    forth, back = [block, turn(block, 1)], [block, turn(block, -1)]
    pack, forth[1], back[1] = lax.optimization_barrier((pack, forth[1], back[1]))
    got = exchange(pack)
    for step in range(HEADS // 2 - 2):
        forth.append(turn(forth[-1], 1))
        back.append(turn(back[-1], -1))
        if step == 0:
            got, forth[-1], back[-1] = lax.optimization_barrier((got, forth[-1], back[-1]))
    far_first, far_last = turn(forth[-1][:split], 1), turn(back[-1][split:], -1)
    x_slots = [((v, count),) for v in forth] + [((far_first, split), (far_last, count - split))]
    x_slots += [((v, count),) for v in back[:0:-1]]
    outs = [v[count:] for v in forth] + [far_last[count - split :]]
    outs = jnp.stack(outs + [v[count:] for v in back[:0:-1]])
    got_c = swap(got, "c")
    got_y = swap(got, "dl")
    got_yc = swap(got_y, "c")
    near = pick(core, jnp.stack([got, got_c]), jnp.stack([got_c, got]))
    away = pick(core, jnp.stack([got_y, got_yc]), jnp.stack([got_yc, got_y]))
    every = pick(pair, jnp.stack([near, away]), jnp.stack([away, near]))
    every = every.transpose(2, 0, 1, 3, 4)
    if far > 1:
        every = lax.all_gather(every, "dh", axis=0)
    else:
        every = every[None]
    every = every.transpose(0, 2, 1, 3, 4, 5)
    w_qkv = jnp.concatenate(
        [every[..., i * rows : (i + 1) * rows, :].reshape(D, HEAD_DIM) for i in range(3)], axis=1
    )
    gain_all = every[..., 3 * rows + 3 * blocks, : 2 * rows].reshape(-1, 2, rows)
    gain_one = gain_all[:, 0].reshape(1, D)
    gain_two = gain_all[:, 1].reshape(1, D)

    def seg_of(blocks_of):
        return (
            blocks_of[:, 3 * rows : 3 * rows + blocks]
            .astype(WIDE)
            .astype(jnp.int32)
            .reshape(HEADS, count)
        )

    seg_own = seg_of(got)
    seg_oth = seg_of(got_c)
    idx = (
        got[:, 3 * rows + blocks : 3 * rows + 2 * blocks].astype(WIDE) * MEM_ROWS
        + got[:, 3 * rows + 2 * blocks : 3 * rows + 3 * blocks].astype(WIDE)
    ).astype(jnp.int32)
    idx = idx.reshape(HEADS, count, 1)

    block_docs = seg_own[:, ::QUERY_BLOCK]
    docs = second_doc.shape[1]
    doc_ids = jnp.arange(docs, dtype=jnp.int32)
    mates = jnp.sum(
        jnp.where(block_docs[:, :, None] == doc_ids, second_doc[0][None, None, :], 0), axis=-1
    )
    seg_all = jnp.concatenate([seg_own, seg_oth], axis=0)
    before = jnp.sum(
        (seg_all.reshape(1, -1) < block_docs[:, :1]).astype(jnp.int32), axis=1
    )
    tab = jnp.concatenate(
        [
            block_docs.reshape(-1),
            mates.reshape(-1),
            before // (2 * count),
            jnp.stack([core, chip]),
        ]
    ).astype(jnp.int32)

    half = HEAD_DIM // 2
    freqs = 10000.0 ** (-jnp.arange(half, dtype=WIDE) * 2.0 / (2 * half))
    positions = ((2 * slots + core) * count)[:, None] + jnp.arange(count, dtype=jnp.int32)[None]
    turned = positions.astype(WIDE)[:, :, None] * freqs
    cosine, sine = jnp.cos(turned), jnp.sin(turned)
    cosine = jnp.concatenate([cosine, cosine], axis=-1)
    sine = jnp.concatenate([-sine, sine], axis=-1)

    half = units + -units % HEAD_DIM
    wide = 2 * half

    def by_owner(w):
        w = w.reshape(rows, far, 2, HEADS, 2, share).transpose(2, 4, 0, 1, 3, 5)
        return jnp.pad(w.reshape(2, 2, rows, units), ((0, 0),) * 3 + ((0, half - units),))

    gu = jnp.concatenate([by_owner(gate_weight), by_owner(up_weight)], axis=-1)
    kept = pick(core, gu[:, 0], gu[:, 1])
    came = swap(pick(core, gu[:, 1], gu[:, 0]), "c")
    gu = pick(core, jnp.stack([kept, came], 1), jnp.stack([came, kept], 1))
    kept = pick(pair, gu[0], gu[1])
    came = swap(pick(pair, gu[1], gu[0]), "dl")
    gu = pick(pair, jnp.stack([kept, came]), jnp.stack([came, kept])).reshape(4 * rows, wide)
    bundle = jnp.concatenate([gu, jnp.pad(down_weight, ((0, 0), (0, wide - D)))], axis=0)
    height = 4 * rows + share
    if far > 1:
        bundle = lax.all_gather(bundle, "dh", axis=0, tiled=True)
    upper = bundle.shape[0] * 4 * rows // height if far == 1 else bundle.shape[0] // 2
    bundle, *_ = lax.optimization_barrier((bundle, far_first, far_last))
    forth, back = [bundle], [bundle]
    for step in range(HEADS // 2 - 1):
        forth.append(turn(forth[-1], 1))
        back.append(turn(back[-1], -1))
    w_slots = forth + [turn(forth[-1][:upper], 1), turn(back[-1][upper:], -1)] + back[:0:-1]

    up_c = swap(upstream, "c")
    up_y = swap(upstream, "dl")
    up_yc = swap(up_y, "c")

    held = ()
    for order in ([0, 1, 7, 2, 6], [3, 5, 4]):
        held = qkv_blocks(
            at_place(mine - jnp.asarray(order, jnp.int32)).astype(jnp.int32),
            [x_slots[i] for i in order],
            gain_one,
            w_qkv,
            cosine,
            sine,
            held,
        )
    queries, own, normed_one = held
    outs_c = swap(outs, "c")
    outs_y = swap(outs, "dl")
    outs_yc = swap(outs_y, "c")
    other = swap(own, "c")
    other, up_c, up_y, up_yc = lax.optimization_barrier((other, up_c, up_y, up_yc))

    seg_thin = seg_own.reshape(HEADS, count, 1)
    seg_own_row = seg_own.reshape(HEADS, 1, count)
    seg_oth_row = seg_oth.reshape(HEADS, 1, count)
    attention, attention_low, lse, memory = attend(
        tab,
        queries,
        own,
        other,
        seg_thin,
        seg_own_row,
        seg_oth_row,
        idx,
        cache_keys[0].reshape(-1, D),
        cache_values[0].reshape(-1, D),
    )

    heads = exchange(attention_low)
    slot_of = lax.rem(mine - jnp.asarray(PLACE, jnp.int32) + HEADS, HEADS).astype(jnp.int32)
    if far == 1:
        sources = [outs, outs_c, outs_y, outs_yc]
    else:
        near = pick(core, jnp.stack([outs, outs_c], 1), jnp.stack([outs_c, outs], 1))
        away = pick(core, jnp.stack([outs_y, outs_yc], 1), jnp.stack([outs_yc, outs_y], 1))
        sources = pick(pair, jnp.stack([near, away]), jnp.stack([away, near]))
        sources = lax.all_gather(jnp.take(sources, slot_of, axis=1), "dh", axis=0)
        sources = [sources.reshape(D, D)]
    where = jnp.concatenate([chips, jnp.stack([pair, core])]).astype(jnp.int32)
    attended, mid, normed_two, out_w = out_block(where, heads, sources, x, gain_two)

    if far == 1:
        gate_w, up_w, down_w = weights(where, w_slots, units)
    else:
        middle = jnp.concatenate(w_slots[HEADS // 2 : HEADS // 2 + 2], axis=0)
        every = jnp.stack(w_slots[: HEADS // 2] + [middle] + w_slots[HEADS // 2 + 2 :])
        every = jnp.take(every, slot_of, axis=0).reshape(HEADS, far, height, wide)
        gu = every[:, :, : 4 * rows].reshape(HEADS, far, 2, 2 * rows, wide)
        gu = gu.transpose(1, 2, 0, 3, 4).reshape(D, wide)
        gate_w, up_w = gu[:, :units], gu[:, half : half + units]
        down_w = every[:, :, 4 * rows :, :D].transpose(1, 0, 2, 3).reshape(units, D)

    n_c = swap(normed_two, "c")
    n_y = swap(normed_two, "dl")
    n_yc = swap(n_y, "c")
    hid_l, gg_l, ug_l, dn_l = ffn(normed_two, n_c, upstream, up_c, gate_w, up_w, down_w)
    hid_r, gg_r, ug_r, dn_r = ffn(n_y, n_yc, up_y, up_yc, gate_w, up_w, down_w)

    def sum_back(near, away):
        there = (away[0].astype(WIDE) + swap(away[1], "c").astype(WIDE)).astype(LOW)
        return near[0], swap(near[1], "c"), swap(there, "dl")

    parts = sum_back(dn_l, dn_r)
    mid_grad, branch, att_grad = mid_block(
        mid, *parts, upstream, gain_two, out_w
    )

    ups = exchange(att_grad)

    hid_l, gg_l, ug_l, hid_r, gg_r, ug_r, branch = lax.optimization_barrier(
        (hid_l, gg_l, ug_l, hid_r, gg_r, ug_r, branch)
    )

    def over_owner(w):
        w = w.reshape(far, 2, HEADS, 2, rows, D)
        kept = pick(core, w[:, :, :, 0], w[:, :, :, 1])
        came = swap(pick(core, w[:, :, :, 1], w[:, :, :, 0]), "c")
        w = kept.astype(WIDE) + came.astype(WIDE)
        kept = pick(pair, w[:, 0], w[:, 1])
        came = swap(pick(pair, w[:, 1], w[:, 0]).astype(LOW), "dl")
        return (kept + came.astype(WIDE)).astype(LOW).reshape(far * HEADS, rows, D)

    out_part = over_owner(
        jnp.einsum("td,te->de", attended, branch, preferred_element_type=WIDE).astype(LOW)
    )

    n_all, u_all = [normed_two, n_c, n_y, n_yc], [upstream, up_c, up_y, up_yc]
    near, away = (hid_l, gg_l, ug_l), (hid_r, gg_r, ug_r)
    strip = wide - D
    if far == 1:
        parts = weight_grads(slot_of, n_all, u_all, near, away, out_part, height, wide)
    else:

        def over_tokens(left, right):
            return jnp.einsum(
                "gtd,gtf->df", left, right, preferred_element_type=WIDE
            ).astype(LOW)

        def by_rows(w):
            w = jnp.pad(w, ((0, 0), (0, half - units)))
            return w.reshape(far, 2, HEADS, 2 * rows, half).transpose(2, 0, 1, 3, 4)

        n_all, u_all = jnp.stack(n_all), jnp.stack(u_all)
        hid, gg, ug = (jnp.concatenate(pieces, axis=0) for pieces in zip(near, away))
        gu = jnp.concatenate(
            [by_rows(over_tokens(n_all, gg)), by_rows(over_tokens(n_all, ug))], axis=-1
        ).reshape(HEADS, far, 4 * rows, wide)
        strips = out_part.reshape(far, HEADS, rows, D // strip, strip)
        strips = strips.transpose(1, 0, 3, 2, 4).reshape(HEADS, far, -1, strip)
        strips = jnp.pad(strips, ((0, 0), (0, 0), (0, share - strips.shape[2]), (0, 0)))
        down = over_tokens(hid, u_all).reshape(far, HEADS, share, D).transpose(1, 0, 2, 3)
        parts = jnp.concatenate([gu, jnp.concatenate([down, strips], axis=-1)], axis=2)
        parts = jnp.take(parts.reshape(HEADS, far * height, wide), chips, axis=0)
    ups, parts = lax.optimization_barrier((ups, parts))

    def plus(block, arrived, start):
        size = arrived.shape[0]
        total = block[start : start + size].astype(WIDE) + arrived.astype(WIDE)
        pieces = [block[:start], total.astype(LOW), block[start + size :]]
        return jnp.concatenate([piece for piece in pieces if piece.shape[0]], axis=0)

    def ring_sum(blocks, split):
        middle = blocks[HEADS // 2]
        forth, back = middle[:split], middle[split:]
        for step in range(1, HEADS // 2):
            forth = plus(blocks[HEADS // 2 + step], turn(forth, 1), 0)
            back = plus(blocks[HEADS // 2 - step], turn(back, -1), split if step == 1 else 0)
        forth, back = turn(forth, 1), turn(back, -1)
        return blocks[0].astype(WIDE) + forth.astype(WIDE) + back.astype(WIDE)

    summed = ring_sum(parts, upper).astype(LOW)
    if far > 1:
        summed = lax.psum_scatter(summed, "dh", scatter_dimension=0, tiled=True)
    down_w_grad = summed[4 * rows : 4 * rows + share, :D].astype(WIDE)
    out_w_grad = jnp.concatenate(
        [
            summed[4 * rows + i * rows : 4 * rows + (i + 1) * rows, D:]
            for i in range(D // strip)
        ],
        axis=1,
    ).astype(WIDE)
    gu = summed[: 4 * rows].reshape(2, 2, rows, wide)
    kept = pick(core, gu[:, 0], gu[:, 1])
    came = swap(pick(core, gu[:, 1], gu[:, 0]), "c")
    gu = pick(core, jnp.stack([kept, came], 1), jnp.stack([came, kept], 1))
    kept = pick(pair, gu[0], gu[1])
    came = swap(pick(pair, gu[1], gu[0]), "dl")
    gu = pick(pair, jnp.stack([kept, came]), jnp.stack([came, kept]))
    gu = jnp.stack([gu[..., :units], gu[..., half : half + units]])
    gu = (
        gu.reshape(2, 2, 2, rows, far, HEADS, share)
        .transpose(0, 3, 4, 1, 5, 2, 6)
        .reshape(2, rows, FF)
        .astype(WIDE)
    )
    gate_w_grad, up_w_grad = gu[0], gu[1]

    out_l = jnp.einsum("gtf,fd->gtd", hid_l, down_w, preferred_element_type=WIDE).astype(LOW)
    out_r = jnp.einsum("gtf,fd->gtd", hid_r, down_w, preferred_element_type=WIDE).astype(LOW)
    output = mid
    for part in sum_back(out_l, out_r):
        output = output + part.astype(WIDE)
    output = output.astype(LOW)

    dq, d_own, d_oth = attend_back(
        tab, queries, ups, attention, lse, own, other, memory, seg_thin, seg_own_row, seg_oth_row
    )
    d_got = swap(d_oth, "c")
    dx, grads = qkv_back(chips.astype(jnp.int32), dq, d_own, d_got, cosine, sine, w_qkv)

    normed_one_grad = ring_sum(dx, split)

    dw = jnp.einsum("std,stg->dg", normed_one, grads, preferred_element_type=WIDE).astype(LOW)
    dw = dw.reshape(far, 2, HEADS, 2, rows, 3 * HEAD_DIM)
    kept = pick(core, dw[:, :, :, 0], dw[:, :, :, 1])
    came = swap(pick(core, dw[:, :, :, 1], dw[:, :, :, 0]), "c")
    dw = kept.astype(WIDE) + came.astype(WIDE)
    kept = pick(pair, dw[:, 0], dw[:, 1])
    came = swap(pick(pair, dw[:, 1], dw[:, 0]).astype(LOW), "dl")
    dw = (kept + came.astype(WIDE)).astype(LOW)
    if far > 1:
        dw = lax.psum_scatter(dw, "dh", scatter_dimension=0, tiled=True)
    qkv_grads = exchange(dw[0]).astype(WIDE)

    wide_x = x.astype(WIDE)
    r = lax.rsqrt(jnp.mean(wide_x * wide_x, axis=-1, keepdims=True) + EPSILON)
    scaled = normed_one_grad * gain_one.astype(WIDE)
    inner = jnp.mean(scaled * wide_x, axis=-1, keepdims=True)
    input_grad = mid_grad + r * scaled - wide_x * (r * r * r * inner)

    q_w_grad, k_w_grad, v_w_grad = (
        qkv_grads[:, :, i * HEAD_DIM : (i + 1) * HEAD_DIM].transpose(1, 0, 2).reshape(rows, D)
        for i in range(3)
    )

    def gain_grad(gain, pairs):
        total = 0.0
        for grad, weight in pairs:
            total = total + jnp.sum(grad * weight.astype(WIDE), axis=1)
        return total / gain.astype(WIDE)

    first_gain_grad = gain_grad(
        first_gain,
        ((q_w_grad, query_weight), (k_w_grad, key_weight), (v_w_grad, value_weight)),
    )
    second_gain_grad = gain_grad(
        second_gain, ((gate_w_grad, gate_weight), (up_w_grad, up_weight))
    )
    return (
        output[None],
        input_grad[None],
        first_gain_grad,
        q_w_grad,
        k_w_grad,
        v_w_grad,
        out_w_grad,
        second_gain_grad,
        gate_w_grad,
        up_w_grad,
        down_w_grad,
    )


def solution(mesh):
    far = mesh.shape["dp"] // 2
    cores = mesh.shape["seq"] // HEADS
    fine = Mesh(mesh.devices.reshape(far, 2, HEADS, cores), ("dh", "dl", "h", "c"))
    dp, seq, every = ("dh", "dl"), ("h", "c"), ("dh", "dl", "h", "c")
    rows = P(every, None)
    return jax.shard_map(
        functools.partial(local, far),
        mesh=fine,
        in_specs=(
            P(dp, seq, None),
            P(dp, seq),
            P(dp, None),
            P(dp, seq, None, None),
            P(dp, None, None, None),
            P(dp, None, None, None),
            P(every),
            rows,
            rows,
            rows,
            rows,
            P(every),
            rows,
            rows,
            rows,
            P(dp, seq, None),
        ),
        out_specs=(
            P(dp, seq, None),
            P(dp, seq, None),
            P(every),
            rows,
            rows,
            rows,
            rows,
            P(every),
            rows,
            rows,
            rows,
        ),
        check_vma=False,
    )
```

```python
import functools
import math

import jax
import jax.numpy as jnp
from jax import lax
from jax.experimental import pallas as pl
from jax.experimental.pallas import tpu as pltpu
from jax.sharding import Mesh
from jax.sharding import PartitionSpec as P

D = 1024
FF = 2816
HEADS = 8
HEAD_DIM = 128
QUERY_BLOCK = 128
MEM_ROWS = 256
EPSILON = 1e-05
NEGATIVE = -1e30
SCALE = 1.0 / math.sqrt(HEAD_DIM)
LOG2 = SCALE * math.log2(math.e)
LOW = jnp.bfloat16
WIDE = jnp.float32

RING = [2 * i for i in range(HEADS // 2)] + [2 * i + 1 for i in reversed(range(HEADS // 2))]
PLACE = [RING.index(i) for i in range(HEADS)]


def dot_nn(a, b):
    return lax.dot_general(a, b, (((1,), (0,)), ((), ())), preferred_element_type=WIDE)


def dot_nt(a, b):
    return lax.dot_general(a, b, (((1,), (1,)), ((), ())), preferred_element_type=WIDE)


def dot_tn(a, b):
    return lax.dot_general(a, b, (((0,), (0,)), ((), ())), preferred_element_type=WIDE)


def swap(block, axis):
    return lax.ppermute(block, axis, [(0, 1), (1, 0)])


def turn(block, distance):
    route = [(RING[i], RING[(i + distance) % HEADS]) for i in range(HEADS)]
    return lax.ppermute(block, "h", route)


def at_place(place):
    place = lax.rem(place + 2 * HEADS, HEADS)
    return jnp.where(place < HEADS // 2, 2 * place, 2 * (HEADS - 1 - place) + 1)


def exchange(blocks):
    return lax.all_to_all(blocks, "h", 0, 0)


def pick(flag, first, second):
    return jnp.where(flag == 0, first, second)


def smem():
    return pl.BlockSpec(memory_space=pltpu.SMEM)


def vmem():
    return pl.BlockSpec(memory_space=pltpu.VMEM)


def qkv_kernel(parts, tab, *refs):
    xs, (gain_ref, w_ref, cos_ref, sin_ref) = refs[: sum(parts)], refs[sum(parts) : sum(parts) + 4]
    q_ref, kv_ref, n_ref, x_ref = refs[-4:]
    i = pl.program_id(0)
    first = 0
    for step, number in enumerate(parts):

        @pl.when(i == step)
        def _(blocks=xs[first : first + number]):
            row = 0
            for block in blocks:
                size = block.shape[0]
                x_ref[row : row + size, :] = block[...]
                row += size

        first += number
    x = x_ref[...].astype(WIDE)
    r = lax.rsqrt(jnp.mean(x * x, axis=-1, keepdims=True) + EPSILON)
    normed = (x * r * gain_ref[...].astype(WIDE)).astype(LOW)
    n_ref[0] = normed
    out = dot_nn(normed, w_ref[...])
    c, s = cos_ref[0], sin_ref[0]

    def rot(v):
        return v * c + pltpu.roll(v, HEAD_DIM // 2, 1) * s

    q_ref[0] = rot(out[:, :HEAD_DIM]).astype(LOW)
    kv_ref[0, 0] = rot(out[:, HEAD_DIM : 2 * HEAD_DIM]).astype(LOW)
    kv_ref[1, 0] = out[:, 2 * HEAD_DIM :].astype(LOW)


def qkv_blocks(chips, xs, gain, w, cos, sin, held):
    count = cos.shape[1]
    flat = [piece for block in xs for piece, _ in block]
    read = [size for block in xs for _, size in block]

    def whole(shape):
        return pl.BlockSpec(shape, lambda i, t: (0, 0))

    def block(*shape):
        return pl.BlockSpec((1, *shape), lambda i, t: (t[i], 0, 0))

    spec = pltpu.PrefetchScalarGridSpec(
        num_scalar_prefetch=1,
        grid=(len(xs),),
        in_specs=[whole((size, D)) for size in read]
        + [whole((1, D)), whole((D, 3 * HEAD_DIM)), block(count, HEAD_DIM), block(count, HEAD_DIM)]
        + [pl.BlockSpec(memory_space=pl.ANY)] * len(held),
        out_specs=[
            block(count, HEAD_DIM),
            pl.BlockSpec((2, 1, count, HEAD_DIM), lambda i, t: (0, t[i], 0, 0)),
            block(count, D),
        ],
        scratch_shapes=[pltpu.VMEM((count, D), LOW)],
    )
    return pl.pallas_call(
        functools.partial(qkv_kernel, [len(block) for block in xs]),
        grid_spec=spec,
        out_shape=[
            jax.ShapeDtypeStruct((HEADS, count, HEAD_DIM), LOW),
            jax.ShapeDtypeStruct((2, HEADS, count, HEAD_DIM), LOW),
            jax.ShapeDtypeStruct((HEADS, count, D), LOW),
        ],
        input_output_aliases={len(flat) + 5 + i: i for i in range(len(held))},
        cost_estimate=pl.CostEstimate(
            flops=2 * len(xs) * count * D * 3 * HEAD_DIM,
            bytes_accessed=5 * len(xs) * count * D,
            transcendentals=0,
        ),
        name=f"qkv{len(xs)}",
    )(chips, *flat, gain, w, cos, sin, *held)


def causal(count):
    rows = lax.broadcasted_iota(jnp.int32, (count, count), 0)
    return lax.broadcasted_iota(jnp.int32, (count, count), 1) <= rows


def attend_kernel(
    tab, q_ref, own_ref, oth_ref, segq_ref, sego_ref, segt_ref, idx_ref, ck_ref, cv_ref,
    o_ref, low_ref, lse_ref, mem_ref,
):
    i = pl.program_id(0)
    parity = tab[40]
    count = q_ref.shape[1]
    q = q_ref[0]
    segq = segq_ref[0]

    s1 = dot_nt(q, own_ref[0, i]) * LOG2
    s2 = dot_nt(q, oth_ref[0, i]) * LOG2
    s1 = jnp.where((sego_ref[i] == segq) & causal(count), s1, NEGATIVE)
    s2 = jnp.where(segt_ref[i] == segq + 64 * (1 - parity), s2, NEGATIVE)
    memory = []
    for b in range(count // QUERY_BLOCK):
        rows = slice(b * QUERY_BLOCK, (b + 1) * QUERY_BLOCK)
        doc = tab[2 * i + b]
        mate = tab[16 + 2 * i + b]
        idx = idx_ref[0, rows, :]
        lane = lax.broadcasted_iota(jnp.int32, (QUERY_BLOCK, MEM_ROWS), 1)
        first = jnp.where(idx == lane, 1.0, 0.0).astype(LOW)
        second = jnp.where(idx == lane + MEM_ROWS, 1.0, 0.0).astype(LOW)
        here = pl.ds(pl.multiple_of(doc * MEM_ROWS, MEM_ROWS), MEM_ROWS)
        there = pl.ds(pl.multiple_of(mate * MEM_ROWS, MEM_ROWS), MEM_ROWS)
        mk = (dot_nn(first, ck_ref[here, :]) + dot_nn(second, ck_ref[there, :])).astype(LOW)
        mv = (dot_nn(first, cv_ref[here, :]) + dot_nn(second, cv_ref[there, :])).astype(LOW)
        mem_ref[0, 0, rows, :] = mk
        mem_ref[1, 0, rows, :] = mv
        s = jnp.where(segq[rows] == doc, dot_nt(q[rows], mk) * LOG2, NEGATIVE)
        memory.append((s, mv))
    sm = jnp.concatenate([s for s, _ in memory], axis=0)
    top = jnp.maximum(
        jnp.max(jnp.maximum(s1, s2), axis=-1, keepdims=True), jnp.max(sm, axis=-1, keepdims=True)
    )
    p1 = jnp.exp2(s1 - top)
    p2 = jnp.exp2(s2 - top)
    pm = jnp.exp2(sm - top)
    total = jnp.sum(p1 + p2, axis=-1, keepdims=True) + jnp.sum(pm, axis=-1, keepdims=True)
    pm = pm.astype(LOW)
    acc = jnp.concatenate(
        [
            dot_nn(pm[b * QUERY_BLOCK : (b + 1) * QUERY_BLOCK], mv)
            for b, (_, mv) in enumerate(memory)
        ],
        axis=0,
    )
    acc = acc + dot_nn(p1.astype(LOW), own_ref[1, i]) + dot_nn(p2.astype(LOW), oth_ref[1, i])

    def body(j, state):
        top, total, acc = state
        s1 = dot_nt(q, own_ref[0, j]) * LOG2
        s2 = dot_nt(q, oth_ref[0, j]) * LOG2
        s1 = jnp.where(sego_ref[j] == segq, s1, NEGATIVE)
        s2 = jnp.where(segt_ref[j] == segq, s2, NEGATIVE)
        fresh = jnp.maximum(top, jnp.max(jnp.maximum(s1, s2), axis=-1, keepdims=True))
        p1 = jnp.exp2(s1 - fresh)
        p2 = jnp.exp2(s2 - fresh)
        decay = jnp.exp2(top - fresh)
        total = total * decay + jnp.sum(p1 + p2, axis=-1, keepdims=True)
        acc = (
            acc * decay
            + dot_nn(p1.astype(LOW), own_ref[1, j])
            + dot_nn(p2.astype(LOW), oth_ref[1, j])
        )
        return fresh, total, acc

    top, total, acc = lax.fori_loop(tab[32 + i], i, body, (top, total, acc))
    out = acc / total
    o_ref[0] = out
    low_ref[0] = out.astype(LOW)
    lse_ref[0] = top + jnp.log2(total)


def attend(tab, q, own, oth, segq, sego, segt, idx, ck, cv):
    count = q.shape[1]
    block = pl.BlockSpec((1, count, HEAD_DIM), lambda i, t: (i, 0, 0))
    thin = pl.BlockSpec((1, count, 1), lambda i, t: (i, 0, 0))
    whole = pl.BlockSpec((2, HEADS, count, HEAD_DIM), lambda i, t: (0, 0, 0, 0))
    segs = pl.BlockSpec((HEADS, 1, count), lambda i, t: (0, 0, 0))
    cache = pl.BlockSpec((ck.shape[0], HEAD_DIM), lambda i, t: (0, t[41]))
    mem = pl.BlockSpec((2, 1, count, HEAD_DIM), lambda i, t: (0, i, 0, 0))
    return pl.pallas_call(
        attend_kernel,
        grid_spec=pltpu.PrefetchScalarGridSpec(
            num_scalar_prefetch=1,
            grid=(HEADS,),
            in_specs=[block, whole, whole, thin, segs, segs, thin, cache, cache],
            out_specs=[block, block, thin, mem],
        ),
        out_shape=[
            jax.ShapeDtypeStruct((HEADS, count, HEAD_DIM), WIDE),
            jax.ShapeDtypeStruct((HEADS, count, HEAD_DIM), LOW),
            jax.ShapeDtypeStruct((HEADS, count, 1), WIDE),
            jax.ShapeDtypeStruct((2, HEADS, count, HEAD_DIM), LOW),
        ],
        cost_estimate=pl.CostEstimate(
            flops=25 * 10**9, bytes_accessed=6 * 2**20, transcendentals=3 * 10**6
        ),
        name="attend",
    )(tab, q, own, oth, segq, sego, segt, idx, ck, cv)


def attend_back_kernel(
    tab, q_ref, up_ref, o_ref, lse_ref, own_ref, oth_ref, mem_ref, segq_ref, sego_ref, segt_ref,
    dq_ref, down_ref, doth_ref, sum_ref,
):
    i = pl.program_id(0)

    @pl.when(i == 0)
    def _():
        sum_ref[...] = jnp.zeros_like(sum_ref)

    parity = tab[40]
    count = q_ref.shape[1]
    q = q_ref[0]
    up = up_ref[0]
    lse = lse_ref[0]
    segq = segq_ref[0]
    delta = jnp.sum(up.astype(WIDE) * o_ref[0], axis=-1, keepdims=True)
    partial = []
    for b in range(count // QUERY_BLOCK):
        rows = slice(b * QUERY_BLOCK, (b + 1) * QUERY_BLOCK)
        mk = mem_ref[0, 0, rows, :]
        mv = mem_ref[1, 0, rows, :]
        ok = segq[rows] == tab[2 * i + b]
        p = jnp.exp2(jnp.where(ok, dot_nt(q[rows], mk) * LOG2 - lse[rows], NEGATIVE))
        ds = (p * (dot_nt(up[rows], mv) - delta[rows])).astype(LOW)
        partial.append(dot_nn(ds, mk))

    def tile(side, ref, j, ok, dq):
        k = ref[0, j]
        v = ref[1, j]
        p = jnp.exp2(jnp.where(ok, dot_nt(q, k) * LOG2 - lse, NEGATIVE))
        ds = (p * (dot_nt(up, v) - delta)).astype(LOW)
        sum_ref[side, 0, j] += dot_tn(ds, q)
        sum_ref[side, 1, j] += dot_tn(p.astype(LOW), up)
        return dq + dot_nn(ds, k)

    dq = jnp.concatenate(partial, axis=0)
    dq = tile(0, own_ref, i, (sego_ref[i] == segq) & causal(count), dq)
    dq = tile(1, oth_ref, i, segt_ref[i] == segq + 64 * (1 - parity), dq)

    def body(j, dq):
        dq = tile(0, own_ref, j, sego_ref[j] == segq, dq)
        return tile(1, oth_ref, j, segt_ref[j] == segq, dq)

    dq_ref[0] = lax.fori_loop(tab[32 + i], i, body, dq)

    @pl.when(i == HEADS - 1)
    def _():
        down_ref[...] = sum_ref[0]
        doth_ref[...] = sum_ref[1].astype(LOW)


def attend_back(tab, q, up, o, lse, own, oth, mem, segq, sego, segt):
    count = q.shape[1]
    block = pl.BlockSpec((1, count, HEAD_DIM), lambda i, t: (i, 0, 0))
    thin = pl.BlockSpec((1, count, 1), lambda i, t: (i, 0, 0))
    whole = pl.BlockSpec((2, HEADS, count, HEAD_DIM), lambda i, t: (0, 0, 0, 0))
    segs = pl.BlockSpec((HEADS, 1, count), lambda i, t: (0, 0, 0))
    memory = pl.BlockSpec((2, 1, count, HEAD_DIM), lambda i, t: (0, i, 0, 0))
    return pl.pallas_call(
        attend_back_kernel,
        grid_spec=pltpu.PrefetchScalarGridSpec(
            num_scalar_prefetch=1,
            grid=(HEADS,),
            in_specs=[block, block, block, thin, whole, whole, memory, thin, segs, segs],
            out_specs=[block, whole, whole],
            scratch_shapes=[pltpu.VMEM((2, 2, HEADS, count, HEAD_DIM), WIDE)],
        ),
        out_shape=[
            jax.ShapeDtypeStruct((HEADS, count, HEAD_DIM), WIDE),
            jax.ShapeDtypeStruct((2, HEADS, count, HEAD_DIM), WIDE),
            jax.ShapeDtypeStruct((2, HEADS, count, HEAD_DIM), LOW),
        ],
        cost_estimate=pl.CostEstimate(
            flops=30 * 10**9, bytes_accessed=10 * 2**20, transcendentals=3 * 10**6
        ),
        name="attend_back",
    )(tab, q, up, o, lse, own, oth, mem, segq, sego, segt)


def place_rows(tab, sources, w_ref):
    rows = sources[0].shape[1]
    for k, source in enumerate(sources):
        pair = tab[8] if k < 2 else 1 - tab[8]
        core = tab[9] if k % 2 == 0 else 1 - tab[9]
        for slot in range(HEADS):
            start = ((pair * HEADS + tab[slot]) * 2 + core) * rows
            w_ref[pl.ds(pl.multiple_of(start, rows), rows), :] = source[slot]


def out_kernel(tab, heads_ref, *refs):
    sources, (x_ref, gain_ref, att_ref, mid_ref, n_ref, w_ref) = refs[:-6], refs[-6:]
    if len(sources) == 1:
        w_ref[...] = sources[0][...]
    else:
        place_rows(tab, sources, w_ref)
    for h in range(HEADS):
        att_ref[:, h * HEAD_DIM : (h + 1) * HEAD_DIM] = heads_ref[h]
    mid = x_ref[...].astype(WIDE) + dot_nn(att_ref[...], w_ref[...])
    mid_ref[...] = mid
    r = lax.rsqrt(jnp.mean(mid * mid, axis=-1, keepdims=True) + EPSILON)
    n_ref[...] = (mid * r * gain_ref[...].astype(WIDE)).astype(LOW)


def out_block(tab, heads, sources, x, gain):
    count = x.shape[0]
    return pl.pallas_call(
        out_kernel,
        in_specs=[smem()] + [vmem()] * (3 + len(sources)),
        out_specs=[vmem()] * 4,
        out_shape=[
            jax.ShapeDtypeStruct((count, D), LOW),
            jax.ShapeDtypeStruct((count, D), WIDE),
            jax.ShapeDtypeStruct((count, D), LOW),
            jax.ShapeDtypeStruct((D, D), LOW),
        ],
        cost_estimate=pl.CostEstimate(
            flops=2 * count * D * D, bytes_accessed=6 * 2**20, transcendentals=0
        ),
        name="out_block",
    )(tab, heads, *sources, x, gain)


def weights_kernel(tab, *refs):
    blocks, (gate_ref, up_ref, down_ref, acc_ref) = refs[:-4], refs[-4:]
    units = gate_ref.shape[1]
    half = blocks[0].shape[1] // 2
    held = [(b, b) for b in blocks[: HEADS // 2]]
    held += [(blocks[HEADS // 2], blocks[HEADS // 2 + 1])]
    held += [(b, b) for b in blocks[HEADS // 2 + 2 :]]
    for slot, (upper, lower) in enumerate(held):
        chip = tab[slot]
        first = blocks[HEADS // 2].shape[0]
        rows = first // 2
        share = down_ref.shape[0] // HEADS
        for pair in range(2):
            here = pl.ds(pl.multiple_of((pair * HEADS + chip) * rows, rows), rows)
            gate_ref[here, :] = upper[pair * rows : (pair + 1) * rows, :units]
            up_ref[here, :] = upper[pair * rows : (pair + 1) * rows, half : half + units]
        start = 0 if lower is not upper else first
        here = pl.ds(pl.multiple_of(chip * share, 8), share)
        acc_ref[here, :] = lower[start : start + share, :D].astype(WIDE)
    down_ref[...] = acc_ref[...].astype(LOW)


def weights(chips, blocks, units):
    return pl.pallas_call(
        weights_kernel,
        in_specs=[smem()] + [vmem()] * len(blocks),
        out_specs=[vmem()] * 3,
        out_shape=[
            jax.ShapeDtypeStruct((D, units), LOW),
            jax.ShapeDtypeStruct((D, units), LOW),
            jax.ShapeDtypeStruct((units, D), LOW),
        ],
        scratch_shapes=[pltpu.VMEM((units, D), WIDE)],
        cost_estimate=pl.CostEstimate(
            flops=0, bytes_accessed=12 * D * units, transcendentals=0
        ),
        name="weights",
    )(chips, *blocks)


def ffn_kernel(na, nb, ga, gb, g_ref, u_ref, d_ref, hid_ref, gg_ref, ug_ref, dn_ref):
    for t, (n_ref, c_ref) in enumerate(((na, ga), (nb, gb))):
        n = n_ref[...]
        gate = dot_nn(n, g_ref[...])
        upper = dot_nn(n, u_ref[...])
        sigma = jax.nn.sigmoid(gate)
        silu = gate * sigma
        hid_ref[t] = (silu * upper).astype(LOW)
        hg = dot_nt(c_ref[...], d_ref[...])
        gg = (hg * upper * sigma * (1.0 + gate * (1.0 - sigma))).astype(LOW)
        ug = (hg * silu).astype(LOW)
        gg_ref[t] = gg
        ug_ref[t] = ug
        dn_ref[t] = (dot_nt(gg, g_ref[...]) + dot_nt(ug, u_ref[...])).astype(LOW)


def ffn(na, nb, ga, gb, g, u, d):
    count = na.shape[0]
    units = g.shape[1]
    return pl.pallas_call(
        ffn_kernel,
        in_specs=[vmem()] * 7,
        out_specs=[vmem()] * 4,
        out_shape=[jax.ShapeDtypeStruct((2, count, units), LOW)] * 3
        + [jax.ShapeDtypeStruct((2, count, D), LOW)],
        cost_estimate=pl.CostEstimate(
            flops=20 * count * D * units,
            bytes_accessed=6 * D * units + 16 * count * D,
            transcendentals=2 * count * units,
        ),
        name="ffn",
    )(na, nb, ga, gb, g, u, d)


def grads_kernel(tab, *refs):
    ns, ups, (hid_l, gg_l, ug_l, hid_r, gg_r, ug_r, parts_ref) = (
        refs[:4], refs[4:8], refs[8:],
    )
    wide = parts_ref.shape[2]
    half = wide // 2
    units = hid_l.shape[2]
    share = units // HEADS
    rows = ns[0].shape[1] // (2 * HEADS)
    edge = units - units % HEAD_DIM

    def tokens(near, away):
        return jnp.concatenate([near[0], near[1], away[0], away[1]], axis=0)

    n = jnp.concatenate([v[...] for v in ns], axis=0)
    up = jnp.concatenate([v[...] for v in ups], axis=0)
    for near, away, start in ((gg_l, gg_r, 0), (ug_l, ug_r, half)):
        total = dot_tn(n, tokens(near, away)).astype(LOW)
        for h in range(HEADS):
            slot = tab[h]
            for pair in range(2):
                first = (pair * HEADS + h) * rows
                here = slice(pair * rows, (pair + 1) * rows)
                parts_ref[slot, here, start + edge : start + half] = jnp.zeros(
                    (rows, half - edge), LOW
                )
                parts_ref[slot, here, start : start + units] = total[first : first + rows]
    total = dot_tn(tokens(hid_l, hid_r), up)
    strip = wide - D
    for h in range(HEADS):
        slot = tab[h]
        piece = total[h * share : (h + 1) * share].astype(LOW)
        parts_ref[slot, 2 * rows : 2 * rows + share, :D] = piece
        parts_ref[slot, 2 * rows : 2 * rows + share, D:] = jnp.zeros((share, strip), LOW)


def weight_grads(slot_of, ns, ups, near, away, height, wide):
    count = ns[0].shape[0]
    units = near[0].shape[2]
    return pl.pallas_call(
        grads_kernel,
        in_specs=[smem()] + [vmem()] * 14,
        out_specs=vmem(),
        out_shape=jax.ShapeDtypeStruct((HEADS, height, wide), LOW),
        cost_estimate=pl.CostEstimate(
            flops=24 * count * D * units, bytes_accessed=14 * 2**20, transcendentals=0
        ),
        name="weight_grads",
    )(slot_of, *ns, *ups, *near, *away)


def strips_kernel(tab, out_ref, strips_ref):
    rows, strip = out_ref.shape[1], strips_ref.shape[2]
    for slot in range(HEADS):
        for i in range(D // strip):
            strips_ref[slot, i * rows : (i + 1) * rows, :] = out_ref[
                tab[slot], :, i * strip : (i + 1) * strip
            ]


def out_strips(chips, out, strip):
    return pl.pallas_call(
        strips_kernel,
        in_specs=[smem(), vmem()],
        out_specs=vmem(),
        out_shape=jax.ShapeDtypeStruct((HEADS, out.shape[1] * D // strip, strip), LOW),
        cost_estimate=pl.CostEstimate(
            flops=0, bytes_accessed=4 * HEADS * out.shape[1] * D, transcendentals=0
        ),
        name="out_strips",
    )(chips, out)


def mid_kernel(mid_ref, pa, pb, pc, up_ref, gain_ref, w_ref, mg_ref, bg_ref, ag_ref):
    mid = mid_ref[...]
    scaled = (pa[...].astype(WIDE) + pb[...].astype(WIDE) + pc[...].astype(WIDE)) * gain_ref[
        ...
    ].astype(WIDE)
    r = lax.rsqrt(jnp.mean(mid * mid, axis=-1, keepdims=True) + EPSILON)
    inner = jnp.mean(scaled * mid, axis=-1, keepdims=True)
    mid_grad = up_ref[...].astype(WIDE) + r * scaled - mid * (r * r * r * inner)
    mg_ref[...] = mid_grad
    branch = mid_grad.astype(LOW)
    bg_ref[...] = branch
    att = dot_nt(branch, w_ref[...]).astype(LOW)
    for h in range(HEADS):
        ag_ref[h] = att[:, h * HEAD_DIM : (h + 1) * HEAD_DIM]


def mid_block(mid, pa, pb, pc, up, gain, w):
    count = mid.shape[0]
    return pl.pallas_call(
        mid_kernel,
        in_specs=[vmem()] * 7,
        out_specs=[vmem()] * 3,
        out_shape=[
            jax.ShapeDtypeStruct((count, D), WIDE),
            jax.ShapeDtypeStruct((count, D), LOW),
            jax.ShapeDtypeStruct((HEADS, count, HEAD_DIM), LOW),
        ],
        cost_estimate=pl.CostEstimate(
            flops=2 * count * D * D, bytes_accessed=6 * 2**20, transcendentals=0
        ),
        name="mid_block",
    )(mid, pa, pb, pc, up, gain, w)


def qkv_back_kernel(tab, dq_ref, own_ref, got_ref, cos_ref, sin_ref, w_ref, dx_ref, g_ref):
    c, s = cos_ref[0], sin_ref[0]

    def rot(v):
        return v * c - pltpu.roll(v, HEAD_DIM // 2, 1) * s

    dq = rot(dq_ref[0] * SCALE).astype(LOW)
    dk = rot((own_ref[0, 0] + got_ref[0, 0].astype(WIDE)) * SCALE).astype(LOW)
    dv = (own_ref[1, 0] + got_ref[1, 0].astype(WIDE)).astype(LOW)
    grads = jnp.concatenate([dq, dk, dv], axis=1)
    g_ref[0] = grads
    dx_ref[0] = dot_nt(grads, w_ref[...]).astype(LOW)


def qkv_back(chips, dq, own, got, cos, sin, w):
    count = dq.shape[1]
    block = pl.BlockSpec((1, count, HEAD_DIM), lambda i, t: (t[i], 0, 0))
    pair = pl.BlockSpec((2, 1, count, HEAD_DIM), lambda i, t: (0, t[i], 0, 0))
    return pl.pallas_call(
        qkv_back_kernel,
        grid_spec=pltpu.PrefetchScalarGridSpec(
            num_scalar_prefetch=1,
            grid=(HEADS,),
            in_specs=[
                block, pair, pair, block, block,
                pl.BlockSpec((D, 3 * HEAD_DIM), lambda i, t: (0, 0)),
            ],
            out_specs=[
                pl.BlockSpec((1, count, D), lambda i, t: (i, 0, 0)),
                pl.BlockSpec((1, count, 3 * HEAD_DIM), lambda i, t: (t[i], 0, 0)),
            ],
        ),
        out_shape=[
            jax.ShapeDtypeStruct((HEADS, count, D), LOW),
            jax.ShapeDtypeStruct((HEADS, count, 3 * HEAD_DIM), LOW),
        ],
        cost_estimate=pl.CostEstimate(
            flops=2 * HEADS * count * D * 3 * HEAD_DIM,
            bytes_accessed=4 * HEADS * count * D,
            transcendentals=0,
        ),
        name="qkv_back",
    )(chips, dq, own, got, cos, sin, w)


def local(
    far,
    tokens,
    segment_ids,
    second_doc,
    memory_index,
    cache_keys,
    cache_values,
    first_gain,
    query_weight,
    key_weight,
    value_weight,
    out_weight,
    second_gain,
    gate_weight,
    up_weight,
    down_weight,
    cotangent,
):
    x = tokens[0]
    upstream = cotangent[0]
    count = x.shape[0]
    blocks = count // QUERY_BLOCK
    rows = query_weight.shape[0]
    share = down_weight.shape[0]
    units = far * HEADS * share
    chip, core, pair = lax.axis_index("h"), lax.axis_index("c"), lax.axis_index("dl")
    mine = jnp.where(chip % 2 == 0, chip // 2, HEADS - 1 - chip // 2)
    slots = jnp.arange(HEADS, dtype=jnp.int32)
    chips = at_place(mine - slots)

    def by_head(w):
        return w.reshape(rows, HEADS, HEAD_DIM).transpose(1, 0, 2)

    picked = memory_index[0].transpose(1, 0, 2)
    seg_rows = jnp.broadcast_to(
        segment_ids[0].astype(LOW).reshape(1, blocks, QUERY_BLOCK), (HEADS, blocks, QUERY_BLOCK)
    )
    gains = jnp.concatenate([first_gain, second_gain])
    gain_rows = jnp.broadcast_to(
        jnp.pad(gains, (0, HEAD_DIM - 2 * rows)).reshape(1, 1, HEAD_DIM), (HEADS, 1, HEAD_DIM)
    )
    pack = jnp.concatenate(
        [
            by_head(query_weight),
            by_head(key_weight),
            by_head(value_weight),
            seg_rows,
            (picked // MEM_ROWS).astype(LOW),
            (picked % MEM_ROWS).astype(LOW),
            gain_rows,
        ],
        axis=1,
    )
    height = pack.shape[1]
    pack = jnp.pad(pack, ((0, 0), (0, -height % 16), (0, 0)))

    block = jnp.concatenate([x, out_weight], axis=0)
    split = count // 2
    forth, back = [block, turn(block, 1)], [block, turn(block, -1)]
    pack, forth[1], back[1], gate_late, up_late = lax.optimization_barrier(
        (pack, forth[1], back[1], gate_weight, up_weight)
    )
    got = exchange(pack)
    for step in range(HEADS // 2 - 2):
        forth.append(turn(forth[-1], 1))
        back.append(turn(back[-1], -1))
        if step == 0:
            got, forth[-1], back[-1], parity = lax.optimization_barrier(
                (got, forth[-1], back[-1], core)
            )
    far_first, far_last = turn(forth[-1][:split], 1), turn(back[-1][split:], -1)
    x_slots = [((v, count),) for v in forth] + [((far_first, split), (far_last, count - split))]
    x_slots += [((v, count),) for v in back[:0:-1]]
    outs = [v[count:] for v in forth] + [far_last[count - split :]]
    outs = jnp.stack(outs + [v[count:] for v in back[:0:-1]])
    got_c = swap(got, "c")
    got_y = swap(got, "dl")
    got_yc = swap(got_y, "c")
    near = pick(core, jnp.stack([got, got_c]), jnp.stack([got_c, got]))
    away = pick(core, jnp.stack([got_y, got_yc]), jnp.stack([got_yc, got_y]))
    every = pick(pair, jnp.stack([near, away]), jnp.stack([away, near]))
    every = every.transpose(2, 0, 1, 3, 4)
    if far > 1:
        every = lax.all_gather(every, "dh", axis=0)
    else:
        every = every[None]
    every = every.transpose(0, 2, 1, 3, 4, 5)
    w_qkv = jnp.concatenate(
        [every[..., i * rows : (i + 1) * rows, :].reshape(D, HEAD_DIM) for i in range(3)], axis=1
    )
    gain_all = every[..., 3 * rows + 3 * blocks, : 2 * rows].reshape(-1, 2, rows)
    gain_one = gain_all[:, 0].reshape(1, D)
    gain_two = gain_all[:, 1].reshape(1, D)

    def seg_of(blocks_of):
        return (
            blocks_of[:, 3 * rows : 3 * rows + blocks]
            .astype(WIDE)
            .astype(jnp.int32)
            .reshape(HEADS, count)
        )

    seg_own = seg_of(got)
    seg_oth = seg_of(got_c)
    idx = (
        got[:, 3 * rows + blocks : 3 * rows + 2 * blocks].astype(WIDE) * MEM_ROWS
        + got[:, 3 * rows + 2 * blocks : 3 * rows + 3 * blocks].astype(WIDE)
    ).astype(jnp.int32)
    idx = idx.reshape(HEADS, count, 1)

    block_docs = seg_own[:, ::QUERY_BLOCK]
    docs = second_doc.shape[1]
    doc_ids = jnp.arange(docs, dtype=jnp.int32)
    mates = jnp.sum(
        jnp.where(block_docs[:, :, None] == doc_ids, second_doc[0][None, None, :], 0), axis=-1
    )
    seg_all = jnp.concatenate([seg_own, seg_oth], axis=0)
    before = jnp.sum(
        (seg_all.reshape(1, -1) < block_docs[:, :1]).astype(jnp.int32), axis=1
    )
    tab = jnp.concatenate(
        [
            block_docs.reshape(-1),
            mates.reshape(-1),
            before // (2 * count),
            jnp.stack([core, chip]),
        ]
    ).astype(jnp.int32)

    half = HEAD_DIM // 2
    freqs = 10000.0 ** (-jnp.arange(half, dtype=WIDE) * 2.0 / (2 * half))
    positions = ((2 * slots + parity) * count)[:, None] + jnp.arange(count, dtype=jnp.int32)[None]
    turned = positions.astype(WIDE)[:, :, None] * freqs
    cosine, sine = jnp.cos(turned), jnp.sin(turned)
    cosine = jnp.concatenate([cosine, cosine], axis=-1)
    sine = jnp.concatenate([-sine, sine], axis=-1)

    half = units + -units % HEAD_DIM
    wide = 2 * half

    def by_owner(w):
        w = w.reshape(rows, far, 2, HEADS, 2, share).transpose(2, 4, 0, 1, 3, 5)
        return jnp.pad(w.reshape(2, 2, rows, units), ((0, 0),) * 3 + ((0, half - units),))

    gu = jnp.concatenate([by_owner(gate_late), by_owner(up_late)], axis=-1)
    kept = pick(core, gu[:, 0], gu[:, 1])
    came = swap(pick(core, gu[:, 1], gu[:, 0]), "c")
    gu = pick(core, jnp.stack([kept, came], 1), jnp.stack([came, kept], 1))
    kept = pick(pair, gu[0], gu[1])
    came = swap(pick(pair, gu[1], gu[0]), "dl")
    gu = pick(pair, jnp.stack([kept, came]), jnp.stack([came, kept])).reshape(4 * rows, wide)
    bundle = jnp.concatenate([gu, jnp.pad(down_weight, ((0, 0), (0, wide - D)))], axis=0)
    height = 4 * rows + share
    if far > 1:
        bundle = lax.all_gather(bundle, "dh", axis=0, tiled=True)
    upper = bundle.shape[0] * 4 * rows // height if far == 1 else bundle.shape[0] // 2
    bundle, *_ = lax.optimization_barrier((bundle, far_first, far_last))
    forth, back = [bundle], [bundle]
    for step in range(HEADS // 2 - 1):
        forth.append(turn(forth[-1], 1))
        back.append(turn(back[-1], -1))
    w_slots = forth + [turn(forth[-1][:upper], 1), turn(back[-1][upper:], -1)] + back[:0:-1]

    held = ()
    for order in ([0, 1, 7, 2, 6], [3, 5, 4]):
        held = qkv_blocks(
            at_place(mine - jnp.asarray(order, jnp.int32)).astype(jnp.int32),
            [x_slots[i] for i in order],
            gain_one,
            w_qkv,
            cosine,
            sine,
            held,
        )
    queries, own, normed_one = held
    outs_c = swap(outs, "c")
    outs_y = swap(outs, "dl")
    outs_yc = swap(outs_y, "c")
    other = swap(own, "c")
    up_late, _ = lax.optimization_barrier((upstream, own))
    up_c = swap(up_late, "c")
    up_y = swap(up_late, "dl")
    up_yc = swap(up_y, "c")

    seg_thin = seg_own.reshape(HEADS, count, 1)
    seg_own_row = seg_own.reshape(HEADS, 1, count)
    seg_oth_row = seg_oth.reshape(HEADS, 1, count)
    attention, attention_low, lse, memory = attend(
        tab,
        queries,
        own,
        other,
        seg_thin,
        seg_own_row,
        seg_oth_row,
        idx,
        cache_keys[0].reshape(-1, D),
        cache_values[0].reshape(-1, D),
    )

    heads = exchange(attention_low)
    heads, up_c, up_y, up_yc = lax.optimization_barrier((heads, up_c, up_y, up_yc))
    slot_of = lax.rem(mine - jnp.asarray(PLACE, jnp.int32) + HEADS, HEADS).astype(jnp.int32)
    if far == 1:
        sources = [outs, outs_c, outs_y, outs_yc]
    else:
        near = pick(core, jnp.stack([outs, outs_c], 1), jnp.stack([outs_c, outs], 1))
        away = pick(core, jnp.stack([outs_y, outs_yc], 1), jnp.stack([outs_yc, outs_y], 1))
        sources = pick(pair, jnp.stack([near, away]), jnp.stack([away, near]))
        sources = lax.all_gather(jnp.take(sources, slot_of, axis=1), "dh", axis=0)
        sources = [sources.reshape(D, D)]
    where = jnp.concatenate([chips, jnp.stack([pair, core])]).astype(jnp.int32)
    attended, mid, normed_two, out_w = out_block(where, heads, sources, x, gain_two)

    if far == 1:
        gate_w, up_w, down_w = weights(where, w_slots, units)
    else:
        middle = jnp.concatenate(w_slots[HEADS // 2 : HEADS // 2 + 2], axis=0)
        every = jnp.stack(w_slots[: HEADS // 2] + [middle] + w_slots[HEADS // 2 + 2 :])
        every = jnp.take(every, slot_of, axis=0).reshape(HEADS, far, height, wide)
        gu = every[:, :, : 4 * rows].reshape(HEADS, far, 2, 2 * rows, wide)
        gu = gu.transpose(1, 2, 0, 3, 4).reshape(D, wide)
        gate_w, up_w = gu[:, :units], gu[:, half : half + units]
        down_w = every[:, :, 4 * rows :, :D].transpose(1, 0, 2, 3).reshape(units, D)

    n_c = swap(normed_two, "c")
    n_y = swap(normed_two, "dl")
    n_yc = swap(n_y, "c")
    hid_l, gg_l, ug_l, dn_l = ffn(normed_two, n_c, upstream, up_c, gate_w, up_w, down_w)
    hid_r, gg_r, ug_r, dn_r = ffn(n_y, n_yc, up_y, up_yc, gate_w, up_w, down_w)

    def to_away(away):
        return (away[0].astype(WIDE) + swap(away[1], "c").astype(WIDE)).astype(LOW)

    there = to_away(dn_r)
    there, hid_l, gg_l, ug_l, hid_r, gg_r, ug_r = lax.optimization_barrier(
        (there, hid_l, gg_l, ug_l, hid_r, gg_r, ug_r)
    )
    n_all, u_all = [normed_two, n_c, n_y, n_yc], [upstream, up_c, up_y, up_yc]
    near, away = (hid_l, gg_l, ug_l), (hid_r, gg_r, ug_r)
    if far == 1:
        parts = weight_grads(slot_of, n_all, u_all, near, away, height, wide)
    else:

        def over_tokens(left, right):
            return jnp.einsum(
                "gtd,gtf->df", left, right, preferred_element_type=WIDE
            ).astype(LOW)

        def by_rows(w):
            w = jnp.pad(w, ((0, 0), (0, half - units)))
            return w.reshape(far, 2, HEADS, 2 * rows, half).transpose(2, 0, 1, 3, 4)

        n_all, u_all = jnp.stack(n_all), jnp.stack(u_all)
        hid, gg, ug = (jnp.concatenate(pieces, axis=0) for pieces in zip(near, away))
        gu = jnp.concatenate(
            [by_rows(over_tokens(n_all, gg)), by_rows(over_tokens(n_all, ug))], axis=-1
        ).reshape(HEADS, far, 4 * rows, wide)
        down = over_tokens(hid, u_all).reshape(far, HEADS, share, D).transpose(1, 0, 2, 3)
        down = jnp.pad(down, ((0, 0), (0, 0), (0, 0), (0, wide - D)))
        parts = jnp.concatenate([gu, down], axis=2)
        parts = jnp.take(parts.reshape(HEADS, far * height, wide), chips, axis=0)

    sums = [dn_l[0], swap(dn_l[1], "c"), swap(there, "dl")]
    sums[2], parts = lax.optimization_barrier((sums[2], parts))
    mid_grad, branch, att_grad = mid_block(mid, *sums, upstream, gain_two, out_w)
    ups = exchange(att_grad)

    def plus(block, arrived, start):
        size = arrived.shape[0]
        total = block[start : start + size].astype(WIDE) + arrived.astype(WIDE)
        pieces = [block[:start], total, block[start + size :]]
        pieces = [piece.astype(LOW) for piece in pieces if piece.shape[0]]
        return jnp.concatenate(pieces, axis=0)

    def ring_first(blocks, split):
        middle = blocks[HEADS // 2]
        return (
            plus(blocks[HEADS // 2 + 1], turn(middle[:split].astype(LOW), 1), 0),
            plus(blocks[HEADS // 2 - 1], turn(middle[split:].astype(LOW), -1), split),
        )

    def ring_next(blocks, forth, back, step):
        return (
            plus(blocks[HEADS // 2 + step], turn(forth, 1), 0),
            plus(blocks[HEADS // 2 - step], turn(back, -1), 0),
        )

    def ring_rest(blocks, forth, back, first=2):
        for step in range(first, HEADS // 2):
            forth, back = ring_next(blocks, forth, back, step)
        forth, back = turn(forth, 1), turn(back, -1)
        return blocks[0].astype(WIDE) + forth.astype(WIDE) + back.astype(WIDE)

    def over_owner(w, width):
        w = w.reshape(far, 2, HEADS, 2, rows, width)
        kept = pick(core, w[:, :, :, 0], w[:, :, :, 1])
        came = swap(pick(core, w[:, :, :, 1], w[:, :, :, 0]), "c")
        w = kept.astype(WIDE) + came.astype(WIDE)
        kept = pick(pair, w[:, 0], w[:, 1])
        came = swap(pick(pair, w[:, 1], w[:, 0]).astype(LOW), "dl")
        w = (kept + came.astype(WIDE)).astype(LOW)
        if far > 1:
            w = lax.psum_scatter(w, "dh", scatter_dimension=0, tiled=True)
        return w[0]

    out_part = over_owner(
        jnp.einsum("td,te->de", attended, branch, preferred_element_type=WIDE).astype(LOW), D
    )
    strip = wide - D
    blocks = [parts[slot].astype(WIDE) for slot in range(HEADS)]
    if far == 1:
        strips = out_strips(where, out_part, strip)
        below = share - strips.shape[1]
        for slot in range(HEADS):
            if slot != HEADS // 2:
                blocks[slot] = blocks[slot] + jnp.pad(
                    strips[slot].astype(WIDE), ((4 * rows, below), (D, 0))
                )
        out_far = turn(strips[HEADS // 2], HEADS // 2)
    forth, back = ring_first(blocks, upper)
    ups, forth, back = lax.optimization_barrier((ups, forth, back))
    forth, back = ring_next(blocks, forth, back, 2)

    dq, d_own, d_oth = attend_back(
        tab, queries, ups, attention, lse, own, other, memory, seg_thin, seg_own_row, seg_oth_row
    )
    d_got = swap(d_oth, "c")
    dq, forth, back = lax.optimization_barrier((dq, forth, back))
    dx, grads = qkv_back(chips.astype(jnp.int32), dq, d_own, d_got, cosine, sine, w_qkv)
    dx_forth, dx_back = ring_first(dx, split)
    grads, hid_l, hid_r, _, _ = lax.optimization_barrier((grads, hid_l, hid_r, dx_forth, dx_back))
    normed_one_grad = ring_rest(dx, dx_forth, dx_back)

    summed = ring_rest(blocks, forth, back, 3).astype(LOW)
    if far > 1:
        summed = lax.psum_scatter(summed, "dh", scatter_dimension=0, tiled=True)
    down_w_grad = summed[4 * rows : 4 * rows + share, :D].astype(WIDE)
    if far == 1:
        out_w_grad = summed[4 * rows : 4 * rows + strips.shape[1], D:].astype(WIDE)
        out_w_grad = out_w_grad + out_far.astype(WIDE)
        out_w_grad = out_w_grad.reshape(D // strip, rows, strip).transpose(1, 0, 2).reshape(rows, D)
    else:
        out_w_grad = jnp.sum(exchange(out_part).astype(WIDE), axis=0)
    gu = summed[: 4 * rows].reshape(2, 2, rows, wide)
    kept = pick(core, gu[:, 0], gu[:, 1])
    came = swap(pick(core, gu[:, 1], gu[:, 0]), "c")
    gu = pick(core, jnp.stack([kept, came], 1), jnp.stack([came, kept], 1))
    kept = pick(pair, gu[0], gu[1])
    came = swap(pick(pair, gu[1], gu[0]), "dl")
    gu = pick(pair, jnp.stack([kept, came]), jnp.stack([came, kept]))
    gu = jnp.stack([gu[..., :units], gu[..., half : half + units]])
    gu = (
        gu.reshape(2, 2, 2, rows, far, HEADS, share)
        .transpose(0, 3, 4, 1, 5, 2, 6)
        .reshape(2, rows, FF)
        .astype(WIDE)
    )
    gate_w_grad, up_w_grad = gu[0], gu[1]

    out_l = jnp.einsum("gtf,fd->gtd", hid_l, down_w, preferred_element_type=WIDE).astype(LOW)
    out_r = jnp.einsum("gtf,fd->gtd", hid_r, down_w, preferred_element_type=WIDE).astype(LOW)
    output = mid
    for part in (out_l[0], swap(out_l[1], "c"), swap(to_away(out_r), "dl")):
        output = output + part.astype(WIDE)
    output = output.astype(LOW)

    dw = jnp.einsum("std,stg->dg", normed_one, grads, preferred_element_type=WIDE).astype(LOW)
    qkv_grads = exchange(over_owner(dw, 3 * HEAD_DIM)).astype(WIDE)

    wide_x = x.astype(WIDE)
    r = lax.rsqrt(jnp.mean(wide_x * wide_x, axis=-1, keepdims=True) + EPSILON)
    scaled = normed_one_grad * gain_one.astype(WIDE)
    inner = jnp.mean(scaled * wide_x, axis=-1, keepdims=True)
    input_grad = mid_grad + r * scaled - wide_x * (r * r * r * inner)

    q_w_grad, k_w_grad, v_w_grad = (
        qkv_grads[:, :, i * HEAD_DIM : (i + 1) * HEAD_DIM].transpose(1, 0, 2).reshape(rows, D)
        for i in range(3)
    )

    def gain_grad(gain, pairs):
        total = 0.0
        for grad, weight in pairs:
            total = total + jnp.sum(grad * weight.astype(WIDE), axis=1)
        return total / gain.astype(WIDE)

    first_gain_grad = gain_grad(
        first_gain,
        ((q_w_grad, query_weight), (k_w_grad, key_weight), (v_w_grad, value_weight)),
    )
    second_gain_grad = gain_grad(
        second_gain, ((gate_w_grad, gate_weight), (up_w_grad, up_weight))
    )
    return (
        output[None],
        input_grad[None],
        first_gain_grad,
        q_w_grad,
        k_w_grad,
        v_w_grad,
        out_w_grad,
        second_gain_grad,
        gate_w_grad,
        up_w_grad,
        down_w_grad,
    )


def solution(mesh):
    far = mesh.shape["dp"] // 2
    cores = mesh.shape["seq"] // HEADS
    fine = Mesh(mesh.devices.reshape(far, 2, HEADS, cores), ("dh", "dl", "h", "c"))
    dp, seq, every = ("dh", "dl"), ("h", "c"), ("dh", "dl", "h", "c")
    rows = P(every, None)
    return jax.shard_map(
        functools.partial(local, far),
        mesh=fine,
        in_specs=(
            P(dp, seq, None),
            P(dp, seq),
            P(dp, None),
            P(dp, seq, None, None),
            P(dp, None, None, None),
            P(dp, None, None, None),
            P(every),
            rows,
            rows,
            rows,
            rows,
            P(every),
            rows,
            rows,
            rows,
            P(dp, seq, None),
        ),
        out_specs=(
            P(dp, seq, None),
            P(dp, seq, None),
            P(every),
            rows,
            rows,
            rows,
            rows,
            P(every),
            rows,
            rows,
            rows,
        ),
        check_vma=False,
    )
```

```python
import functools
import math

import jax
import jax.numpy as jnp
from jax import lax
from jax.experimental import pallas as pl
from jax.experimental.pallas import tpu as pltpu
from jax.sharding import Mesh
from jax.sharding import PartitionSpec as P

D = 1024
FF = 2816
HEADS = 8
HEAD_DIM = 128
QUERY_BLOCK = 128
MEM_ROWS = 256
EPSILON = 1e-05
NEGATIVE = -1e30
SCALE = 1.0 / math.sqrt(HEAD_DIM)
LOG2 = SCALE * math.log2(math.e)
LOW = jnp.bfloat16
WIDE = jnp.float32

RING = [2 * i for i in range(HEADS // 2)] + [2 * i + 1 for i in reversed(range(HEADS // 2))]
PLACE = [RING.index(i) for i in range(HEADS)]


def dot_nn(a, b):
    return lax.dot_general(a, b, (((1,), (0,)), ((), ())), preferred_element_type=WIDE)


def dot_nt(a, b):
    return lax.dot_general(a, b, (((1,), (1,)), ((), ())), preferred_element_type=WIDE)


def dot_tn(a, b):
    return lax.dot_general(a, b, (((0,), (0,)), ((), ())), preferred_element_type=WIDE)


def swap(block, axis):
    return lax.ppermute(block, axis, [(0, 1), (1, 0)])


def turn(block, distance):
    route = [(RING[i], RING[(i + distance) % HEADS]) for i in range(HEADS)]
    return lax.ppermute(block, "h", route)


def at_place(place):
    place = lax.rem(place + 2 * HEADS, HEADS)
    return jnp.where(place < HEADS // 2, 2 * place, 2 * (HEADS - 1 - place) + 1)


def exchange(blocks):
    return lax.all_to_all(blocks, "h", 0, 0)


def pick(flag, first, second):
    return jnp.where(flag == 0, first, second)


def smem():
    return pl.BlockSpec(memory_space=pltpu.SMEM)


def vmem():
    return pl.BlockSpec(memory_space=pltpu.VMEM)


def qkv_kernel(parts, tab, *refs):
    xs, (gain_ref, w_ref, cos_ref, sin_ref) = refs[: sum(parts)], refs[sum(parts) : sum(parts) + 4]
    q_ref, kv_ref, n_ref, x_ref = refs[-4:]
    i = pl.program_id(0)
    first = 0
    for step, number in enumerate(parts):

        @pl.when(i == step)
        def _(blocks=xs[first : first + number]):
            row = 0
            for block in blocks:
                size = block.shape[0]
                x_ref[row : row + size, :] = block[...]
                row += size

        first += number
    x = x_ref[...].astype(WIDE)
    r = lax.rsqrt(jnp.mean(x * x, axis=-1, keepdims=True) + EPSILON)
    normed = (x * r * gain_ref[...].astype(WIDE)).astype(LOW)
    n_ref[0] = normed
    out = dot_nn(normed, w_ref[...])
    c, s = cos_ref[0], sin_ref[0]

    def rot(v):
        return v * c + pltpu.roll(v, HEAD_DIM // 2, 1) * s

    q_ref[0] = rot(out[:, :HEAD_DIM]).astype(LOW)
    kv_ref[0, 0] = rot(out[:, HEAD_DIM : 2 * HEAD_DIM]).astype(LOW)
    kv_ref[1, 0] = out[:, 2 * HEAD_DIM :].astype(LOW)


def qkv_blocks(chips, xs, gain, w, cos, sin, held):
    count = cos.shape[1]
    flat = [piece for block in xs for piece, _ in block]
    read = [size for block in xs for _, size in block]

    def whole(shape):
        return pl.BlockSpec(shape, lambda i, t: (0, 0))

    def block(*shape):
        return pl.BlockSpec((1, *shape), lambda i, t: (t[i], 0, 0))

    spec = pltpu.PrefetchScalarGridSpec(
        num_scalar_prefetch=1,
        grid=(len(xs),),
        in_specs=[whole((size, D)) for size in read]
        + [whole((1, D)), whole((D, 3 * HEAD_DIM)), block(count, HEAD_DIM), block(count, HEAD_DIM)]
        + [pl.BlockSpec(memory_space=pl.ANY)] * len(held),
        out_specs=[
            block(count, HEAD_DIM),
            pl.BlockSpec((2, 1, count, HEAD_DIM), lambda i, t: (0, t[i], 0, 0)),
            block(count, D),
        ],
        scratch_shapes=[pltpu.VMEM((count, D), LOW)],
    )
    return pl.pallas_call(
        functools.partial(qkv_kernel, [len(block) for block in xs]),
        grid_spec=spec,
        out_shape=[
            jax.ShapeDtypeStruct((HEADS, count, HEAD_DIM), LOW),
            jax.ShapeDtypeStruct((2, HEADS, count, HEAD_DIM), LOW),
            jax.ShapeDtypeStruct((HEADS, count, D), LOW),
        ],
        input_output_aliases={len(flat) + 5 + i: i for i in range(len(held))},
        cost_estimate=pl.CostEstimate(
            flops=2 * len(xs) * count * D * 3 * HEAD_DIM,
            bytes_accessed=5 * len(xs) * count * D,
            transcendentals=0,
        ),
        name=f"qkv{len(xs)}",
    )(chips, *flat, gain, w, cos, sin, *held)


def causal(count):
    rows = lax.broadcasted_iota(jnp.int32, (count, count), 0)
    return lax.broadcasted_iota(jnp.int32, (count, count), 1) <= rows


def attend_kernel(
    tab, q_ref, own_ref, oth_ref, segq_ref, sego_ref, segt_ref, idx_ref, ck_ref, cv_ref,
    o_ref, low_ref, lse_ref, mem_ref,
):
    i = pl.program_id(0)
    parity = tab[40]
    count = q_ref.shape[1]
    q = q_ref[0]
    segq = segq_ref[0]

    s1 = dot_nt(q, own_ref[0, i]) * LOG2
    s2 = dot_nt(q, oth_ref[0, i]) * LOG2
    s1 = jnp.where((sego_ref[i] == segq) & causal(count), s1, NEGATIVE)
    s2 = jnp.where(segt_ref[i] == segq + 64 * (1 - parity), s2, NEGATIVE)
    memory = []
    for b in range(count // QUERY_BLOCK):
        rows = slice(b * QUERY_BLOCK, (b + 1) * QUERY_BLOCK)
        doc = tab[2 * i + b]
        mate = tab[16 + 2 * i + b]
        idx = idx_ref[0, rows, :]
        lane = lax.broadcasted_iota(jnp.int32, (QUERY_BLOCK, MEM_ROWS), 1)
        first = jnp.where(idx == lane, 1.0, 0.0).astype(LOW)
        second = jnp.where(idx == lane + MEM_ROWS, 1.0, 0.0).astype(LOW)
        here = pl.ds(pl.multiple_of(doc * MEM_ROWS, MEM_ROWS), MEM_ROWS)
        there = pl.ds(pl.multiple_of(mate * MEM_ROWS, MEM_ROWS), MEM_ROWS)
        mk = (dot_nn(first, ck_ref[here, :]) + dot_nn(second, ck_ref[there, :])).astype(LOW)
        mv = (dot_nn(first, cv_ref[here, :]) + dot_nn(second, cv_ref[there, :])).astype(LOW)
        mem_ref[0, 0, rows, :] = mk
        mem_ref[1, 0, rows, :] = mv
        s = jnp.where(segq[rows] == doc, dot_nt(q[rows], mk) * LOG2, NEGATIVE)
        memory.append((s, mv))
    sm = jnp.concatenate([s for s, _ in memory], axis=0)
    top = jnp.maximum(
        jnp.max(jnp.maximum(s1, s2), axis=-1, keepdims=True), jnp.max(sm, axis=-1, keepdims=True)
    )
    p1 = jnp.exp2(s1 - top)
    p2 = jnp.exp2(s2 - top)
    pm = jnp.exp2(sm - top)
    total = jnp.sum(p1 + p2, axis=-1, keepdims=True) + jnp.sum(pm, axis=-1, keepdims=True)
    pm = pm.astype(LOW)
    acc = jnp.concatenate(
        [
            dot_nn(pm[b * QUERY_BLOCK : (b + 1) * QUERY_BLOCK], mv)
            for b, (_, mv) in enumerate(memory)
        ],
        axis=0,
    )
    acc = acc + dot_nn(p1.astype(LOW), own_ref[1, i]) + dot_nn(p2.astype(LOW), oth_ref[1, i])

    def body(j, state):
        top, total, acc = state
        s1 = dot_nt(q, own_ref[0, j]) * LOG2
        s2 = dot_nt(q, oth_ref[0, j]) * LOG2
        s1 = jnp.where(sego_ref[j] == segq, s1, NEGATIVE)
        s2 = jnp.where(segt_ref[j] == segq, s2, NEGATIVE)
        fresh = jnp.maximum(top, jnp.max(jnp.maximum(s1, s2), axis=-1, keepdims=True))
        p1 = jnp.exp2(s1 - fresh)
        p2 = jnp.exp2(s2 - fresh)
        decay = jnp.exp2(top - fresh)
        total = total * decay + jnp.sum(p1 + p2, axis=-1, keepdims=True)
        acc = (
            acc * decay
            + dot_nn(p1.astype(LOW), own_ref[1, j])
            + dot_nn(p2.astype(LOW), oth_ref[1, j])
        )
        return fresh, total, acc

    top, total, acc = lax.fori_loop(tab[32 + i], i, body, (top, total, acc))
    out = acc / total
    o_ref[0] = out
    low_ref[0] = out.astype(LOW)
    lse_ref[0] = top + jnp.log2(total)


def attend(tab, q, own, oth, segq, sego, segt, idx, ck, cv):
    count = q.shape[1]
    block = pl.BlockSpec((1, count, HEAD_DIM), lambda i, t: (i, 0, 0))
    thin = pl.BlockSpec((1, count, 1), lambda i, t: (i, 0, 0))
    whole = pl.BlockSpec((2, HEADS, count, HEAD_DIM), lambda i, t: (0, 0, 0, 0))
    segs = pl.BlockSpec((HEADS, 1, count), lambda i, t: (0, 0, 0))
    cache = pl.BlockSpec((ck.shape[0], HEAD_DIM), lambda i, t: (0, t[41]))
    mem = pl.BlockSpec((2, 1, count, HEAD_DIM), lambda i, t: (0, i, 0, 0))
    return pl.pallas_call(
        attend_kernel,
        grid_spec=pltpu.PrefetchScalarGridSpec(
            num_scalar_prefetch=1,
            grid=(HEADS,),
            in_specs=[block, whole, whole, thin, segs, segs, thin, cache, cache],
            out_specs=[block, block, thin, mem],
        ),
        out_shape=[
            jax.ShapeDtypeStruct((HEADS, count, HEAD_DIM), WIDE),
            jax.ShapeDtypeStruct((HEADS, count, HEAD_DIM), LOW),
            jax.ShapeDtypeStruct((HEADS, count, 1), WIDE),
            jax.ShapeDtypeStruct((2, HEADS, count, HEAD_DIM), LOW),
        ],
        cost_estimate=pl.CostEstimate(
            flops=25 * 10**9, bytes_accessed=6 * 2**20, transcendentals=3 * 10**6
        ),
        name="attend",
    )(tab, q, own, oth, segq, sego, segt, idx, ck, cv)


def attend_back_kernel(
    tab, q_ref, up_ref, o_ref, lse_ref, own_ref, oth_ref, mem_ref, segq_ref, sego_ref, segt_ref,
    dq_ref, down_ref, doth_ref, sum_ref,
):
    i = pl.program_id(0)

    @pl.when(i == 0)
    def _():
        sum_ref[...] = jnp.zeros_like(sum_ref)

    parity = tab[40]
    count = q_ref.shape[1]
    q = q_ref[0]
    up = up_ref[0]
    lse = lse_ref[0]
    segq = segq_ref[0]
    delta = jnp.sum(up.astype(WIDE) * o_ref[0], axis=-1, keepdims=True)
    partial = []
    for b in range(count // QUERY_BLOCK):
        rows = slice(b * QUERY_BLOCK, (b + 1) * QUERY_BLOCK)
        mk = mem_ref[0, 0, rows, :]
        mv = mem_ref[1, 0, rows, :]
        ok = segq[rows] == tab[2 * i + b]
        p = jnp.exp2(jnp.where(ok, dot_nt(q[rows], mk) * LOG2 - lse[rows], NEGATIVE))
        ds = (p * (dot_nt(up[rows], mv) - delta[rows])).astype(LOW)
        partial.append(dot_nn(ds, mk))

    def tile(side, ref, j, ok, dq):
        k = ref[0, j]
        v = ref[1, j]
        p = jnp.exp2(jnp.where(ok, dot_nt(q, k) * LOG2 - lse, NEGATIVE))
        ds = (p * (dot_nt(up, v) - delta)).astype(LOW)
        sum_ref[side, 0, j] += dot_tn(ds, q)
        sum_ref[side, 1, j] += dot_tn(p.astype(LOW), up)
        return dq + dot_nn(ds, k)

    dq = jnp.concatenate(partial, axis=0)
    dq = tile(0, own_ref, i, (sego_ref[i] == segq) & causal(count), dq)
    dq = tile(1, oth_ref, i, segt_ref[i] == segq + 64 * (1 - parity), dq)

    def body(j, dq):
        dq = tile(0, own_ref, j, sego_ref[j] == segq, dq)
        return tile(1, oth_ref, j, segt_ref[j] == segq, dq)

    dq_ref[0] = lax.fori_loop(tab[32 + i], i, body, dq)

    @pl.when(i == HEADS - 1)
    def _():
        down_ref[...] = sum_ref[0]
        doth_ref[...] = sum_ref[1].astype(LOW)


def attend_back(tab, q, up, o, lse, own, oth, mem, segq, sego, segt):
    count = q.shape[1]
    block = pl.BlockSpec((1, count, HEAD_DIM), lambda i, t: (i, 0, 0))
    thin = pl.BlockSpec((1, count, 1), lambda i, t: (i, 0, 0))
    whole = pl.BlockSpec((2, HEADS, count, HEAD_DIM), lambda i, t: (0, 0, 0, 0))
    segs = pl.BlockSpec((HEADS, 1, count), lambda i, t: (0, 0, 0))
    memory = pl.BlockSpec((2, 1, count, HEAD_DIM), lambda i, t: (0, i, 0, 0))
    return pl.pallas_call(
        attend_back_kernel,
        grid_spec=pltpu.PrefetchScalarGridSpec(
            num_scalar_prefetch=1,
            grid=(HEADS,),
            in_specs=[block, block, block, thin, whole, whole, memory, thin, segs, segs],
            out_specs=[block, whole, whole],
            scratch_shapes=[pltpu.VMEM((2, 2, HEADS, count, HEAD_DIM), WIDE)],
        ),
        out_shape=[
            jax.ShapeDtypeStruct((HEADS, count, HEAD_DIM), WIDE),
            jax.ShapeDtypeStruct((2, HEADS, count, HEAD_DIM), WIDE),
            jax.ShapeDtypeStruct((2, HEADS, count, HEAD_DIM), LOW),
        ],
        cost_estimate=pl.CostEstimate(
            flops=30 * 10**9, bytes_accessed=10 * 2**20, transcendentals=3 * 10**6
        ),
        name="attend_back",
    )(tab, q, up, o, lse, own, oth, mem, segq, sego, segt)


def place_rows(tab, sources, w_ref):
    rows = sources[0].shape[1]
    for k, source in enumerate(sources):
        pair = tab[8] if k < 2 else 1 - tab[8]
        core = tab[9] if k % 2 == 0 else 1 - tab[9]
        for slot in range(HEADS):
            start = ((pair * HEADS + tab[slot]) * 2 + core) * rows
            w_ref[pl.ds(pl.multiple_of(start, rows), rows), :] = source[slot]


def out_kernel(tab, heads_ref, *refs):
    sources, (x_ref, gain_ref, att_ref, mid_ref, n_ref, w_ref) = refs[:-6], refs[-6:]
    if len(sources) == 1:
        w_ref[...] = sources[0][...]
    else:
        place_rows(tab, sources, w_ref)
    for h in range(HEADS):
        att_ref[:, h * HEAD_DIM : (h + 1) * HEAD_DIM] = heads_ref[h]
    mid = x_ref[...].astype(WIDE) + dot_nn(att_ref[...], w_ref[...])
    mid_ref[...] = mid
    r = lax.rsqrt(jnp.mean(mid * mid, axis=-1, keepdims=True) + EPSILON)
    n_ref[...] = (mid * r * gain_ref[...].astype(WIDE)).astype(LOW)


def out_block(tab, heads, sources, x, gain):
    count = x.shape[0]
    return pl.pallas_call(
        out_kernel,
        in_specs=[smem()] + [vmem()] * (3 + len(sources)),
        out_specs=[vmem()] * 4,
        out_shape=[
            jax.ShapeDtypeStruct((count, D), LOW),
            jax.ShapeDtypeStruct((count, D), WIDE),
            jax.ShapeDtypeStruct((count, D), LOW),
            jax.ShapeDtypeStruct((D, D), LOW),
        ],
        cost_estimate=pl.CostEstimate(
            flops=2 * count * D * D, bytes_accessed=6 * 2**20, transcendentals=0
        ),
        name="out_block",
    )(tab, heads, *sources, x, gain)


def fold(block, deep):
    half, rest = D // 2, block.shape[0] - deep
    middle = jnp.concatenate([block[deep:, :half], block[: deep - rest, half:]], axis=0)
    last = block[deep - rest :, half:]
    last = jnp.concatenate([last, jnp.zeros((deep - last.shape[0], half), last.dtype)], axis=0)
    return block[:deep, :half], middle, last


def unfolded(block, share):
    deep, half = block.shape[0], D // 2
    rest = share - deep
    return [
        (0, deep, 0, block[:, :half]),
        (deep, rest, 0, block[:rest, half:D]),
        (0, deep - rest, half, block[rest:, half:D]),
        (deep - rest, share - deep + rest, half, block[: share - deep + rest, D:]),
    ]


def weights_kernel(tab, *refs):
    blocks, (gate_ref, up_ref, down_ref, acc_ref) = refs[:-4], refs[-4:]
    units = gate_ref.shape[1]
    height, wide = blocks[0].shape
    half = wide // 2
    share = units // HEADS
    rows = D // (2 * HEADS)
    middle = blocks[HEADS // 2].shape[0]
    for slot in range(HEADS):
        chip = tab[slot]
        if slot == HEADS // 2:
            pieces = [(0, blocks[slot]), (middle, blocks[slot + 1])]
        else:
            pieces = [(0, blocks[slot if slot < HEADS // 2 else slot + 1])]
        for start, ref in pieces:
            stop = start + ref.shape[0]
            for pair in range(2):
                first, last = max(start, pair * rows), min(stop, (pair + 1) * rows)
                if first < last:
                    size = last - first
                    here = (pair * HEADS + chip) * rows + first - pair * rows
                    here = pl.ds(pl.multiple_of(here, math.gcd(rows, first)), size)
                    gate_ref[here, :] = ref[first - start : last - start, :units]
                    up_ref[here, :] = ref[first - start : last - start, half : half + units]
        lower = ref[2 * rows - start :, :].astype(WIDE)
        for row, size, column, piece in unfolded(lower, share):
            here = pl.ds(pl.multiple_of(chip * share + row, 8), size)
            acc_ref[here, column : column + D // 2] = piece
    down_ref[...] = acc_ref[...].astype(LOW)


def weights(chips, blocks, units):
    return pl.pallas_call(
        weights_kernel,
        in_specs=[smem()] + [vmem()] * len(blocks),
        out_specs=[vmem()] * 3,
        out_shape=[
            jax.ShapeDtypeStruct((D, units), LOW),
            jax.ShapeDtypeStruct((D, units), LOW),
            jax.ShapeDtypeStruct((units, D), LOW),
        ],
        scratch_shapes=[pltpu.VMEM((units, D), WIDE)],
        cost_estimate=pl.CostEstimate(
            flops=0, bytes_accessed=12 * D * units, transcendentals=0
        ),
        name="weights",
    )(chips, *blocks)


def ffn_kernel(na, nb, ga, gb, g_ref, u_ref, d_ref, hid_ref, gg_ref, ug_ref, dn_ref):
    for t, (n_ref, c_ref) in enumerate(((na, ga), (nb, gb))):
        n = n_ref[...]
        gate = dot_nn(n, g_ref[...])
        upper = dot_nn(n, u_ref[...])
        sigma = jax.nn.sigmoid(gate)
        silu = gate * sigma
        hid_ref[t] = (silu * upper).astype(LOW)
        hg = dot_nt(c_ref[...], d_ref[...])
        gg = (hg * upper * sigma * (1.0 + gate * (1.0 - sigma))).astype(LOW)
        ug = (hg * silu).astype(LOW)
        gg_ref[t] = gg
        ug_ref[t] = ug
        dn_ref[t] = (dot_nt(gg, g_ref[...]) + dot_nt(ug, u_ref[...])).astype(LOW)


def ffn(na, nb, ga, gb, g, u, d):
    count = na.shape[0]
    units = g.shape[1]
    return pl.pallas_call(
        ffn_kernel,
        in_specs=[vmem()] * 7,
        out_specs=[vmem()] * 4,
        out_shape=[jax.ShapeDtypeStruct((2, count, units), LOW)] * 3
        + [jax.ShapeDtypeStruct((2, count, D), LOW)],
        cost_estimate=pl.CostEstimate(
            flops=20 * count * D * units,
            bytes_accessed=6 * D * units + 16 * count * D,
            transcendentals=2 * count * units,
        ),
        name="ffn",
    )(na, nb, ga, gb, g, u, d)


def grads_kernel(tab, *refs):
    ns, ups, (hid_l, gg_l, ug_l, hid_r, gg_r, ug_r, parts_ref) = (
        refs[:4], refs[4:8], refs[8:],
    )
    wide = parts_ref.shape[2]
    half = wide // 2
    units = hid_l.shape[2]
    share = units // HEADS
    rows = ns[0].shape[1] // (2 * HEADS)
    edge = units - units % HEAD_DIM

    def tokens(near, away):
        return jnp.concatenate([near[0], near[1], away[0], away[1]], axis=0)

    n = jnp.concatenate([v[...] for v in ns], axis=0)
    up = jnp.concatenate([v[...] for v in ups], axis=0)
    for near, away, start in ((gg_l, gg_r, 0), (ug_l, ug_r, half)):
        total = dot_tn(n, tokens(near, away)).astype(LOW)
        for h in range(HEADS):
            slot = tab[h]
            for pair in range(2):
                first = (pair * HEADS + h) * rows
                here = slice(pair * rows, (pair + 1) * rows)
                parts_ref[slot, here, start + edge : start + half] = jnp.zeros(
                    (rows, half - edge), LOW
                )
                parts_ref[slot, here, start : start + units] = total[first : first + rows]
    total = dot_tn(tokens(hid_l, hid_r), up)
    deep = parts_ref.shape[1] - 2 * rows
    for h in range(HEADS):
        for i, piece in enumerate(fold(total[h * share : (h + 1) * share], deep)):
            columns = slice(i * D // 2, (i + 1) * D // 2)
            parts_ref[tab[h], 2 * rows :, columns] = piece.astype(LOW)


def weight_grads(slot_of, ns, ups, near, away, height, wide):
    count = ns[0].shape[0]
    units = near[0].shape[2]
    return pl.pallas_call(
        grads_kernel,
        in_specs=[smem()] + [vmem()] * 14,
        out_specs=vmem(),
        out_shape=jax.ShapeDtypeStruct((HEADS, height, wide), LOW),
        cost_estimate=pl.CostEstimate(
            flops=24 * count * D * units, bytes_accessed=14 * 2**20, transcendentals=0
        ),
        name="weight_grads",
    )(slot_of, *ns, *ups, *near, *away)


def mid_kernel(mid_ref, pa, pb, pc, up_ref, gain_ref, w_ref, mg_ref, bg_ref, ag_ref):
    mid = mid_ref[...]
    scaled = (pa[...].astype(WIDE) + pb[...].astype(WIDE) + pc[...].astype(WIDE)) * gain_ref[
        ...
    ].astype(WIDE)
    r = lax.rsqrt(jnp.mean(mid * mid, axis=-1, keepdims=True) + EPSILON)
    inner = jnp.mean(scaled * mid, axis=-1, keepdims=True)
    mid_grad = up_ref[...].astype(WIDE) + r * scaled - mid * (r * r * r * inner)
    mg_ref[...] = mid_grad
    branch = mid_grad.astype(LOW)
    bg_ref[...] = branch
    att = dot_nt(branch, w_ref[...]).astype(LOW)
    for h in range(HEADS):
        ag_ref[h] = att[:, h * HEAD_DIM : (h + 1) * HEAD_DIM]


def mid_block(mid, pa, pb, pc, up, gain, w):
    count = mid.shape[0]
    return pl.pallas_call(
        mid_kernel,
        in_specs=[vmem()] * 7,
        out_specs=[vmem()] * 3,
        out_shape=[
            jax.ShapeDtypeStruct((count, D), WIDE),
            jax.ShapeDtypeStruct((count, D), LOW),
            jax.ShapeDtypeStruct((HEADS, count, HEAD_DIM), LOW),
        ],
        cost_estimate=pl.CostEstimate(
            flops=2 * count * D * D, bytes_accessed=6 * 2**20, transcendentals=0
        ),
        name="mid_block",
    )(mid, pa, pb, pc, up, gain, w)


def qkv_back_kernel(tab, dq_ref, own_ref, got_ref, cos_ref, sin_ref, w_ref, dx_ref, g_ref):
    c, s = cos_ref[0], sin_ref[0]

    def rot(v):
        return v * c - pltpu.roll(v, HEAD_DIM // 2, 1) * s

    dq = rot(dq_ref[0] * SCALE).astype(LOW)
    dk = rot((own_ref[0, 0] + got_ref[0, 0].astype(WIDE)) * SCALE).astype(LOW)
    dv = (own_ref[1, 0] + got_ref[1, 0].astype(WIDE)).astype(LOW)
    grads = jnp.concatenate([dq, dk, dv], axis=1)
    g_ref[0] = grads
    dx_ref[0] = dot_nt(grads, w_ref[...]).astype(LOW)


def qkv_back(chips, dq, own, got, cos, sin, w):
    count = dq.shape[1]
    block = pl.BlockSpec((1, count, HEAD_DIM), lambda i, t: (t[i], 0, 0))
    pair = pl.BlockSpec((2, 1, count, HEAD_DIM), lambda i, t: (0, t[i], 0, 0))
    return pl.pallas_call(
        qkv_back_kernel,
        grid_spec=pltpu.PrefetchScalarGridSpec(
            num_scalar_prefetch=1,
            grid=(HEADS,),
            in_specs=[
                block, pair, pair, block, block,
                pl.BlockSpec((D, 3 * HEAD_DIM), lambda i, t: (0, 0)),
            ],
            out_specs=[
                pl.BlockSpec((1, count, D), lambda i, t: (i, 0, 0)),
                pl.BlockSpec((1, count, 3 * HEAD_DIM), lambda i, t: (t[i], 0, 0)),
            ],
        ),
        out_shape=[
            jax.ShapeDtypeStruct((HEADS, count, D), LOW),
            jax.ShapeDtypeStruct((HEADS, count, 3 * HEAD_DIM), LOW),
        ],
        cost_estimate=pl.CostEstimate(
            flops=2 * HEADS * count * D * 3 * HEAD_DIM,
            bytes_accessed=4 * HEADS * count * D,
            transcendentals=0,
        ),
        name="qkv_back",
    )(chips, dq, own, got, cos, sin, w)


def local(
    far,
    tokens,
    segment_ids,
    second_doc,
    memory_index,
    cache_keys,
    cache_values,
    first_gain,
    query_weight,
    key_weight,
    value_weight,
    out_weight,
    second_gain,
    gate_weight,
    up_weight,
    down_weight,
    cotangent,
):
    x = tokens[0]
    upstream = cotangent[0]
    count = x.shape[0]
    blocks = count // QUERY_BLOCK
    rows = query_weight.shape[0]
    share = down_weight.shape[0]
    units = far * HEADS * share
    chip, core, pair = lax.axis_index("h"), lax.axis_index("c"), lax.axis_index("dl")
    mine = jnp.where(chip % 2 == 0, chip // 2, HEADS - 1 - chip // 2)
    slots = jnp.arange(HEADS, dtype=jnp.int32)
    chips = at_place(mine - slots)

    def by_head(w):
        return w.reshape(rows, HEADS, HEAD_DIM).transpose(1, 0, 2)

    picked = memory_index[0].transpose(1, 0, 2)
    seg_rows = jnp.broadcast_to(
        segment_ids[0].astype(LOW).reshape(1, blocks, QUERY_BLOCK), (HEADS, blocks, QUERY_BLOCK)
    )
    gains = jnp.concatenate([first_gain, second_gain])
    gain_rows = jnp.broadcast_to(
        jnp.pad(gains, (0, HEAD_DIM - 2 * rows)).reshape(1, 1, HEAD_DIM), (HEADS, 1, HEAD_DIM)
    )
    pack = jnp.concatenate(
        [
            by_head(query_weight),
            by_head(key_weight),
            by_head(value_weight),
            seg_rows,
            (picked // MEM_ROWS).astype(LOW),
            (picked % MEM_ROWS).astype(LOW),
            gain_rows,
        ],
        axis=1,
    )
    height = pack.shape[1]
    pack = jnp.pad(pack, ((0, 0), (0, -height % 16), (0, 0)))

    block = jnp.concatenate([x, out_weight], axis=0)
    split = count // 2
    forth, back = [block, turn(block, 1)], [block, turn(block, -1)]
    pack, forth[1], back[1], gate_late, up_late = lax.optimization_barrier(
        (pack, forth[1], back[1], gate_weight, up_weight)
    )
    got = exchange(pack)
    for step in range(HEADS // 2 - 2):
        forth.append(turn(forth[-1], 1))
        back.append(turn(back[-1], -1))
        if step == 1:
            got, forth[-1], back[-1], parity = lax.optimization_barrier(
                (got, forth[-1], back[-1], core)
            )
    far_first, far_last = turn(forth[-1][:split], 1), turn(back[-1][split:], -1)
    x_slots = [((v, count),) for v in forth] + [((far_first, split), (far_last, count - split))]
    x_slots += [((v, count),) for v in back[:0:-1]]
    outs = [v[count:] for v in forth] + [far_last[count - split :]]
    outs = jnp.stack(outs + [v[count:] for v in back[:0:-1]])
    got_c = swap(got, "c")
    got_y = swap(got, "dl")
    got_yc = swap(got_y, "c")
    near = pick(core, jnp.stack([got, got_c]), jnp.stack([got_c, got]))
    away = pick(core, jnp.stack([got_y, got_yc]), jnp.stack([got_yc, got_y]))
    every = pick(pair, jnp.stack([near, away]), jnp.stack([away, near]))
    every = every.transpose(2, 0, 1, 3, 4)
    if far > 1:
        every = lax.all_gather(every, "dh", axis=0)
    else:
        every = every[None]
    every = every.transpose(0, 2, 1, 3, 4, 5)
    w_qkv = jnp.concatenate(
        [every[..., i * rows : (i + 1) * rows, :].reshape(D, HEAD_DIM) for i in range(3)], axis=1
    )
    gain_all = every[..., 3 * rows + 3 * blocks, : 2 * rows].reshape(-1, 2, rows)
    gain_one = gain_all[:, 0].reshape(1, D)
    gain_two = gain_all[:, 1].reshape(1, D)

    def seg_of(blocks_of):
        return (
            blocks_of[:, 3 * rows : 3 * rows + blocks]
            .astype(WIDE)
            .astype(jnp.int32)
            .reshape(HEADS, count)
        )

    seg_own = seg_of(got)
    seg_oth = seg_of(got_c)
    idx = (
        got[:, 3 * rows + blocks : 3 * rows + 2 * blocks].astype(WIDE) * MEM_ROWS
        + got[:, 3 * rows + 2 * blocks : 3 * rows + 3 * blocks].astype(WIDE)
    ).astype(jnp.int32)
    idx = idx.reshape(HEADS, count, 1)

    block_docs = seg_own[:, ::QUERY_BLOCK]
    docs = second_doc.shape[1]
    doc_ids = jnp.arange(docs, dtype=jnp.int32)
    mates = jnp.sum(
        jnp.where(block_docs[:, :, None] == doc_ids, second_doc[0][None, None, :], 0), axis=-1
    )
    seg_all = jnp.concatenate([seg_own, seg_oth], axis=0)
    before = jnp.sum(
        (seg_all.reshape(1, -1) < block_docs[:, :1]).astype(jnp.int32), axis=1
    )
    tab = jnp.concatenate(
        [
            block_docs.reshape(-1),
            mates.reshape(-1),
            before // (2 * count),
            jnp.stack([core, chip]),
        ]
    ).astype(jnp.int32)

    half = HEAD_DIM // 2
    freqs = 10000.0 ** (-jnp.arange(half, dtype=WIDE) * 2.0 / (2 * half))
    positions = ((2 * slots + parity) * count)[:, None] + jnp.arange(count, dtype=jnp.int32)[None]
    turned = positions.astype(WIDE)[:, :, None] * freqs
    cosine, sine = jnp.cos(turned), jnp.sin(turned)
    cosine = jnp.concatenate([cosine, cosine], axis=-1)
    sine = jnp.concatenate([-sine, sine], axis=-1)

    half = units + -units % HEAD_DIM
    wide = 2 * half

    def by_owner(w):
        w = w.reshape(rows, far, 2, HEADS, 2, share).transpose(2, 4, 0, 1, 3, 5)
        return jnp.pad(w.reshape(2, 2, rows, units), ((0, 0),) * 3 + ((0, half - units),))

    gu = jnp.concatenate([by_owner(gate_late), by_owner(up_late)], axis=-1)
    kept = pick(core, gu[:, 0], gu[:, 1])
    came = swap(pick(core, gu[:, 1], gu[:, 0]), "c")
    gu = pick(core, jnp.stack([kept, came], 1), jnp.stack([came, kept], 1))
    kept = pick(pair, gu[0], gu[1])
    came = swap(pick(pair, gu[1], gu[0]), "dl")
    gu = pick(pair, jnp.stack([kept, came]), jnp.stack([came, kept])).reshape(4 * rows, wide)
    if far == 1:
        deep = 2 * rows
        lower = jnp.concatenate(fold(down_weight, deep), axis=1)
    else:
        deep = share
        lower = jnp.pad(down_weight, ((0, 0), (0, wide - D)))
    bundle = jnp.concatenate([gu, lower], axis=0)
    height = 4 * rows + deep
    if far > 1:
        bundle = lax.all_gather(bundle, "dh", axis=0, tiled=True)
    upper = bundle.shape[0] // 2
    bundle, *_ = lax.optimization_barrier((bundle, far_first, far_last))
    forth, back = [bundle], [bundle]
    for step in range(HEADS // 2 - 1):
        forth.append(turn(forth[-1], 1))
        back.append(turn(back[-1], -1))
    w_slots = forth + [turn(forth[-1][:upper], 1), turn(back[-1][upper:], -1)] + back[:0:-1]

    held = ()
    for order in ([0, 1, 7, 2, 6], [3, 5, 4]):
        held = qkv_blocks(
            at_place(mine - jnp.asarray(order, jnp.int32)).astype(jnp.int32),
            [x_slots[i] for i in order],
            gain_one,
            w_qkv,
            cosine,
            sine,
            held,
        )
    queries, own, normed_one = held
    outs_c = swap(outs, "c")
    outs_y = swap(outs, "dl")
    outs_yc = swap(outs_y, "c")
    other = swap(own, "c")
    up_late, _ = lax.optimization_barrier((upstream, own))
    up_c = swap(up_late, "c")
    up_y = swap(up_late, "dl")
    up_yc = swap(up_y, "c")

    seg_thin = seg_own.reshape(HEADS, count, 1)
    seg_own_row = seg_own.reshape(HEADS, 1, count)
    seg_oth_row = seg_oth.reshape(HEADS, 1, count)
    attention, attention_low, lse, memory = attend(
        tab,
        queries,
        own,
        other,
        seg_thin,
        seg_own_row,
        seg_oth_row,
        idx,
        cache_keys[0].reshape(-1, D),
        cache_values[0].reshape(-1, D),
    )

    heads = exchange(attention_low)
    heads, up_c, up_y, up_yc = lax.optimization_barrier((heads, up_c, up_y, up_yc))
    slot_of = lax.rem(mine - jnp.asarray(PLACE, jnp.int32) + HEADS, HEADS).astype(jnp.int32)
    if far == 1:
        sources = [outs, outs_c, outs_y, outs_yc]
    else:
        near = pick(core, jnp.stack([outs, outs_c], 1), jnp.stack([outs_c, outs], 1))
        away = pick(core, jnp.stack([outs_y, outs_yc], 1), jnp.stack([outs_yc, outs_y], 1))
        sources = pick(pair, jnp.stack([near, away]), jnp.stack([away, near]))
        sources = lax.all_gather(jnp.take(sources, slot_of, axis=1), "dh", axis=0)
        sources = [sources.reshape(D, D)]
    where = jnp.concatenate([chips, jnp.stack([pair, core])]).astype(jnp.int32)
    attended, mid, normed_two, out_w = out_block(where, heads, sources, x, gain_two)

    if far == 1:
        gate_w, up_w, down_w = weights(where, w_slots, units)
    else:
        middle = jnp.concatenate(w_slots[HEADS // 2 : HEADS // 2 + 2], axis=0)
        every = jnp.stack(w_slots[: HEADS // 2] + [middle] + w_slots[HEADS // 2 + 2 :])
        every = jnp.take(every, slot_of, axis=0).reshape(HEADS, far, height, wide)
        gu = every[:, :, : 4 * rows].reshape(HEADS, far, 2, 2 * rows, wide)
        gu = gu.transpose(1, 2, 0, 3, 4).reshape(D, wide)
        gate_w, up_w = gu[:, :units], gu[:, half : half + units]
        down_w = every[:, :, 4 * rows :, :D].transpose(1, 0, 2, 3).reshape(units, D)

    n_c = swap(normed_two, "c")
    n_y = swap(normed_two, "dl")
    n_yc = swap(n_y, "c")
    hid_l, gg_l, ug_l, dn_l = ffn(normed_two, n_c, upstream, up_c, gate_w, up_w, down_w)
    hid_r, gg_r, ug_r, dn_r = ffn(n_y, n_yc, up_y, up_yc, gate_w, up_w, down_w)

    def to_away(away):
        return (away[0].astype(WIDE) + swap(away[1], "c").astype(WIDE)).astype(LOW)

    there = to_away(dn_r)
    there, hid_l, gg_l, ug_l, hid_r, gg_r, ug_r = lax.optimization_barrier(
        (there, hid_l, gg_l, ug_l, hid_r, gg_r, ug_r)
    )
    n_all, u_all = [normed_two, n_c, n_y, n_yc], [upstream, up_c, up_y, up_yc]
    near, away = (hid_l, gg_l, ug_l), (hid_r, gg_r, ug_r)
    if far == 1:
        parts = weight_grads(slot_of, n_all, u_all, near, away, height, wide)
    else:

        def over_tokens(left, right):
            return jnp.einsum(
                "gtd,gtf->df", left, right, preferred_element_type=WIDE
            ).astype(LOW)

        def by_rows(w):
            w = jnp.pad(w, ((0, 0), (0, half - units)))
            return w.reshape(far, 2, HEADS, 2 * rows, half).transpose(2, 0, 1, 3, 4)

        n_all, u_all = jnp.stack(n_all), jnp.stack(u_all)
        hid, gg, ug = (jnp.concatenate(pieces, axis=0) for pieces in zip(near, away))
        gu = jnp.concatenate(
            [by_rows(over_tokens(n_all, gg)), by_rows(over_tokens(n_all, ug))], axis=-1
        ).reshape(HEADS, far, 4 * rows, wide)
        down = over_tokens(hid, u_all).reshape(far, HEADS, share, D).transpose(1, 0, 2, 3)
        down = jnp.pad(down, ((0, 0), (0, 0), (0, 0), (0, wide - D)))
        parts = jnp.concatenate([gu, down], axis=2)
        parts = jnp.take(parts.reshape(HEADS, far * height, wide), chips, axis=0)

    sums = [dn_l[0], swap(dn_l[1], "c"), swap(there, "dl")]
    sums[2], parts = lax.optimization_barrier((sums[2], parts))
    mid_grad, branch, att_grad = mid_block(mid, *sums, upstream, gain_two, out_w)
    ups = exchange(att_grad)

    def plus(block, arrived, start):
        size = arrived.shape[0]
        total = block[start : start + size].astype(WIDE) + arrived.astype(WIDE)
        pieces = [block[:start], total, block[start + size :]]
        pieces = [piece.astype(LOW) for piece in pieces if piece.shape[0]]
        return jnp.concatenate(pieces, axis=0)

    def ring_first(blocks, split):
        middle = blocks[HEADS // 2]
        return (
            plus(blocks[HEADS // 2 + 1], turn(middle[:split].astype(LOW), 1), 0),
            plus(blocks[HEADS // 2 - 1], turn(middle[split:].astype(LOW), -1), split),
        )

    def ring_next(blocks, forth, back, step):
        return (
            plus(blocks[HEADS // 2 + step], turn(forth, 1), 0),
            plus(blocks[HEADS // 2 - step], turn(back, -1), 0),
        )

    def ring_last(blocks, forth, back):
        return blocks[0].astype(WIDE) + forth.astype(WIDE) + back.astype(WIDE)

    def over_owner(w, width):
        w = w.reshape(far, 2, HEADS, 2, rows, width)
        kept = pick(core, w[:, :, :, 0], w[:, :, :, 1])
        came = swap(pick(core, w[:, :, :, 1], w[:, :, :, 0]), "c")
        w = kept.astype(WIDE) + came.astype(WIDE)
        kept = pick(pair, w[:, 0], w[:, 1])
        came = swap(pick(pair, w[:, 1], w[:, 0]).astype(LOW), "dl")
        w = (kept + came.astype(WIDE)).astype(LOW)
        if far > 1:
            w = lax.psum_scatter(w, "dh", scatter_dimension=0, tiled=True)
        return w[0]

    blocks = [parts[slot] for slot in range(HEADS)]
    forth, back = ring_first(blocks, upper)
    branch, forth, back = lax.optimization_barrier((branch, forth, back))
    out_part = over_owner(
        jnp.einsum("td,te->de", attended, branch, preferred_element_type=WIDE).astype(LOW), D
    )
    forth, back = ring_next(blocks, forth, back, 2)
    ups, out_part, forth, back = lax.optimization_barrier((ups, out_part, forth, back))
    forth, back = ring_next(blocks, forth, back, 3)

    dq, d_own, d_oth = attend_back(
        tab, queries, ups, attention, lse, own, other, memory, seg_thin, seg_own_row, seg_oth_row
    )
    d_got = swap(d_oth, "c")
    dq, forth, back = lax.optimization_barrier((dq, forth, back))
    dx, grads = qkv_back(chips.astype(jnp.int32), dq, d_own, d_got, cosine, sine, w_qkv)
    out_part = exchange(out_part)
    forth, back = turn(forth, 1), turn(back, -1)
    dx, forth, back = lax.optimization_barrier((dx, forth, back))
    dx_forth, dx_back = ring_first(dx, split)
    grads, out_part, dx_forth, dx_back = lax.optimization_barrier(
        (grads, out_part, dx_forth, dx_back)
    )
    out_w_grad = jnp.sum(out_part.astype(WIDE), axis=0)

    dw = jnp.einsum("std,stg->dg", normed_one, grads, preferred_element_type=WIDE).astype(LOW)
    dw = over_owner(dw, 3 * HEAD_DIM)
    dx_forth, dx_back = ring_next(dx, dx_forth, dx_back, 2)
    dw, hid_l, hid_r, dx_forth, dx_back, forth, back = lax.optimization_barrier(
        (dw, hid_l, hid_r, dx_forth, dx_back, forth, back)
    )
    qkv_grads = exchange(dw).astype(WIDE)
    dx_forth, dx_back = ring_next(dx, dx_forth, dx_back, 3)
    normed_one_grad = ring_last(dx, turn(dx_forth, 1), turn(dx_back, -1))

    summed = ring_last(blocks, forth, back).astype(LOW)
    if far > 1:
        summed = lax.psum_scatter(summed, "dh", scatter_dimension=0, tiled=True)
    lower = summed[4 * rows :].astype(WIDE)
    if far == 1:
        half_d = D // 2
        rest = share - deep
        left = jnp.concatenate([lower[:, :half_d], lower[:rest, half_d:D]], axis=0)
        right = jnp.concatenate([lower[rest:, half_d:D], lower[: 2 * rest, D:]], axis=0)
        down_w_grad = jnp.concatenate([left, right], axis=1)
    else:
        down_w_grad = lower[:, :D]
    gu = summed[: 4 * rows].reshape(2, 2, rows, wide)
    kept = pick(core, gu[:, 0], gu[:, 1])
    came = swap(pick(core, gu[:, 1], gu[:, 0]), "c")
    gu = pick(core, jnp.stack([kept, came], 1), jnp.stack([came, kept], 1))
    kept = pick(pair, gu[0], gu[1])
    came = swap(pick(pair, gu[1], gu[0]), "dl")
    gu = pick(pair, jnp.stack([kept, came]), jnp.stack([came, kept]))
    gu = jnp.stack([gu[..., :units], gu[..., half : half + units]])
    gu = (
        gu.reshape(2, 2, 2, rows, far, HEADS, share)
        .transpose(0, 3, 4, 1, 5, 2, 6)
        .reshape(2, rows, FF)
        .astype(WIDE)
    )
    gate_w_grad, up_w_grad = gu[0], gu[1]

    out_l = jnp.einsum("gtf,fd->gtd", hid_l, down_w, preferred_element_type=WIDE).astype(LOW)
    out_r = jnp.einsum("gtf,fd->gtd", hid_r, down_w, preferred_element_type=WIDE).astype(LOW)
    output = mid
    for part in (out_l[0], swap(out_l[1], "c"), swap(to_away(out_r), "dl")):
        output = output + part.astype(WIDE)
    output = output.astype(LOW)

    wide_x = x.astype(WIDE)
    r = lax.rsqrt(jnp.mean(wide_x * wide_x, axis=-1, keepdims=True) + EPSILON)
    scaled = normed_one_grad * gain_one.astype(WIDE)
    inner = jnp.mean(scaled * wide_x, axis=-1, keepdims=True)
    input_grad = mid_grad + r * scaled - wide_x * (r * r * r * inner)

    q_w_grad, k_w_grad, v_w_grad = (
        qkv_grads[:, :, i * HEAD_DIM : (i + 1) * HEAD_DIM].transpose(1, 0, 2).reshape(rows, D)
        for i in range(3)
    )

    def gain_grad(gain, pairs):
        total = 0.0
        for grad, weight in pairs:
            total = total + jnp.sum(grad * weight.astype(WIDE), axis=1)
        return total / gain.astype(WIDE)

    first_gain_grad = gain_grad(
        first_gain,
        ((q_w_grad, query_weight), (k_w_grad, key_weight), (v_w_grad, value_weight)),
    )
    second_gain_grad = gain_grad(
        second_gain, ((gate_w_grad, gate_weight), (up_w_grad, up_weight))
    )
    return (
        output[None],
        input_grad[None],
        first_gain_grad,
        q_w_grad,
        k_w_grad,
        v_w_grad,
        out_w_grad,
        second_gain_grad,
        gate_w_grad,
        up_w_grad,
        down_w_grad,
    )


def solution(mesh):
    far = mesh.shape["dp"] // 2
    cores = mesh.shape["seq"] // HEADS
    fine = Mesh(mesh.devices.reshape(far, 2, HEADS, cores), ("dh", "dl", "h", "c"))
    dp, seq, every = ("dh", "dl"), ("h", "c"), ("dh", "dl", "h", "c")
    rows = P(every, None)
    return jax.shard_map(
        functools.partial(local, far),
        mesh=fine,
        in_specs=(
            P(dp, seq, None),
            P(dp, seq),
            P(dp, None),
            P(dp, seq, None, None),
            P(dp, None, None, None),
            P(dp, None, None, None),
            P(every),
            rows,
            rows,
            rows,
            rows,
            P(every),
            rows,
            rows,
            rows,
            P(dp, seq, None),
        ),
        out_specs=(
            P(dp, seq, None),
            P(dp, seq, None),
            P(every),
            rows,
            rows,
            rows,
            rows,
            P(every),
            rows,
            rows,
            rows,
        ),
        check_vma=False,
    )
```

```python
import functools
import math

import jax
import jax.numpy as jnp
from jax import lax
from jax.experimental import pallas as pl
from jax.experimental.pallas import tpu as pltpu
from jax.sharding import Mesh
from jax.sharding import PartitionSpec as P

D = 1024
FF = 2816
HEADS = 8
HEAD_DIM = 128
QUERY_BLOCK = 128
MEM_ROWS = 256
EPSILON = 1e-05
NEGATIVE = -1e30
SCALE = 1.0 / math.sqrt(HEAD_DIM)
LOG2 = SCALE * math.log2(math.e)
LOW = jnp.bfloat16
WIDE = jnp.float32

RING = [2 * i for i in range(HEADS // 2)] + [2 * i + 1 for i in reversed(range(HEADS // 2))]
PLACE = [RING.index(i) for i in range(HEADS)]


def dot_nn(a, b):
    return lax.dot_general(a, b, (((1,), (0,)), ((), ())), preferred_element_type=WIDE)


def dot_nt(a, b):
    return lax.dot_general(a, b, (((1,), (1,)), ((), ())), preferred_element_type=WIDE)


def dot_tn(a, b):
    return lax.dot_general(a, b, (((0,), (0,)), ((), ())), preferred_element_type=WIDE)


def swap(block, axis):
    return lax.ppermute(block, axis, [(0, 1), (1, 0)])


def turn(block, distance):
    route = [(RING[i], RING[(i + distance) % HEADS]) for i in range(HEADS)]
    return lax.ppermute(block, "h", route)


def at_place(place):
    place = lax.rem(place + 2 * HEADS, HEADS)
    return jnp.where(place < HEADS // 2, 2 * place, 2 * (HEADS - 1 - place) + 1)


def exchange(blocks):
    return lax.all_to_all(blocks, "h", 0, 0)


def pick(flag, first, second):
    return jnp.where(flag == 0, first, second)


def smem():
    return pl.BlockSpec(memory_space=pltpu.SMEM)


def vmem():
    return pl.BlockSpec(memory_space=pltpu.VMEM)


def qkv_kernel(parts, tab, *refs):
    xs, (gain_ref, w_ref, cos_ref, sin_ref) = refs[: sum(parts)], refs[sum(parts) : sum(parts) + 4]
    q_ref, kv_ref, n_ref, x_ref = refs[-4:]
    i = pl.program_id(0)
    first = 0
    for step, number in enumerate(parts):

        @pl.when(i == step)
        def _(blocks=xs[first : first + number]):
            row = 0
            for block in blocks:
                size = block.shape[0]
                x_ref[row : row + size, :] = block[...]
                row += size

        first += number
    x = x_ref[...].astype(WIDE)
    r = lax.rsqrt(jnp.mean(x * x, axis=-1, keepdims=True) + EPSILON)
    normed = (x * r * gain_ref[...].astype(WIDE)).astype(LOW)
    n_ref[0] = normed
    out = dot_nn(normed, w_ref[...])
    c, s = cos_ref[0], sin_ref[0]

    def rot(v):
        return v * c + pltpu.roll(v, HEAD_DIM // 2, 1) * s

    q_ref[0] = rot(out[:, :HEAD_DIM]).astype(LOW)
    kv_ref[0, 0] = rot(out[:, HEAD_DIM : 2 * HEAD_DIM]).astype(LOW)
    kv_ref[1, 0] = out[:, 2 * HEAD_DIM :].astype(LOW)


def qkv_blocks(chips, xs, gain, w, cos, sin, held):
    count = cos.shape[1]
    flat = [piece for block in xs for piece, _ in block]
    read = [size for block in xs for _, size in block]

    def whole(shape):
        return pl.BlockSpec(shape, lambda i, t: (0, 0))

    def block(*shape):
        return pl.BlockSpec((1, *shape), lambda i, t: (t[i], 0, 0))

    spec = pltpu.PrefetchScalarGridSpec(
        num_scalar_prefetch=1,
        grid=(len(xs),),
        in_specs=[whole((size, D)) for size in read]
        + [whole((1, D)), whole((D, 3 * HEAD_DIM)), block(count, HEAD_DIM), block(count, HEAD_DIM)]
        + [pl.BlockSpec(memory_space=pl.ANY)] * len(held),
        out_specs=[
            block(count, HEAD_DIM),
            pl.BlockSpec((2, 1, count, HEAD_DIM), lambda i, t: (0, t[i], 0, 0)),
            block(count, D),
        ],
        scratch_shapes=[pltpu.VMEM((count, D), LOW)],
    )
    return pl.pallas_call(
        functools.partial(qkv_kernel, [len(block) for block in xs]),
        grid_spec=spec,
        out_shape=[
            jax.ShapeDtypeStruct((HEADS, count, HEAD_DIM), LOW),
            jax.ShapeDtypeStruct((2, HEADS, count, HEAD_DIM), LOW),
            jax.ShapeDtypeStruct((HEADS, count, D), LOW),
        ],
        input_output_aliases={len(flat) + 5 + i: i for i in range(len(held))},
        cost_estimate=pl.CostEstimate(
            flops=2 * len(xs) * count * D * 3 * HEAD_DIM,
            bytes_accessed=5 * len(xs) * count * D,
            transcendentals=0,
        ),
        name=f"qkv{len(xs)}",
    )(chips, *flat, gain, w, cos, sin, *held)


def causal(count):
    rows = lax.broadcasted_iota(jnp.int32, (count, count), 0)
    return lax.broadcasted_iota(jnp.int32, (count, count), 1) <= rows


def attend_kernel(
    begin, tab, q_ref, own_ref, oth_ref, segq_ref, sego_ref, segt_ref, idx_ref, ck_ref, cv_ref,
    *rest,
):
    o_ref, low_ref, lse_ref, mem_ref = rest[-4:]
    i = pl.program_id(0) + begin
    parity = tab[40]
    count = q_ref.shape[1]
    q = q_ref[0]
    segq = segq_ref[0]

    s1 = dot_nt(q, own_ref[0, i]) * LOG2
    s2 = dot_nt(q, oth_ref[0, i]) * LOG2
    s1 = jnp.where((sego_ref[i] == segq) & causal(count), s1, NEGATIVE)
    s2 = jnp.where(segt_ref[i] == segq + 64 * (1 - parity), s2, NEGATIVE)
    memory = []
    for b in range(count // QUERY_BLOCK):
        rows = slice(b * QUERY_BLOCK, (b + 1) * QUERY_BLOCK)
        doc = tab[2 * i + b]
        mate = tab[16 + 2 * i + b]
        idx = idx_ref[0, rows, :]
        lane = lax.broadcasted_iota(jnp.int32, (QUERY_BLOCK, MEM_ROWS), 1)
        first = jnp.where(idx == lane, 1.0, 0.0).astype(LOW)
        second = jnp.where(idx == lane + MEM_ROWS, 1.0, 0.0).astype(LOW)
        here = pl.ds(pl.multiple_of(doc * MEM_ROWS, MEM_ROWS), MEM_ROWS)
        there = pl.ds(pl.multiple_of(mate * MEM_ROWS, MEM_ROWS), MEM_ROWS)
        mk = (dot_nn(first, ck_ref[here, :]) + dot_nn(second, ck_ref[there, :])).astype(LOW)
        mv = (dot_nn(first, cv_ref[here, :]) + dot_nn(second, cv_ref[there, :])).astype(LOW)
        mem_ref[0, 0, rows, :] = mk
        mem_ref[1, 0, rows, :] = mv
        s = jnp.where(segq[rows] == doc, dot_nt(q[rows], mk) * LOG2, NEGATIVE)
        memory.append((s, mv))
    sm = jnp.concatenate([s for s, _ in memory], axis=0)
    top = jnp.maximum(
        jnp.max(jnp.maximum(s1, s2), axis=-1, keepdims=True), jnp.max(sm, axis=-1, keepdims=True)
    )
    p1 = jnp.exp2(s1 - top)
    p2 = jnp.exp2(s2 - top)
    pm = jnp.exp2(sm - top)
    total = jnp.sum(p1 + p2, axis=-1, keepdims=True) + jnp.sum(pm, axis=-1, keepdims=True)
    pm = pm.astype(LOW)
    acc = jnp.concatenate(
        [
            dot_nn(pm[b * QUERY_BLOCK : (b + 1) * QUERY_BLOCK], mv)
            for b, (_, mv) in enumerate(memory)
        ],
        axis=0,
    )
    acc = acc + dot_nn(p1.astype(LOW), own_ref[1, i]) + dot_nn(p2.astype(LOW), oth_ref[1, i])

    def body(j, state):
        top, total, acc = state
        s1 = dot_nt(q, own_ref[0, j]) * LOG2
        s2 = dot_nt(q, oth_ref[0, j]) * LOG2
        s1 = jnp.where(sego_ref[j] == segq, s1, NEGATIVE)
        s2 = jnp.where(segt_ref[j] == segq, s2, NEGATIVE)
        fresh = jnp.maximum(top, jnp.max(jnp.maximum(s1, s2), axis=-1, keepdims=True))
        p1 = jnp.exp2(s1 - fresh)
        p2 = jnp.exp2(s2 - fresh)
        decay = jnp.exp2(top - fresh)
        total = total * decay + jnp.sum(p1 + p2, axis=-1, keepdims=True)
        acc = (
            acc * decay
            + dot_nn(p1.astype(LOW), own_ref[1, j])
            + dot_nn(p2.astype(LOW), oth_ref[1, j])
        )
        return fresh, total, acc

    top, total, acc = lax.fori_loop(tab[32 + i], i, body, (top, total, acc))
    out = acc / total
    o_ref[0] = out
    low_ref[0] = out.astype(LOW)
    lse_ref[0] = top + jnp.log2(total)


def attend(tab, q, own, oth, segq, sego, segt, idx, ck, cv, begin, held):
    count = q.shape[1]
    block = pl.BlockSpec((1, count, HEAD_DIM), lambda i, t: (i + begin, 0, 0))
    thin = pl.BlockSpec((1, count, 1), lambda i, t: (i + begin, 0, 0))
    whole = pl.BlockSpec((2, HEADS, count, HEAD_DIM), lambda i, t: (0, 0, 0, 0))
    segs = pl.BlockSpec((HEADS, 1, count), lambda i, t: (0, 0, 0))
    cache = pl.BlockSpec((ck.shape[0], HEAD_DIM), lambda i, t: (0, t[41]))
    mem = pl.BlockSpec((2, 1, count, HEAD_DIM), lambda i, t: (0, i + begin, 0, 0))
    return pl.pallas_call(
        functools.partial(attend_kernel, begin),
        grid_spec=pltpu.PrefetchScalarGridSpec(
            num_scalar_prefetch=1,
            grid=(HEADS // 2,),
            in_specs=[block, whole, whole, thin, segs, segs, thin, cache, cache]
            + [pl.BlockSpec(memory_space=pl.ANY)] * len(held),
            out_specs=[block, block, thin, mem],
        ),
        out_shape=[
            jax.ShapeDtypeStruct((HEADS, count, HEAD_DIM), WIDE),
            jax.ShapeDtypeStruct((HEADS, count, HEAD_DIM), LOW),
            jax.ShapeDtypeStruct((HEADS, count, 1), WIDE),
            jax.ShapeDtypeStruct((2, HEADS, count, HEAD_DIM), LOW),
        ],
        input_output_aliases={10 + i: i for i in range(len(held))},
        cost_estimate=pl.CostEstimate(
            flops=12 * 10**9, bytes_accessed=4 * 2**20, transcendentals=2 * 10**6
        ),
        name=f"attend{begin}",
    )(tab, q, own, oth, segq, sego, segt, idx, ck, cv, *held)


def attend_back_kernel(
    tab, q_ref, up_ref, o_ref, lse_ref, own_ref, oth_ref, mem_ref, segq_ref, sego_ref, segt_ref,
    dq_ref, down_ref, doth_ref, sum_ref,
):
    i = pl.program_id(0)

    @pl.when(i == 0)
    def _():
        sum_ref[...] = jnp.zeros_like(sum_ref)

    parity = tab[40]
    count = q_ref.shape[1]
    q = q_ref[0]
    up = up_ref[0]
    lse = lse_ref[0]
    segq = segq_ref[0]
    delta = jnp.sum(up.astype(WIDE) * o_ref[0], axis=-1, keepdims=True)
    partial = []
    for b in range(count // QUERY_BLOCK):
        rows = slice(b * QUERY_BLOCK, (b + 1) * QUERY_BLOCK)
        mk = mem_ref[0, 0, rows, :]
        mv = mem_ref[1, 0, rows, :]
        ok = segq[rows] == tab[2 * i + b]
        p = jnp.exp2(jnp.where(ok, dot_nt(q[rows], mk) * LOG2 - lse[rows], NEGATIVE))
        ds = (p * (dot_nt(up[rows], mv) - delta[rows])).astype(LOW)
        partial.append(dot_nn(ds, mk))

    def tile(side, ref, j, ok, dq):
        k = ref[0, j]
        v = ref[1, j]
        p = jnp.exp2(jnp.where(ok, dot_nt(q, k) * LOG2 - lse, NEGATIVE))
        ds = (p * (dot_nt(up, v) - delta)).astype(LOW)
        sum_ref[side, 0, j] += dot_tn(ds, q)
        sum_ref[side, 1, j] += dot_tn(p.astype(LOW), up)
        return dq + dot_nn(ds, k)

    dq = jnp.concatenate(partial, axis=0)
    dq = tile(0, own_ref, i, (sego_ref[i] == segq) & causal(count), dq)
    dq = tile(1, oth_ref, i, segt_ref[i] == segq + 64 * (1 - parity), dq)

    def body(j, dq):
        dq = tile(0, own_ref, j, sego_ref[j] == segq, dq)
        return tile(1, oth_ref, j, segt_ref[j] == segq, dq)

    dq_ref[0] = lax.fori_loop(tab[32 + i], i, body, dq)

    @pl.when(i == HEADS - 1)
    def _():
        down_ref[...] = sum_ref[0]
        doth_ref[...] = sum_ref[1].astype(LOW)


def attend_back(tab, q, up, o, lse, own, oth, mem, segq, sego, segt):
    count = q.shape[1]
    block = pl.BlockSpec((1, count, HEAD_DIM), lambda i, t: (i, 0, 0))
    thin = pl.BlockSpec((1, count, 1), lambda i, t: (i, 0, 0))
    whole = pl.BlockSpec((2, HEADS, count, HEAD_DIM), lambda i, t: (0, 0, 0, 0))
    segs = pl.BlockSpec((HEADS, 1, count), lambda i, t: (0, 0, 0))
    memory = pl.BlockSpec((2, 1, count, HEAD_DIM), lambda i, t: (0, i, 0, 0))
    return pl.pallas_call(
        attend_back_kernel,
        grid_spec=pltpu.PrefetchScalarGridSpec(
            num_scalar_prefetch=1,
            grid=(HEADS,),
            in_specs=[block, block, block, thin, whole, whole, memory, thin, segs, segs],
            out_specs=[block, whole, whole],
            scratch_shapes=[pltpu.VMEM((2, 2, HEADS, count, HEAD_DIM), WIDE)],
        ),
        out_shape=[
            jax.ShapeDtypeStruct((HEADS, count, HEAD_DIM), WIDE),
            jax.ShapeDtypeStruct((2, HEADS, count, HEAD_DIM), WIDE),
            jax.ShapeDtypeStruct((2, HEADS, count, HEAD_DIM), LOW),
        ],
        cost_estimate=pl.CostEstimate(
            flops=30 * 10**9, bytes_accessed=10 * 2**20, transcendentals=3 * 10**6
        ),
        name="attend_back",
    )(tab, q, up, o, lse, own, oth, mem, segq, sego, segt)


def place_rows(tab, sources, w_ref):
    rows = sources[0].shape[1]
    for k, source in enumerate(sources):
        pair = tab[8] if k < 2 else 1 - tab[8]
        core = tab[9] if k % 2 == 0 else 1 - tab[9]
        for slot in range(HEADS):
            start = ((pair * HEADS + tab[slot]) * 2 + core) * rows
            w_ref[pl.ds(pl.multiple_of(start, rows), rows), :] = source[slot]


def out_kernel(tab, heads_ref, *refs):
    sources, (x_ref, gain_ref, att_ref, mid_ref, n_ref, w_ref) = refs[:-6], refs[-6:]
    if len(sources) == 1:
        w_ref[...] = sources[0][...]
    else:
        place_rows(tab, sources, w_ref)
    for h in range(HEADS):
        att_ref[:, h * HEAD_DIM : (h + 1) * HEAD_DIM] = heads_ref[h]
    mid = x_ref[...].astype(WIDE) + dot_nn(att_ref[...], w_ref[...])
    mid_ref[...] = mid
    r = lax.rsqrt(jnp.mean(mid * mid, axis=-1, keepdims=True) + EPSILON)
    n_ref[...] = (mid * r * gain_ref[...].astype(WIDE)).astype(LOW)


def out_block(tab, heads, sources, x, gain):
    count = x.shape[0]
    return pl.pallas_call(
        out_kernel,
        in_specs=[smem()] + [vmem()] * (3 + len(sources)),
        out_specs=[vmem()] * 4,
        out_shape=[
            jax.ShapeDtypeStruct((count, D), LOW),
            jax.ShapeDtypeStruct((count, D), WIDE),
            jax.ShapeDtypeStruct((count, D), LOW),
            jax.ShapeDtypeStruct((D, D), LOW),
        ],
        cost_estimate=pl.CostEstimate(
            flops=2 * count * D * D, bytes_accessed=6 * 2**20, transcendentals=0
        ),
        name="out_block",
    )(tab, heads, *sources, x, gain)


def fold(block, deep):
    half, rest = D // 2, block.shape[0] - deep
    middle = jnp.concatenate([block[deep:, :half], block[: deep - rest, half:]], axis=0)
    last = block[deep - rest :, half:]
    last = jnp.concatenate([last, jnp.zeros((deep - last.shape[0], half), last.dtype)], axis=0)
    return block[:deep, :half], middle, last


def unfolded(block, share):
    deep, half = block.shape[0], D // 2
    rest = share - deep
    return [
        (0, deep, 0, block[:, :half]),
        (deep, rest, 0, block[:rest, half:D]),
        (0, deep - rest, half, block[rest:, half:D]),
        (deep - rest, share - deep + rest, half, block[: share - deep + rest, D:]),
    ]


def weights_kernel(tab, *refs):
    blocks, (gate_ref, up_ref, down_ref, acc_ref) = refs[:-4], refs[-4:]
    units = gate_ref.shape[1]
    height, wide = blocks[0].shape
    half = wide // 2
    share = units // HEADS
    rows = D // (2 * HEADS)
    middle = blocks[HEADS // 2].shape[0]
    for slot in range(HEADS):
        chip = tab[slot]
        if slot == HEADS // 2:
            pieces = [(0, blocks[slot]), (middle, blocks[slot + 1])]
        else:
            pieces = [(0, blocks[slot if slot < HEADS // 2 else slot + 1])]
        for start, ref in pieces:
            stop = start + ref.shape[0]
            for pair in range(2):
                first, last = max(start, pair * rows), min(stop, (pair + 1) * rows)
                if first < last:
                    size = last - first
                    here = (pair * HEADS + chip) * rows + first - pair * rows
                    here = pl.ds(pl.multiple_of(here, math.gcd(rows, first)), size)
                    gate_ref[here, :] = ref[first - start : last - start, :units]
                    up_ref[here, :] = ref[first - start : last - start, half : half + units]
        lower = ref[2 * rows - start :, :].astype(WIDE)
        for row, size, column, piece in unfolded(lower, share):
            here = pl.ds(pl.multiple_of(chip * share + row, 8), size)
            acc_ref[here, column : column + D // 2] = piece
    down_ref[...] = acc_ref[...].astype(LOW)


def weights(chips, blocks, units):
    return pl.pallas_call(
        weights_kernel,
        in_specs=[smem()] + [vmem()] * len(blocks),
        out_specs=[vmem()] * 3,
        out_shape=[
            jax.ShapeDtypeStruct((D, units), LOW),
            jax.ShapeDtypeStruct((D, units), LOW),
            jax.ShapeDtypeStruct((units, D), LOW),
        ],
        scratch_shapes=[pltpu.VMEM((units, D), WIDE)],
        cost_estimate=pl.CostEstimate(
            flops=0, bytes_accessed=12 * D * units, transcendentals=0
        ),
        name="weights",
    )(chips, *blocks)


def ffn_kernel(na, nb, ga, gb, g_ref, u_ref, d_ref, hid_ref, gg_ref, ug_ref, dn_ref, out_ref):
    for t, (n_ref, c_ref) in enumerate(((na, ga), (nb, gb))):
        n = n_ref[...]
        gate = dot_nn(n, g_ref[...])
        upper = dot_nn(n, u_ref[...])
        sigma = jax.nn.sigmoid(gate)
        silu = gate * sigma
        hid = (silu * upper).astype(LOW)
        hid_ref[t] = hid
        out_ref[t] = dot_nn(hid, d_ref[...]).astype(LOW)
        hg = dot_nt(c_ref[...], d_ref[...])
        gg = (hg * upper * sigma * (1.0 + gate * (1.0 - sigma))).astype(LOW)
        ug = (hg * silu).astype(LOW)
        gg_ref[t] = gg
        ug_ref[t] = ug
        dn_ref[t] = (dot_nt(gg, g_ref[...]) + dot_nt(ug, u_ref[...])).astype(LOW)


def ffn(na, nb, ga, gb, g, u, d):
    count = na.shape[0]
    units = g.shape[1]
    return pl.pallas_call(
        ffn_kernel,
        in_specs=[vmem()] * 7,
        out_specs=[vmem()] * 5,
        out_shape=[jax.ShapeDtypeStruct((2, count, units), LOW)] * 3
        + [jax.ShapeDtypeStruct((2, count, D), LOW)] * 2,
        cost_estimate=pl.CostEstimate(
            flops=24 * count * D * units,
            bytes_accessed=6 * D * units + 16 * count * D,
            transcendentals=2 * count * units,
        ),
        name="ffn",
    )(na, nb, ga, gb, g, u, d)


def grads_kernel(tab, *refs):
    ns, ups, (hid_l, gg_l, ug_l, hid_r, gg_r, ug_r, parts_ref) = (
        refs[:4], refs[4:8], refs[8:],
    )
    wide = parts_ref.shape[2]
    half = wide // 2
    units = hid_l.shape[2]
    share = units // HEADS
    rows = ns[0].shape[1] // (2 * HEADS)
    edge = units - units % HEAD_DIM

    def tokens(near, away):
        return jnp.concatenate([near[0], near[1], away[0], away[1]], axis=0)

    n = jnp.concatenate([v[...] for v in ns], axis=0)
    up = jnp.concatenate([v[...] for v in ups], axis=0)
    for near, away, start in ((gg_l, gg_r, 0), (ug_l, ug_r, half)):
        total = dot_tn(n, tokens(near, away)).astype(LOW)
        for h in range(HEADS):
            slot = tab[h]
            for pair in range(2):
                first = (pair * HEADS + h) * rows
                here = slice(pair * rows, (pair + 1) * rows)
                parts_ref[slot, here, start + edge : start + half] = jnp.zeros(
                    (rows, half - edge), LOW
                )
                parts_ref[slot, here, start : start + units] = total[first : first + rows]
    total = dot_tn(tokens(hid_l, hid_r), up)
    strip = wide - D
    for h in range(HEADS):
        slot = tab[h]
        piece = total[h * share : (h + 1) * share].astype(LOW)
        parts_ref[slot, 2 * rows : 2 * rows + share, :D] = piece
        parts_ref[slot, 2 * rows : 2 * rows + share, D:] = jnp.zeros((share, strip), LOW)


def weight_grads(slot_of, ns, ups, near, away, height, wide):
    count = ns[0].shape[0]
    units = near[0].shape[2]
    return pl.pallas_call(
        grads_kernel,
        in_specs=[smem()] + [vmem()] * 14,
        out_specs=vmem(),
        out_shape=jax.ShapeDtypeStruct((HEADS, height, wide), LOW),
        cost_estimate=pl.CostEstimate(
            flops=24 * count * D * units, bytes_accessed=14 * 2**20, transcendentals=0
        ),
        name="weight_grads",
    )(slot_of, *ns, *ups, *near, *away)


def strips_kernel(tab, out_ref, strips_ref):
    rows, strip = out_ref.shape[1], strips_ref.shape[2]
    for slot in range(HEADS):
        for i in range(D // strip):
            strips_ref[slot, i * rows : (i + 1) * rows, :] = out_ref[
                tab[slot], :, i * strip : (i + 1) * strip
            ]


def out_strips(chips, out, strip):
    return pl.pallas_call(
        strips_kernel,
        in_specs=[smem(), vmem()],
        out_specs=vmem(),
        out_shape=jax.ShapeDtypeStruct((HEADS, out.shape[1] * D // strip, strip), LOW),
        cost_estimate=pl.CostEstimate(
            flops=0, bytes_accessed=4 * HEADS * out.shape[1] * D, transcendentals=0
        ),
        name="out_strips",
    )(chips, out)


def mid_kernel(mid_ref, pa, pb, pc, up_ref, gain_ref, w_ref, mg_ref, bg_ref, ag_ref):
    mid = mid_ref[...]
    scaled = (pa[...].astype(WIDE) + pb[...].astype(WIDE) + pc[...].astype(WIDE)) * gain_ref[
        ...
    ].astype(WIDE)
    r = lax.rsqrt(jnp.mean(mid * mid, axis=-1, keepdims=True) + EPSILON)
    inner = jnp.mean(scaled * mid, axis=-1, keepdims=True)
    mid_grad = up_ref[...].astype(WIDE) + r * scaled - mid * (r * r * r * inner)
    mg_ref[...] = mid_grad
    branch = mid_grad.astype(LOW)
    bg_ref[...] = branch
    att = dot_nt(branch, w_ref[...]).astype(LOW)
    for h in range(HEADS):
        ag_ref[h] = att[:, h * HEAD_DIM : (h + 1) * HEAD_DIM]


def mid_block(mid, pa, pb, pc, up, gain, w):
    count = mid.shape[0]
    return pl.pallas_call(
        mid_kernel,
        in_specs=[vmem()] * 7,
        out_specs=[vmem()] * 3,
        out_shape=[
            jax.ShapeDtypeStruct((count, D), WIDE),
            jax.ShapeDtypeStruct((count, D), LOW),
            jax.ShapeDtypeStruct((HEADS, count, HEAD_DIM), LOW),
        ],
        cost_estimate=pl.CostEstimate(
            flops=2 * count * D * D, bytes_accessed=6 * 2**20, transcendentals=0
        ),
        name="mid_block",
    )(mid, pa, pb, pc, up, gain, w)


def qkv_back_kernel(tab, dq_ref, own_ref, got_ref, cos_ref, sin_ref, n_ref, w_ref, dx_ref, dw_ref, sum_ref):
    i = pl.program_id(0)
    c, s = cos_ref[0], sin_ref[0]

    def rot(v):
        return v * c - pltpu.roll(v, HEAD_DIM // 2, 1) * s

    dq = rot(dq_ref[0] * SCALE).astype(LOW)
    dk = rot((own_ref[0, 0] + got_ref[0, 0].astype(WIDE)) * SCALE).astype(LOW)
    dv = (own_ref[1, 0] + got_ref[1, 0].astype(WIDE)).astype(LOW)
    grads = jnp.concatenate([dq, dk, dv], axis=1)
    dx_ref[0] = dot_nt(grads, w_ref[...]).astype(LOW)
    part = dot_tn(n_ref[0], grads)

    @pl.when(i == 0)
    def _():
        sum_ref[...] = part

    @pl.when(i > 0)
    def _():
        sum_ref[...] += part

    @pl.when(i == HEADS - 1)
    def _():
        dw_ref[...] = sum_ref[...].astype(LOW)


def qkv_back(chips, dq, own, got, cos, sin, normed, w):
    count = dq.shape[1]
    block = pl.BlockSpec((1, count, HEAD_DIM), lambda i, t: (t[i], 0, 0))
    pair = pl.BlockSpec((2, 1, count, HEAD_DIM), lambda i, t: (0, t[i], 0, 0))
    weight = pl.BlockSpec((D, 3 * HEAD_DIM), lambda i, t: (0, 0))
    return pl.pallas_call(
        qkv_back_kernel,
        grid_spec=pltpu.PrefetchScalarGridSpec(
            num_scalar_prefetch=1,
            grid=(HEADS,),
            in_specs=[
                block, pair, pair, block, block,
                pl.BlockSpec((1, count, D), lambda i, t: (t[i], 0, 0)),
                weight,
            ],
            out_specs=[pl.BlockSpec((1, count, D), lambda i, t: (i, 0, 0)), weight],
            scratch_shapes=[pltpu.VMEM((D, 3 * HEAD_DIM), WIDE)],
        ),
        out_shape=[
            jax.ShapeDtypeStruct((HEADS, count, D), LOW),
            jax.ShapeDtypeStruct((D, 3 * HEAD_DIM), LOW),
        ],
        cost_estimate=pl.CostEstimate(
            flops=4 * HEADS * count * D * 3 * HEAD_DIM,
            bytes_accessed=6 * HEADS * count * D,
            transcendentals=0,
        ),
        name="qkv_back",
    )(chips, dq, own, got, cos, sin, normed, w)


def local(
    far,
    tokens,
    segment_ids,
    second_doc,
    memory_index,
    cache_keys,
    cache_values,
    first_gain,
    query_weight,
    key_weight,
    value_weight,
    out_weight,
    second_gain,
    gate_weight,
    up_weight,
    down_weight,
    cotangent,
):
    x = tokens[0]
    upstream = cotangent[0]
    count = x.shape[0]
    blocks = count // QUERY_BLOCK
    rows = query_weight.shape[0]
    share = down_weight.shape[0]
    units = far * HEADS * share
    chip, core, pair = lax.axis_index("h"), lax.axis_index("c"), lax.axis_index("dl")
    mine = jnp.where(chip % 2 == 0, chip // 2, HEADS - 1 - chip // 2)
    slots = jnp.arange(HEADS, dtype=jnp.int32)
    chips = at_place(mine - slots)

    def by_head(w):
        return w.reshape(rows, HEADS, HEAD_DIM).transpose(1, 0, 2)

    picked = memory_index[0].transpose(1, 0, 2)
    seg_rows = jnp.broadcast_to(
        segment_ids[0].astype(LOW).reshape(1, blocks, QUERY_BLOCK), (HEADS, blocks, QUERY_BLOCK)
    )
    gains = jnp.concatenate([first_gain, second_gain])
    gain_rows = jnp.broadcast_to(
        jnp.pad(gains, (0, HEAD_DIM - 2 * rows)).reshape(1, 1, HEAD_DIM), (HEADS, 1, HEAD_DIM)
    )
    pack = jnp.concatenate(
        [
            by_head(query_weight),
            by_head(key_weight),
            by_head(value_weight),
            seg_rows,
            (picked // MEM_ROWS).astype(LOW),
            (picked % MEM_ROWS).astype(LOW),
            gain_rows,
        ],
        axis=1,
    )
    height = pack.shape[1]
    pack = jnp.pad(pack, ((0, 0), (0, -height % 16), (0, 0)))

    block = jnp.concatenate([x, out_weight], axis=0)
    split = count // 2
    forth, back = [block, turn(block, 1)], [block, turn(block, -1)]
    pack, forth[1], back[1], gate_late, up_late = lax.optimization_barrier(
        (pack, forth[1], back[1], gate_weight, up_weight)
    )
    got = exchange(pack)
    for step in range(HEADS // 2 - 2):
        forth.append(turn(forth[-1], 1))
        back.append(turn(back[-1], -1))
        if step == 1:
            _, forth[-1], back[-1], parity = lax.optimization_barrier(
                (got, forth[-1], back[-1], core)
            )
    far_first, far_last = turn(forth[-1][:split], 1), turn(back[-1][split:], -1)
    x_slots = [((v, count),) for v in forth] + [((far_first, split), (far_last, count - split))]
    x_slots += [((v, count),) for v in back[:0:-1]]
    outs = [v[count:] for v in forth] + [far_last[count - split :]]
    outs += [v[count:] for v in back[:0:-1]]
    got_c = swap(got, "c")
    got_y = swap(got, "dl")
    got_yc = swap(got_y, "c")
    near = pick(core, jnp.stack([got, got_c]), jnp.stack([got_c, got]))
    away = pick(core, jnp.stack([got_y, got_yc]), jnp.stack([got_yc, got_y]))
    every = pick(pair, jnp.stack([near, away]), jnp.stack([away, near]))
    every = every.transpose(2, 0, 1, 3, 4)
    if far > 1:
        every = lax.all_gather(every, "dh", axis=0)
    else:
        every = every[None]
    every = every.transpose(0, 2, 1, 3, 4, 5)
    w_qkv = jnp.concatenate(
        [every[..., i * rows : (i + 1) * rows, :].reshape(D, HEAD_DIM) for i in range(3)], axis=1
    )
    gain_all = every[..., 3 * rows + 3 * blocks, : 2 * rows].reshape(-1, 2, rows)
    gain_one = gain_all[:, 0].reshape(1, D)
    gain_two = gain_all[:, 1].reshape(1, D)

    def seg_of(blocks_of):
        return (
            blocks_of[:, 3 * rows : 3 * rows + blocks]
            .astype(WIDE)
            .astype(jnp.int32)
            .reshape(HEADS, count)
        )

    seg_own = seg_of(got)
    seg_oth = seg_of(got_c)
    idx = (
        got[:, 3 * rows + blocks : 3 * rows + 2 * blocks].astype(WIDE) * MEM_ROWS
        + got[:, 3 * rows + 2 * blocks : 3 * rows + 3 * blocks].astype(WIDE)
    ).astype(jnp.int32)
    idx = idx.reshape(HEADS, count, 1)

    block_docs = seg_own[:, ::QUERY_BLOCK]
    docs = second_doc.shape[1]
    doc_ids = jnp.arange(docs, dtype=jnp.int32)
    mates = jnp.sum(
        jnp.where(block_docs[:, :, None] == doc_ids, second_doc[0][None, None, :], 0), axis=-1
    )
    seg_all = jnp.concatenate([seg_own, seg_oth], axis=0)
    before = jnp.sum(
        (seg_all.reshape(1, -1) < block_docs[:, :1]).astype(jnp.int32), axis=1
    )
    tab = jnp.concatenate(
        [
            block_docs.reshape(-1),
            mates.reshape(-1),
            before // (2 * count),
            jnp.stack([core, chip]),
        ]
    ).astype(jnp.int32)

    half = HEAD_DIM // 2
    freqs = 10000.0 ** (-jnp.arange(half, dtype=WIDE) * 2.0 / (2 * half))
    positions = ((2 * slots + parity) * count)[:, None] + jnp.arange(count, dtype=jnp.int32)[None]
    turned = positions.astype(WIDE)[:, :, None] * freqs
    cosine, sine = jnp.cos(turned), jnp.sin(turned)
    cosine = jnp.concatenate([cosine, cosine], axis=-1)
    sine = jnp.concatenate([-sine, sine], axis=-1)

    half = units + -units % HEAD_DIM
    wide = 2 * half

    def by_owner(w):
        w = w.reshape(rows, far, 2, HEADS, 2, share).transpose(2, 4, 0, 1, 3, 5)
        return jnp.pad(w.reshape(2, 2, rows, units), ((0, 0),) * 3 + ((0, half - units),))

    gu = jnp.concatenate([by_owner(gate_late), by_owner(up_late)], axis=-1)
    kept = pick(core, gu[:, 0], gu[:, 1])
    came = swap(pick(core, gu[:, 1], gu[:, 0]), "c")
    gu = pick(core, jnp.stack([kept, came], 1), jnp.stack([came, kept], 1))
    kept = pick(pair, gu[0], gu[1])
    came = swap(pick(pair, gu[1], gu[0]), "dl")
    gu = pick(pair, jnp.stack([kept, came]), jnp.stack([came, kept])).reshape(4 * rows, wide)
    if far == 1:
        deep = 2 * rows
        lower = jnp.concatenate(fold(down_weight, deep), axis=1)
    else:
        deep = share
        lower = jnp.pad(down_weight, ((0, 0), (0, wide - D)))
    bundle = jnp.concatenate([gu, lower], axis=0)
    height = 4 * rows + share
    if far > 1:
        bundle = lax.all_gather(bundle, "dh", axis=0, tiled=True)
    upper = bundle.shape[0] // 2
    bundle, *_ = lax.optimization_barrier((bundle, far_first, far_last))
    forth, back = [bundle, turn(bundle, 1)], [bundle, turn(bundle, -1)]

    held = ()
    for order in ([0, 1, 7, 2, 6], [3, 5, 4]):
        held = qkv_blocks(
            at_place(mine - jnp.asarray(order, jnp.int32)).astype(jnp.int32),
            [x_slots[i] for i in order],
            gain_one,
            w_qkv,
            cosine,
            sine,
            held,
        )
    queries, own, normed_one = held
    other = swap(own, "c")
    seg_thin = seg_own.reshape(HEADS, count, 1)
    seg_own_row = seg_own.reshape(HEADS, 1, count)
    seg_oth_row = seg_oth.reshape(HEADS, 1, count)
    cached = [cache[0].reshape(-1, D) for cache in (cache_keys, cache_values)]
    half_attended = attend(
        tab, queries, own, other, seg_thin, seg_own_row, seg_oth_row, idx, *cached, 0, ()
    )
    first_lse, forth[1], back[1] = lax.optimization_barrier(
        (half_attended[2], forth[1], back[1])
    )
    attention, attention_low, lse, memory = attend(
        tab,
        queries,
        own,
        other,
        seg_thin,
        seg_own_row,
        seg_oth_row,
        idx,
        *cached,
        HEADS // 2,
        (*half_attended[:2], first_lse, half_attended[3]),
    )
    w_forth, w_back = turn(forth[1], 1), turn(back[1], -1)
    attention_low, w_forth, w_back = lax.optimization_barrier((attention_low, w_forth, w_back))
    forth.append(w_forth)
    back.append(w_back)

    *outs, up_late, _ = lax.optimization_barrier((*outs, upstream, attention_low))
    up_c = swap(up_late, "c")
    up_y = swap(up_late, "dl")
    up_yc = swap(up_y, "c")
    outs = jnp.stack(outs)
    outs_c = swap(outs, "c")
    outs_y = swap(outs, "dl")
    outs_yc = swap(outs_y, "c")
    heads = exchange(attention_low)
    w_forth, w_back = turn(w_forth, 1), turn(w_back, -1)
    heads, w_forth, w_back, up_c, up_y, up_yc = lax.optimization_barrier(
        (heads, w_forth, w_back, up_c, up_y, up_yc)
    )
    forth.append(w_forth)
    back.append(w_back)
    w_first, w_last = turn(w_forth[:upper], 1), turn(w_back[upper:], -1)
    slot_of = lax.rem(mine - jnp.asarray(PLACE, jnp.int32) + HEADS, HEADS).astype(jnp.int32)
    if far == 1:
        sources = [outs, outs_c, outs_y, outs_yc]
    else:
        near = pick(core, jnp.stack([outs, outs_c], 1), jnp.stack([outs_c, outs], 1))
        away = pick(core, jnp.stack([outs_y, outs_yc], 1), jnp.stack([outs_yc, outs_y], 1))
        sources = pick(pair, jnp.stack([near, away]), jnp.stack([away, near]))
        sources = lax.all_gather(jnp.take(sources, slot_of, axis=1), "dh", axis=0)
        sources = [sources.reshape(D, D)]
    where = jnp.concatenate([chips, jnp.stack([pair, core])]).astype(jnp.int32)
    attended, mid, normed_two, out_w = out_block(where, heads, sources, x, gain_two)
    normed_two, w_first, w_last = lax.optimization_barrier((normed_two, w_first, w_last))
    w_slots = forth + [w_first, w_last] + back[:0:-1]

    if far == 1:
        gate_w, up_w, down_w = weights(where, w_slots, units)
    else:
        middle = jnp.concatenate(w_slots[HEADS // 2 : HEADS // 2 + 2], axis=0)
        every = jnp.stack(w_slots[: HEADS // 2] + [middle] + w_slots[HEADS // 2 + 2 :])
        every = jnp.take(every, slot_of, axis=0).reshape(HEADS, far, height, wide)
        gu = every[:, :, : 4 * rows].reshape(HEADS, far, 2, 2 * rows, wide)
        gu = gu.transpose(1, 2, 0, 3, 4).reshape(D, wide)
        gate_w, up_w = gu[:, :units], gu[:, half : half + units]
        down_w = every[:, :, 4 * rows :, :D].transpose(1, 0, 2, 3).reshape(units, D)

    n_c = swap(normed_two, "c")
    n_y = swap(normed_two, "dl")
    n_yc = swap(n_y, "c")
    hid_l, gg_l, ug_l, dn_l, out_l = ffn(normed_two, n_c, upstream, up_c, gate_w, up_w, down_w)
    n_y, n_yc, dn_l = lax.optimization_barrier((n_y, n_yc, dn_l))
    hid_r, gg_r, ug_r, dn_r, out_r = ffn(n_y, n_yc, up_y, up_yc, gate_w, up_w, down_w)

    def to_away(away):
        return (away[0].astype(WIDE) + swap(away[1], "c").astype(WIDE)).astype(LOW)

    there = to_away(dn_r)
    there, hid_l, gg_l, ug_l, hid_r, gg_r, ug_r = lax.optimization_barrier(
        (there, hid_l, gg_l, ug_l, hid_r, gg_r, ug_r)
    )
    n_all, u_all = [normed_two, n_c, n_y, n_yc], [upstream, up_c, up_y, up_yc]
    near, away = (hid_l, gg_l, ug_l), (hid_r, gg_r, ug_r)
    if far == 1:
        parts = weight_grads(slot_of, n_all, u_all, near, away, height, wide)
    else:

        def over_tokens(left, right):
            return jnp.einsum(
                "gtd,gtf->df", left, right, preferred_element_type=WIDE
            ).astype(LOW)

        def by_rows(w):
            w = jnp.pad(w, ((0, 0), (0, half - units)))
            return w.reshape(far, 2, HEADS, 2 * rows, half).transpose(2, 0, 1, 3, 4)

        n_all, u_all = jnp.stack(n_all), jnp.stack(u_all)
        hid, gg, ug = (jnp.concatenate(pieces, axis=0) for pieces in zip(near, away))
        gu = jnp.concatenate(
            [by_rows(over_tokens(n_all, gg)), by_rows(over_tokens(n_all, ug))], axis=-1
        ).reshape(HEADS, far, 4 * rows, wide)
        down = over_tokens(hid, u_all).reshape(far, HEADS, share, D).transpose(1, 0, 2, 3)
        down = jnp.pad(down, ((0, 0), (0, 0), (0, 0), (0, wide - D)))
        parts = jnp.concatenate([gu, down], axis=2)
        parts = jnp.take(parts.reshape(HEADS, far * height, wide), chips, axis=0)

    out_l, out_r, _ = lax.optimization_barrier((out_l, out_r, parts))
    output = mid
    for part in (out_l[0], swap(out_l[1], "c"), swap(to_away(out_r), "dl")):
        output = output + part.astype(WIDE)
    output = output.astype(LOW)

    sums = [dn_l[0], swap(dn_l[1], "c"), swap(there, "dl")]
    sums[2], parts = lax.optimization_barrier((sums[2], parts))
    mid_grad, branch, att_grad = mid_block(mid, *sums, upstream, gain_two, out_w)
    ups = exchange(att_grad)

    def plus(block, arrived, start):
        size = arrived.shape[0]
        total = block[start : start + size].astype(WIDE) + arrived.astype(WIDE)
        pieces = [block[:start], total, block[start + size :]]
        pieces = [piece.astype(LOW) for piece in pieces if piece.shape[0]]
        return jnp.concatenate(pieces, axis=0)

    def ring_first(blocks, split):
        middle = blocks[HEADS // 2]
        return (
            plus(blocks[HEADS // 2 + 1], turn(middle[:split].astype(LOW), 1), 0),
            plus(blocks[HEADS // 2 - 1], turn(middle[split:].astype(LOW), -1), split),
        )

    def ring_next(blocks, forth, back, step):
        return (
            plus(blocks[HEADS // 2 + step], turn(forth, 1), 0),
            plus(blocks[HEADS // 2 - step], turn(back, -1), 0),
        )

    def ring_last(blocks, forth, back):
        return blocks[0].astype(WIDE) + forth.astype(WIDE) + back.astype(WIDE)

    def over_owner(w, width):
        w = w.reshape(far, 2, HEADS, 2, rows, width)
        kept = pick(core, w[:, :, :, 0], w[:, :, :, 1])
        came = swap(pick(core, w[:, :, :, 1], w[:, :, :, 0]), "c")
        w = kept.astype(WIDE) + came.astype(WIDE)
        kept = pick(pair, w[:, 0], w[:, 1])
        came = swap(pick(pair, w[:, 1], w[:, 0]).astype(LOW), "dl")
        w = (kept + came.astype(WIDE)).astype(LOW)
        if far > 1:
            w = lax.psum_scatter(w, "dh", scatter_dimension=0, tiled=True)
        return w[0]

    out_part = over_owner(
        jnp.einsum("td,te->de", attended, branch, preferred_element_type=WIDE).astype(LOW), D
    )
    strip = wide - D
    upper = 4 * rows if far == 1 else parts.shape[1] // 2
    blocks = [parts[slot].astype(WIDE) for slot in range(HEADS)]
    if far == 1:
        strips = out_strips(where, out_part, strip)
        below = share - strips.shape[1]
        for slot in range(HEADS):
            if slot != HEADS // 2:
                blocks[slot] = blocks[slot] + jnp.pad(
                    strips[slot].astype(WIDE), ((4 * rows, below), (D, 0))
                )
        out_far = turn(strips[HEADS // 2], HEADS // 2)
    else:
        out_far = exchange(out_part)
    forth, back = ring_first(blocks, upper)
    ups, forth, back = lax.optimization_barrier((ups, forth, back))
    forth, back = ring_next(blocks, forth, back, 2)

    dq, d_own, d_oth = attend_back(
        tab, queries, ups, attention, lse, own, other, memory, seg_thin, seg_own_row, seg_oth_row
    )
    d_got = swap(d_oth, "c")
    dq, out_far, forth, back = lax.optimization_barrier((dq, out_far, forth, back))
    dx, dw = qkv_back(
        chips.astype(jnp.int32), dq, d_own, d_got, cosine, sine, normed_one, w_qkv
    )
    arrived_forth, arrived_back = turn(forth, 1), turn(back, -1)
    dx, arrived_forth, arrived_back = lax.optimization_barrier((dx, arrived_forth, arrived_back))
    dx_forth, dx_back = ring_first(dx, split)
    dx_forth, dx_back, arrived_forth, arrived_back = lax.optimization_barrier(
        (dx_forth, dx_back, arrived_forth, arrived_back)
    )
    forth = plus(blocks[HEADS - 1], arrived_forth, 0)
    back = plus(blocks[1], arrived_back, 0)

    dw = over_owner(dw, 3 * HEAD_DIM)
    dx_forth, dx_back = ring_next(dx, dx_forth, dx_back, 2)
    dw, dx_forth, dx_back = lax.optimization_barrier((dw, dx_forth, dx_back))
    qkv_grads = exchange(dw).astype(WIDE)
    dx_forth, dx_back = ring_next(dx, dx_forth, dx_back, 3)
    normed_one_grad = ring_last(dx, turn(dx_forth, 1), turn(dx_back, -1))

    summed = ring_last(blocks, turn(forth, 1), turn(back, -1)).astype(LOW)
    if far > 1:
        summed = lax.psum_scatter(summed, "dh", scatter_dimension=0, tiled=True)
    down_w_grad = summed[4 * rows : 4 * rows + share, :D].astype(WIDE)
    if far == 1:
        out_w_grad = summed[4 * rows : 4 * rows + strips.shape[1], D:].astype(WIDE)
        out_w_grad = out_w_grad + out_far.astype(WIDE)
        out_w_grad = out_w_grad.reshape(D // strip, rows, strip).transpose(1, 0, 2).reshape(rows, D)
    else:
        out_w_grad = jnp.sum(out_far.astype(WIDE), axis=0)
    gu = summed[: 4 * rows].reshape(2, 2, rows, wide)
    kept = pick(core, gu[:, 0], gu[:, 1])
    came = swap(pick(core, gu[:, 1], gu[:, 0]), "c")
    gu = pick(core, jnp.stack([kept, came], 1), jnp.stack([came, kept], 1))
    kept = pick(pair, gu[0], gu[1])
    came = swap(pick(pair, gu[1], gu[0]), "dl")
    gu = pick(pair, jnp.stack([kept, came]), jnp.stack([came, kept]))
    gu = jnp.stack([gu[..., :units], gu[..., half : half + units]])
    gu = (
        gu.reshape(2, 2, 2, rows, far, HEADS, share)
        .transpose(0, 3, 4, 1, 5, 2, 6)
        .reshape(2, rows, FF)
        .astype(WIDE)
    )
    gate_w_grad, up_w_grad = gu[0], gu[1]

    wide_x = x.astype(WIDE)
    r = lax.rsqrt(jnp.mean(wide_x * wide_x, axis=-1, keepdims=True) + EPSILON)
    scaled = normed_one_grad * gain_one.astype(WIDE)
    inner = jnp.mean(scaled * wide_x, axis=-1, keepdims=True)
    input_grad = mid_grad + r * scaled - wide_x * (r * r * r * inner)

    q_w_grad, k_w_grad, v_w_grad = (
        qkv_grads[:, :, i * HEAD_DIM : (i + 1) * HEAD_DIM].transpose(1, 0, 2).reshape(rows, D)
        for i in range(3)
    )

    def gain_grad(gain, pairs):
        total = 0.0
        for grad, weight in pairs:
            total = total + jnp.sum(grad * weight.astype(WIDE), axis=1)
        return total / gain.astype(WIDE)

    first_gain_grad = gain_grad(
        first_gain,
        ((q_w_grad, query_weight), (k_w_grad, key_weight), (v_w_grad, value_weight)),
    )
    second_gain_grad = gain_grad(
        second_gain, ((gate_w_grad, gate_weight), (up_w_grad, up_weight))
    )
    return (
        output[None],
        input_grad[None],
        first_gain_grad,
        q_w_grad,
        k_w_grad,
        v_w_grad,
        out_w_grad,
        second_gain_grad,
        gate_w_grad,
        up_w_grad,
        down_w_grad,
    )


def solution(mesh):
    far = mesh.shape["dp"] // 2
    cores = mesh.shape["seq"] // HEADS
    fine = Mesh(mesh.devices.reshape(far, 2, HEADS, cores), ("dh", "dl", "h", "c"))
    dp, seq, every = ("dh", "dl"), ("h", "c"), ("dh", "dl", "h", "c")
    rows = P(every, None)
    return jax.shard_map(
        functools.partial(local, far),
        mesh=fine,
        in_specs=(
            P(dp, seq, None),
            P(dp, seq),
            P(dp, None),
            P(dp, seq, None, None),
            P(dp, None, None, None),
            P(dp, None, None, None),
            P(every),
            rows,
            rows,
            rows,
            rows,
            P(every),
            rows,
            rows,
            rows,
            P(dp, seq, None),
        ),
        out_specs=(
            P(dp, seq, None),
            P(dp, seq, None),
            P(every),
            rows,
            rows,
            rows,
            rows,
            P(every),
            rows,
            rows,
            rows,
        ),
        check_vma=False,
    )
```

```python
import functools
import math

import jax
import jax.numpy as jnp
from jax import lax
from jax.experimental import pallas as pl
from jax.experimental.pallas import tpu as pltpu
from jax.sharding import Mesh
from jax.sharding import PartitionSpec as P

D = 1024
FF = 2816
HEADS = 8
HEAD_DIM = 128
QUERY_BLOCK = 128
MEM_ROWS = 256
EPSILON = 1e-05
NEGATIVE = -1e30
SCALE = 1.0 / math.sqrt(HEAD_DIM)
LOG2 = SCALE * math.log2(math.e)
LOW = jnp.bfloat16
WIDE = jnp.float32

RING = [2 * i for i in range(HEADS // 2)] + [2 * i + 1 for i in reversed(range(HEADS // 2))]
PLACE = [RING.index(i) for i in range(HEADS)]


def dot_nn(a, b):
    return lax.dot_general(a, b, (((1,), (0,)), ((), ())), preferred_element_type=WIDE)


def dot_nt(a, b):
    return lax.dot_general(a, b, (((1,), (1,)), ((), ())), preferred_element_type=WIDE)


def dot_tn(a, b):
    return lax.dot_general(a, b, (((0,), (0,)), ((), ())), preferred_element_type=WIDE)


def swap(block, axis):
    return lax.ppermute(block, axis, [(0, 1), (1, 0)])


def turn(block, distance):
    route = [(RING[i], RING[(i + distance) % HEADS]) for i in range(HEADS)]
    return lax.ppermute(block, "h", route)


def at_place(place):
    place = lax.rem(place + 2 * HEADS, HEADS)
    return jnp.where(place < HEADS // 2, 2 * place, 2 * (HEADS - 1 - place) + 1)


def exchange(blocks):
    return lax.all_to_all(blocks, "h", 0, 0)


def pick(flag, first, second):
    return jnp.where(flag == 0, first, second)


def smem():
    return pl.BlockSpec(memory_space=pltpu.SMEM)


def vmem():
    return pl.BlockSpec(memory_space=pltpu.VMEM)


def qkv_kernel(parts, tab, *refs):
    xs, (gain_ref, w_ref, cos_ref, sin_ref) = refs[: sum(parts)], refs[sum(parts) : sum(parts) + 4]
    q_ref, kv_ref, n_ref, x_ref = refs[-4:]
    i = pl.program_id(0)
    first = 0
    for step, number in enumerate(parts):

        @pl.when(i == step)
        def _(blocks=xs[first : first + number]):
            row = 0
            for block in blocks:
                size = block.shape[0]
                x_ref[row : row + size, :] = block[...]
                row += size

        first += number
    x = x_ref[...].astype(WIDE)
    r = lax.rsqrt(jnp.mean(x * x, axis=-1, keepdims=True) + EPSILON)
    normed = (x * r * gain_ref[...].astype(WIDE)).astype(LOW)
    n_ref[0] = normed
    out = dot_nn(normed, w_ref[...])
    c, s = cos_ref[0], sin_ref[0]

    def rot(v):
        return v * c + pltpu.roll(v, HEAD_DIM // 2, 1) * s

    q_ref[0] = rot(out[:, :HEAD_DIM]).astype(LOW)
    kv_ref[0, 0] = rot(out[:, HEAD_DIM : 2 * HEAD_DIM]).astype(LOW)
    kv_ref[1, 0] = out[:, 2 * HEAD_DIM :].astype(LOW)


def qkv_blocks(chips, xs, gain, w, cos, sin, held):
    count = cos.shape[1]
    flat = [piece for block in xs for piece, _ in block]
    read = [size for block in xs for _, size in block]

    def whole(shape):
        return pl.BlockSpec(shape, lambda i, t: (0, 0))

    def block(*shape):
        return pl.BlockSpec((1, *shape), lambda i, t: (t[i], 0, 0))

    spec = pltpu.PrefetchScalarGridSpec(
        num_scalar_prefetch=1,
        grid=(len(xs),),
        in_specs=[whole((size, D)) for size in read]
        + [whole((1, D)), whole((D, 3 * HEAD_DIM)), block(count, HEAD_DIM), block(count, HEAD_DIM)]
        + [pl.BlockSpec(memory_space=pl.ANY)] * len(held),
        out_specs=[
            block(count, HEAD_DIM),
            pl.BlockSpec((2, 1, count, HEAD_DIM), lambda i, t: (0, t[i], 0, 0)),
            block(count, D),
        ],
        scratch_shapes=[pltpu.VMEM((count, D), LOW)],
    )
    return pl.pallas_call(
        functools.partial(qkv_kernel, [len(block) for block in xs]),
        grid_spec=spec,
        out_shape=[
            jax.ShapeDtypeStruct((HEADS, count, HEAD_DIM), LOW),
            jax.ShapeDtypeStruct((2, HEADS, count, HEAD_DIM), LOW),
            jax.ShapeDtypeStruct((HEADS, count, D), LOW),
        ],
        input_output_aliases={len(flat) + 5 + i: i for i in range(len(held))},
        cost_estimate=pl.CostEstimate(
            flops=2 * len(xs) * count * D * 3 * HEAD_DIM,
            bytes_accessed=5 * len(xs) * count * D,
            transcendentals=0,
        ),
        name=f"qkv{len(xs)}",
    )(chips, *flat, gain, w, cos, sin, *held)


def causal(count):
    rows = lax.broadcasted_iota(jnp.int32, (count, count), 0)
    return lax.broadcasted_iota(jnp.int32, (count, count), 1) <= rows


def attend_kernel(
    tab, q_ref, own_ref, oth_ref, segq_ref, sego_ref, segt_ref, idx_ref, ck_ref, cv_ref,
    o_ref, low_ref, lse_ref, mem_ref,
):
    i = pl.program_id(0)
    parity = tab[40]
    count = q_ref.shape[1]
    q = q_ref[0]
    segq = segq_ref[0]

    s1 = dot_nt(q, own_ref[0, i]) * LOG2
    s2 = dot_nt(q, oth_ref[0, i]) * LOG2
    s1 = jnp.where((sego_ref[i] == segq) & causal(count), s1, NEGATIVE)
    s2 = jnp.where(segt_ref[i] == segq + 64 * (1 - parity), s2, NEGATIVE)
    memory = []
    for b in range(count // QUERY_BLOCK):
        rows = slice(b * QUERY_BLOCK, (b + 1) * QUERY_BLOCK)
        doc = tab[2 * i + b]
        mate = tab[16 + 2 * i + b]
        idx = idx_ref[0, rows, :]
        lane = lax.broadcasted_iota(jnp.int32, (QUERY_BLOCK, MEM_ROWS), 1)
        first = jnp.where(idx == lane, 1.0, 0.0).astype(LOW)
        second = jnp.where(idx == lane + MEM_ROWS, 1.0, 0.0).astype(LOW)
        here = pl.ds(pl.multiple_of(doc * MEM_ROWS, MEM_ROWS), MEM_ROWS)
        there = pl.ds(pl.multiple_of(mate * MEM_ROWS, MEM_ROWS), MEM_ROWS)
        mk = (dot_nn(first, ck_ref[here, :]) + dot_nn(second, ck_ref[there, :])).astype(LOW)
        mv = (dot_nn(first, cv_ref[here, :]) + dot_nn(second, cv_ref[there, :])).astype(LOW)
        mem_ref[0, 0, rows, :] = mk
        mem_ref[1, 0, rows, :] = mv
        s = jnp.where(segq[rows] == doc, dot_nt(q[rows], mk) * LOG2, NEGATIVE)
        memory.append((s, mv))
    sm = jnp.concatenate([s for s, _ in memory], axis=0)
    top = jnp.maximum(
        jnp.max(jnp.maximum(s1, s2), axis=-1, keepdims=True), jnp.max(sm, axis=-1, keepdims=True)
    )
    p1 = jnp.exp2(s1 - top)
    p2 = jnp.exp2(s2 - top)
    pm = jnp.exp2(sm - top)
    total = jnp.sum(p1 + p2, axis=-1, keepdims=True) + jnp.sum(pm, axis=-1, keepdims=True)
    pm = pm.astype(LOW)
    acc = jnp.concatenate(
        [
            dot_nn(pm[b * QUERY_BLOCK : (b + 1) * QUERY_BLOCK], mv)
            for b, (_, mv) in enumerate(memory)
        ],
        axis=0,
    )
    acc = acc + dot_nn(p1.astype(LOW), own_ref[1, i]) + dot_nn(p2.astype(LOW), oth_ref[1, i])

    def body(j, state):
        top, total, acc = state
        s1 = dot_nt(q, own_ref[0, j]) * LOG2
        s2 = dot_nt(q, oth_ref[0, j]) * LOG2
        s1 = jnp.where(sego_ref[j] == segq, s1, NEGATIVE)
        s2 = jnp.where(segt_ref[j] == segq, s2, NEGATIVE)
        fresh = jnp.maximum(top, jnp.max(jnp.maximum(s1, s2), axis=-1, keepdims=True))
        p1 = jnp.exp2(s1 - fresh)
        p2 = jnp.exp2(s2 - fresh)
        decay = jnp.exp2(top - fresh)
        total = total * decay + jnp.sum(p1 + p2, axis=-1, keepdims=True)
        acc = (
            acc * decay
            + dot_nn(p1.astype(LOW), own_ref[1, j])
            + dot_nn(p2.astype(LOW), oth_ref[1, j])
        )
        return fresh, total, acc

    top, total, acc = lax.fori_loop(tab[32 + i], i, body, (top, total, acc))
    out = acc / total
    o_ref[0] = out
    low_ref[0] = out.astype(LOW)
    lse_ref[0] = top + jnp.log2(total)


def attend(tab, q, own, oth, segq, sego, segt, idx, ck, cv):
    count = q.shape[1]
    block = pl.BlockSpec((1, count, HEAD_DIM), lambda i, t: (i, 0, 0))
    thin = pl.BlockSpec((1, count, 1), lambda i, t: (i, 0, 0))
    whole = pl.BlockSpec((2, HEADS, count, HEAD_DIM), lambda i, t: (0, 0, 0, 0))
    segs = pl.BlockSpec((HEADS, 1, count), lambda i, t: (0, 0, 0))
    cache = pl.BlockSpec((ck.shape[0], HEAD_DIM), lambda i, t: (0, t[41]))
    mem = pl.BlockSpec((2, 1, count, HEAD_DIM), lambda i, t: (0, i, 0, 0))
    return pl.pallas_call(
        attend_kernel,
        grid_spec=pltpu.PrefetchScalarGridSpec(
            num_scalar_prefetch=1,
            grid=(HEADS,),
            in_specs=[block, whole, whole, thin, segs, segs, thin, cache, cache],
            out_specs=[block, block, thin, mem],
        ),
        out_shape=[
            jax.ShapeDtypeStruct((HEADS, count, HEAD_DIM), WIDE),
            jax.ShapeDtypeStruct((HEADS, count, HEAD_DIM), LOW),
            jax.ShapeDtypeStruct((HEADS, count, 1), WIDE),
            jax.ShapeDtypeStruct((2, HEADS, count, HEAD_DIM), LOW),
        ],
        cost_estimate=pl.CostEstimate(
            flops=25 * 10**9, bytes_accessed=6 * 2**20, transcendentals=3 * 10**6
        ),
        name="attend",
    )(tab, q, own, oth, segq, sego, segt, idx, ck, cv)


def attend_back_kernel(
    tab, q_ref, up_ref, o_ref, lse_ref, own_ref, oth_ref, mem_ref, segq_ref, sego_ref, segt_ref,
    dq_ref, down_ref, doth_ref, sum_ref,
):
    i = pl.program_id(0)

    @pl.when(i == 0)
    def _():
        sum_ref[...] = jnp.zeros_like(sum_ref)

    parity = tab[40]
    count = q_ref.shape[1]
    q = q_ref[0]
    up = up_ref[0]
    lse = lse_ref[0]
    segq = segq_ref[0]
    delta = jnp.sum(up.astype(WIDE) * o_ref[0], axis=-1, keepdims=True)
    partial = []
    for b in range(count // QUERY_BLOCK):
        rows = slice(b * QUERY_BLOCK, (b + 1) * QUERY_BLOCK)
        mk = mem_ref[0, 0, rows, :]
        mv = mem_ref[1, 0, rows, :]
        ok = segq[rows] == tab[2 * i + b]
        p = jnp.exp2(jnp.where(ok, dot_nt(q[rows], mk) * LOG2 - lse[rows], NEGATIVE))
        ds = (p * (dot_nt(up[rows], mv) - delta[rows])).astype(LOW)
        partial.append(dot_nn(ds, mk))

    def tile(side, ref, j, ok, dq):
        k = ref[0, j]
        v = ref[1, j]
        p = jnp.exp2(jnp.where(ok, dot_nt(q, k) * LOG2 - lse, NEGATIVE))
        ds = (p * (dot_nt(up, v) - delta)).astype(LOW)
        sum_ref[side, 0, j] += dot_tn(ds, q)
        sum_ref[side, 1, j] += dot_tn(p.astype(LOW), up)
        return dq + dot_nn(ds, k)

    dq = jnp.concatenate(partial, axis=0)
    dq = tile(0, own_ref, i, (sego_ref[i] == segq) & causal(count), dq)
    dq = tile(1, oth_ref, i, segt_ref[i] == segq + 64 * (1 - parity), dq)

    def body(j, dq):
        dq = tile(0, own_ref, j, sego_ref[j] == segq, dq)
        return tile(1, oth_ref, j, segt_ref[j] == segq, dq)

    dq_ref[0] = lax.fori_loop(tab[32 + i], i, body, dq)

    @pl.when(i == HEADS - 1)
    def _():
        down_ref[...] = sum_ref[0]
        doth_ref[...] = sum_ref[1].astype(LOW)


def attend_back(tab, q, up, o, lse, own, oth, mem, segq, sego, segt):
    count = q.shape[1]
    block = pl.BlockSpec((1, count, HEAD_DIM), lambda i, t: (i, 0, 0))
    thin = pl.BlockSpec((1, count, 1), lambda i, t: (i, 0, 0))
    whole = pl.BlockSpec((2, HEADS, count, HEAD_DIM), lambda i, t: (0, 0, 0, 0))
    segs = pl.BlockSpec((HEADS, 1, count), lambda i, t: (0, 0, 0))
    memory = pl.BlockSpec((2, 1, count, HEAD_DIM), lambda i, t: (0, i, 0, 0))
    return pl.pallas_call(
        attend_back_kernel,
        grid_spec=pltpu.PrefetchScalarGridSpec(
            num_scalar_prefetch=1,
            grid=(HEADS,),
            in_specs=[block, block, block, thin, whole, whole, memory, thin, segs, segs],
            out_specs=[block, whole, whole],
            scratch_shapes=[pltpu.VMEM((2, 2, HEADS, count, HEAD_DIM), WIDE)],
        ),
        out_shape=[
            jax.ShapeDtypeStruct((HEADS, count, HEAD_DIM), WIDE),
            jax.ShapeDtypeStruct((2, HEADS, count, HEAD_DIM), WIDE),
            jax.ShapeDtypeStruct((2, HEADS, count, HEAD_DIM), LOW),
        ],
        cost_estimate=pl.CostEstimate(
            flops=30 * 10**9, bytes_accessed=10 * 2**20, transcendentals=3 * 10**6
        ),
        name="attend_back",
    )(tab, q, up, o, lse, own, oth, mem, segq, sego, segt)


def place_rows(tab, sources, w_ref):
    rows = sources[0].shape[1]
    for k, source in enumerate(sources):
        pair = tab[8] if k < 2 else 1 - tab[8]
        core = tab[9] if k % 2 == 0 else 1 - tab[9]
        for slot in range(HEADS):
            start = ((pair * HEADS + tab[slot]) * 2 + core) * rows
            w_ref[pl.ds(pl.multiple_of(start, rows), rows), :] = source[slot]


def out_kernel(tab, heads_ref, *refs):
    sources, (x_ref, gain_ref, att_ref, mid_ref, n_ref, w_ref) = refs[:-6], refs[-6:]
    if len(sources) == 1:
        w_ref[...] = sources[0][...]
    else:
        place_rows(tab, sources, w_ref)
    for h in range(HEADS):
        att_ref[:, h * HEAD_DIM : (h + 1) * HEAD_DIM] = heads_ref[h]
    mid = x_ref[...].astype(WIDE) + dot_nn(att_ref[...], w_ref[...])
    mid_ref[...] = mid
    r = lax.rsqrt(jnp.mean(mid * mid, axis=-1, keepdims=True) + EPSILON)
    n_ref[...] = (mid * r * gain_ref[...].astype(WIDE)).astype(LOW)


def out_block(tab, heads, sources, x, gain):
    count = x.shape[0]
    return pl.pallas_call(
        out_kernel,
        in_specs=[smem()] + [vmem()] * (3 + len(sources)),
        out_specs=[vmem()] * 4,
        out_shape=[
            jax.ShapeDtypeStruct((count, D), LOW),
            jax.ShapeDtypeStruct((count, D), WIDE),
            jax.ShapeDtypeStruct((count, D), LOW),
            jax.ShapeDtypeStruct((D, D), LOW),
        ],
        cost_estimate=pl.CostEstimate(
            flops=2 * count * D * D, bytes_accessed=6 * 2**20, transcendentals=0
        ),
        name="out_block",
    )(tab, heads, *sources, x, gain)


def fold(block, deep):
    half, rest = D // 2, block.shape[0] - deep
    middle = jnp.concatenate([block[deep:, :half], block[: deep - rest, half:]], axis=0)
    last = block[deep - rest :, half:]
    last = jnp.concatenate([last, jnp.zeros((deep - last.shape[0], half), last.dtype)], axis=0)
    return block[:deep, :half], middle, last


def unfolded(block, share):
    deep, half = block.shape[0], D // 2
    rest = share - deep
    return [
        (0, deep, 0, block[:, :half]),
        (deep, rest, 0, block[:rest, half:D]),
        (0, deep - rest, half, block[rest:, half:D]),
        (deep - rest, share - deep + rest, half, block[: share - deep + rest, D:]),
    ]


def weights_kernel(tab, *refs):
    blocks, (gate_ref, up_ref, down_ref, acc_ref) = refs[:-4], refs[-4:]
    units = gate_ref.shape[1]
    height, wide = blocks[0].shape
    half = wide // 2
    share = units // HEADS
    rows = D // (2 * HEADS)
    middle = blocks[HEADS // 2].shape[0]
    for slot in range(HEADS):
        chip = tab[slot]
        if slot == HEADS // 2:
            pieces = [(0, blocks[slot]), (middle, blocks[slot + 1])]
        else:
            pieces = [(0, blocks[slot if slot < HEADS // 2 else slot + 1])]
        for start, ref in pieces:
            stop = start + ref.shape[0]
            for pair in range(2):
                first, last = max(start, pair * rows), min(stop, (pair + 1) * rows)
                if first < last:
                    size = last - first
                    here = (pair * HEADS + chip) * rows + first - pair * rows
                    here = pl.ds(pl.multiple_of(here, math.gcd(rows, first)), size)
                    gate_ref[here, :] = ref[first - start : last - start, :units]
                    up_ref[here, :] = ref[first - start : last - start, half : half + units]
        lower = ref[2 * rows - start :, :].astype(WIDE)
        for row, size, column, piece in unfolded(lower, share):
            here = pl.ds(pl.multiple_of(chip * share + row, 8), size)
            acc_ref[here, column : column + D // 2] = piece
    down_ref[...] = acc_ref[...].astype(LOW)


def weights(chips, blocks, units):
    return pl.pallas_call(
        weights_kernel,
        in_specs=[smem()] + [vmem()] * len(blocks),
        out_specs=[vmem()] * 3,
        out_shape=[
            jax.ShapeDtypeStruct((D, units), LOW),
            jax.ShapeDtypeStruct((D, units), LOW),
            jax.ShapeDtypeStruct((units, D), LOW),
        ],
        scratch_shapes=[pltpu.VMEM((units, D), WIDE)],
        cost_estimate=pl.CostEstimate(
            flops=0, bytes_accessed=12 * D * units, transcendentals=0
        ),
        name="weights",
    )(chips, *blocks)


def ffn_kernel(na, nb, ga, gb, g_ref, u_ref, d_ref, hid_ref, gg_ref, ug_ref, dn_ref, out_ref):
    for t, (n_ref, c_ref) in enumerate(((na, ga), (nb, gb))):
        n = n_ref[...]
        gate = dot_nn(n, g_ref[...])
        upper = dot_nn(n, u_ref[...])
        sigma = jax.nn.sigmoid(gate)
        silu = gate * sigma
        hid = (silu * upper).astype(LOW)
        hid_ref[t] = hid
        out_ref[t] = dot_nn(hid, d_ref[...]).astype(LOW)
        hg = dot_nt(c_ref[...], d_ref[...])
        gg = (hg * upper * sigma * (1.0 + gate * (1.0 - sigma))).astype(LOW)
        ug = (hg * silu).astype(LOW)
        gg_ref[t] = gg
        ug_ref[t] = ug
        dn_ref[t] = (dot_nt(gg, g_ref[...]) + dot_nt(ug, u_ref[...])).astype(LOW)


def ffn(na, nb, ga, gb, g, u, d):
    count = na.shape[0]
    units = g.shape[1]
    return pl.pallas_call(
        ffn_kernel,
        in_specs=[vmem()] * 7,
        out_specs=[vmem()] * 5,
        out_shape=[jax.ShapeDtypeStruct((2, count, units), LOW)] * 3
        + [jax.ShapeDtypeStruct((2, count, D), LOW)] * 2,
        cost_estimate=pl.CostEstimate(
            flops=24 * count * D * units,
            bytes_accessed=6 * D * units + 16 * count * D,
            transcendentals=2 * count * units,
        ),
        name="ffn",
    )(na, nb, ga, gb, g, u, d)


def grads_kernel(tab, *refs):
    ns, ups, (hid_l, gg_l, ug_l, hid_r, gg_r, ug_r, parts_ref) = (
        refs[:4], refs[4:8], refs[8:],
    )
    wide = parts_ref.shape[2]
    half = wide // 2
    units = hid_l.shape[2]
    share = units // HEADS
    rows = ns[0].shape[1] // (2 * HEADS)
    edge = units - units % HEAD_DIM

    def tokens(near, away):
        return jnp.concatenate([near[0], near[1], away[0], away[1]], axis=0)

    n = jnp.concatenate([v[...] for v in ns], axis=0)
    up = jnp.concatenate([v[...] for v in ups], axis=0)
    for near, away, start in ((gg_l, gg_r, 0), (ug_l, ug_r, half)):
        total = dot_tn(n, tokens(near, away)).astype(LOW)
        for h in range(HEADS):
            slot = tab[h]
            for pair in range(2):
                first = (pair * HEADS + h) * rows
                here = slice(pair * rows, (pair + 1) * rows)
                parts_ref[slot, here, start + edge : start + half] = jnp.zeros(
                    (rows, half - edge), LOW
                )
                parts_ref[slot, here, start : start + units] = total[first : first + rows]
    total = dot_tn(tokens(hid_l, hid_r), up)
    strip = wide - D
    for h in range(HEADS):
        slot = tab[h]
        piece = total[h * share : (h + 1) * share].astype(LOW)
        parts_ref[slot, 2 * rows : 2 * rows + share, :D] = piece
        parts_ref[slot, 2 * rows : 2 * rows + share, D:] = jnp.zeros((share, strip), LOW)


def weight_grads(slot_of, ns, ups, near, away, height, wide):
    count = ns[0].shape[0]
    units = near[0].shape[2]
    return pl.pallas_call(
        grads_kernel,
        in_specs=[smem()] + [vmem()] * 14,
        out_specs=vmem(),
        out_shape=jax.ShapeDtypeStruct((HEADS, height, wide), LOW),
        cost_estimate=pl.CostEstimate(
            flops=24 * count * D * units, bytes_accessed=14 * 2**20, transcendentals=0
        ),
        name="weight_grads",
    )(slot_of, *ns, *ups, *near, *away)


def strips_kernel(tab, out_ref, strips_ref):
    rows, strip = out_ref.shape[1], strips_ref.shape[2]
    for slot in range(HEADS):
        for i in range(D // strip):
            strips_ref[slot, i * rows : (i + 1) * rows, :] = out_ref[
                tab[slot], :, i * strip : (i + 1) * strip
            ]


def out_strips(chips, out, strip):
    return pl.pallas_call(
        strips_kernel,
        in_specs=[smem(), vmem()],
        out_specs=vmem(),
        out_shape=jax.ShapeDtypeStruct((HEADS, out.shape[1] * D // strip, strip), LOW),
        cost_estimate=pl.CostEstimate(
            flops=0, bytes_accessed=4 * HEADS * out.shape[1] * D, transcendentals=0
        ),
        name="out_strips",
    )(chips, out)


def mid_kernel(mid_ref, pa, pb, pc, up_ref, gain_ref, w_ref, mg_ref, bg_ref, ag_ref):
    mid = mid_ref[...]
    scaled = (pa[...].astype(WIDE) + pb[...].astype(WIDE) + pc[...].astype(WIDE)) * gain_ref[
        ...
    ].astype(WIDE)
    r = lax.rsqrt(jnp.mean(mid * mid, axis=-1, keepdims=True) + EPSILON)
    inner = jnp.mean(scaled * mid, axis=-1, keepdims=True)
    mid_grad = up_ref[...].astype(WIDE) + r * scaled - mid * (r * r * r * inner)
    mg_ref[...] = mid_grad
    branch = mid_grad.astype(LOW)
    bg_ref[...] = branch
    att = dot_nt(branch, w_ref[...]).astype(LOW)
    for h in range(HEADS):
        ag_ref[h] = att[:, h * HEAD_DIM : (h + 1) * HEAD_DIM]


def mid_block(mid, pa, pb, pc, up, gain, w):
    count = mid.shape[0]
    return pl.pallas_call(
        mid_kernel,
        in_specs=[vmem()] * 7,
        out_specs=[vmem()] * 3,
        out_shape=[
            jax.ShapeDtypeStruct((count, D), WIDE),
            jax.ShapeDtypeStruct((count, D), LOW),
            jax.ShapeDtypeStruct((HEADS, count, HEAD_DIM), LOW),
        ],
        cost_estimate=pl.CostEstimate(
            flops=2 * count * D * D, bytes_accessed=6 * 2**20, transcendentals=0
        ),
        name="mid_block",
    )(mid, pa, pb, pc, up, gain, w)


def qkv_back_kernel(tab, dq_ref, own_ref, got_ref, cos_ref, sin_ref, n_ref, w_ref, dx_ref, dw_ref, sum_ref):
    i = pl.program_id(0)
    c, s = cos_ref[0], sin_ref[0]

    def rot(v):
        return v * c - pltpu.roll(v, HEAD_DIM // 2, 1) * s

    dq = rot(dq_ref[0] * SCALE).astype(LOW)
    dk = rot((own_ref[0, 0] + got_ref[0, 0].astype(WIDE)) * SCALE).astype(LOW)
    dv = (own_ref[1, 0] + got_ref[1, 0].astype(WIDE)).astype(LOW)
    grads = jnp.concatenate([dq, dk, dv], axis=1)
    dx_ref[0] = dot_nt(grads, w_ref[...]).astype(LOW)
    part = dot_tn(n_ref[0], grads)

    @pl.when(i == 0)
    def _():
        sum_ref[...] = part

    @pl.when(i > 0)
    def _():
        sum_ref[...] += part

    @pl.when(i == HEADS - 1)
    def _():
        dw_ref[...] = sum_ref[...].astype(LOW)


def qkv_back(chips, dq, own, got, cos, sin, normed, w):
    count = dq.shape[1]
    block = pl.BlockSpec((1, count, HEAD_DIM), lambda i, t: (t[i], 0, 0))
    pair = pl.BlockSpec((2, 1, count, HEAD_DIM), lambda i, t: (0, t[i], 0, 0))
    weight = pl.BlockSpec((D, 3 * HEAD_DIM), lambda i, t: (0, 0))
    return pl.pallas_call(
        qkv_back_kernel,
        grid_spec=pltpu.PrefetchScalarGridSpec(
            num_scalar_prefetch=1,
            grid=(HEADS,),
            in_specs=[
                block, pair, pair, block, block,
                pl.BlockSpec((1, count, D), lambda i, t: (t[i], 0, 0)),
                weight,
            ],
            out_specs=[pl.BlockSpec((1, count, D), lambda i, t: (i, 0, 0)), weight],
            scratch_shapes=[pltpu.VMEM((D, 3 * HEAD_DIM), WIDE)],
        ),
        out_shape=[
            jax.ShapeDtypeStruct((HEADS, count, D), LOW),
            jax.ShapeDtypeStruct((D, 3 * HEAD_DIM), LOW),
        ],
        cost_estimate=pl.CostEstimate(
            flops=4 * HEADS * count * D * 3 * HEAD_DIM,
            bytes_accessed=6 * HEADS * count * D,
            transcendentals=0,
        ),
        name="qkv_back",
    )(chips, dq, own, got, cos, sin, normed, w)


def local(
    far,
    tokens,
    segment_ids,
    second_doc,
    memory_index,
    cache_keys,
    cache_values,
    first_gain,
    query_weight,
    key_weight,
    value_weight,
    out_weight,
    second_gain,
    gate_weight,
    up_weight,
    down_weight,
    cotangent,
):
    x = tokens[0]
    upstream = cotangent[0]
    count = x.shape[0]
    blocks = count // QUERY_BLOCK
    rows = query_weight.shape[0]
    share = down_weight.shape[0]
    units = far * HEADS * share
    chip, core, pair = lax.axis_index("h"), lax.axis_index("c"), lax.axis_index("dl")
    mine = jnp.where(chip % 2 == 0, chip // 2, HEADS - 1 - chip // 2)
    slots = jnp.arange(HEADS, dtype=jnp.int32)
    chips = at_place(mine - slots)

    def by_head(w):
        return w.reshape(rows, HEADS, HEAD_DIM).transpose(1, 0, 2)

    picked = memory_index[0].transpose(1, 0, 2)
    seg_rows = jnp.broadcast_to(
        segment_ids[0].astype(LOW).reshape(1, blocks, QUERY_BLOCK), (HEADS, blocks, QUERY_BLOCK)
    )
    gains = jnp.concatenate([first_gain, second_gain])
    gain_rows = jnp.broadcast_to(
        jnp.pad(gains, (0, HEAD_DIM - 2 * rows)).reshape(1, 1, HEAD_DIM), (HEADS, 1, HEAD_DIM)
    )
    pack = jnp.concatenate(
        [
            by_head(query_weight),
            by_head(key_weight),
            by_head(value_weight),
            seg_rows,
            (picked // MEM_ROWS).astype(LOW),
            (picked % MEM_ROWS).astype(LOW),
            gain_rows,
        ],
        axis=1,
    )
    height = pack.shape[1]
    pack = jnp.pad(pack, ((0, 0), (0, -height % 16), (0, 0)))

    block = jnp.concatenate([x, out_weight], axis=0)
    split = count // 2
    got = exchange(pack)
    up_c = swap(upstream, "c")
    up_y = swap(upstream, "dl")
    up_yc = swap(up_y, "c")
    got, up_c, up_y, up_yc, x_forth, x_back, parity = lax.optimization_barrier(
        (got, up_c, up_y, up_yc, turn(block, 1), turn(block, -1), core)
    )
    forth, back = [block, x_forth, turn(x_forth, 1)], [block, x_back, turn(x_back, -1)]
    got_c = swap(got, "c")
    got_y = swap(got, "dl")
    got_yc = swap(got_y, "c")
    near = pick(core, jnp.stack([got, got_c]), jnp.stack([got_c, got]))
    away = pick(core, jnp.stack([got_y, got_yc]), jnp.stack([got_yc, got_y]))
    every = pick(pair, jnp.stack([near, away]), jnp.stack([away, near]))
    every = every.transpose(2, 0, 1, 3, 4)
    if far > 1:
        every = lax.all_gather(every, "dh", axis=0)
    else:
        every = every[None]
    every = every.transpose(0, 2, 1, 3, 4, 5)
    w_qkv = jnp.concatenate(
        [every[..., i * rows : (i + 1) * rows, :].reshape(D, HEAD_DIM) for i in range(3)], axis=1
    )
    gain_all = every[..., 3 * rows + 3 * blocks, : 2 * rows].reshape(-1, 2, rows)
    gain_one = gain_all[:, 0].reshape(1, D)
    gain_two = gain_all[:, 1].reshape(1, D)

    def seg_of(blocks_of):
        return (
            blocks_of[:, 3 * rows : 3 * rows + blocks]
            .astype(WIDE)
            .astype(jnp.int32)
            .reshape(HEADS, count)
        )

    seg_own = seg_of(got)
    seg_oth = seg_of(got_c)
    idx = (
        got[:, 3 * rows + blocks : 3 * rows + 2 * blocks].astype(WIDE) * MEM_ROWS
        + got[:, 3 * rows + 2 * blocks : 3 * rows + 3 * blocks].astype(WIDE)
    ).astype(jnp.int32)
    idx = idx.reshape(HEADS, count, 1)

    block_docs = seg_own[:, ::QUERY_BLOCK]
    docs = second_doc.shape[1]
    doc_ids = jnp.arange(docs, dtype=jnp.int32)
    mates = jnp.sum(
        jnp.where(block_docs[:, :, None] == doc_ids, second_doc[0][None, None, :], 0), axis=-1
    )
    seg_all = jnp.concatenate([seg_own, seg_oth], axis=0)
    before = jnp.sum(
        (seg_all.reshape(1, -1) < block_docs[:, :1]).astype(jnp.int32), axis=1
    )
    tab = jnp.concatenate(
        [
            block_docs.reshape(-1),
            mates.reshape(-1),
            before // (2 * count),
            jnp.stack([core, chip]),
        ]
    ).astype(jnp.int32)

    half = HEAD_DIM // 2
    freqs = 10000.0 ** (-jnp.arange(half, dtype=WIDE) * 2.0 / (2 * half))
    positions = ((2 * slots + parity) * count)[:, None] + jnp.arange(count, dtype=jnp.int32)[None]
    turned = positions.astype(WIDE)[:, :, None] * freqs
    cosine, sine = jnp.cos(turned), jnp.sin(turned)
    cosine = jnp.concatenate([cosine, cosine], axis=-1)
    sine = jnp.concatenate([-sine, sine], axis=-1)

    seg_thin = seg_own.reshape(HEADS, count, 1)
    early = (w_qkv, gain_one, cosine, sine, tab, seg_thin, idx)
    early, gate_late, up_late, forth[2], back[2] = lax.optimization_barrier(
        (early, gate_weight, up_weight, forth[2], back[2])
    )
    w_qkv, gain_one, cosine, sine, tab, seg_thin, idx = early
    forth.append(turn(forth[2], 1))
    back.append(turn(back[2], -1))
    at_near, at_far = [0, 1, 7, 2, 6], [3, 5, 4]

    def chips_at(order):
        return at_place(mine - jnp.asarray(order, jnp.int32)).astype(jnp.int32)

    near_slots = [forth[0], forth[1], back[1], forth[2], back[2]]
    held = qkv_blocks(
        chips_at(at_near), [((v, count),) for v in near_slots], gain_one, w_qkv, cosine, sine, ()
    )
    half = units + -units % HEAD_DIM
    wide = 2 * half

    def by_owner(w):
        w = w.reshape(rows, far, 2, HEADS, 2, share).transpose(2, 4, 0, 1, 3, 5)
        return jnp.pad(w.reshape(2, 2, rows, units), ((0, 0),) * 3 + ((0, half - units),))

    gu = jnp.concatenate([by_owner(gate_late), by_owner(up_late)], axis=-1)
    kept = pick(core, gu[:, 0], gu[:, 1])
    came = swap(pick(core, gu[:, 1], gu[:, 0]), "c")
    gu = pick(core, jnp.stack([kept, came], 1), jnp.stack([came, kept], 1))
    kept = pick(pair, gu[0], gu[1])
    came = swap(pick(pair, gu[1], gu[0]), "dl")
    gu = pick(pair, jnp.stack([kept, came]), jnp.stack([came, kept])).reshape(4 * rows, wide)
    if far == 1:
        deep = 2 * rows
        lower = jnp.concatenate(fold(down_weight, deep), axis=1)
    else:
        deep = share
        lower = jnp.pad(down_weight, ((0, 0), (0, wide - D)))
    bundle = jnp.concatenate([gu, lower], axis=0)
    height = 4 * rows + share
    if far > 1:
        bundle = lax.all_gather(bundle, "dh", axis=0, tiled=True)
    upper = bundle.shape[0] // 2
    *held, bundle, forth[3], back[3] = lax.optimization_barrier(
        (*held, bundle, forth[3], back[3])
    )
    far_first, far_last = turn(forth[3][:split], 1), turn(back[3][split:], -1)
    bundle, *_ = lax.optimization_barrier((bundle, far_first, far_last))
    w_forth, w_back = [bundle, turn(bundle, 1)], [bundle, turn(bundle, -1)]

    far_slots = [
        ((forth[3], count),),
        ((back[3], count),),
        ((far_first, split), (far_last, count - split)),
    ]
    queries, own, normed_one = qkv_blocks(
        chips_at(at_far), far_slots, gain_one, w_qkv, cosine, sine, tuple(held)
    )
    other = swap(own, "c")
    seg_own_row = seg_own.reshape(HEADS, 1, count)
    seg_oth_row = seg_oth.reshape(HEADS, 1, count)
    cached = [cache[0].reshape(-1, D) for cache in (cache_keys, cache_values)]
    queries, w_forth[1], w_back[1] = lax.optimization_barrier((queries, w_forth[1], w_back[1]))
    attention, attention_low, lse, memory = attend(
        tab, queries, own, other, seg_thin, seg_own_row, seg_oth_row, idx, *cached
    )
    w_forth.append(turn(w_forth[1], 1))
    w_back.append(turn(w_back[1], -1))
    out_rows = [*forth, far_last, *back[:0:-1]]
    *out_rows, attention_low, w_forth[2], w_back[2] = lax.optimization_barrier(
        (*out_rows, attention_low, w_forth[2], w_back[2])
    )

    heads = exchange(attention_low)
    w_forth.append(turn(w_forth[2], 1))
    w_back.append(turn(w_back[2], -1))
    outs = jnp.stack([v[-rows:] for v in out_rows])
    outs_c = swap(outs, "c")
    outs_y = swap(outs, "dl")
    outs_yc = swap(outs_y, "c")
    heads, w_forth[3], w_back[3] = lax.optimization_barrier((heads, w_forth[3], w_back[3]))
    w_first, w_last = turn(w_forth[3][:upper], 1), turn(w_back[3][upper:], -1)
    slot_of = lax.rem(mine - jnp.asarray(PLACE, jnp.int32) + HEADS, HEADS).astype(jnp.int32)
    if far == 1:
        sources = [outs, outs_c, outs_y, outs_yc]
    else:
        near = pick(core, jnp.stack([outs, outs_c], 1), jnp.stack([outs_c, outs], 1))
        away = pick(core, jnp.stack([outs_y, outs_yc], 1), jnp.stack([outs_yc, outs_y], 1))
        sources = pick(pair, jnp.stack([near, away]), jnp.stack([away, near]))
        sources = lax.all_gather(jnp.take(sources, slot_of, axis=1), "dh", axis=0)
        sources = [sources.reshape(D, D)]
    where = jnp.concatenate([chips, jnp.stack([pair, core])]).astype(jnp.int32)
    attended, mid, normed_two, out_w = out_block(where, heads, sources, x, gain_two)
    normed_two, w_first, w_last = lax.optimization_barrier((normed_two, w_first, w_last))
    w_slots = w_forth + [w_first, w_last] + w_back[:0:-1]

    if far == 1:
        gate_w, up_w, down_w = weights(where, w_slots, units)
    else:
        middle = jnp.concatenate(w_slots[HEADS // 2 : HEADS // 2 + 2], axis=0)
        every = jnp.stack(w_slots[: HEADS // 2] + [middle] + w_slots[HEADS // 2 + 2 :])
        every = jnp.take(every, slot_of, axis=0).reshape(HEADS, far, height, wide)
        gu = every[:, :, : 4 * rows].reshape(HEADS, far, 2, 2 * rows, wide)
        gu = gu.transpose(1, 2, 0, 3, 4).reshape(D, wide)
        gate_w, up_w = gu[:, :units], gu[:, half : half + units]
        down_w = every[:, :, 4 * rows :, :D].transpose(1, 0, 2, 3).reshape(units, D)

    n_c = swap(normed_two, "c")
    n_y = swap(normed_two, "dl")
    hid_l, gg_l, ug_l, dn_l, out_l = ffn(normed_two, n_c, upstream, up_c, gate_w, up_w, down_w)
    n_y, dn_l = lax.optimization_barrier((n_y, dn_l))
    n_yc = swap(n_y, "c")
    hid_r, gg_r, ug_r, dn_r, out_r = ffn(n_y, n_yc, up_y, up_yc, gate_w, up_w, down_w)

    def to_away(away):
        return (away[0].astype(WIDE) + swap(away[1], "c").astype(WIDE)).astype(LOW)

    there = to_away(dn_r)
    there, hid_l, gg_l, ug_l, hid_r, gg_r, ug_r = lax.optimization_barrier(
        (there, hid_l, gg_l, ug_l, hid_r, gg_r, ug_r)
    )
    n_all, u_all = [normed_two, n_c, n_y, n_yc], [upstream, up_c, up_y, up_yc]
    near, away = (hid_l, gg_l, ug_l), (hid_r, gg_r, ug_r)
    if far == 1:
        parts = weight_grads(slot_of, n_all, u_all, near, away, height, wide)
    else:

        def over_tokens(left, right):
            return jnp.einsum(
                "gtd,gtf->df", left, right, preferred_element_type=WIDE
            ).astype(LOW)

        def by_rows(w):
            w = jnp.pad(w, ((0, 0), (0, half - units)))
            return w.reshape(far, 2, HEADS, 2 * rows, half).transpose(2, 0, 1, 3, 4)

        n_all, u_all = jnp.stack(n_all), jnp.stack(u_all)
        hid, gg, ug = (jnp.concatenate(pieces, axis=0) for pieces in zip(near, away))
        gu = jnp.concatenate(
            [by_rows(over_tokens(n_all, gg)), by_rows(over_tokens(n_all, ug))], axis=-1
        ).reshape(HEADS, far, 4 * rows, wide)
        down = over_tokens(hid, u_all).reshape(far, HEADS, share, D).transpose(1, 0, 2, 3)
        down = jnp.pad(down, ((0, 0), (0, 0), (0, 0), (0, wide - D)))
        parts = jnp.concatenate([gu, down], axis=2)
        parts = jnp.take(parts.reshape(HEADS, far * height, wide), chips, axis=0)

    out_l, out_r, _ = lax.optimization_barrier((out_l, out_r, parts))
    output = mid
    for part in (out_l[0], swap(out_l[1], "c"), swap(to_away(out_r), "dl")):
        output = output + part.astype(WIDE)
    output = output.astype(LOW)

    sums = [dn_l[0], swap(dn_l[1], "c"), swap(there, "dl")]
    sums[2], parts = lax.optimization_barrier((sums[2], parts))
    mid_grad, branch, att_grad = mid_block(mid, *sums, upstream, gain_two, out_w)
    ups = exchange(att_grad)

    def plus(block, arrived, start):
        size = arrived.shape[0]
        total = block[start : start + size].astype(WIDE) + arrived.astype(WIDE)
        pieces = [block[:start], total, block[start + size :]]
        pieces = [piece.astype(LOW) for piece in pieces if piece.shape[0]]
        return jnp.concatenate(pieces, axis=0)

    def ring_first(blocks, split):
        middle = blocks[HEADS // 2]
        return (
            plus(blocks[HEADS // 2 + 1], turn(middle[:split].astype(LOW), 1), 0),
            plus(blocks[HEADS // 2 - 1], turn(middle[split:].astype(LOW), -1), split),
        )

    def ring_next(blocks, forth, back, step):
        return (
            plus(blocks[HEADS // 2 + step], turn(forth, 1), 0),
            plus(blocks[HEADS // 2 - step], turn(back, -1), 0),
        )

    def ring_last(blocks, forth, back):
        return blocks[0].astype(WIDE) + forth.astype(WIDE) + back.astype(WIDE)

    def over_owner(w, width):
        w = w.reshape(far, 2, HEADS, 2, rows, width)
        kept = pick(core, w[:, :, :, 0], w[:, :, :, 1])
        came = swap(pick(core, w[:, :, :, 1], w[:, :, :, 0]), "c")
        w = kept.astype(WIDE) + came.astype(WIDE)
        kept = pick(pair, w[:, 0], w[:, 1])
        came = swap(pick(pair, w[:, 1], w[:, 0]).astype(LOW), "dl")
        w = (kept + came.astype(WIDE)).astype(LOW)
        if far > 1:
            w = lax.psum_scatter(w, "dh", scatter_dimension=0, tiled=True)
        return w[0]

    out_part = over_owner(
        jnp.einsum("td,te->de", attended, branch, preferred_element_type=WIDE).astype(LOW), D
    )
    strip = wide - D
    upper = 4 * rows if far == 1 else parts.shape[1] // 2
    blocks = [parts[slot].astype(WIDE) for slot in range(HEADS)]
    if far == 1:
        strips = out_strips(where, out_part, strip)
        below = share - strips.shape[1]
        for slot in range(HEADS):
            if slot != HEADS // 2:
                blocks[slot] = blocks[slot] + jnp.pad(
                    strips[slot].astype(WIDE), ((4 * rows, below), (D, 0))
                )
        out_far = turn(strips[HEADS // 2], HEADS // 2)
    else:
        out_far = exchange(out_part)
    forth, back = ring_first(blocks, upper)
    ups, forth, back = lax.optimization_barrier((ups, forth, back))
    forth, back = ring_next(blocks, forth, back, 2)

    dq, d_own, d_oth = attend_back(
        tab, queries, ups, attention, lse, own, other, memory, seg_thin, seg_own_row, seg_oth_row
    )
    d_got = swap(d_oth, "c")
    dq, forth, back = lax.optimization_barrier((dq, forth, back))
    dx, dw = qkv_back(
        chips.astype(jnp.int32), dq, d_own, d_got, cosine, sine, normed_one, w_qkv
    )
    arrived_forth, arrived_back = turn(forth, 1), turn(back, -1)
    dx, out_far, arrived_forth, arrived_back = lax.optimization_barrier(
        (dx, out_far, arrived_forth, arrived_back)
    )
    dx_forth, dx_back = ring_first(dx, split)
    dx_forth, dx_back, arrived_forth, arrived_back = lax.optimization_barrier(
        (dx_forth, dx_back, arrived_forth, arrived_back)
    )
    forth = plus(blocks[HEADS - 1], arrived_forth, 0)
    back = plus(blocks[1], arrived_back, 0)

    dw = over_owner(dw, 3 * HEAD_DIM)
    dx_forth, dx_back = ring_next(dx, dx_forth, dx_back, 2)
    dw, dx_forth, dx_back = lax.optimization_barrier((dw, dx_forth, dx_back))
    qkv_grads = exchange(dw).astype(WIDE)
    dx_forth, dx_back = ring_next(dx, dx_forth, dx_back, 3)
    normed_one_grad = ring_last(dx, turn(dx_forth, 1), turn(dx_back, -1))

    summed = ring_last(blocks, turn(forth, 1), turn(back, -1)).astype(LOW)
    if far > 1:
        summed = lax.psum_scatter(summed, "dh", scatter_dimension=0, tiled=True)
    down_w_grad = summed[4 * rows : 4 * rows + share, :D].astype(WIDE)
    if far == 1:
        out_w_grad = summed[4 * rows : 4 * rows + strips.shape[1], D:].astype(WIDE)
        out_w_grad = out_w_grad + out_far.astype(WIDE)
        out_w_grad = out_w_grad.reshape(D // strip, rows, strip).transpose(1, 0, 2).reshape(rows, D)
    else:
        out_w_grad = jnp.sum(out_far.astype(WIDE), axis=0)
    gu = summed[: 4 * rows].reshape(2, 2, rows, wide)
    kept = pick(core, gu[:, 0], gu[:, 1])
    came = swap(pick(core, gu[:, 1], gu[:, 0]), "c")
    gu = pick(core, jnp.stack([kept, came], 1), jnp.stack([came, kept], 1))
    kept = pick(pair, gu[0], gu[1])
    came = swap(pick(pair, gu[1], gu[0]), "dl")
    gu = pick(pair, jnp.stack([kept, came]), jnp.stack([came, kept]))
    gu = jnp.stack([gu[..., :units], gu[..., half : half + units]])
    gu = (
        gu.reshape(2, 2, 2, rows, far, HEADS, share)
        .transpose(0, 3, 4, 1, 5, 2, 6)
        .reshape(2, rows, FF)
        .astype(WIDE)
    )
    gate_w_grad, up_w_grad = gu[0], gu[1]

    wide_x = x.astype(WIDE)
    r = lax.rsqrt(jnp.mean(wide_x * wide_x, axis=-1, keepdims=True) + EPSILON)
    scaled = normed_one_grad * gain_one.astype(WIDE)
    inner = jnp.mean(scaled * wide_x, axis=-1, keepdims=True)
    input_grad = mid_grad + r * scaled - wide_x * (r * r * r * inner)

    q_w_grad, k_w_grad, v_w_grad = (
        qkv_grads[:, :, i * HEAD_DIM : (i + 1) * HEAD_DIM].transpose(1, 0, 2).reshape(rows, D)
        for i in range(3)
    )

    def gain_grad(gain, pairs):
        total = 0.0
        for grad, weight in pairs:
            total = total + jnp.sum(grad * weight.astype(WIDE), axis=1)
        return total / gain.astype(WIDE)

    first_gain_grad = gain_grad(
        first_gain,
        ((q_w_grad, query_weight), (k_w_grad, key_weight), (v_w_grad, value_weight)),
    )
    second_gain_grad = gain_grad(
        second_gain, ((gate_w_grad, gate_weight), (up_w_grad, up_weight))
    )
    return (
        output[None],
        input_grad[None],
        first_gain_grad,
        q_w_grad,
        k_w_grad,
        v_w_grad,
        out_w_grad,
        second_gain_grad,
        gate_w_grad,
        up_w_grad,
        down_w_grad,
    )


def solution(mesh):
    far = mesh.shape["dp"] // 2
    cores = mesh.shape["seq"] // HEADS
    fine = Mesh(mesh.devices.reshape(far, 2, HEADS, cores), ("dh", "dl", "h", "c"))
    dp, seq, every = ("dh", "dl"), ("h", "c"), ("dh", "dl", "h", "c")
    rows = P(every, None)
    return jax.shard_map(
        functools.partial(local, far),
        mesh=fine,
        in_specs=(
            P(dp, seq, None),
            P(dp, seq),
            P(dp, None),
            P(dp, seq, None, None),
            P(dp, None, None, None),
            P(dp, None, None, None),
            P(every),
            rows,
            rows,
            rows,
            rows,
            P(every),
            rows,
            rows,
            rows,
            P(dp, seq, None),
        ),
        out_specs=(
            P(dp, seq, None),
            P(dp, seq, None),
            P(every),
            rows,
            rows,
            rows,
            rows,
            P(every),
            rows,
            rows,
            rows,
        ),
        check_vma=False,
    )
```

```python
import functools
import math

import jax
import jax.numpy as jnp
from jax import lax
from jax.experimental import pallas as pl
from jax.experimental.pallas import tpu as pltpu
from jax.sharding import Mesh
from jax.sharding import PartitionSpec as P

D = 1024
FF = 2816
HEADS = 8
HEAD_DIM = 128
QUERY_BLOCK = 128
MEM_ROWS = 256
EPSILON = 1e-05
NEGATIVE = -1e30
SCALE = 1.0 / math.sqrt(HEAD_DIM)
LOG2 = SCALE * math.log2(math.e)
LOW = jnp.bfloat16
WIDE = jnp.float32

RING = [2 * i for i in range(HEADS // 2)] + [2 * i + 1 for i in reversed(range(HEADS // 2))]
PLACE = [RING.index(i) for i in range(HEADS)]


def dot_nn(a, b):
    return lax.dot_general(a, b, (((1,), (0,)), ((), ())), preferred_element_type=WIDE)


def dot_nt(a, b):
    return lax.dot_general(a, b, (((1,), (1,)), ((), ())), preferred_element_type=WIDE)


def dot_tn(a, b):
    return lax.dot_general(a, b, (((0,), (0,)), ((), ())), preferred_element_type=WIDE)


def swap(block, axis):
    return lax.ppermute(block, axis, [(0, 1), (1, 0)])


def turn(block, distance):
    route = [(RING[i], RING[(i + distance) % HEADS]) for i in range(HEADS)]
    return lax.ppermute(block, "h", route)


def at_place(place):
    place = lax.rem(place + 2 * HEADS, HEADS)
    return jnp.where(place < HEADS // 2, 2 * place, 2 * (HEADS - 1 - place) + 1)


def exchange(blocks):
    return lax.all_to_all(blocks, "h", 0, 0)


def pick(flag, first, second):
    return jnp.where(flag == 0, first, second)


def smem():
    return pl.BlockSpec(memory_space=pltpu.SMEM)


def vmem():
    return pl.BlockSpec(memory_space=pltpu.VMEM)


def qkv_kernel(parts, tab, *refs):
    xs, (gain_ref, w_ref, cos_ref, sin_ref) = refs[: sum(parts)], refs[sum(parts) : sum(parts) + 4]
    q_ref, kv_ref, n_ref, x_ref = refs[-4:]
    i = pl.program_id(0)
    first = 0
    for step, number in enumerate(parts):

        @pl.when(i == step)
        def _(blocks=xs[first : first + number]):
            row = 0
            for block in blocks:
                size = block.shape[0]
                x_ref[row : row + size, :] = block[...]
                row += size

        first += number
    x = x_ref[...].astype(WIDE)
    r = lax.rsqrt(jnp.mean(x * x, axis=-1, keepdims=True) + EPSILON)
    normed = (x * r * gain_ref[...].astype(WIDE)).astype(LOW)
    n_ref[0] = normed
    out = dot_nn(normed, w_ref[...])
    c, s = cos_ref[0], sin_ref[0]

    def rot(v):
        return v * c + pltpu.roll(v, HEAD_DIM // 2, 1) * s

    q_ref[0] = rot(out[:, :HEAD_DIM]).astype(LOW)
    kv_ref[0, 0] = rot(out[:, HEAD_DIM : 2 * HEAD_DIM]).astype(LOW)
    kv_ref[1, 0] = out[:, 2 * HEAD_DIM :].astype(LOW)


def qkv_blocks(chips, xs, gain, w, cos, sin, held):
    count = cos.shape[1]
    flat = [piece for block in xs for piece, _ in block]
    read = [size for block in xs for _, size in block]

    def whole(shape):
        return pl.BlockSpec(shape, lambda i, t: (0, 0))

    def block(*shape):
        return pl.BlockSpec((1, *shape), lambda i, t: (t[i], 0, 0))

    spec = pltpu.PrefetchScalarGridSpec(
        num_scalar_prefetch=1,
        grid=(len(xs),),
        in_specs=[whole((size, D)) for size in read]
        + [whole((1, D)), whole((D, 3 * HEAD_DIM)), block(count, HEAD_DIM), block(count, HEAD_DIM)]
        + [pl.BlockSpec(memory_space=pl.ANY)] * len(held),
        out_specs=[
            block(count, HEAD_DIM),
            pl.BlockSpec((2, 1, count, HEAD_DIM), lambda i, t: (0, t[i], 0, 0)),
            block(count, D),
        ],
        scratch_shapes=[pltpu.VMEM((count, D), LOW)],
    )
    return pl.pallas_call(
        functools.partial(qkv_kernel, [len(block) for block in xs]),
        grid_spec=spec,
        out_shape=[
            jax.ShapeDtypeStruct((HEADS, count, HEAD_DIM), LOW),
            jax.ShapeDtypeStruct((2, HEADS, count, HEAD_DIM), LOW),
            jax.ShapeDtypeStruct((HEADS, count, D), LOW),
        ],
        input_output_aliases={len(flat) + 5 + i: i for i in range(len(held))},
        cost_estimate=pl.CostEstimate(
            flops=len(xs) * count * D, bytes_accessed=len(xs) * count, transcendentals=0
        ),
        name=f"qkv{len(xs)}",
    )(chips, *flat, gain, w, cos, sin, *held)


def causal(count):
    rows = lax.broadcasted_iota(jnp.int32, (count, count), 0)
    return lax.broadcasted_iota(jnp.int32, (count, count), 1) <= rows


def attend_kernel(
    tab, q_ref, own_ref, oth_ref, segq_ref, sego_ref, segt_ref, idx_ref, ck_ref, cv_ref,
    o_ref, low_ref, lse_ref, mem_ref,
):
    i = pl.program_id(0)
    parity = tab[40]
    count = q_ref.shape[1]
    q = q_ref[0]
    segq = segq_ref[0]

    s1 = dot_nt(q, own_ref[0, i]) * LOG2
    s2 = dot_nt(q, oth_ref[0, i]) * LOG2
    s1 = jnp.where((sego_ref[i] == segq) & causal(count), s1, NEGATIVE)
    s2 = jnp.where(segt_ref[i] == segq + 64 * (1 - parity), s2, NEGATIVE)
    memory = []
    for b in range(count // QUERY_BLOCK):
        rows = slice(b * QUERY_BLOCK, (b + 1) * QUERY_BLOCK)
        doc = tab[2 * i + b]
        mate = tab[16 + 2 * i + b]
        idx = idx_ref[0, rows, :]
        lane = lax.broadcasted_iota(jnp.int32, (QUERY_BLOCK, MEM_ROWS), 1)
        first = jnp.where(idx == lane, 1.0, 0.0).astype(LOW)
        second = jnp.where(idx == lane + MEM_ROWS, 1.0, 0.0).astype(LOW)
        here = pl.ds(pl.multiple_of(doc * MEM_ROWS, MEM_ROWS), MEM_ROWS)
        there = pl.ds(pl.multiple_of(mate * MEM_ROWS, MEM_ROWS), MEM_ROWS)
        mk = (dot_nn(first, ck_ref[here, :]) + dot_nn(second, ck_ref[there, :])).astype(LOW)
        mv = (dot_nn(first, cv_ref[here, :]) + dot_nn(second, cv_ref[there, :])).astype(LOW)
        mem_ref[0, 0, rows, :] = mk
        mem_ref[1, 0, rows, :] = mv
        s = jnp.where(segq[rows] == doc, dot_nt(q[rows], mk) * LOG2, NEGATIVE)
        memory.append((s, mv))
    sm = jnp.concatenate([s for s, _ in memory], axis=0)
    top = jnp.maximum(
        jnp.max(jnp.maximum(s1, s2), axis=-1, keepdims=True), jnp.max(sm, axis=-1, keepdims=True)
    )
    p1 = jnp.exp2(s1 - top)
    p2 = jnp.exp2(s2 - top)
    pm = jnp.exp2(sm - top)
    total = jnp.sum(p1 + p2, axis=-1, keepdims=True) + jnp.sum(pm, axis=-1, keepdims=True)
    pm = pm.astype(LOW)
    acc = jnp.concatenate(
        [
            dot_nn(pm[b * QUERY_BLOCK : (b + 1) * QUERY_BLOCK], mv)
            for b, (_, mv) in enumerate(memory)
        ],
        axis=0,
    )
    acc = acc + dot_nn(p1.astype(LOW), own_ref[1, i]) + dot_nn(p2.astype(LOW), oth_ref[1, i])

    def body(j, state):
        top, total, acc = state
        s1 = dot_nt(q, own_ref[0, j]) * LOG2
        s2 = dot_nt(q, oth_ref[0, j]) * LOG2
        s1 = jnp.where(sego_ref[j] == segq, s1, NEGATIVE)
        s2 = jnp.where(segt_ref[j] == segq, s2, NEGATIVE)
        fresh = jnp.maximum(top, jnp.max(jnp.maximum(s1, s2), axis=-1, keepdims=True))
        p1 = jnp.exp2(s1 - fresh)
        p2 = jnp.exp2(s2 - fresh)
        decay = jnp.exp2(top - fresh)
        total = total * decay + jnp.sum(p1 + p2, axis=-1, keepdims=True)
        acc = (
            acc * decay
            + dot_nn(p1.astype(LOW), own_ref[1, j])
            + dot_nn(p2.astype(LOW), oth_ref[1, j])
        )
        return fresh, total, acc

    top, total, acc = lax.fori_loop(tab[32 + i], i, body, (top, total, acc))
    out = acc / total
    o_ref[0] = out
    low_ref[0] = out.astype(LOW)
    lse_ref[0] = top + jnp.log2(total)


def attend(tab, q, own, oth, segq, sego, segt, idx, ck, cv):
    count = q.shape[1]
    block = pl.BlockSpec((1, count, HEAD_DIM), lambda i, t: (i, 0, 0))
    thin = pl.BlockSpec((1, count, 1), lambda i, t: (i, 0, 0))
    whole = pl.BlockSpec((2, HEADS, count, HEAD_DIM), lambda i, t: (0, 0, 0, 0))
    segs = pl.BlockSpec((HEADS, 1, count), lambda i, t: (0, 0, 0))
    cache = pl.BlockSpec((ck.shape[0], HEAD_DIM), lambda i, t: (0, t[41]))
    mem = pl.BlockSpec((2, 1, count, HEAD_DIM), lambda i, t: (0, i, 0, 0))
    return pl.pallas_call(
        attend_kernel,
        grid_spec=pltpu.PrefetchScalarGridSpec(
            num_scalar_prefetch=1,
            grid=(HEADS,),
            in_specs=[block, whole, whole, thin, segs, segs, thin, cache, cache],
            out_specs=[block, block, thin, mem],
        ),
        out_shape=[
            jax.ShapeDtypeStruct((HEADS, count, HEAD_DIM), WIDE),
            jax.ShapeDtypeStruct((HEADS, count, HEAD_DIM), LOW),
            jax.ShapeDtypeStruct((HEADS, count, 1), WIDE),
            jax.ShapeDtypeStruct((2, HEADS, count, HEAD_DIM), LOW),
        ],
        cost_estimate=pl.CostEstimate(
            flops=25 * 10**9, bytes_accessed=6 * 2**20, transcendentals=3 * 10**6
        ),
        name="attend",
    )(tab, q, own, oth, segq, sego, segt, idx, ck, cv)


def attend_back_kernel(
    tab, q_ref, up_ref, o_ref, lse_ref, own_ref, oth_ref, mem_ref, segq_ref, sego_ref, segt_ref,
    dq_ref, down_ref, doth_ref, sum_ref,
):
    i = pl.program_id(0)

    @pl.when(i == 0)
    def _():
        sum_ref[...] = jnp.zeros_like(sum_ref)

    parity = tab[40]
    count = q_ref.shape[1]
    q = q_ref[0]
    up = up_ref[0]
    lse = lse_ref[0]
    segq = segq_ref[0]
    delta = jnp.sum(up.astype(WIDE) * o_ref[0], axis=-1, keepdims=True)
    partial = []
    for b in range(count // QUERY_BLOCK):
        rows = slice(b * QUERY_BLOCK, (b + 1) * QUERY_BLOCK)
        mk = mem_ref[0, 0, rows, :]
        mv = mem_ref[1, 0, rows, :]
        ok = segq[rows] == tab[2 * i + b]
        p = jnp.exp2(jnp.where(ok, dot_nt(q[rows], mk) * LOG2 - lse[rows], NEGATIVE))
        ds = (p * (dot_nt(up[rows], mv) - delta[rows])).astype(LOW)
        partial.append(dot_nn(ds, mk))

    def tile(side, ref, j, ok, dq):
        k = ref[0, j]
        v = ref[1, j]
        p = jnp.exp2(jnp.where(ok, dot_nt(q, k) * LOG2 - lse, NEGATIVE))
        ds = (p * (dot_nt(up, v) - delta)).astype(LOW)
        sum_ref[side, 0, j] += dot_tn(ds, q)
        sum_ref[side, 1, j] += dot_tn(p.astype(LOW), up)
        return dq + dot_nn(ds, k)

    dq = jnp.concatenate(partial, axis=0)
    dq = tile(0, own_ref, i, (sego_ref[i] == segq) & causal(count), dq)
    dq = tile(1, oth_ref, i, segt_ref[i] == segq + 64 * (1 - parity), dq)

    def body(j, dq):
        dq = tile(0, own_ref, j, sego_ref[j] == segq, dq)
        return tile(1, oth_ref, j, segt_ref[j] == segq, dq)

    dq_ref[0] = lax.fori_loop(tab[32 + i], i, body, dq)

    @pl.when(i == HEADS - 1)
    def _():
        down_ref[...] = sum_ref[0]
        doth_ref[...] = sum_ref[1].astype(LOW)


def attend_back(tab, q, up, o, lse, own, oth, mem, segq, sego, segt):
    count = q.shape[1]
    block = pl.BlockSpec((1, count, HEAD_DIM), lambda i, t: (i, 0, 0))
    thin = pl.BlockSpec((1, count, 1), lambda i, t: (i, 0, 0))
    whole = pl.BlockSpec((2, HEADS, count, HEAD_DIM), lambda i, t: (0, 0, 0, 0))
    segs = pl.BlockSpec((HEADS, 1, count), lambda i, t: (0, 0, 0))
    memory = pl.BlockSpec((2, 1, count, HEAD_DIM), lambda i, t: (0, i, 0, 0))
    return pl.pallas_call(
        attend_back_kernel,
        grid_spec=pltpu.PrefetchScalarGridSpec(
            num_scalar_prefetch=1,
            grid=(HEADS,),
            in_specs=[block, block, block, thin, whole, whole, memory, thin, segs, segs],
            out_specs=[block, whole, whole],
            scratch_shapes=[pltpu.VMEM((2, 2, HEADS, count, HEAD_DIM), WIDE)],
        ),
        out_shape=[
            jax.ShapeDtypeStruct((HEADS, count, HEAD_DIM), WIDE),
            jax.ShapeDtypeStruct((2, HEADS, count, HEAD_DIM), WIDE),
            jax.ShapeDtypeStruct((2, HEADS, count, HEAD_DIM), LOW),
        ],
        cost_estimate=pl.CostEstimate(
            flops=30 * 10**9, bytes_accessed=10 * 2**20, transcendentals=3 * 10**6
        ),
        name="attend_back",
    )(tab, q, up, o, lse, own, oth, mem, segq, sego, segt)


def place_rows(tab, sources, w_ref):
    rows = sources[0].shape[1]
    for k, source in enumerate(sources):
        pair = tab[8] if k < 2 else 1 - tab[8]
        core = tab[9] if k % 2 == 0 else 1 - tab[9]
        for slot in range(HEADS):
            start = ((pair * HEADS + tab[slot]) * 2 + core) * rows
            w_ref[pl.ds(pl.multiple_of(start, rows), rows), :] = source[slot]


def out_kernel(tab, heads_ref, *refs):
    sources, (x_ref, gain_ref, att_ref, mid_ref, n_ref, w_ref) = refs[:-6], refs[-6:]
    if len(sources) == 1:
        w_ref[...] = sources[0][...]
    else:
        place_rows(tab, sources, w_ref)
    for h in range(HEADS):
        att_ref[:, h * HEAD_DIM : (h + 1) * HEAD_DIM] = heads_ref[h]
    mid = x_ref[...].astype(WIDE) + dot_nn(att_ref[...], w_ref[...])
    mid_ref[...] = mid
    r = lax.rsqrt(jnp.mean(mid * mid, axis=-1, keepdims=True) + EPSILON)
    n_ref[...] = (mid * r * gain_ref[...].astype(WIDE)).astype(LOW)


def out_block(tab, heads, sources, x, gain):
    count = x.shape[0]
    return pl.pallas_call(
        out_kernel,
        in_specs=[smem()] + [vmem()] * (3 + len(sources)),
        out_specs=[vmem()] * 4,
        out_shape=[
            jax.ShapeDtypeStruct((count, D), LOW),
            jax.ShapeDtypeStruct((count, D), WIDE),
            jax.ShapeDtypeStruct((count, D), LOW),
            jax.ShapeDtypeStruct((D, D), LOW),
        ],
        cost_estimate=pl.CostEstimate(
            flops=2 * count * D * D, bytes_accessed=6 * 2**20, transcendentals=0
        ),
        name="out_block",
    )(tab, heads, *sources, x, gain)


def fold(block, deep):
    half, rest = D // 2, block.shape[0] - deep
    middle = jnp.concatenate([block[deep:, :half], block[: deep - rest, half:]], axis=0)
    last = block[deep - rest :, half:]
    last = jnp.concatenate([last, jnp.zeros((deep - last.shape[0], half), last.dtype)], axis=0)
    return block[:deep, :half], middle, last


def unfolded(block, share):
    deep, half = block.shape[0], D // 2
    rest = share - deep
    return [
        (0, deep, 0, block[:, :half]),
        (deep, rest, 0, block[:rest, half:D]),
        (0, deep - rest, half, block[rest:, half:D]),
        (deep - rest, share - deep + rest, half, block[: share - deep + rest, D:]),
    ]


def weights_kernel(tab, *refs):
    blocks, (gate_ref, up_ref, down_ref, acc_ref) = refs[:-4], refs[-4:]
    units = gate_ref.shape[1]
    height, wide = blocks[0].shape
    half = wide // 2
    share = units // HEADS
    rows = D // (2 * HEADS)
    middle = blocks[HEADS // 2].shape[0]
    for slot in range(HEADS):
        chip = tab[slot]
        if slot == HEADS // 2:
            pieces = [(0, blocks[slot]), (middle, blocks[slot + 1])]
        else:
            pieces = [(0, blocks[slot if slot < HEADS // 2 else slot + 1])]
        for start, ref in pieces:
            stop = start + ref.shape[0]
            for pair in range(2):
                first, last = max(start, pair * rows), min(stop, (pair + 1) * rows)
                if first < last:
                    size = last - first
                    here = (pair * HEADS + chip) * rows + first - pair * rows
                    here = pl.ds(pl.multiple_of(here, math.gcd(rows, first)), size)
                    gate_ref[here, :] = ref[first - start : last - start, :units]
                    up_ref[here, :] = ref[first - start : last - start, half : half + units]
        lower = ref[2 * rows - start :, :].astype(WIDE)
        for row, size, column, piece in unfolded(lower, share):
            here = pl.ds(pl.multiple_of(chip * share + row, 8), size)
            acc_ref[here, column : column + D // 2] = piece
    down_ref[...] = acc_ref[...].astype(LOW)


def weights(chips, blocks, units):
    return pl.pallas_call(
        weights_kernel,
        in_specs=[smem()] + [vmem()] * len(blocks),
        out_specs=[vmem()] * 3,
        out_shape=[
            jax.ShapeDtypeStruct((D, units), LOW),
            jax.ShapeDtypeStruct((D, units), LOW),
            jax.ShapeDtypeStruct((units, D), LOW),
        ],
        scratch_shapes=[pltpu.VMEM((units, D), WIDE)],
        cost_estimate=pl.CostEstimate(
            flops=0, bytes_accessed=12 * D * units, transcendentals=0
        ),
        name="weights",
    )(chips, *blocks)


def ffn_kernel(na, nb, ga, gb, g_ref, u_ref, d_ref, hid_ref, gg_ref, ug_ref, dn_ref, out_ref):
    for t, (n_ref, c_ref) in enumerate(((na, ga), (nb, gb))):
        n = n_ref[...]
        gate = dot_nn(n, g_ref[...])
        upper = dot_nn(n, u_ref[...])
        sigma = jax.nn.sigmoid(gate)
        silu = gate * sigma
        hid = (silu * upper).astype(LOW)
        hid_ref[t] = hid
        out_ref[t] = dot_nn(hid, d_ref[...]).astype(LOW)
        hg = dot_nt(c_ref[...], d_ref[...])
        gg = (hg * upper * sigma * (1.0 + gate * (1.0 - sigma))).astype(LOW)
        ug = (hg * silu).astype(LOW)
        gg_ref[t] = gg
        ug_ref[t] = ug
        dn_ref[t] = (dot_nt(gg, g_ref[...]) + dot_nt(ug, u_ref[...])).astype(LOW)


def ffn(na, nb, ga, gb, g, u, d):
    count = na.shape[0]
    units = g.shape[1]
    return pl.pallas_call(
        ffn_kernel,
        in_specs=[vmem()] * 7,
        out_specs=[vmem()] * 5,
        out_shape=[jax.ShapeDtypeStruct((2, count, units), LOW)] * 3
        + [jax.ShapeDtypeStruct((2, count, D), LOW)] * 2,
        cost_estimate=pl.CostEstimate(
            flops=24 * count * D * units,
            bytes_accessed=6 * D * units + 16 * count * D,
            transcendentals=2 * count * units,
        ),
        name="ffn",
    )(na, nb, ga, gb, g, u, d)


def grads_kernel(tab, *refs):
    ns, ups, (hid_l, gg_l, ug_l, hid_r, gg_r, ug_r, parts_ref) = (
        refs[:4], refs[4:8], refs[8:],
    )
    wide = parts_ref.shape[2]
    half = wide // 2
    units = hid_l.shape[2]
    share = units // HEADS
    rows = ns[0].shape[1] // (2 * HEADS)
    edge = units - units % HEAD_DIM

    def tokens(near, away):
        return jnp.concatenate([near[0], near[1], away[0], away[1]], axis=0)

    n = jnp.concatenate([v[...] for v in ns], axis=0)
    up = jnp.concatenate([v[...] for v in ups], axis=0)
    for near, away, start in ((gg_l, gg_r, 0), (ug_l, ug_r, half)):
        total = dot_tn(n, tokens(near, away)).astype(LOW)
        for h in range(HEADS):
            slot = tab[h]
            for pair in range(2):
                first = (pair * HEADS + h) * rows
                here = slice(pair * rows, (pair + 1) * rows)
                parts_ref[slot, here, start + edge : start + half] = jnp.zeros(
                    (rows, half - edge), LOW
                )
                parts_ref[slot, here, start : start + units] = total[first : first + rows]
    total = dot_tn(tokens(hid_l, hid_r), up)
    deep = parts_ref.shape[1] - 2 * rows
    for h in range(HEADS):
        for i, piece in enumerate(fold(total[h * share : (h + 1) * share], deep)):
            columns = slice(i * D // 2, (i + 1) * D // 2)
            parts_ref[tab[h], 2 * rows :, columns] = piece.astype(LOW)


def weight_grads(slot_of, ns, ups, near, away, height, wide):
    count = ns[0].shape[0]
    units = near[0].shape[2]
    return pl.pallas_call(
        grads_kernel,
        in_specs=[smem()] + [vmem()] * 14,
        out_specs=vmem(),
        out_shape=jax.ShapeDtypeStruct((HEADS, height, wide), LOW),
        cost_estimate=pl.CostEstimate(
            flops=24 * count * D * units, bytes_accessed=14 * 2**20, transcendentals=0
        ),
        name="weight_grads",
    )(slot_of, *ns, *ups, *near, *away)


def mid_kernel(mid_ref, pa, pb, pc, up_ref, gain_ref, w_ref, mg_ref, bg_ref, ag_ref):
    mid = mid_ref[...]
    scaled = (pa[...].astype(WIDE) + pb[...].astype(WIDE) + pc[...].astype(WIDE)) * gain_ref[
        ...
    ].astype(WIDE)
    r = lax.rsqrt(jnp.mean(mid * mid, axis=-1, keepdims=True) + EPSILON)
    inner = jnp.mean(scaled * mid, axis=-1, keepdims=True)
    mid_grad = up_ref[...].astype(WIDE) + r * scaled - mid * (r * r * r * inner)
    mg_ref[...] = mid_grad
    branch = mid_grad.astype(LOW)
    bg_ref[...] = branch
    att = dot_nt(branch, w_ref[...]).astype(LOW)
    for h in range(HEADS):
        ag_ref[h] = att[:, h * HEAD_DIM : (h + 1) * HEAD_DIM]


def mid_block(mid, pa, pb, pc, up, gain, w):
    count = mid.shape[0]
    return pl.pallas_call(
        mid_kernel,
        in_specs=[vmem()] * 7,
        out_specs=[vmem()] * 3,
        out_shape=[
            jax.ShapeDtypeStruct((count, D), WIDE),
            jax.ShapeDtypeStruct((count, D), LOW),
            jax.ShapeDtypeStruct((HEADS, count, HEAD_DIM), LOW),
        ],
        cost_estimate=pl.CostEstimate(
            flops=2 * count * D * D, bytes_accessed=6 * 2**20, transcendentals=0
        ),
        name="mid_block",
    )(mid, pa, pb, pc, up, gain, w)


def qkv_back_kernel(tab, dq_ref, own_ref, got_ref, cos_ref, sin_ref, n_ref, w_ref, dx_ref, dw_ref, sum_ref):
    i = pl.program_id(0)
    c, s = cos_ref[0], sin_ref[0]

    def rot(v):
        return v * c - pltpu.roll(v, HEAD_DIM // 2, 1) * s

    dq = rot(dq_ref[0] * SCALE).astype(LOW)
    dk = rot((own_ref[0, 0] + got_ref[0, 0].astype(WIDE)) * SCALE).astype(LOW)
    dv = (own_ref[1, 0] + got_ref[1, 0].astype(WIDE)).astype(LOW)
    grads = jnp.concatenate([dq, dk, dv], axis=1)
    dx_ref[0] = dot_nt(grads, w_ref[...]).astype(LOW)
    part = dot_tn(n_ref[0], grads)

    @pl.when(i == 0)
    def _():
        sum_ref[...] = part

    @pl.when(i > 0)
    def _():
        sum_ref[...] += part

    @pl.when(i == HEADS - 1)
    def _():
        dw_ref[...] = sum_ref[...].astype(LOW)


def qkv_back(chips, dq, own, got, cos, sin, normed, w):
    count = dq.shape[1]
    block = pl.BlockSpec((1, count, HEAD_DIM), lambda i, t: (t[i], 0, 0))
    pair = pl.BlockSpec((2, 1, count, HEAD_DIM), lambda i, t: (0, t[i], 0, 0))
    weight = pl.BlockSpec((D, 3 * HEAD_DIM), lambda i, t: (0, 0))
    return pl.pallas_call(
        qkv_back_kernel,
        grid_spec=pltpu.PrefetchScalarGridSpec(
            num_scalar_prefetch=1,
            grid=(HEADS,),
            in_specs=[
                block, pair, pair, block, block,
                pl.BlockSpec((1, count, D), lambda i, t: (t[i], 0, 0)),
                weight,
            ],
            out_specs=[pl.BlockSpec((1, count, D), lambda i, t: (i, 0, 0)), weight],
            scratch_shapes=[pltpu.VMEM((D, 3 * HEAD_DIM), WIDE)],
        ),
        out_shape=[
            jax.ShapeDtypeStruct((HEADS, count, D), LOW),
            jax.ShapeDtypeStruct((D, 3 * HEAD_DIM), LOW),
        ],
        cost_estimate=pl.CostEstimate(
            flops=4 * HEADS * count * D * 3 * HEAD_DIM,
            bytes_accessed=6 * HEADS * count * D,
            transcendentals=0,
        ),
        name="qkv_back",
    )(chips, dq, own, got, cos, sin, normed, w)


def local(
    far,
    tokens,
    segment_ids,
    second_doc,
    memory_index,
    cache_keys,
    cache_values,
    first_gain,
    query_weight,
    key_weight,
    value_weight,
    out_weight,
    second_gain,
    gate_weight,
    up_weight,
    down_weight,
    cotangent,
):
    x = tokens[0]
    upstream = cotangent[0]
    count = x.shape[0]
    blocks = count // QUERY_BLOCK
    rows = query_weight.shape[0]
    share = down_weight.shape[0]
    units = far * HEADS * share
    chip, core, pair = lax.axis_index("h"), lax.axis_index("c"), lax.axis_index("dl")
    mine = jnp.where(chip % 2 == 0, chip // 2, HEADS - 1 - chip // 2)
    slots = jnp.arange(HEADS, dtype=jnp.int32)
    chips = at_place(mine - slots)

    def by_head(w):
        return w.reshape(rows, HEADS, HEAD_DIM).transpose(1, 0, 2)

    picked = memory_index[0].transpose(1, 0, 2)
    seg_rows = jnp.broadcast_to(
        segment_ids[0].astype(LOW).reshape(1, blocks, QUERY_BLOCK), (HEADS, blocks, QUERY_BLOCK)
    )
    gains = jnp.concatenate([first_gain, second_gain])
    gain_rows = jnp.broadcast_to(
        jnp.pad(gains, (0, HEAD_DIM - 2 * rows)).reshape(1, 1, HEAD_DIM), (HEADS, 1, HEAD_DIM)
    )
    pack = jnp.concatenate(
        [
            by_head(query_weight),
            by_head(key_weight),
            by_head(value_weight),
            seg_rows,
            (picked // MEM_ROWS).astype(LOW),
            (picked % MEM_ROWS).astype(LOW),
            gain_rows,
        ],
        axis=1,
    )
    height = pack.shape[1]
    pack = jnp.pad(pack, ((0, 0), (0, -height % 16), (0, 0)))

    block = jnp.concatenate([x, out_weight], axis=0)
    split = count // 2
    got = exchange(pack)
    up_c = swap(upstream, "c")
    up_y = swap(upstream, "dl")
    up_yc = swap(up_y, "c")
    got, x_forth, x_back, parity = lax.optimization_barrier(
        (got, turn(block, 1), turn(block, -1), core)
    )
    forth, back = [block, x_forth, turn(x_forth, 1)], [block, x_back, turn(x_back, -1)]
    got_c = swap(got, "c")
    got_y = swap(got, "dl")
    got_yc = swap(got_y, "c")
    near = pick(core, jnp.stack([got, got_c]), jnp.stack([got_c, got]))
    away = pick(core, jnp.stack([got_y, got_yc]), jnp.stack([got_yc, got_y]))
    every = pick(pair, jnp.stack([near, away]), jnp.stack([away, near]))
    every = every.transpose(2, 0, 1, 3, 4)
    if far > 1:
        every = lax.all_gather(every, "dh", axis=0)
    else:
        every = every[None]
    every = every.transpose(0, 2, 1, 3, 4, 5)
    w_qkv = jnp.concatenate(
        [every[..., i * rows : (i + 1) * rows, :].reshape(D, HEAD_DIM) for i in range(3)], axis=1
    )
    gain_all = every[..., 3 * rows + 3 * blocks, : 2 * rows].reshape(-1, 2, rows)
    gain_one = gain_all[:, 0].reshape(1, D)
    gain_two = gain_all[:, 1].reshape(1, D)

    def seg_of(blocks_of):
        return (
            blocks_of[:, 3 * rows : 3 * rows + blocks]
            .astype(WIDE)
            .astype(jnp.int32)
            .reshape(HEADS, count)
        )

    seg_own = seg_of(got)
    seg_oth = seg_of(got_c)
    idx = (
        got[:, 3 * rows + blocks : 3 * rows + 2 * blocks].astype(WIDE) * MEM_ROWS
        + got[:, 3 * rows + 2 * blocks : 3 * rows + 3 * blocks].astype(WIDE)
    ).astype(jnp.int32)
    idx = idx.reshape(HEADS, count, 1)

    block_docs = seg_own[:, ::QUERY_BLOCK]
    docs = second_doc.shape[1]
    doc_ids = jnp.arange(docs, dtype=jnp.int32)
    mates = jnp.sum(
        jnp.where(block_docs[:, :, None] == doc_ids, second_doc[0][None, None, :], 0), axis=-1
    )
    seg_all = jnp.concatenate([seg_own, seg_oth], axis=0)
    before = jnp.sum(
        (seg_all.reshape(1, -1) < block_docs[:, :1]).astype(jnp.int32), axis=1
    )
    tab = jnp.concatenate(
        [
            block_docs.reshape(-1),
            mates.reshape(-1),
            before // (2 * count),
            jnp.stack([core, chip]),
        ]
    ).astype(jnp.int32)

    half = HEAD_DIM // 2
    freqs = 10000.0 ** (-jnp.arange(half, dtype=WIDE) * 2.0 / (2 * half))
    positions = ((2 * slots + parity) * count)[:, None] + jnp.arange(count, dtype=jnp.int32)[None]
    turned = positions.astype(WIDE)[:, :, None] * freqs
    cosine, sine = jnp.cos(turned), jnp.sin(turned)
    cosine = jnp.concatenate([cosine, cosine], axis=-1)
    sine = jnp.concatenate([-sine, sine], axis=-1)

    seg_thin = seg_own.reshape(HEADS, count, 1)
    early = (w_qkv, gain_one, cosine, sine, tab, seg_thin, idx, up_c, up_y, up_yc)
    early, gate_late, up_late, forth[2], back[2] = lax.optimization_barrier(
        (early, gate_weight, up_weight, forth[2], back[2])
    )
    w_qkv, gain_one, cosine, sine, tab, seg_thin, idx, up_c, up_y, up_yc = early
    forth.append(turn(forth[2], 1))
    back.append(turn(back[2], -1))
    at_near, at_far = [0, 1, 7, 2, 6], [3, 5, 4]

    def chips_at(order):
        return at_place(mine - jnp.asarray(order, jnp.int32)).astype(jnp.int32)

    near_slots = [forth[0], forth[1], back[1], forth[2], back[2]]
    held = qkv_blocks(
        chips_at(at_near), [((v, count),) for v in near_slots], gain_one, w_qkv, cosine, sine, ()
    )
    half = units + -units % HEAD_DIM
    wide = 2 * half

    def by_owner(w):
        w = w.reshape(rows, far, 2, HEADS, 2, share).transpose(2, 4, 0, 1, 3, 5)
        return jnp.pad(w.reshape(2, 2, rows, units), ((0, 0),) * 3 + ((0, half - units),))

    gu = jnp.concatenate([by_owner(gate_late), by_owner(up_late)], axis=-1)
    kept = pick(core, gu[:, 0], gu[:, 1])
    came = swap(pick(core, gu[:, 1], gu[:, 0]), "c")
    gu = pick(core, jnp.stack([kept, came], 1), jnp.stack([came, kept], 1))
    kept = pick(pair, gu[0], gu[1])
    came = swap(pick(pair, gu[1], gu[0]), "dl")
    gu = pick(pair, jnp.stack([kept, came]), jnp.stack([came, kept])).reshape(4 * rows, wide)
    if far == 1:
        deep = 2 * rows
        lower = jnp.concatenate(fold(down_weight, deep), axis=1)
    else:
        deep = share
        lower = jnp.pad(down_weight, ((0, 0), (0, wide - D)))
    bundle = jnp.concatenate([gu, lower], axis=0)
    height = 4 * rows + deep
    if far > 1:
        bundle = lax.all_gather(bundle, "dh", axis=0, tiled=True)
    upper = bundle.shape[0] // 2
    *held, bundle, forth[3], back[3] = lax.optimization_barrier(
        (*held, bundle, forth[3], back[3])
    )
    far_first, far_last = turn(forth[3][:split], 1), turn(back[3][split:], -1)
    bundle, *_ = lax.optimization_barrier((bundle, far_first, far_last))
    w_forth, w_back = [bundle, turn(bundle, 1)], [bundle, turn(bundle, -1)]

    far_slots = [
        ((forth[3], count),),
        ((back[3], count),),
        ((far_first, split), (far_last, count - split)),
    ]
    queries, own, normed_one = qkv_blocks(
        chips_at(at_far), far_slots, gain_one, w_qkv, cosine, sine, tuple(held)
    )
    queries, own, w_forth[1], w_back[1] = lax.optimization_barrier(
        (queries, own, w_forth[1], w_back[1])
    )
    other = swap(own, "c")
    seg_own_row = seg_own.reshape(HEADS, 1, count)
    seg_oth_row = seg_oth.reshape(HEADS, 1, count)
    cached = [cache[0].reshape(-1, D) for cache in (cache_keys, cache_values)]
    attention, attention_low, lse, memory = attend(
        tab, queries, own, other, seg_thin, seg_own_row, seg_oth_row, idx, *cached
    )
    w_forth.append(turn(w_forth[1], 1))
    w_back.append(turn(w_back[1], -1))
    out_rows = [*forth, far_last, *back[:0:-1]]
    *out_rows, attention_low, w_forth[2], w_back[2] = lax.optimization_barrier(
        (*out_rows, attention_low, w_forth[2], w_back[2])
    )

    heads = exchange(attention_low)
    w_forth.append(turn(w_forth[2], 1))
    w_back.append(turn(w_back[2], -1))
    outs = jnp.stack([v[-rows:] for v in out_rows])
    outs_c = swap(outs, "c")
    outs_y = swap(outs, "dl")
    outs_yc = swap(outs_y, "c")
    heads, w_forth[3], w_back[3] = lax.optimization_barrier((heads, w_forth[3], w_back[3]))
    w_first, w_last = turn(w_forth[3][:upper], 1), turn(w_back[3][upper:], -1)
    slot_of = lax.rem(mine - jnp.asarray(PLACE, jnp.int32) + HEADS, HEADS).astype(jnp.int32)
    if far == 1:
        sources = [outs, outs_c, outs_y, outs_yc]
    else:
        near = pick(core, jnp.stack([outs, outs_c], 1), jnp.stack([outs_c, outs], 1))
        away = pick(core, jnp.stack([outs_y, outs_yc], 1), jnp.stack([outs_yc, outs_y], 1))
        sources = pick(pair, jnp.stack([near, away]), jnp.stack([away, near]))
        sources = lax.all_gather(jnp.take(sources, slot_of, axis=1), "dh", axis=0)
        sources = [sources.reshape(D, D)]
    where = jnp.concatenate([chips, jnp.stack([pair, core])]).astype(jnp.int32)
    attended, mid, normed_two, out_w = out_block(where, heads, sources, x, gain_two)
    normed_two, w_first, w_last = lax.optimization_barrier((normed_two, w_first, w_last))
    w_slots = w_forth + [w_first, w_last] + w_back[:0:-1]

    if far == 1:
        gate_w, up_w, down_w = weights(where, w_slots, units)
    else:
        middle = jnp.concatenate(w_slots[HEADS // 2 : HEADS // 2 + 2], axis=0)
        every = jnp.stack(w_slots[: HEADS // 2] + [middle] + w_slots[HEADS // 2 + 2 :])
        every = jnp.take(every, slot_of, axis=0).reshape(HEADS, far, height, wide)
        gu = every[:, :, : 4 * rows].reshape(HEADS, far, 2, 2 * rows, wide)
        gu = gu.transpose(1, 2, 0, 3, 4).reshape(D, wide)
        gate_w, up_w = gu[:, :units], gu[:, half : half + units]
        down_w = every[:, :, 4 * rows :, :D].transpose(1, 0, 2, 3).reshape(units, D)

    n_c = swap(normed_two, "c")
    n_y = swap(normed_two, "dl")
    hid_l, gg_l, ug_l, dn_l, out_l = ffn(normed_two, n_c, upstream, up_c, gate_w, up_w, down_w)
    n_y, dn_l = lax.optimization_barrier((n_y, dn_l))
    n_yc = swap(n_y, "c")
    hid_r, gg_r, ug_r, dn_r, out_r = ffn(n_y, n_yc, up_y, up_yc, gate_w, up_w, down_w)

    def to_away(away):
        return (away[0].astype(WIDE) + swap(away[1], "c").astype(WIDE)).astype(LOW)

    there = to_away(dn_r)
    there, hid_l, gg_l, ug_l, hid_r, gg_r, ug_r = lax.optimization_barrier(
        (there, hid_l, gg_l, ug_l, hid_r, gg_r, ug_r)
    )
    n_all, u_all = [normed_two, n_c, n_y, n_yc], [upstream, up_c, up_y, up_yc]
    near, away = (hid_l, gg_l, ug_l), (hid_r, gg_r, ug_r)
    if far == 1:
        parts = weight_grads(slot_of, n_all, u_all, near, away, height, wide)
    else:

        def over_tokens(left, right):
            return jnp.einsum(
                "gtd,gtf->df", left, right, preferred_element_type=WIDE
            ).astype(LOW)

        def by_rows(w):
            w = jnp.pad(w, ((0, 0), (0, half - units)))
            return w.reshape(far, 2, HEADS, 2 * rows, half).transpose(2, 0, 1, 3, 4)

        n_all, u_all = jnp.stack(n_all), jnp.stack(u_all)
        hid, gg, ug = (jnp.concatenate(pieces, axis=0) for pieces in zip(near, away))
        gu = jnp.concatenate(
            [by_rows(over_tokens(n_all, gg)), by_rows(over_tokens(n_all, ug))], axis=-1
        ).reshape(HEADS, far, 4 * rows, wide)
        down = over_tokens(hid, u_all).reshape(far, HEADS, share, D).transpose(1, 0, 2, 3)
        down = jnp.pad(down, ((0, 0), (0, 0), (0, 0), (0, wide - D)))
        parts = jnp.concatenate([gu, down], axis=2)
        parts = jnp.take(parts.reshape(HEADS, far * height, wide), chips, axis=0)

    sums = [dn_l[0], swap(dn_l[1], "c"), swap(there, "dl")]
    sums[2], parts = lax.optimization_barrier((sums[2], parts))
    mid_grad, branch, att_grad = mid_block(mid, *sums, upstream, gain_two, out_w)
    ups = exchange(att_grad)

    def plus(block, arrived, start):
        size = arrived.shape[0]
        total = block[start : start + size].astype(WIDE) + arrived.astype(WIDE)
        pieces = [block[:start], total, block[start + size :]]
        pieces = [piece.astype(LOW) for piece in pieces if piece.shape[0]]
        return jnp.concatenate(pieces, axis=0)

    def ring_first(blocks, split):
        middle = blocks[HEADS // 2]
        return (
            plus(blocks[HEADS // 2 + 1], turn(middle[:split].astype(LOW), 1), 0),
            plus(blocks[HEADS // 2 - 1], turn(middle[split:].astype(LOW), -1), split),
        )

    def ring_next(blocks, forth, back, step):
        return (
            plus(blocks[HEADS // 2 + step], turn(forth, 1), 0),
            plus(blocks[HEADS // 2 - step], turn(back, -1), 0),
        )

    def ring_last(blocks, forth, back):
        return blocks[0].astype(WIDE) + forth.astype(WIDE) + back.astype(WIDE)

    def over_cores(w, width):
        w = w.reshape(far, 2, HEADS, 2, rows, width)
        kept = pick(core, w[:, :, :, 0], w[:, :, :, 1])
        came = swap(pick(core, w[:, :, :, 1], w[:, :, :, 0]), "c")
        return kept.astype(WIDE) + came.astype(WIDE)

    def over_pairs(w):
        kept = pick(pair, w[:, 0], w[:, 1])
        came = swap(pick(pair, w[:, 1], w[:, 0]).astype(LOW), "dl")
        w = (kept + came.astype(WIDE)).astype(LOW)
        if far > 1:
            w = lax.psum_scatter(w, "dh", scatter_dimension=0, tiled=True)
        return w[0]

    out_part = over_cores(
        jnp.einsum("td,te->de", attended, branch, preferred_element_type=WIDE).astype(LOW), D
    )
    blocks = [parts[slot] for slot in range(HEADS)]
    forth, back = ring_first(blocks, upper)
    ups, out_part, forth, back = lax.optimization_barrier((ups, out_part, forth, back))
    forth, back = ring_next(blocks, forth, back, 2)

    dq, d_own, d_oth = attend_back(
        tab, queries, ups, attention, lse, own, other, memory, seg_thin, seg_own_row, seg_oth_row
    )
    d_got = swap(d_oth, "c")
    out_part = over_pairs(out_part)
    dq, out_part, forth, back = lax.optimization_barrier((dq, out_part, forth, back))
    dx, dw = qkv_back(
        chips.astype(jnp.int32), dq, d_own, d_got, cosine, sine, normed_one, w_qkv
    )
    arrived_forth, arrived_back = turn(forth, 1), turn(back, -1)
    dx, arrived_forth, arrived_back = lax.optimization_barrier((dx, arrived_forth, arrived_back))
    dx_forth, dx_back = ring_first(dx, split)
    dw, dx_forth, dx_back = lax.optimization_barrier((dw, dx_forth, dx_back))
    forth = plus(blocks[HEADS - 1], arrived_forth, 0)
    back = plus(blocks[1], arrived_back, 0)

    dw = over_pairs(over_cores(dw, 3 * HEAD_DIM))
    dw = jnp.concatenate([dw, out_part], axis=-1)
    dx_forth, dx_back = ring_next(dx, dx_forth, dx_back, 2)
    dw, out_l, out_r, dx_forth, dx_back = lax.optimization_barrier(
        (dw, out_l, out_r, dx_forth, dx_back)
    )
    dw = exchange(dw).astype(WIDE)
    qkv_grads = dw[..., : 3 * HEAD_DIM]
    out_w_grad = jnp.sum(dw[..., 3 * HEAD_DIM :], axis=0)
    dx_forth, dx_back = ring_next(dx, dx_forth, dx_back, 3)
    normed_one_grad = ring_last(dx, turn(dx_forth, 1), turn(dx_back, -1))
    output = mid
    for part in (out_l[0], swap(out_l[1], "c"), swap(to_away(out_r), "dl")):
        output = output + part.astype(WIDE)
    output = output.astype(LOW)

    summed = ring_last(blocks, turn(forth, 1), turn(back, -1)).astype(LOW)
    if far > 1:
        summed = lax.psum_scatter(summed, "dh", scatter_dimension=0, tiled=True)
    lower = summed[4 * rows :].astype(WIDE)
    if far == 1:
        half_d = D // 2
        rest = share - deep
        left = jnp.concatenate([lower[:, :half_d], lower[:rest, half_d:D]], axis=0)
        right = jnp.concatenate([lower[rest:, half_d:D], lower[: 2 * rest, D:]], axis=0)
        down_w_grad = jnp.concatenate([left, right], axis=1)
    else:
        down_w_grad = lower[:, :D]
    gu = summed[: 4 * rows].reshape(2, 2, rows, wide)
    kept = pick(core, gu[:, 0], gu[:, 1])
    came = swap(pick(core, gu[:, 1], gu[:, 0]), "c")
    gu = pick(core, jnp.stack([kept, came], 1), jnp.stack([came, kept], 1))
    kept = pick(pair, gu[0], gu[1])
    came = swap(pick(pair, gu[1], gu[0]), "dl")
    gu = pick(pair, jnp.stack([kept, came]), jnp.stack([came, kept]))
    gu = jnp.stack([gu[..., :units], gu[..., half : half + units]])
    gu = (
        gu.reshape(2, 2, 2, rows, far, HEADS, share)
        .transpose(0, 3, 4, 1, 5, 2, 6)
        .reshape(2, rows, FF)
        .astype(WIDE)
    )
    gate_w_grad, up_w_grad = gu[0], gu[1]

    wide_x = x.astype(WIDE)
    r = lax.rsqrt(jnp.mean(wide_x * wide_x, axis=-1, keepdims=True) + EPSILON)
    scaled = normed_one_grad * gain_one.astype(WIDE)
    inner = jnp.mean(scaled * wide_x, axis=-1, keepdims=True)
    input_grad = mid_grad + r * scaled - wide_x * (r * r * r * inner)

    q_w_grad, k_w_grad, v_w_grad = (
        qkv_grads[:, :, i * HEAD_DIM : (i + 1) * HEAD_DIM].transpose(1, 0, 2).reshape(rows, D)
        for i in range(3)
    )

    def gain_grad(gain, pairs):
        total = 0.0
        for grad, weight in pairs:
            total = total + jnp.sum(grad * weight.astype(WIDE), axis=1)
        return total / gain.astype(WIDE)

    first_gain_grad = gain_grad(
        first_gain,
        ((q_w_grad, query_weight), (k_w_grad, key_weight), (v_w_grad, value_weight)),
    )
    second_gain_grad = gain_grad(
        second_gain, ((gate_w_grad, gate_weight), (up_w_grad, up_weight))
    )
    return (
        output[None],
        input_grad[None],
        first_gain_grad,
        q_w_grad,
        k_w_grad,
        v_w_grad,
        out_w_grad,
        second_gain_grad,
        gate_w_grad,
        up_w_grad,
        down_w_grad,
    )


def solution(mesh):
    far = mesh.shape["dp"] // 2
    cores = mesh.shape["seq"] // HEADS
    fine = Mesh(mesh.devices.reshape(far, 2, HEADS, cores), ("dh", "dl", "h", "c"))
    dp, seq, every = ("dh", "dl"), ("h", "c"), ("dh", "dl", "h", "c")
    rows = P(every, None)
    return jax.shard_map(
        functools.partial(local, far),
        mesh=fine,
        in_specs=(
            P(dp, seq, None),
            P(dp, seq),
            P(dp, None),
            P(dp, seq, None, None),
            P(dp, None, None, None),
            P(dp, None, None, None),
            P(every),
            rows,
            rows,
            rows,
            rows,
            P(every),
            rows,
            rows,
            rows,
            P(dp, seq, None),
        ),
        out_specs=(
            P(dp, seq, None),
            P(dp, seq, None),
            P(every),
            rows,
            rows,
            rows,
            rows,
            P(every),
            rows,
            rows,
            rows,
        ),
        check_vma=False,
    )
```

```python
import functools
import math

import jax
import jax.numpy as jnp
from jax import lax
from jax.experimental import pallas as pl
from jax.experimental.pallas import tpu as pltpu
from jax.sharding import Mesh
from jax.sharding import PartitionSpec as P

D = 1024
FF = 2816
HEADS = 8
HEAD_DIM = 128
QUERY_BLOCK = 128
MEM_ROWS = 256
EPSILON = 1e-05
NEGATIVE = -1e30
SCALE = 1.0 / math.sqrt(HEAD_DIM)
LOG2 = SCALE * math.log2(math.e)
LOW = jnp.bfloat16
WIDE = jnp.float32

RING = [2 * i for i in range(HEADS // 2)] + [2 * i + 1 for i in reversed(range(HEADS // 2))]
PLACE = [RING.index(i) for i in range(HEADS)]


def dot_nn(a, b):
    return lax.dot_general(a, b, (((1,), (0,)), ((), ())), preferred_element_type=WIDE)


def dot_nt(a, b):
    return lax.dot_general(a, b, (((1,), (1,)), ((), ())), preferred_element_type=WIDE)


def dot_tn(a, b):
    return lax.dot_general(a, b, (((0,), (0,)), ((), ())), preferred_element_type=WIDE)


def swap(block, axis):
    return lax.ppermute(block, axis, [(0, 1), (1, 0)])


def turn(block, distance):
    route = [(RING[i], RING[(i + distance) % HEADS]) for i in range(HEADS)]
    return lax.ppermute(block, "h", route)


def at_place(place):
    place = lax.rem(place + 2 * HEADS, HEADS)
    return jnp.where(place < HEADS // 2, 2 * place, 2 * (HEADS - 1 - place) + 1)


def exchange(blocks):
    return lax.all_to_all(blocks, "h", 0, 0)


def pick(flag, first, second):
    return jnp.where(flag == 0, first, second)


def smem():
    return pl.BlockSpec(memory_space=pltpu.SMEM)


def vmem():
    return pl.BlockSpec(memory_space=pltpu.VMEM)


def qkv_kernel(parts, tab, *refs):
    xs, (gain_ref, w_ref, cos_ref, sin_ref) = refs[: sum(parts)], refs[sum(parts) : sum(parts) + 4]
    q_ref, kv_ref, n_ref, x_ref = refs[-4:]
    i = pl.program_id(0)
    first = 0
    for step, number in enumerate(parts):

        @pl.when(i == step)
        def _(blocks=xs[first : first + number]):
            row = 0
            for block in blocks:
                size = block.shape[0]
                x_ref[row : row + size, :] = block[...]
                row += size

        first += number
    x = x_ref[...].astype(WIDE)
    r = lax.rsqrt(jnp.mean(x * x, axis=-1, keepdims=True) + EPSILON)
    normed = (x * r * gain_ref[...].astype(WIDE)).astype(LOW)
    n_ref[0] = normed
    out = dot_nn(normed, w_ref[...])
    c, s = cos_ref[0], sin_ref[0]

    def rot(v):
        return v * c + pltpu.roll(v, HEAD_DIM // 2, 1) * s

    q_ref[0] = rot(out[:, :HEAD_DIM]).astype(LOW)
    kv_ref[0, 0] = rot(out[:, HEAD_DIM : 2 * HEAD_DIM]).astype(LOW)
    kv_ref[1, 0] = out[:, 2 * HEAD_DIM :].astype(LOW)


def qkv_blocks(chips, xs, gain, w, cos, sin, held):
    count = cos.shape[1]
    flat = [piece for block in xs for piece, _ in block]
    read = [size for block in xs for _, size in block]

    def whole(shape):
        return pl.BlockSpec(shape, lambda i, t: (0, 0))

    def block(*shape):
        return pl.BlockSpec((1, *shape), lambda i, t: (t[i], 0, 0))

    spec = pltpu.PrefetchScalarGridSpec(
        num_scalar_prefetch=1,
        grid=(len(xs),),
        in_specs=[whole((size, D)) for size in read]
        + [whole((1, D)), whole((D, 3 * HEAD_DIM)), block(count, HEAD_DIM), block(count, HEAD_DIM)]
        + [pl.BlockSpec(memory_space=pl.ANY)] * len(held),
        out_specs=[
            block(count, HEAD_DIM),
            pl.BlockSpec((2, 1, count, HEAD_DIM), lambda i, t: (0, t[i], 0, 0)),
            block(count, D),
        ],
        scratch_shapes=[pltpu.VMEM((count, D), LOW)],
    )
    return pl.pallas_call(
        functools.partial(qkv_kernel, [len(block) for block in xs]),
        grid_spec=spec,
        out_shape=[
            jax.ShapeDtypeStruct((HEADS, count, HEAD_DIM), LOW),
            jax.ShapeDtypeStruct((2, HEADS, count, HEAD_DIM), LOW),
            jax.ShapeDtypeStruct((HEADS, count, D), LOW),
        ],
        input_output_aliases={len(flat) + 5 + i: i for i in range(len(held))},
        cost_estimate=pl.CostEstimate(
            flops=len(xs) * count * D, bytes_accessed=len(xs) * count, transcendentals=0
        ),
        name=f"qkv{len(xs)}",
    )(chips, *flat, gain, w, cos, sin, *held)


def causal(count):
    rows = lax.broadcasted_iota(jnp.int32, (count, count), 0)
    return lax.broadcasted_iota(jnp.int32, (count, count), 1) <= rows


def attend_kernel(
    tab, q_ref, own_ref, oth_ref, segq_ref, sego_ref, segt_ref, idx_ref, ck_ref, cv_ref,
    o_ref, low_ref, lse_ref, mem_ref,
):
    i = pl.program_id(0)
    parity = tab[40]
    count = q_ref.shape[1]
    q = q_ref[0]
    segq = segq_ref[0]

    s1 = dot_nt(q, own_ref[0, i]) * LOG2
    s2 = dot_nt(q, oth_ref[0, i]) * LOG2
    s1 = jnp.where((sego_ref[i] == segq) & causal(count), s1, NEGATIVE)
    s2 = jnp.where(segt_ref[i] == segq + 64 * (1 - parity), s2, NEGATIVE)
    memory = []
    for b in range(count // QUERY_BLOCK):
        rows = slice(b * QUERY_BLOCK, (b + 1) * QUERY_BLOCK)
        doc = tab[2 * i + b]
        mate = tab[16 + 2 * i + b]
        idx = idx_ref[0, rows, :]
        lane = lax.broadcasted_iota(jnp.int32, (QUERY_BLOCK, MEM_ROWS), 1)
        first = jnp.where(idx == lane, 1.0, 0.0).astype(LOW)
        second = jnp.where(idx == lane + MEM_ROWS, 1.0, 0.0).astype(LOW)
        here = pl.ds(pl.multiple_of(doc * MEM_ROWS, MEM_ROWS), MEM_ROWS)
        there = pl.ds(pl.multiple_of(mate * MEM_ROWS, MEM_ROWS), MEM_ROWS)
        mk = (dot_nn(first, ck_ref[here, :]) + dot_nn(second, ck_ref[there, :])).astype(LOW)
        mv = (dot_nn(first, cv_ref[here, :]) + dot_nn(second, cv_ref[there, :])).astype(LOW)
        mem_ref[0, 0, rows, :] = mk
        mem_ref[1, 0, rows, :] = mv
        s = jnp.where(segq[rows] == doc, dot_nt(q[rows], mk) * LOG2, NEGATIVE)
        memory.append((s, mv))
    sm = jnp.concatenate([s for s, _ in memory], axis=0)
    top = jnp.maximum(
        jnp.max(jnp.maximum(s1, s2), axis=-1, keepdims=True), jnp.max(sm, axis=-1, keepdims=True)
    )
    p1 = jnp.exp2(s1 - top)
    p2 = jnp.exp2(s2 - top)
    pm = jnp.exp2(sm - top)
    total = jnp.sum(p1 + p2, axis=-1, keepdims=True) + jnp.sum(pm, axis=-1, keepdims=True)
    pm = pm.astype(LOW)
    acc = jnp.concatenate(
        [
            dot_nn(pm[b * QUERY_BLOCK : (b + 1) * QUERY_BLOCK], mv)
            for b, (_, mv) in enumerate(memory)
        ],
        axis=0,
    )
    acc = acc + dot_nn(p1.astype(LOW), own_ref[1, i]) + dot_nn(p2.astype(LOW), oth_ref[1, i])

    def body(j, state):
        top, total, acc = state
        s1 = dot_nt(q, own_ref[0, j]) * LOG2
        s2 = dot_nt(q, oth_ref[0, j]) * LOG2
        s1 = jnp.where(sego_ref[j] == segq, s1, NEGATIVE)
        s2 = jnp.where(segt_ref[j] == segq, s2, NEGATIVE)
        fresh = jnp.maximum(top, jnp.max(jnp.maximum(s1, s2), axis=-1, keepdims=True))
        p1 = jnp.exp2(s1 - fresh)
        p2 = jnp.exp2(s2 - fresh)
        decay = jnp.exp2(top - fresh)
        total = total * decay + jnp.sum(p1 + p2, axis=-1, keepdims=True)
        acc = (
            acc * decay
            + dot_nn(p1.astype(LOW), own_ref[1, j])
            + dot_nn(p2.astype(LOW), oth_ref[1, j])
        )
        return fresh, total, acc

    top, total, acc = lax.fori_loop(tab[32 + i], i, body, (top, total, acc))
    out = acc / total
    o_ref[0] = out
    low_ref[0] = out.astype(LOW)
    lse_ref[0] = top + jnp.log2(total)


def attend(tab, q, own, oth, segq, sego, segt, idx, ck, cv):
    count = q.shape[1]
    block = pl.BlockSpec((1, count, HEAD_DIM), lambda i, t: (i, 0, 0))
    thin = pl.BlockSpec((1, count, 1), lambda i, t: (i, 0, 0))
    whole = pl.BlockSpec((2, HEADS, count, HEAD_DIM), lambda i, t: (0, 0, 0, 0))
    segs = pl.BlockSpec((HEADS, 1, count), lambda i, t: (0, 0, 0))
    cache = pl.BlockSpec((ck.shape[0], HEAD_DIM), lambda i, t: (0, t[41]))
    mem = pl.BlockSpec((2, 1, count, HEAD_DIM), lambda i, t: (0, i, 0, 0))
    return pl.pallas_call(
        attend_kernel,
        grid_spec=pltpu.PrefetchScalarGridSpec(
            num_scalar_prefetch=1,
            grid=(HEADS,),
            in_specs=[block, whole, whole, thin, segs, segs, thin, cache, cache],
            out_specs=[block, block, thin, mem],
        ),
        out_shape=[
            jax.ShapeDtypeStruct((HEADS, count, HEAD_DIM), WIDE),
            jax.ShapeDtypeStruct((HEADS, count, HEAD_DIM), LOW),
            jax.ShapeDtypeStruct((HEADS, count, 1), WIDE),
            jax.ShapeDtypeStruct((2, HEADS, count, HEAD_DIM), LOW),
        ],
        cost_estimate=pl.CostEstimate(
            flops=25 * 10**9, bytes_accessed=6 * 2**20, transcendentals=3 * 10**6
        ),
        name="attend",
    )(tab, q, own, oth, segq, sego, segt, idx, ck, cv)


def attend_back_kernel(
    tab, q_ref, up_ref, o_ref, lse_ref, own_ref, oth_ref, mem_ref, segq_ref, sego_ref, segt_ref,
    dq_ref, down_ref, doth_ref, sum_ref,
):
    i = pl.program_id(0)

    @pl.when(i == 0)
    def _():
        sum_ref[...] = jnp.zeros_like(sum_ref)

    parity = tab[40]
    count = q_ref.shape[1]
    q = q_ref[0]
    up = up_ref[0]
    lse = lse_ref[0]
    segq = segq_ref[0]
    delta = jnp.sum(up.astype(WIDE) * o_ref[0], axis=-1, keepdims=True)
    partial = []
    for b in range(count // QUERY_BLOCK):
        rows = slice(b * QUERY_BLOCK, (b + 1) * QUERY_BLOCK)
        mk = mem_ref[0, 0, rows, :]
        mv = mem_ref[1, 0, rows, :]
        ok = segq[rows] == tab[2 * i + b]
        p = jnp.exp2(jnp.where(ok, dot_nt(q[rows], mk) * LOG2 - lse[rows], NEGATIVE))
        ds = (p * (dot_nt(up[rows], mv) - delta[rows])).astype(LOW)
        partial.append(dot_nn(ds, mk))

    def tile(side, ref, j, ok, dq):
        k = ref[0, j]
        v = ref[1, j]
        p = jnp.exp2(jnp.where(ok, dot_nt(q, k) * LOG2 - lse, NEGATIVE))
        ds = (p * (dot_nt(up, v) - delta)).astype(LOW)
        sum_ref[side, 0, j] += dot_tn(ds, q)
        sum_ref[side, 1, j] += dot_tn(p.astype(LOW), up)
        return dq + dot_nn(ds, k)

    dq = jnp.concatenate(partial, axis=0)
    dq = tile(0, own_ref, i, (sego_ref[i] == segq) & causal(count), dq)
    dq = tile(1, oth_ref, i, segt_ref[i] == segq + 64 * (1 - parity), dq)

    def body(j, dq):
        dq = tile(0, own_ref, j, sego_ref[j] == segq, dq)
        return tile(1, oth_ref, j, segt_ref[j] == segq, dq)

    dq_ref[0] = lax.fori_loop(tab[32 + i], i, body, dq)

    @pl.when(i == HEADS - 1)
    def _():
        down_ref[...] = sum_ref[0]
        doth_ref[...] = sum_ref[1].astype(LOW)


def attend_back(tab, q, up, o, lse, own, oth, mem, segq, sego, segt):
    count = q.shape[1]
    block = pl.BlockSpec((1, count, HEAD_DIM), lambda i, t: (i, 0, 0))
    thin = pl.BlockSpec((1, count, 1), lambda i, t: (i, 0, 0))
    whole = pl.BlockSpec((2, HEADS, count, HEAD_DIM), lambda i, t: (0, 0, 0, 0))
    segs = pl.BlockSpec((HEADS, 1, count), lambda i, t: (0, 0, 0))
    memory = pl.BlockSpec((2, 1, count, HEAD_DIM), lambda i, t: (0, i, 0, 0))
    return pl.pallas_call(
        attend_back_kernel,
        grid_spec=pltpu.PrefetchScalarGridSpec(
            num_scalar_prefetch=1,
            grid=(HEADS,),
            in_specs=[block, block, block, thin, whole, whole, memory, thin, segs, segs],
            out_specs=[block, whole, whole],
            scratch_shapes=[pltpu.VMEM((2, 2, HEADS, count, HEAD_DIM), WIDE)],
        ),
        out_shape=[
            jax.ShapeDtypeStruct((HEADS, count, HEAD_DIM), WIDE),
            jax.ShapeDtypeStruct((2, HEADS, count, HEAD_DIM), WIDE),
            jax.ShapeDtypeStruct((2, HEADS, count, HEAD_DIM), LOW),
        ],
        cost_estimate=pl.CostEstimate(
            flops=30 * 10**9, bytes_accessed=10 * 2**20, transcendentals=3 * 10**6
        ),
        name="attend_back",
    )(tab, q, up, o, lse, own, oth, mem, segq, sego, segt)


def place_rows(tab, sources, w_ref):
    rows = sources[0].shape[1]
    for k, source in enumerate(sources):
        pair = tab[8] if k < 2 else 1 - tab[8]
        core = tab[9] if k % 2 == 0 else 1 - tab[9]
        for slot in range(HEADS):
            start = ((pair * HEADS + tab[slot]) * 2 + core) * rows
            w_ref[pl.ds(pl.multiple_of(start, rows), rows), :] = source[slot]


def out_kernel(tab, heads_ref, *refs):
    sources, (x_ref, gain_ref, att_ref, mid_ref, n_ref, w_ref) = refs[:-6], refs[-6:]
    if len(sources) == 1:
        w_ref[...] = sources[0][...]
    else:
        place_rows(tab, sources, w_ref)
    for h in range(HEADS):
        att_ref[:, h * HEAD_DIM : (h + 1) * HEAD_DIM] = heads_ref[h]
    mid = x_ref[...].astype(WIDE) + dot_nn(att_ref[...], w_ref[...])
    mid_ref[...] = mid
    r = lax.rsqrt(jnp.mean(mid * mid, axis=-1, keepdims=True) + EPSILON)
    n_ref[...] = (mid * r * gain_ref[...].astype(WIDE)).astype(LOW)


def out_block(tab, heads, sources, x, gain):
    count = x.shape[0]
    return pl.pallas_call(
        out_kernel,
        in_specs=[smem()] + [vmem()] * (3 + len(sources)),
        out_specs=[vmem()] * 4,
        out_shape=[
            jax.ShapeDtypeStruct((count, D), LOW),
            jax.ShapeDtypeStruct((count, D), WIDE),
            jax.ShapeDtypeStruct((count, D), LOW),
            jax.ShapeDtypeStruct((D, D), LOW),
        ],
        cost_estimate=pl.CostEstimate(
            flops=2 * count * D * D, bytes_accessed=6 * 2**20, transcendentals=0
        ),
        name="out_block",
    )(tab, heads, *sources, x, gain)


def fold(block, deep):
    half, rest = D // 2, block.shape[0] - deep
    middle = jnp.concatenate([block[deep:, :half], block[: deep - rest, half:]], axis=0)
    last = block[deep - rest :, half:]
    last = jnp.concatenate([last, jnp.zeros((deep - last.shape[0], half), last.dtype)], axis=0)
    return block[:deep, :half], middle, last


def unfolded(block, share):
    deep, half = block.shape[0], D // 2
    rest = share - deep
    return [
        (0, deep, 0, block[:, :half]),
        (deep, rest, 0, block[:rest, half:D]),
        (0, deep - rest, half, block[rest:, half:D]),
        (deep - rest, share - deep + rest, half, block[: share - deep + rest, D:]),
    ]


def weights_kernel(tab, *refs):
    blocks, (gate_ref, up_ref, down_ref, acc_ref) = refs[:-4], refs[-4:]
    units = gate_ref.shape[1]
    height, wide = blocks[0].shape
    half = wide // 2
    share = units // HEADS
    rows = D // (2 * HEADS)
    middle = blocks[HEADS // 2].shape[0]
    for slot in range(HEADS):
        chip = tab[slot]
        if slot == HEADS // 2:
            pieces = [(0, blocks[slot]), (middle, blocks[slot + 1])]
        else:
            pieces = [(0, blocks[slot if slot < HEADS // 2 else slot + 1])]
        for start, ref in pieces:
            stop = start + ref.shape[0]
            for pair in range(2):
                first, last = max(start, pair * rows), min(stop, (pair + 1) * rows)
                if first < last:
                    size = last - first
                    here = (pair * HEADS + chip) * rows + first - pair * rows
                    here = pl.ds(pl.multiple_of(here, math.gcd(rows, first)), size)
                    gate_ref[here, :] = ref[first - start : last - start, :units]
                    up_ref[here, :] = ref[first - start : last - start, half : half + units]
        lower = ref[2 * rows - start :, :].astype(WIDE)
        for row, size, column, piece in unfolded(lower, share):
            here = pl.ds(pl.multiple_of(chip * share + row, 8), size)
            acc_ref[here, column : column + D // 2] = piece
    down_ref[...] = acc_ref[...].astype(LOW)


def weights(chips, blocks, units):
    return pl.pallas_call(
        weights_kernel,
        in_specs=[smem()] + [vmem()] * len(blocks),
        out_specs=[vmem()] * 3,
        out_shape=[
            jax.ShapeDtypeStruct((D, units), LOW),
            jax.ShapeDtypeStruct((D, units), LOW),
            jax.ShapeDtypeStruct((units, D), LOW),
        ],
        scratch_shapes=[pltpu.VMEM((units, D), WIDE)],
        cost_estimate=pl.CostEstimate(
            flops=0, bytes_accessed=12 * D * units, transcendentals=0
        ),
        name="weights",
    )(chips, *blocks)


def ffn_kernel(na, nb, ga, gb, g_ref, u_ref, d_ref, hid_ref, gg_ref, ug_ref, dn_ref, out_ref):
    for t, (n_ref, c_ref) in enumerate(((na, ga), (nb, gb))):
        n = n_ref[...]
        gate = dot_nn(n, g_ref[...])
        upper = dot_nn(n, u_ref[...])
        sigma = jax.nn.sigmoid(gate)
        silu = gate * sigma
        hid = (silu * upper).astype(LOW)
        hid_ref[t] = hid
        out_ref[t] = dot_nn(hid, d_ref[...]).astype(LOW)
        hg = dot_nt(c_ref[...], d_ref[...])
        gg = (hg * upper * sigma * (1.0 + gate * (1.0 - sigma))).astype(LOW)
        ug = (hg * silu).astype(LOW)
        gg_ref[t] = gg
        ug_ref[t] = ug
        dn_ref[t] = (dot_nt(gg, g_ref[...]) + dot_nt(ug, u_ref[...])).astype(LOW)


def ffn(na, nb, ga, gb, g, u, d):
    count = na.shape[0]
    units = g.shape[1]
    return pl.pallas_call(
        ffn_kernel,
        in_specs=[vmem()] * 7,
        out_specs=[vmem()] * 5,
        out_shape=[jax.ShapeDtypeStruct((2, count, units), LOW)] * 3
        + [jax.ShapeDtypeStruct((2, count, D), LOW)] * 2,
        cost_estimate=pl.CostEstimate(
            flops=24 * count * D * units,
            bytes_accessed=6 * D * units + 16 * count * D,
            transcendentals=2 * count * units,
        ),
        name="ffn",
    )(na, nb, ga, gb, g, u, d)


def grads_kernel(tab, *refs):
    ns, ups, (hid_l, gg_l, ug_l, hid_r, gg_r, ug_r, parts_ref) = (
        refs[:4], refs[4:8], refs[8:],
    )
    wide = parts_ref.shape[2]
    half = wide // 2
    units = hid_l.shape[2]
    share = units // HEADS
    rows = ns[0].shape[1] // (2 * HEADS)
    edge = units - units % HEAD_DIM

    def tokens(near, away):
        return jnp.concatenate([near[0], near[1], away[0], away[1]], axis=0)

    n = jnp.concatenate([v[...] for v in ns], axis=0)
    up = jnp.concatenate([v[...] for v in ups], axis=0)
    for near, away, start in ((gg_l, gg_r, 0), (ug_l, ug_r, half)):
        total = dot_tn(n, tokens(near, away)).astype(LOW)
        for h in range(HEADS):
            slot = tab[h]
            for pair in range(2):
                first = (pair * HEADS + h) * rows
                here = slice(pair * rows, (pair + 1) * rows)
                parts_ref[slot, here, start + edge : start + half] = jnp.zeros(
                    (rows, half - edge), LOW
                )
                parts_ref[slot, here, start : start + units] = total[first : first + rows]
    total = dot_tn(tokens(hid_l, hid_r), up)
    strip = wide - D
    for h in range(HEADS):
        slot = tab[h]
        piece = total[h * share : (h + 1) * share].astype(LOW)
        parts_ref[slot, 2 * rows : 2 * rows + share, :D] = piece
        parts_ref[slot, 2 * rows : 2 * rows + share, D:] = jnp.zeros((share, strip), LOW)


def weight_grads(slot_of, ns, ups, near, away, height, wide):
    count = ns[0].shape[0]
    units = near[0].shape[2]
    return pl.pallas_call(
        grads_kernel,
        in_specs=[smem()] + [vmem()] * 14,
        out_specs=vmem(),
        out_shape=jax.ShapeDtypeStruct((HEADS, height, wide), LOW),
        cost_estimate=pl.CostEstimate(
            flops=24 * count * D * units, bytes_accessed=14 * 2**20, transcendentals=0
        ),
        name="weight_grads",
    )(slot_of, *ns, *ups, *near, *away)


def strips_kernel(tab, out_ref, strips_ref):
    rows, strip = out_ref.shape[1], strips_ref.shape[2]
    for slot in range(HEADS):
        for i in range(D // strip):
            strips_ref[slot, i * rows : (i + 1) * rows, :] = out_ref[
                tab[slot], :, i * strip : (i + 1) * strip
            ]


def out_strips(chips, out, strip):
    return pl.pallas_call(
        strips_kernel,
        in_specs=[smem(), vmem()],
        out_specs=vmem(),
        out_shape=jax.ShapeDtypeStruct((HEADS, out.shape[1] * D // strip, strip), LOW),
        cost_estimate=pl.CostEstimate(
            flops=0, bytes_accessed=4 * HEADS * out.shape[1] * D, transcendentals=0
        ),
        name="out_strips",
    )(chips, out)


def mid_kernel(mid_ref, pa, pb, pc, up_ref, gain_ref, w_ref, mg_ref, bg_ref, ag_ref):
    mid = mid_ref[...]
    scaled = (pa[...].astype(WIDE) + pb[...].astype(WIDE) + pc[...].astype(WIDE)) * gain_ref[
        ...
    ].astype(WIDE)
    r = lax.rsqrt(jnp.mean(mid * mid, axis=-1, keepdims=True) + EPSILON)
    inner = jnp.mean(scaled * mid, axis=-1, keepdims=True)
    mid_grad = up_ref[...].astype(WIDE) + r * scaled - mid * (r * r * r * inner)
    mg_ref[...] = mid_grad
    branch = mid_grad.astype(LOW)
    bg_ref[...] = branch
    att = dot_nt(branch, w_ref[...]).astype(LOW)
    for h in range(HEADS):
        ag_ref[h] = att[:, h * HEAD_DIM : (h + 1) * HEAD_DIM]


def mid_block(mid, pa, pb, pc, up, gain, w):
    count = mid.shape[0]
    return pl.pallas_call(
        mid_kernel,
        in_specs=[vmem()] * 7,
        out_specs=[vmem()] * 3,
        out_shape=[
            jax.ShapeDtypeStruct((count, D), WIDE),
            jax.ShapeDtypeStruct((count, D), LOW),
            jax.ShapeDtypeStruct((HEADS, count, HEAD_DIM), LOW),
        ],
        cost_estimate=pl.CostEstimate(
            flops=2 * count * D * D, bytes_accessed=6 * 2**20, transcendentals=0
        ),
        name="mid_block",
    )(mid, pa, pb, pc, up, gain, w)


def qkv_back_kernel(tab, dq_ref, own_ref, got_ref, cos_ref, sin_ref, n_ref, w_ref, dx_ref, dw_ref, sum_ref):
    i = pl.program_id(0)
    c, s = cos_ref[0], sin_ref[0]

    def rot(v):
        return v * c - pltpu.roll(v, HEAD_DIM // 2, 1) * s

    dq = rot(dq_ref[0] * SCALE).astype(LOW)
    dk = rot((own_ref[0, 0] + got_ref[0, 0].astype(WIDE)) * SCALE).astype(LOW)
    dv = (own_ref[1, 0] + got_ref[1, 0].astype(WIDE)).astype(LOW)
    grads = jnp.concatenate([dq, dk, dv], axis=1)
    dx_ref[0] = dot_nt(grads, w_ref[...]).astype(LOW)
    part = dot_tn(n_ref[0], grads)

    @pl.when(i == 0)
    def _():
        sum_ref[...] = part

    @pl.when(i > 0)
    def _():
        sum_ref[...] += part

    @pl.when(i == HEADS - 1)
    def _():
        dw_ref[...] = sum_ref[...].astype(LOW)


def qkv_back(chips, dq, own, got, cos, sin, normed, w):
    count = dq.shape[1]
    block = pl.BlockSpec((1, count, HEAD_DIM), lambda i, t: (t[i], 0, 0))
    pair = pl.BlockSpec((2, 1, count, HEAD_DIM), lambda i, t: (0, t[i], 0, 0))
    weight = pl.BlockSpec((D, 3 * HEAD_DIM), lambda i, t: (0, 0))
    return pl.pallas_call(
        qkv_back_kernel,
        grid_spec=pltpu.PrefetchScalarGridSpec(
            num_scalar_prefetch=1,
            grid=(HEADS,),
            in_specs=[
                block, pair, pair, block, block,
                pl.BlockSpec((1, count, D), lambda i, t: (t[i], 0, 0)),
                weight,
            ],
            out_specs=[pl.BlockSpec((1, count, D), lambda i, t: (i, 0, 0)), weight],
            scratch_shapes=[pltpu.VMEM((D, 3 * HEAD_DIM), WIDE)],
        ),
        out_shape=[
            jax.ShapeDtypeStruct((HEADS, count, D), LOW),
            jax.ShapeDtypeStruct((D, 3 * HEAD_DIM), LOW),
        ],
        cost_estimate=pl.CostEstimate(
            flops=4 * HEADS * count * D * 3 * HEAD_DIM,
            bytes_accessed=6 * HEADS * count * D,
            transcendentals=0,
        ),
        name="qkv_back",
    )(chips, dq, own, got, cos, sin, normed, w)


def local(
    far,
    tokens,
    segment_ids,
    second_doc,
    memory_index,
    cache_keys,
    cache_values,
    first_gain,
    query_weight,
    key_weight,
    value_weight,
    out_weight,
    second_gain,
    gate_weight,
    up_weight,
    down_weight,
    cotangent,
):
    x = tokens[0]
    upstream = cotangent[0]
    count = x.shape[0]
    blocks = count // QUERY_BLOCK
    rows = query_weight.shape[0]
    share = down_weight.shape[0]
    units = far * HEADS * share
    chip, core, pair = lax.axis_index("h"), lax.axis_index("c"), lax.axis_index("dl")
    mine = jnp.where(chip % 2 == 0, chip // 2, HEADS - 1 - chip // 2)
    slots = jnp.arange(HEADS, dtype=jnp.int32)
    chips = at_place(mine - slots)

    def by_head(w):
        return w.reshape(rows, HEADS, HEAD_DIM).transpose(1, 0, 2)

    picked = memory_index[0].transpose(1, 0, 2)
    seg_rows = jnp.broadcast_to(
        segment_ids[0].astype(LOW).reshape(1, blocks, QUERY_BLOCK), (HEADS, blocks, QUERY_BLOCK)
    )
    gains = jnp.concatenate([first_gain, second_gain])
    gain_rows = jnp.broadcast_to(
        jnp.pad(gains, (0, HEAD_DIM - 2 * rows)).reshape(1, 1, HEAD_DIM), (HEADS, 1, HEAD_DIM)
    )
    pack = jnp.concatenate(
        [
            by_head(query_weight),
            by_head(key_weight),
            by_head(value_weight),
            seg_rows,
            (picked // MEM_ROWS).astype(LOW),
            (picked % MEM_ROWS).astype(LOW),
            gain_rows,
        ],
        axis=1,
    )
    height = pack.shape[1]
    pack = jnp.pad(pack, ((0, 0), (0, -height % 16), (0, 0)))

    block = jnp.concatenate([x, out_weight], axis=0)
    split = count // 2
    got = exchange(pack)
    up_c = swap(upstream, "c")
    up_y = swap(upstream, "dl")
    up_yc = swap(up_y, "c")
    got, x_forth, x_back, parity = lax.optimization_barrier(
        (got, turn(block, 1), turn(block, -1), core)
    )
    forth, back = [block, x_forth, turn(x_forth, 1)], [block, x_back, turn(x_back, -1)]
    got_c = swap(got, "c")
    got_y = swap(got, "dl")
    got_yc = swap(got_y, "c")
    near = pick(core, jnp.stack([got, got_c]), jnp.stack([got_c, got]))
    away = pick(core, jnp.stack([got_y, got_yc]), jnp.stack([got_yc, got_y]))
    every = pick(pair, jnp.stack([near, away]), jnp.stack([away, near]))
    every = every.transpose(2, 0, 1, 3, 4)
    if far > 1:
        every = lax.all_gather(every, "dh", axis=0)
    else:
        every = every[None]
    every = every.transpose(0, 2, 1, 3, 4, 5)
    w_qkv = jnp.concatenate(
        [every[..., i * rows : (i + 1) * rows, :].reshape(D, HEAD_DIM) for i in range(3)], axis=1
    )
    gain_all = every[..., 3 * rows + 3 * blocks, : 2 * rows].reshape(-1, 2, rows)
    gain_one = gain_all[:, 0].reshape(1, D)
    gain_two = gain_all[:, 1].reshape(1, D)

    def seg_of(blocks_of):
        return (
            blocks_of[:, 3 * rows : 3 * rows + blocks]
            .astype(WIDE)
            .astype(jnp.int32)
            .reshape(HEADS, count)
        )

    seg_own = seg_of(got)
    seg_oth = seg_of(got_c)
    idx = (
        got[:, 3 * rows + blocks : 3 * rows + 2 * blocks].astype(WIDE) * MEM_ROWS
        + got[:, 3 * rows + 2 * blocks : 3 * rows + 3 * blocks].astype(WIDE)
    ).astype(jnp.int32)
    idx = idx.reshape(HEADS, count, 1)

    block_docs = seg_own[:, ::QUERY_BLOCK]
    docs = second_doc.shape[1]
    doc_ids = jnp.arange(docs, dtype=jnp.int32)
    mates = jnp.sum(
        jnp.where(block_docs[:, :, None] == doc_ids, second_doc[0][None, None, :], 0), axis=-1
    )
    seg_all = jnp.concatenate([seg_own, seg_oth], axis=0)
    before = jnp.sum(
        (seg_all.reshape(1, -1) < block_docs[:, :1]).astype(jnp.int32), axis=1
    )
    tab = jnp.concatenate(
        [
            block_docs.reshape(-1),
            mates.reshape(-1),
            before // (2 * count),
            jnp.stack([core, chip]),
        ]
    ).astype(jnp.int32)

    half = HEAD_DIM // 2
    freqs = 10000.0 ** (-jnp.arange(half, dtype=WIDE) * 2.0 / (2 * half))
    positions = ((2 * slots + parity) * count)[:, None] + jnp.arange(count, dtype=jnp.int32)[None]
    turned = positions.astype(WIDE)[:, :, None] * freqs
    cosine, sine = jnp.cos(turned), jnp.sin(turned)
    cosine = jnp.concatenate([cosine, cosine], axis=-1)
    sine = jnp.concatenate([-sine, sine], axis=-1)

    seg_thin = seg_own.reshape(HEADS, count, 1)
    early = (w_qkv, gain_one, cosine, sine, tab, up_c, up_y, up_yc)
    early, gate_late, up_late, forth[2], back[2] = lax.optimization_barrier(
        (early, gate_weight, up_weight, forth[2], back[2])
    )
    w_qkv, gain_one, cosine, sine, tab, up_c, up_y, up_yc = early
    forth.append(turn(forth[2], 1))
    back.append(turn(back[2], -1))
    at_near, at_far = [0, 1, 7, 2, 6], [3, 5, 4]

    def chips_at(order):
        return at_place(mine - jnp.asarray(order, jnp.int32)).astype(jnp.int32)

    near_slots = [forth[0], forth[1], back[1], forth[2], back[2]]
    held = qkv_blocks(
        chips_at(at_near), [((v, count),) for v in near_slots], gain_one, w_qkv, cosine, sine, ()
    )
    half = units + -units % HEAD_DIM
    wide = 2 * half

    def by_owner(w):
        w = w.reshape(rows, far, 2, HEADS, 2, share).transpose(2, 4, 0, 1, 3, 5)
        return jnp.pad(w.reshape(2, 2, rows, units), ((0, 0),) * 3 + ((0, half - units),))

    gu = jnp.concatenate([by_owner(gate_late), by_owner(up_late)], axis=-1)
    kept = pick(core, gu[:, 0], gu[:, 1])
    came = swap(pick(core, gu[:, 1], gu[:, 0]), "c")
    gu = pick(core, jnp.stack([kept, came], 1), jnp.stack([came, kept], 1))
    kept = pick(pair, gu[0], gu[1])
    came = swap(pick(pair, gu[1], gu[0]), "dl")
    gu = pick(pair, jnp.stack([kept, came]), jnp.stack([came, kept])).reshape(4 * rows, wide)
    if far == 1:
        deep = 2 * rows
        lower = jnp.concatenate(fold(down_weight, deep), axis=1)
    else:
        deep = share
        lower = jnp.pad(down_weight, ((0, 0), (0, wide - D)))
    bundle = jnp.concatenate([gu, lower], axis=0)
    height = 4 * rows + share
    if far > 1:
        bundle = lax.all_gather(bundle, "dh", axis=0, tiled=True)
    upper = bundle.shape[0] // 2
    *held, bundle, forth[3], back[3] = lax.optimization_barrier(
        (*held, bundle, forth[3], back[3])
    )
    far_first, far_last = turn(forth[3][:split], 1), turn(back[3][split:], -1)
    bundle, *_ = lax.optimization_barrier((bundle, far_first, far_last))
    w_forth, w_back = [bundle, turn(bundle, 1)], [bundle, turn(bundle, -1)]

    far_slots = [
        ((forth[3], count),),
        ((back[3], count),),
        ((far_first, split), (far_last, count - split)),
    ]
    queries, own, normed_one = qkv_blocks(
        chips_at(at_far), far_slots, gain_one, w_qkv, cosine, sine, tuple(held)
    )
    outs = jnp.stack([v[-rows:] for v in (*forth, far_last, *back[:0:-1])])
    queries, own, outs, w_forth[1], w_back[1] = lax.optimization_barrier(
        (queries, own, outs, w_forth[1], w_back[1])
    )
    other = swap(own, "c")
    outs_c = swap(outs, "c")
    outs_y = swap(outs, "dl")
    seg_own_row = seg_own.reshape(HEADS, 1, count)
    seg_oth_row = seg_oth.reshape(HEADS, 1, count)
    cached = [cache[0].reshape(-1, D) for cache in (cache_keys, cache_values)]
    attention, attention_low, lse, memory = attend(
        tab, queries, own, other, seg_thin, seg_own_row, seg_oth_row, idx, *cached
    )
    w_forth.append(turn(w_forth[1], 1))
    w_back.append(turn(w_back[1], -1))
    attention_low, outs_y, w_forth[2], w_back[2] = lax.optimization_barrier(
        (attention_low, outs_y, w_forth[2], w_back[2])
    )

    heads = exchange(attention_low)
    w_forth.append(turn(w_forth[2], 1))
    w_back.append(turn(w_back[2], -1))
    outs_yc = swap(outs_y, "c")
    heads, w_forth[3], w_back[3] = lax.optimization_barrier((heads, w_forth[3], w_back[3]))
    w_first, w_last = turn(w_forth[3][:upper], 1), turn(w_back[3][upper:], -1)
    slot_of = lax.rem(mine - jnp.asarray(PLACE, jnp.int32) + HEADS, HEADS).astype(jnp.int32)
    if far == 1:
        sources = [outs, outs_c, outs_y, outs_yc]
    else:
        near = pick(core, jnp.stack([outs, outs_c], 1), jnp.stack([outs_c, outs], 1))
        away = pick(core, jnp.stack([outs_y, outs_yc], 1), jnp.stack([outs_yc, outs_y], 1))
        sources = pick(pair, jnp.stack([near, away]), jnp.stack([away, near]))
        sources = lax.all_gather(jnp.take(sources, slot_of, axis=1), "dh", axis=0)
        sources = [sources.reshape(D, D)]
    where = jnp.concatenate([chips, jnp.stack([pair, core])]).astype(jnp.int32)
    attended, mid, normed_two, out_w = out_block(where, heads, sources, x, gain_two)
    normed_two, w_first, w_last = lax.optimization_barrier((normed_two, w_first, w_last))
    w_slots = w_forth + [w_first, w_last] + w_back[:0:-1]

    if far == 1:
        gate_w, up_w, down_w = weights(where, w_slots, units)
    else:
        middle = jnp.concatenate(w_slots[HEADS // 2 : HEADS // 2 + 2], axis=0)
        every = jnp.stack(w_slots[: HEADS // 2] + [middle] + w_slots[HEADS // 2 + 2 :])
        every = jnp.take(every, slot_of, axis=0).reshape(HEADS, far, height, wide)
        gu = every[:, :, : 4 * rows].reshape(HEADS, far, 2, 2 * rows, wide)
        gu = gu.transpose(1, 2, 0, 3, 4).reshape(D, wide)
        gate_w, up_w = gu[:, :units], gu[:, half : half + units]
        down_w = every[:, :, 4 * rows :, :D].transpose(1, 0, 2, 3).reshape(units, D)

    n_c = swap(normed_two, "c")
    n_y = swap(normed_two, "dl")
    hid_l, gg_l, ug_l, dn_l, out_l = ffn(normed_two, n_c, upstream, up_c, gate_w, up_w, down_w)
    n_y, dn_l = lax.optimization_barrier((n_y, dn_l))
    n_yc = swap(n_y, "c")
    hid_r, gg_r, ug_r, dn_r, out_r = ffn(n_y, n_yc, up_y, up_yc, gate_w, up_w, down_w)

    def to_away(away):
        return (away[0].astype(WIDE) + swap(away[1], "c").astype(WIDE)).astype(LOW)

    there = to_away(dn_r)
    there, hid_l, gg_l, ug_l, hid_r, gg_r, ug_r = lax.optimization_barrier(
        (there, hid_l, gg_l, ug_l, hid_r, gg_r, ug_r)
    )
    n_all, u_all = [normed_two, n_c, n_y, n_yc], [upstream, up_c, up_y, up_yc]
    near, away = (hid_l, gg_l, ug_l), (hid_r, gg_r, ug_r)
    if far == 1:
        parts = weight_grads(slot_of, n_all, u_all, near, away, height, wide)
    else:

        def over_tokens(left, right):
            return jnp.einsum(
                "gtd,gtf->df", left, right, preferred_element_type=WIDE
            ).astype(LOW)

        def by_rows(w):
            w = jnp.pad(w, ((0, 0), (0, half - units)))
            return w.reshape(far, 2, HEADS, 2 * rows, half).transpose(2, 0, 1, 3, 4)

        n_all, u_all = jnp.stack(n_all), jnp.stack(u_all)
        hid, gg, ug = (jnp.concatenate(pieces, axis=0) for pieces in zip(near, away))
        gu = jnp.concatenate(
            [by_rows(over_tokens(n_all, gg)), by_rows(over_tokens(n_all, ug))], axis=-1
        ).reshape(HEADS, far, 4 * rows, wide)
        down = over_tokens(hid, u_all).reshape(far, HEADS, share, D).transpose(1, 0, 2, 3)
        down = jnp.pad(down, ((0, 0), (0, 0), (0, 0), (0, wide - D)))
        parts = jnp.concatenate([gu, down], axis=2)
        parts = jnp.take(parts.reshape(HEADS, far * height, wide), chips, axis=0)

    out_l, out_r, _ = lax.optimization_barrier((out_l, out_r, parts))
    output = mid
    for part in (out_l[0], swap(out_l[1], "c"), swap(to_away(out_r), "dl")):
        output = output + part.astype(WIDE)
    output = output.astype(LOW)

    sums = [dn_l[0], swap(dn_l[1], "c"), swap(there, "dl")]
    sums[2], parts = lax.optimization_barrier((sums[2], parts))
    mid_grad, branch, att_grad = mid_block(mid, *sums, upstream, gain_two, out_w)
    ups = exchange(att_grad)

    def plus(block, arrived, start):
        size = arrived.shape[0]
        total = block[start : start + size].astype(WIDE) + arrived.astype(WIDE)
        pieces = [block[:start], total, block[start + size :]]
        pieces = [piece.astype(LOW) for piece in pieces if piece.shape[0]]
        return jnp.concatenate(pieces, axis=0)

    def ring_first(blocks, split):
        middle = blocks[HEADS // 2]
        return (
            plus(blocks[HEADS // 2 + 1], turn(middle[:split].astype(LOW), 1), 0),
            plus(blocks[HEADS // 2 - 1], turn(middle[split:].astype(LOW), -1), split),
        )

    def ring_next(blocks, forth, back, step):
        return (
            plus(blocks[HEADS // 2 + step], turn(forth, 1), 0),
            plus(blocks[HEADS // 2 - step], turn(back, -1), 0),
        )

    def ring_last(blocks, forth, back):
        return blocks[0].astype(WIDE) + forth.astype(WIDE) + back.astype(WIDE)

    def over_owner(w, width):
        w = w.reshape(far, 2, HEADS, 2, rows, width)
        kept = pick(core, w[:, :, :, 0], w[:, :, :, 1])
        came = swap(pick(core, w[:, :, :, 1], w[:, :, :, 0]), "c")
        w = kept.astype(WIDE) + came.astype(WIDE)
        kept = pick(pair, w[:, 0], w[:, 1])
        came = swap(pick(pair, w[:, 1], w[:, 0]).astype(LOW), "dl")
        w = (kept + came.astype(WIDE)).astype(LOW)
        if far > 1:
            w = lax.psum_scatter(w, "dh", scatter_dimension=0, tiled=True)
        return w[0]

    out_part = over_owner(
        jnp.einsum("td,te->de", attended, branch, preferred_element_type=WIDE).astype(LOW), D
    )
    strip = wide - D
    upper = 4 * rows if far == 1 else parts.shape[1] // 2
    blocks = [parts[slot].astype(WIDE) for slot in range(HEADS)]
    if far == 1:
        strips = out_strips(where, out_part, strip)
        below = share - strips.shape[1]
        for slot in range(HEADS):
            if slot != HEADS // 2:
                blocks[slot] = blocks[slot] + jnp.pad(
                    strips[slot].astype(WIDE), ((4 * rows, below), (D, 0))
                )
        out_far = turn(strips[HEADS // 2], HEADS // 2)
    else:
        out_far = exchange(out_part)
    forth, back = ring_first(blocks, upper)
    ups, forth, back = lax.optimization_barrier((ups, forth, back))
    forth, back = ring_next(blocks, forth, back, 2)

    dq, d_own, d_oth = attend_back(
        tab, queries, ups, attention, lse, own, other, memory, seg_thin, seg_own_row, seg_oth_row
    )
    d_got = swap(d_oth, "c")
    dq, forth, back = lax.optimization_barrier((dq, forth, back))
    dx, dw = qkv_back(
        chips.astype(jnp.int32), dq, d_own, d_got, cosine, sine, normed_one, w_qkv
    )
    arrived_forth, arrived_back = turn(forth, 1), turn(back, -1)
    dx, arrived_forth, arrived_back = lax.optimization_barrier((dx, arrived_forth, arrived_back))
    dx_forth, dx_back = ring_first(dx, split)
    dw, dx_forth, dx_back, arrived_forth, arrived_back = lax.optimization_barrier(
        (dw, dx_forth, dx_back, arrived_forth, arrived_back)
    )
    forth = plus(blocks[HEADS - 1], arrived_forth, 0)
    back = plus(blocks[1], arrived_back, 0)

    dw = over_owner(dw, 3 * HEAD_DIM)
    dx_forth, dx_back = ring_next(dx, dx_forth, dx_back, 2)
    dw, dx_forth, dx_back = lax.optimization_barrier((dw, dx_forth, dx_back))
    qkv_grads = exchange(dw).astype(WIDE)
    dx_forth, dx_back = ring_next(dx, dx_forth, dx_back, 3)
    normed_one_grad = ring_last(dx, turn(dx_forth, 1), turn(dx_back, -1))

    summed = ring_last(blocks, turn(forth, 1), turn(back, -1)).astype(LOW)
    if far > 1:
        summed = lax.psum_scatter(summed, "dh", scatter_dimension=0, tiled=True)
    down_w_grad = summed[4 * rows : 4 * rows + share, :D].astype(WIDE)
    if far == 1:
        out_w_grad = summed[4 * rows : 4 * rows + strips.shape[1], D:].astype(WIDE)
        out_w_grad = out_w_grad + out_far.astype(WIDE)
        out_w_grad = out_w_grad.reshape(D // strip, rows, strip).transpose(1, 0, 2).reshape(rows, D)
    else:
        out_w_grad = jnp.sum(out_far.astype(WIDE), axis=0)
    gu = summed[: 4 * rows].reshape(2, 2, rows, wide)
    kept = pick(core, gu[:, 0], gu[:, 1])
    came = swap(pick(core, gu[:, 1], gu[:, 0]), "c")
    gu = pick(core, jnp.stack([kept, came], 1), jnp.stack([came, kept], 1))
    kept = pick(pair, gu[0], gu[1])
    came = swap(pick(pair, gu[1], gu[0]), "dl")
    gu = pick(pair, jnp.stack([kept, came]), jnp.stack([came, kept]))
    gu = jnp.stack([gu[..., :units], gu[..., half : half + units]])
    gu = (
        gu.reshape(2, 2, 2, rows, far, HEADS, share)
        .transpose(0, 3, 4, 1, 5, 2, 6)
        .reshape(2, rows, FF)
        .astype(WIDE)
    )
    gate_w_grad, up_w_grad = gu[0], gu[1]

    wide_x = x.astype(WIDE)
    r = lax.rsqrt(jnp.mean(wide_x * wide_x, axis=-1, keepdims=True) + EPSILON)
    scaled = normed_one_grad * gain_one.astype(WIDE)
    inner = jnp.mean(scaled * wide_x, axis=-1, keepdims=True)
    input_grad = mid_grad + r * scaled - wide_x * (r * r * r * inner)

    q_w_grad, k_w_grad, v_w_grad = (
        qkv_grads[:, :, i * HEAD_DIM : (i + 1) * HEAD_DIM].transpose(1, 0, 2).reshape(rows, D)
        for i in range(3)
    )

    def gain_grad(gain, pairs):
        total = 0.0
        for grad, weight in pairs:
            total = total + jnp.sum(grad * weight.astype(WIDE), axis=1)
        return total / gain.astype(WIDE)

    first_gain_grad = gain_grad(
        first_gain,
        ((q_w_grad, query_weight), (k_w_grad, key_weight), (v_w_grad, value_weight)),
    )
    second_gain_grad = gain_grad(
        second_gain, ((gate_w_grad, gate_weight), (up_w_grad, up_weight))
    )
    return (
        output[None],
        input_grad[None],
        first_gain_grad,
        q_w_grad,
        k_w_grad,
        v_w_grad,
        out_w_grad,
        second_gain_grad,
        gate_w_grad,
        up_w_grad,
        down_w_grad,
    )


def solution(mesh):
    far = mesh.shape["dp"] // 2
    cores = mesh.shape["seq"] // HEADS
    fine = Mesh(mesh.devices.reshape(far, 2, HEADS, cores), ("dh", "dl", "h", "c"))
    dp, seq, every = ("dh", "dl"), ("h", "c"), ("dh", "dl", "h", "c")
    rows = P(every, None)
    return jax.shard_map(
        functools.partial(local, far),
        mesh=fine,
        in_specs=(
            P(dp, seq, None),
            P(dp, seq),
            P(dp, None),
            P(dp, seq, None, None),
            P(dp, None, None, None),
            P(dp, None, None, None),
            P(every),
            rows,
            rows,
            rows,
            rows,
            P(every),
            rows,
            rows,
            rows,
            P(dp, seq, None),
        ),
        out_specs=(
            P(dp, seq, None),
            P(dp, seq, None),
            P(every),
            rows,
            rows,
            rows,
            rows,
            P(every),
            rows,
            rows,
            rows,
        ),
        check_vma=False,
    )
```

```python
import functools
import math

import jax
import jax.numpy as jnp
import numpy as np
from jax import lax
from jax.experimental import pallas as pl
from jax.experimental.pallas import tpu as pltpu
from jax.sharding import Mesh
from jax.sharding import PartitionSpec as P

D = 1024
FF = 2816
HEADS = 8
HEAD_DIM = 128
QUERY_BLOCK = 128
MEM_ROWS = 256
EPSILON = 1e-05
NEGATIVE = -1e30
SCALE = 1.0 / math.sqrt(HEAD_DIM)
LOG2 = SCALE * math.log2(math.e)
LOW = jnp.bfloat16
WIDE = jnp.float32

RING = [2 * i for i in range(HEADS // 2)] + [2 * i + 1 for i in reversed(range(HEADS // 2))]
PLACE = [RING.index(i) for i in range(HEADS)]


def dot_nn(a, b):
    return lax.dot_general(a, b, (((1,), (0,)), ((), ())), preferred_element_type=WIDE)


def dot_nt(a, b):
    return lax.dot_general(a, b, (((1,), (1,)), ((), ())), preferred_element_type=WIDE)


def dot_tn(a, b):
    return lax.dot_general(a, b, (((0,), (0,)), ((), ())), preferred_element_type=WIDE)


def swap(block, axis):
    return lax.ppermute(block, axis, [(0, 1), (1, 0)])


def turn(block, distance):
    route = [(RING[i], RING[(i + distance) % HEADS]) for i in range(HEADS)]
    return lax.ppermute(block, "h", route)


def at_place(place):
    place = lax.rem(place + 2 * HEADS, HEADS)
    return jnp.where(place < HEADS // 2, 2 * place, 2 * (HEADS - 1 - place) + 1)


def exchange(blocks):
    return lax.all_to_all(blocks, "h", 0, 0)


def pick(flag, first, second):
    return jnp.where(flag == 0, first, second)


def smem():
    return pl.BlockSpec(memory_space=pltpu.SMEM)


def vmem():
    return pl.BlockSpec(memory_space=pltpu.VMEM)


def turn_tables(count):
    half = HEAD_DIM // 2
    freqs = 10000.0 ** (-np.arange(half, dtype=np.float64) * 2.0 / HEAD_DIM)
    freqs = np.concatenate([freqs, freqs])

    def table(positions):
        angles = positions[:, None] * freqs
        return np.stack([np.cos(angles), np.sin(angles)]).astype(np.float32)

    return table(np.arange(count)), table(np.arange(2 * HEADS) * count).transpose(1, 0, 2)


def turning(loc_ref, base_ref):
    cl, sl = loc_ref[0], loc_ref[1]
    cb, sb = base_ref[0, 0:1, :], base_ref[0, 1:2, :]
    sine = sl * cb + cl * sb
    lane = lax.broadcasted_iota(jnp.int32, sine.shape, 1)
    return cl * cb - sl * sb, jnp.where(lane < HEAD_DIM // 2, -sine, sine)


def qkv_kernel(parts, tab, *refs):
    xs, (gain_ref, w_ref, loc_ref, base_ref) = refs[: sum(parts)], refs[sum(parts) : sum(parts) + 4]
    q_ref, kv_ref, n_ref, x_ref = refs[-4:]
    i = pl.program_id(0)
    first = 0
    for step, number in enumerate(parts):

        @pl.when(i == step)
        def _(blocks=xs[first : first + number]):
            row = 0
            for block in blocks:
                size = block.shape[0]
                x_ref[row : row + size, :] = block[...]
                row += size

        first += number
    x = x_ref[...].astype(WIDE)
    r = lax.rsqrt(jnp.mean(x * x, axis=-1, keepdims=True) + EPSILON)
    normed = (x * r * gain_ref[...].astype(WIDE)).astype(LOW)
    n_ref[0] = normed
    out = dot_nn(normed, w_ref[...])
    c, s = turning(loc_ref, base_ref)

    def rot(v):
        return v * c + pltpu.roll(v, HEAD_DIM // 2, 1) * s

    q_ref[0] = rot(out[:, :HEAD_DIM]).astype(LOW)
    kv_ref[0, 0] = rot(out[:, HEAD_DIM : 2 * HEAD_DIM]).astype(LOW)
    kv_ref[1, 0] = out[:, 2 * HEAD_DIM :].astype(LOW)


def qkv_blocks(chips, xs, gain, w, loc, base, held):
    count = loc.shape[1]
    steps = len(xs)
    flat = [piece for block in xs for piece, _ in block]
    read = [size for block in xs for _, size in block]

    def whole(shape):
        return pl.BlockSpec(shape, lambda i, t: (0, 0))

    def block(*shape):
        return pl.BlockSpec((1, *shape), lambda i, t: (t[i], 0, 0))

    spec = pltpu.PrefetchScalarGridSpec(
        num_scalar_prefetch=1,
        grid=(len(xs),),
        in_specs=[whole((size, D)) for size in read]
        + [
            whole((1, D)),
            whole((D, 3 * HEAD_DIM)),
            pl.BlockSpec((2, count, HEAD_DIM), lambda i, t: (0, 0, 0)),
            pl.BlockSpec((1, 2, HEAD_DIM), lambda i, t: (2 * t[i] + t[steps], 0, 0)),
        ]
        + [pl.BlockSpec(memory_space=pl.ANY)] * len(held),
        out_specs=[
            block(count, HEAD_DIM),
            pl.BlockSpec((2, 1, count, HEAD_DIM), lambda i, t: (0, t[i], 0, 0)),
            block(count, D),
        ],
        scratch_shapes=[pltpu.VMEM((count, D), LOW)],
    )
    return pl.pallas_call(
        functools.partial(qkv_kernel, [len(block) for block in xs]),
        grid_spec=spec,
        out_shape=[
            jax.ShapeDtypeStruct((HEADS, count, HEAD_DIM), LOW),
            jax.ShapeDtypeStruct((2, HEADS, count, HEAD_DIM), LOW),
            jax.ShapeDtypeStruct((HEADS, count, D), LOW),
        ],
        input_output_aliases={len(flat) + 5 + i: i for i in range(len(held))},
        cost_estimate=pl.CostEstimate(
            flops=len(xs) * count * D, bytes_accessed=len(xs) * count, transcendentals=0
        ),
        name=f"qkv{len(xs)}",
    )(chips, *flat, gain, w, loc, base, *held)


def causal(count):
    rows = lax.broadcasted_iota(jnp.int32, (count, count), 0)
    return lax.broadcasted_iota(jnp.int32, (count, count), 1) <= rows


def attend_kernel(
    tab, q_ref, own_ref, oth_ref, segq_ref, sego_ref, segt_ref, idx_ref, ck_ref, cv_ref,
    o_ref, low_ref, lse_ref, mem_ref,
):
    i = pl.program_id(0)
    parity = tab[40]
    count = q_ref.shape[1]
    q = q_ref[0]
    segq = segq_ref[0]

    s1 = dot_nt(q, own_ref[0, i]) * LOG2
    s2 = dot_nt(q, oth_ref[0, i]) * LOG2
    s1 = jnp.where((sego_ref[i] == segq) & causal(count), s1, NEGATIVE)
    s2 = jnp.where(segt_ref[i] == segq + 64 * (1 - parity), s2, NEGATIVE)
    memory = []
    for b in range(count // QUERY_BLOCK):
        rows = slice(b * QUERY_BLOCK, (b + 1) * QUERY_BLOCK)
        doc = tab[2 * i + b]
        mate = tab[16 + 2 * i + b]
        idx = idx_ref[0, rows, :]
        lane = lax.broadcasted_iota(jnp.int32, (QUERY_BLOCK, MEM_ROWS), 1)
        first = jnp.where(idx == lane, 1.0, 0.0).astype(LOW)
        second = jnp.where(idx == lane + MEM_ROWS, 1.0, 0.0).astype(LOW)
        here = pl.ds(pl.multiple_of(doc * MEM_ROWS, MEM_ROWS), MEM_ROWS)
        there = pl.ds(pl.multiple_of(mate * MEM_ROWS, MEM_ROWS), MEM_ROWS)
        mk = (dot_nn(first, ck_ref[here, :]) + dot_nn(second, ck_ref[there, :])).astype(LOW)
        mv = (dot_nn(first, cv_ref[here, :]) + dot_nn(second, cv_ref[there, :])).astype(LOW)
        mem_ref[0, 0, rows, :] = mk
        mem_ref[1, 0, rows, :] = mv
        s = jnp.where(segq[rows] == doc, dot_nt(q[rows], mk) * LOG2, NEGATIVE)
        memory.append((s, mv))
    sm = jnp.concatenate([s for s, _ in memory], axis=0)
    top = jnp.maximum(
        jnp.max(jnp.maximum(s1, s2), axis=-1, keepdims=True), jnp.max(sm, axis=-1, keepdims=True)
    )
    p1 = jnp.exp2(s1 - top)
    p2 = jnp.exp2(s2 - top)
    pm = jnp.exp2(sm - top)
    total = jnp.sum(p1 + p2, axis=-1, keepdims=True) + jnp.sum(pm, axis=-1, keepdims=True)
    pm = pm.astype(LOW)
    acc = jnp.concatenate(
        [
            dot_nn(pm[b * QUERY_BLOCK : (b + 1) * QUERY_BLOCK], mv)
            for b, (_, mv) in enumerate(memory)
        ],
        axis=0,
    )
    acc = acc + dot_nn(p1.astype(LOW), own_ref[1, i]) + dot_nn(p2.astype(LOW), oth_ref[1, i])

    def body(j, state):
        top, total, acc = state
        s1 = dot_nt(q, own_ref[0, j]) * LOG2
        s2 = dot_nt(q, oth_ref[0, j]) * LOG2
        s1 = jnp.where(sego_ref[j] == segq, s1, NEGATIVE)
        s2 = jnp.where(segt_ref[j] == segq, s2, NEGATIVE)
        fresh = jnp.maximum(top, jnp.max(jnp.maximum(s1, s2), axis=-1, keepdims=True))
        p1 = jnp.exp2(s1 - fresh)
        p2 = jnp.exp2(s2 - fresh)
        decay = jnp.exp2(top - fresh)
        total = total * decay + jnp.sum(p1 + p2, axis=-1, keepdims=True)
        acc = (
            acc * decay
            + dot_nn(p1.astype(LOW), own_ref[1, j])
            + dot_nn(p2.astype(LOW), oth_ref[1, j])
        )
        return fresh, total, acc

    top, total, acc = lax.fori_loop(tab[32 + i], i, body, (top, total, acc))
    out = acc / total
    o_ref[0] = out
    low_ref[0] = out.astype(LOW)
    lse_ref[0] = top + jnp.log2(total)


def attend(tab, q, own, oth, segq, sego, segt, idx, ck, cv):
    count = q.shape[1]
    block = pl.BlockSpec((1, count, HEAD_DIM), lambda i, t: (i, 0, 0))
    thin = pl.BlockSpec((1, count, 1), lambda i, t: (i, 0, 0))
    whole = pl.BlockSpec((2, HEADS, count, HEAD_DIM), lambda i, t: (0, 0, 0, 0))
    segs = pl.BlockSpec((HEADS, 1, count), lambda i, t: (0, 0, 0))
    cache = pl.BlockSpec((ck.shape[0], HEAD_DIM), lambda i, t: (0, t[41]))
    mem = pl.BlockSpec((2, 1, count, HEAD_DIM), lambda i, t: (0, i, 0, 0))
    return pl.pallas_call(
        attend_kernel,
        grid_spec=pltpu.PrefetchScalarGridSpec(
            num_scalar_prefetch=1,
            grid=(HEADS,),
            in_specs=[block, whole, whole, thin, segs, segs, thin, cache, cache],
            out_specs=[block, block, thin, mem],
        ),
        out_shape=[
            jax.ShapeDtypeStruct((HEADS, count, HEAD_DIM), WIDE),
            jax.ShapeDtypeStruct((HEADS, count, HEAD_DIM), LOW),
            jax.ShapeDtypeStruct((HEADS, count, 1), WIDE),
            jax.ShapeDtypeStruct((2, HEADS, count, HEAD_DIM), LOW),
        ],
        cost_estimate=pl.CostEstimate(
            flops=25 * 10**9, bytes_accessed=6 * 2**20, transcendentals=3 * 10**6
        ),
        name="attend",
    )(tab, q, own, oth, segq, sego, segt, idx, ck, cv)


def attend_back_kernel(
    tab, q_ref, up_ref, o_ref, lse_ref, own_ref, oth_ref, mem_ref, segq_ref, sego_ref, segt_ref,
    dq_ref, down_ref, doth_ref, sum_ref,
):
    i = pl.program_id(0)

    @pl.when(i == 0)
    def _():
        sum_ref[...] = jnp.zeros_like(sum_ref)

    parity = tab[40]
    count = q_ref.shape[1]
    q = q_ref[0]
    up = up_ref[0]
    lse = lse_ref[0]
    segq = segq_ref[0]
    delta = jnp.sum(up.astype(WIDE) * o_ref[0], axis=-1, keepdims=True)
    partial = []
    for b in range(count // QUERY_BLOCK):
        rows = slice(b * QUERY_BLOCK, (b + 1) * QUERY_BLOCK)
        mk = mem_ref[0, 0, rows, :]
        mv = mem_ref[1, 0, rows, :]
        ok = segq[rows] == tab[2 * i + b]
        p = jnp.exp2(jnp.where(ok, dot_nt(q[rows], mk) * LOG2 - lse[rows], NEGATIVE))
        ds = (p * (dot_nt(up[rows], mv) - delta[rows])).astype(LOW)
        partial.append(dot_nn(ds, mk))

    def tile(side, ref, j, ok, dq):
        k = ref[0, j]
        v = ref[1, j]
        p = jnp.exp2(jnp.where(ok, dot_nt(q, k) * LOG2 - lse, NEGATIVE))
        ds = (p * (dot_nt(up, v) - delta)).astype(LOW)
        sum_ref[side, 0, j] += dot_tn(ds, q)
        sum_ref[side, 1, j] += dot_tn(p.astype(LOW), up)
        return dq + dot_nn(ds, k)

    dq = jnp.concatenate(partial, axis=0)
    dq = tile(0, own_ref, i, (sego_ref[i] == segq) & causal(count), dq)
    dq = tile(1, oth_ref, i, segt_ref[i] == segq + 64 * (1 - parity), dq)

    def body(j, dq):
        dq = tile(0, own_ref, j, sego_ref[j] == segq, dq)
        return tile(1, oth_ref, j, segt_ref[j] == segq, dq)

    dq_ref[0] = lax.fori_loop(tab[32 + i], i, body, dq)

    @pl.when(i == HEADS - 1)
    def _():
        down_ref[...] = sum_ref[0]
        doth_ref[...] = sum_ref[1].astype(LOW)


def attend_back(tab, q, up, o, lse, own, oth, mem, segq, sego, segt):
    count = q.shape[1]
    block = pl.BlockSpec((1, count, HEAD_DIM), lambda i, t: (i, 0, 0))
    thin = pl.BlockSpec((1, count, 1), lambda i, t: (i, 0, 0))
    whole = pl.BlockSpec((2, HEADS, count, HEAD_DIM), lambda i, t: (0, 0, 0, 0))
    segs = pl.BlockSpec((HEADS, 1, count), lambda i, t: (0, 0, 0))
    memory = pl.BlockSpec((2, 1, count, HEAD_DIM), lambda i, t: (0, i, 0, 0))
    return pl.pallas_call(
        attend_back_kernel,
        grid_spec=pltpu.PrefetchScalarGridSpec(
            num_scalar_prefetch=1,
            grid=(HEADS,),
            in_specs=[block, block, block, thin, whole, whole, memory, thin, segs, segs],
            out_specs=[block, whole, whole],
            scratch_shapes=[pltpu.VMEM((2, 2, HEADS, count, HEAD_DIM), WIDE)],
        ),
        out_shape=[
            jax.ShapeDtypeStruct((HEADS, count, HEAD_DIM), WIDE),
            jax.ShapeDtypeStruct((2, HEADS, count, HEAD_DIM), WIDE),
            jax.ShapeDtypeStruct((2, HEADS, count, HEAD_DIM), LOW),
        ],
        cost_estimate=pl.CostEstimate(
            flops=30 * 10**9, bytes_accessed=10 * 2**20, transcendentals=3 * 10**6
        ),
        name="attend_back",
    )(tab, q, up, o, lse, own, oth, mem, segq, sego, segt)


def place_rows(tab, sources, w_ref):
    rows = sources[0].shape[1]
    for k, source in enumerate(sources):
        pair = tab[8] if k < 2 else 1 - tab[8]
        core = tab[9] if k % 2 == 0 else 1 - tab[9]
        for slot in range(HEADS):
            start = ((pair * HEADS + tab[slot]) * 2 + core) * rows
            w_ref[pl.ds(pl.multiple_of(start, rows), rows), :] = source[slot]


def out_kernel(tab, heads_ref, *refs):
    sources, (x_ref, gain_ref, att_ref, mid_ref, n_ref, w_ref) = refs[:-6], refs[-6:]
    if len(sources) == 1:
        w_ref[...] = sources[0][...]
    else:
        place_rows(tab, sources, w_ref)
    for h in range(HEADS):
        att_ref[:, h * HEAD_DIM : (h + 1) * HEAD_DIM] = heads_ref[h]
    mid = x_ref[...].astype(WIDE) + dot_nn(att_ref[...], w_ref[...])
    mid_ref[...] = mid
    r = lax.rsqrt(jnp.mean(mid * mid, axis=-1, keepdims=True) + EPSILON)
    n_ref[...] = (mid * r * gain_ref[...].astype(WIDE)).astype(LOW)


def out_block(tab, heads, sources, x, gain):
    count = x.shape[0]
    return pl.pallas_call(
        out_kernel,
        in_specs=[smem()] + [vmem()] * (3 + len(sources)),
        out_specs=[vmem()] * 4,
        out_shape=[
            jax.ShapeDtypeStruct((count, D), LOW),
            jax.ShapeDtypeStruct((count, D), WIDE),
            jax.ShapeDtypeStruct((count, D), LOW),
            jax.ShapeDtypeStruct((D, D), LOW),
        ],
        cost_estimate=pl.CostEstimate(
            flops=2 * count * D * D, bytes_accessed=6 * 2**20, transcendentals=0
        ),
        name="out_block",
    )(tab, heads, *sources, x, gain)


def fold(block, deep):
    half, rest = D // 2, block.shape[0] - deep
    middle = jnp.concatenate([block[deep:, :half], block[: deep - rest, half:]], axis=0)
    last = block[deep - rest :, half:]
    last = jnp.concatenate([last, jnp.zeros((deep - last.shape[0], half), last.dtype)], axis=0)
    return block[:deep, :half], middle, last


def unfolded(block, share):
    deep, half = block.shape[0], D // 2
    rest = share - deep
    return [
        (0, deep, 0, block[:, :half]),
        (deep, rest, 0, block[:rest, half:D]),
        (0, deep - rest, half, block[rest:, half:D]),
        (deep - rest, share - deep + rest, half, block[: share - deep + rest, D:]),
    ]


def weights_kernel(tab, *refs):
    blocks, (gate_ref, up_ref, down_ref, acc_ref) = refs[:-4], refs[-4:]
    units = gate_ref.shape[1]
    height, wide = blocks[0].shape
    half = wide // 2
    share = units // HEADS
    rows = D // (2 * HEADS)
    middle = blocks[HEADS // 2].shape[0]
    for slot in range(HEADS):
        chip = tab[slot]
        if slot == HEADS // 2:
            pieces = [(0, blocks[slot]), (middle, blocks[slot + 1])]
        else:
            pieces = [(0, blocks[slot if slot < HEADS // 2 else slot + 1])]
        for start, ref in pieces:
            stop = start + ref.shape[0]
            for pair in range(2):
                first, last = max(start, pair * rows), min(stop, (pair + 1) * rows)
                if first < last:
                    size = last - first
                    here = (pair * HEADS + chip) * rows + first - pair * rows
                    here = pl.ds(pl.multiple_of(here, math.gcd(rows, first)), size)
                    gate_ref[here, :] = ref[first - start : last - start, :units]
                    up_ref[here, :] = ref[first - start : last - start, half : half + units]
        lower = ref[2 * rows - start :, :].astype(WIDE)
        for row, size, column, piece in unfolded(lower, share):
            here = pl.ds(pl.multiple_of(chip * share + row, 8), size)
            acc_ref[here, column : column + D // 2] = piece
    down_ref[...] = acc_ref[...].astype(LOW)


def weights(chips, blocks, units):
    return pl.pallas_call(
        weights_kernel,
        in_specs=[smem()] + [vmem()] * len(blocks),
        out_specs=[vmem()] * 3,
        out_shape=[
            jax.ShapeDtypeStruct((D, units), LOW),
            jax.ShapeDtypeStruct((D, units), LOW),
            jax.ShapeDtypeStruct((units, D), LOW),
        ],
        scratch_shapes=[pltpu.VMEM((units, D), WIDE)],
        cost_estimate=pl.CostEstimate(
            flops=0, bytes_accessed=12 * D * units, transcendentals=0
        ),
        name="weights",
    )(chips, *blocks)


def ffn_kernel(na, nb, ga, gb, g_ref, u_ref, d_ref, hid_ref, gg_ref, ug_ref, dn_ref, out_ref, n_ref, c_ref):
    for step, (tokens, cotangent) in enumerate(((na, ga), (nb, gb))):

        @pl.when(pl.program_id(0) == step)
        def _(tokens=tokens, cotangent=cotangent):
            n_ref[...] = tokens[...]
            c_ref[...] = cotangent[...]

    n = n_ref[...]
    gate = dot_nn(n, g_ref[...])
    upper = dot_nn(n, u_ref[...])
    sigma = jax.nn.sigmoid(gate)
    silu = gate * sigma
    hid = (silu * upper).astype(LOW)
    hid_ref[0] = hid
    hg = dot_nt(c_ref[...], d_ref[...])
    gg = (hg * upper * sigma * (1.0 + gate * (1.0 - sigma))).astype(LOW)
    ug = (hg * silu).astype(LOW)
    gg_ref[0] = gg
    ug_ref[0] = ug
    dn_ref[0] = (dot_nt(gg, g_ref[...]) + dot_nt(ug, u_ref[...])).astype(LOW)
    out_ref[0] = dot_nn(hid, d_ref[...]).astype(LOW)


def ffn(na, nb, ga, gb, g, u, d):
    count = na.shape[0]
    units = g.shape[1]

    def whole(rows, columns):
        return pl.BlockSpec((rows, columns), lambda i: (0, 0))

    def block(columns):
        return pl.BlockSpec((1, count, columns), lambda i: (i, 0, 0))

    return pl.pallas_call(
        ffn_kernel,
        grid=(2,),
        in_specs=[whole(count, D)] * 4 + [whole(D, units)] * 2 + [whole(units, D)],
        out_specs=[block(units)] * 3 + [block(D)] * 2,
        scratch_shapes=[pltpu.VMEM((count, D), LOW)] * 2,
        out_shape=[jax.ShapeDtypeStruct((2, count, units), LOW)] * 3
        + [jax.ShapeDtypeStruct((2, count, D), LOW)] * 2,
        cost_estimate=pl.CostEstimate(
            flops=24 * count * D * units,
            bytes_accessed=6 * D * units + 16 * count * D,
            transcendentals=2 * count * units,
        ),
        name="ffn",
    )(na, nb, ga, gb, g, u, d)


def grads_kernel(tab, *refs):
    ns, ups, (hid_l, gg_l, ug_l, hid_r, gg_r, ug_r, parts_ref) = (
        refs[:4], refs[4:8], refs[8:],
    )
    wide = parts_ref.shape[2]
    half = wide // 2
    units = hid_l.shape[2]
    share = units // HEADS
    rows = ns[0].shape[1] // (2 * HEADS)
    edge = units - units % HEAD_DIM

    def tokens(near, away):
        return jnp.concatenate([near[0], near[1], away[0], away[1]], axis=0)

    n = jnp.concatenate([v[...] for v in ns], axis=0)
    up = jnp.concatenate([v[...] for v in ups], axis=0)
    for near, away, start in ((gg_l, gg_r, 0), (ug_l, ug_r, half)):
        total = dot_tn(n, tokens(near, away)).astype(LOW)
        for h in range(HEADS):
            slot = tab[h]
            for pair in range(2):
                first = (pair * HEADS + h) * rows
                here = slice(pair * rows, (pair + 1) * rows)
                parts_ref[slot, here, start + edge : start + half] = jnp.zeros(
                    (rows, half - edge), LOW
                )
                parts_ref[slot, here, start : start + units] = total[first : first + rows]
    total = dot_tn(tokens(hid_l, hid_r), up)
    strip = wide - D
    for h in range(HEADS):
        slot = tab[h]
        piece = total[h * share : (h + 1) * share].astype(LOW)
        parts_ref[slot, 2 * rows : 2 * rows + share, :D] = piece
        parts_ref[slot, 2 * rows : 2 * rows + share, D:] = jnp.zeros((share, strip), LOW)


def weight_grads(slot_of, ns, ups, near, away, height, wide):
    count = ns[0].shape[0]
    units = near[0].shape[2]
    return pl.pallas_call(
        grads_kernel,
        in_specs=[smem()] + [vmem()] * 14,
        out_specs=vmem(),
        out_shape=jax.ShapeDtypeStruct((HEADS, height, wide), LOW),
        cost_estimate=pl.CostEstimate(
            flops=24 * count * D * units, bytes_accessed=14 * 2**20, transcendentals=0
        ),
        name="weight_grads",
    )(slot_of, *ns, *ups, *near, *away)


def strips_kernel(tab, out_ref, strips_ref):
    rows, strip = out_ref.shape[1], strips_ref.shape[2]
    for slot in range(HEADS):
        for i in range(D // strip):
            strips_ref[slot, i * rows : (i + 1) * rows, :] = out_ref[
                tab[slot], :, i * strip : (i + 1) * strip
            ]


def out_strips(chips, out, strip):
    return pl.pallas_call(
        strips_kernel,
        in_specs=[smem(), vmem()],
        out_specs=vmem(),
        out_shape=jax.ShapeDtypeStruct((HEADS, out.shape[1] * D // strip, strip), LOW),
        cost_estimate=pl.CostEstimate(
            flops=0, bytes_accessed=4 * HEADS * out.shape[1] * D, transcendentals=0
        ),
        name="out_strips",
    )(chips, out)


def mid_kernel(mid_ref, pa, pb, pc, up_ref, gain_ref, w_ref, mg_ref, bg_ref, ag_ref):
    mid = mid_ref[...]
    scaled = (pa[...].astype(WIDE) + pb[...].astype(WIDE) + pc[...].astype(WIDE)) * gain_ref[
        ...
    ].astype(WIDE)
    r = lax.rsqrt(jnp.mean(mid * mid, axis=-1, keepdims=True) + EPSILON)
    inner = jnp.mean(scaled * mid, axis=-1, keepdims=True)
    mid_grad = up_ref[...].astype(WIDE) + r * scaled - mid * (r * r * r * inner)
    mg_ref[...] = mid_grad
    branch = mid_grad.astype(LOW)
    bg_ref[...] = branch
    att = dot_nt(branch, w_ref[...]).astype(LOW)
    for h in range(HEADS):
        ag_ref[h] = att[:, h * HEAD_DIM : (h + 1) * HEAD_DIM]


def mid_block(mid, pa, pb, pc, up, gain, w):
    count = mid.shape[0]
    return pl.pallas_call(
        mid_kernel,
        in_specs=[vmem()] * 7,
        out_specs=[vmem()] * 3,
        out_shape=[
            jax.ShapeDtypeStruct((count, D), WIDE),
            jax.ShapeDtypeStruct((count, D), LOW),
            jax.ShapeDtypeStruct((HEADS, count, HEAD_DIM), LOW),
        ],
        cost_estimate=pl.CostEstimate(
            flops=2 * count * D * D, bytes_accessed=6 * 2**20, transcendentals=0
        ),
        name="mid_block",
    )(mid, pa, pb, pc, up, gain, w)


def qkv_back_kernel(
    tab, dq_ref, own_ref, got_ref, loc_ref, base_ref, n_ref, w_ref, dx_ref, dw_ref, sum_ref
):
    i = pl.program_id(0)
    c, s = turning(loc_ref, base_ref)

    def rot(v):
        return v * c - pltpu.roll(v, HEAD_DIM // 2, 1) * s

    dq = rot(dq_ref[0] * SCALE).astype(LOW)
    dk = rot((own_ref[0, 0] + got_ref[0, 0].astype(WIDE)) * SCALE).astype(LOW)
    dv = (own_ref[1, 0] + got_ref[1, 0].astype(WIDE)).astype(LOW)
    grads = jnp.concatenate([dq, dk, dv], axis=1)
    dx_ref[0] = dot_nt(grads, w_ref[...]).astype(LOW)
    part = dot_tn(n_ref[0], grads)

    @pl.when(i == 0)
    def _():
        sum_ref[...] = part

    @pl.when(i > 0)
    def _():
        sum_ref[...] += part

    @pl.when(i == HEADS - 1)
    def _():
        dw_ref[...] = sum_ref[...].astype(LOW)


def qkv_back(chips, dq, own, got, loc, base, normed, w):
    count = dq.shape[1]
    block = pl.BlockSpec((1, count, HEAD_DIM), lambda i, t: (t[i], 0, 0))
    pair = pl.BlockSpec((2, 1, count, HEAD_DIM), lambda i, t: (0, t[i], 0, 0))
    weight = pl.BlockSpec((D, 3 * HEAD_DIM), lambda i, t: (0, 0))
    return pl.pallas_call(
        qkv_back_kernel,
        grid_spec=pltpu.PrefetchScalarGridSpec(
            num_scalar_prefetch=1,
            grid=(HEADS,),
            in_specs=[
                block, pair, pair,
                pl.BlockSpec((2, count, HEAD_DIM), lambda i, t: (0, 0, 0)),
                pl.BlockSpec((1, 2, HEAD_DIM), lambda i, t: (2 * t[i] + t[HEADS], 0, 0)),
                pl.BlockSpec((1, count, D), lambda i, t: (t[i], 0, 0)),
                weight,
            ],
            out_specs=[pl.BlockSpec((1, count, D), lambda i, t: (i, 0, 0)), weight],
            scratch_shapes=[pltpu.VMEM((D, 3 * HEAD_DIM), WIDE)],
        ),
        out_shape=[
            jax.ShapeDtypeStruct((HEADS, count, D), LOW),
            jax.ShapeDtypeStruct((D, 3 * HEAD_DIM), LOW),
        ],
        cost_estimate=pl.CostEstimate(
            flops=4 * HEADS * count * D * 3 * HEAD_DIM,
            bytes_accessed=6 * HEADS * count * D,
            transcendentals=0,
        ),
        name="qkv_back",
    )(chips, dq, own, got, loc, base, normed, w)


def local(
    far,
    tokens,
    segment_ids,
    second_doc,
    memory_index,
    cache_keys,
    cache_values,
    first_gain,
    query_weight,
    key_weight,
    value_weight,
    out_weight,
    second_gain,
    gate_weight,
    up_weight,
    down_weight,
    cotangent,
):
    x = tokens[0]
    upstream = cotangent[0]
    count = x.shape[0]
    blocks = count // QUERY_BLOCK
    rows = query_weight.shape[0]
    share = down_weight.shape[0]
    units = far * HEADS * share
    chip, core, pair = lax.axis_index("h"), lax.axis_index("c"), lax.axis_index("dl")
    mine = jnp.where(chip % 2 == 0, chip // 2, HEADS - 1 - chip // 2)
    slots = jnp.arange(HEADS, dtype=jnp.int32)
    chips = at_place(mine - slots)

    def by_head(w):
        return w.reshape(rows, HEADS, HEAD_DIM).transpose(1, 0, 2)

    picked = memory_index[0].transpose(1, 0, 2)
    seg_rows = jnp.broadcast_to(
        segment_ids[0].astype(LOW).reshape(1, blocks, QUERY_BLOCK), (HEADS, blocks, QUERY_BLOCK)
    )
    gains = jnp.concatenate([first_gain, second_gain])
    gain_rows = jnp.broadcast_to(
        jnp.pad(gains, (0, HEAD_DIM - 2 * rows)).reshape(1, 1, HEAD_DIM), (HEADS, 1, HEAD_DIM)
    )
    pack = jnp.concatenate(
        [
            by_head(query_weight),
            by_head(key_weight),
            by_head(value_weight),
            seg_rows,
            (picked // MEM_ROWS).astype(LOW),
            (picked % MEM_ROWS).astype(LOW),
            gain_rows,
        ],
        axis=1,
    )
    height = pack.shape[1]
    pack = jnp.pad(pack, ((0, 0), (0, -height % 16), (0, 0)))

    block = jnp.concatenate([x, out_weight], axis=0)
    split = count // 2
    got = exchange(pack)
    up_c = swap(upstream, "c")
    up_y = swap(upstream, "dl")
    up_yc = swap(up_y, "c")
    got, x_forth, x_back = lax.optimization_barrier((got, turn(block, 1), turn(block, -1)))
    forth, back = [block, x_forth, turn(x_forth, 1)], [block, x_back, turn(x_back, -1)]
    got_c = swap(got, "c")
    got_y = swap(got, "dl")
    got_yc = swap(got_y, "c")
    near = pick(core, jnp.stack([got, got_c]), jnp.stack([got_c, got]))
    away = pick(core, jnp.stack([got_y, got_yc]), jnp.stack([got_yc, got_y]))
    every = pick(pair, jnp.stack([near, away]), jnp.stack([away, near]))
    every = every.transpose(2, 0, 1, 3, 4)
    if far > 1:
        every = lax.all_gather(every, "dh", axis=0)
    else:
        every = every[None]
    every = every.transpose(0, 2, 1, 3, 4, 5)
    w_qkv = jnp.concatenate(
        [every[..., i * rows : (i + 1) * rows, :].reshape(D, HEAD_DIM) for i in range(3)], axis=1
    )
    gain_all = every[..., 3 * rows + 3 * blocks, : 2 * rows].reshape(-1, 2, rows)
    gain_one = gain_all[:, 0].reshape(1, D)
    gain_two = gain_all[:, 1].reshape(1, D)

    def seg_of(blocks_of):
        return (
            blocks_of[:, 3 * rows : 3 * rows + blocks]
            .astype(WIDE)
            .astype(jnp.int32)
            .reshape(HEADS, count)
        )

    seg_own = seg_of(got)
    seg_oth = seg_of(got_c)
    idx = (
        got[:, 3 * rows + blocks : 3 * rows + 2 * blocks].astype(WIDE) * MEM_ROWS
        + got[:, 3 * rows + 2 * blocks : 3 * rows + 3 * blocks].astype(WIDE)
    ).astype(jnp.int32)
    idx = idx.reshape(HEADS, count, 1)

    block_docs = seg_own[:, ::QUERY_BLOCK]
    docs = second_doc.shape[1]
    doc_ids = jnp.arange(docs, dtype=jnp.int32)
    mates = jnp.sum(
        jnp.where(block_docs[:, :, None] == doc_ids, second_doc[0][None, None, :], 0), axis=-1
    )
    seg_all = jnp.concatenate([seg_own, seg_oth], axis=0)
    before = jnp.sum(
        (seg_all.reshape(1, -1) < block_docs[:, :1]).astype(jnp.int32), axis=1
    )
    tab = jnp.concatenate(
        [
            block_docs.reshape(-1),
            mates.reshape(-1),
            before // (2 * count),
            jnp.stack([core, chip]),
        ]
    ).astype(jnp.int32)

    loc, base = (jnp.asarray(table) for table in turn_tables(count))

    seg_thin = seg_own.reshape(HEADS, count, 1)
    early = (w_qkv, gain_one, tab, up_c, up_y, up_yc)
    early, gate_late, up_late, forth[2], back[2] = lax.optimization_barrier(
        (early, gate_weight, up_weight, forth[2], back[2])
    )
    w_qkv, gain_one, tab, up_c, up_y, up_yc = early
    forth.append(turn(forth[2], 1))
    back.append(turn(back[2], -1))
    at_near, at_far = [0, 1, 7, 2, 6], [3, 5, 4]

    def chips_at(order):
        places = at_place(mine - jnp.asarray(list(order), jnp.int32))
        return jnp.concatenate([places, core[None]]).astype(jnp.int32)

    near_slots = [forth[0], forth[1], back[1], forth[2], back[2]]
    held = qkv_blocks(
        chips_at(at_near), [((v, count),) for v in near_slots], gain_one, w_qkv, loc, base, ()
    )
    half = units + -units % HEAD_DIM
    wide = 2 * half

    def by_owner(w):
        w = w.reshape(rows, far, 2, HEADS, 2, share).transpose(2, 4, 0, 1, 3, 5)
        return jnp.pad(w.reshape(2, 2, rows, units), ((0, 0),) * 3 + ((0, half - units),))

    gu = jnp.concatenate([by_owner(gate_late), by_owner(up_late)], axis=-1)
    kept = pick(core, gu[:, 0], gu[:, 1])
    came = swap(pick(core, gu[:, 1], gu[:, 0]), "c")
    gu = pick(core, jnp.stack([kept, came], 1), jnp.stack([came, kept], 1))
    kept = pick(pair, gu[0], gu[1])
    came = swap(pick(pair, gu[1], gu[0]), "dl")
    gu = pick(pair, jnp.stack([kept, came]), jnp.stack([came, kept])).reshape(4 * rows, wide)
    if far == 1:
        deep = 2 * rows
        lower = jnp.concatenate(fold(down_weight, deep), axis=1)
    else:
        deep = share
        lower = jnp.pad(down_weight, ((0, 0), (0, wide - D)))
    bundle = jnp.concatenate([gu, lower], axis=0)
    height = 4 * rows + share
    if far > 1:
        bundle = lax.all_gather(bundle, "dh", axis=0, tiled=True)
    upper = bundle.shape[0] // 2
    *held, bundle, forth[3], back[3] = lax.optimization_barrier(
        (*held, bundle, forth[3], back[3])
    )
    far_first, far_last = turn(forth[3][:split], 1), turn(back[3][split:], -1)
    bundle, *_ = lax.optimization_barrier((bundle, far_first, far_last))
    w_forth, w_back = [bundle, turn(bundle, 1)], [bundle, turn(bundle, -1)]

    far_slots = [
        ((forth[3], count),),
        ((back[3], count),),
        ((far_first, split), (far_last, count - split)),
    ]
    queries, own, normed_one = qkv_blocks(
        chips_at(at_far), far_slots, gain_one, w_qkv, loc, base, tuple(held)
    )
    outs = jnp.stack([v[-rows:] for v in (*forth, far_last, *back[:0:-1])])
    queries, own, outs, w_forth[1], w_back[1] = lax.optimization_barrier(
        (queries, own, outs, w_forth[1], w_back[1])
    )
    other = swap(own, "c")
    outs_c = swap(outs, "c")
    outs_y = swap(outs, "dl")
    seg_own_row = seg_own.reshape(HEADS, 1, count)
    seg_oth_row = seg_oth.reshape(HEADS, 1, count)
    cached = [cache[0].reshape(-1, D) for cache in (cache_keys, cache_values)]
    attention, attention_low, lse, memory = attend(
        tab, queries, own, other, seg_thin, seg_own_row, seg_oth_row, idx, *cached
    )
    w_forth.append(turn(w_forth[1], 1))
    w_back.append(turn(w_back[1], -1))
    attention_low, outs_y, w_forth[2], w_back[2] = lax.optimization_barrier(
        (attention_low, outs_y, w_forth[2], w_back[2])
    )

    heads = exchange(attention_low)
    w_forth.append(turn(w_forth[2], 1))
    w_back.append(turn(w_back[2], -1))
    outs_yc = swap(outs_y, "c")
    heads, w_forth[3], w_back[3] = lax.optimization_barrier((heads, w_forth[3], w_back[3]))
    w_first, w_last = turn(w_forth[3][:upper], 1), turn(w_back[3][upper:], -1)
    slot_of = lax.rem(mine - jnp.asarray(PLACE, jnp.int32) + HEADS, HEADS).astype(jnp.int32)
    if far == 1:
        sources = [outs, outs_c, outs_y, outs_yc]
    else:
        near = pick(core, jnp.stack([outs, outs_c], 1), jnp.stack([outs_c, outs], 1))
        away = pick(core, jnp.stack([outs_y, outs_yc], 1), jnp.stack([outs_yc, outs_y], 1))
        sources = pick(pair, jnp.stack([near, away]), jnp.stack([away, near]))
        sources = lax.all_gather(jnp.take(sources, slot_of, axis=1), "dh", axis=0)
        sources = [sources.reshape(D, D)]
    where = jnp.concatenate([chips, jnp.stack([pair, core])]).astype(jnp.int32)
    attended, mid, normed_two, out_w = out_block(where, heads, sources, x, gain_two)
    normed_two, w_first, w_last = lax.optimization_barrier((normed_two, w_first, w_last))
    w_slots = w_forth + [w_first, w_last] + w_back[:0:-1]

    if far == 1:
        gate_w, up_w, down_w = weights(where, w_slots, units)
    else:
        middle = jnp.concatenate(w_slots[HEADS // 2 : HEADS // 2 + 2], axis=0)
        every = jnp.stack(w_slots[: HEADS // 2] + [middle] + w_slots[HEADS // 2 + 2 :])
        every = jnp.take(every, slot_of, axis=0).reshape(HEADS, far, height, wide)
        gu = every[:, :, : 4 * rows].reshape(HEADS, far, 2, 2 * rows, wide)
        gu = gu.transpose(1, 2, 0, 3, 4).reshape(D, wide)
        gate_w, up_w = gu[:, :units], gu[:, half : half + units]
        down_w = every[:, :, 4 * rows :, :D].transpose(1, 0, 2, 3).reshape(units, D)

    n_c = swap(normed_two, "c")
    n_y = swap(normed_two, "dl")
    hid_l, gg_l, ug_l, dn_l, out_l = ffn(normed_two, n_c, upstream, up_c, gate_w, up_w, down_w)
    n_y, dn_l = lax.optimization_barrier((n_y, dn_l))
    n_yc = swap(n_y, "c")
    hid_r, gg_r, ug_r, dn_r, out_r = ffn(n_y, n_yc, up_y, up_yc, gate_w, up_w, down_w)

    def to_away(away):
        return (away[0].astype(WIDE) + swap(away[1], "c").astype(WIDE)).astype(LOW)

    there = to_away(dn_r)
    there, hid_l, gg_l, ug_l, hid_r, gg_r, ug_r = lax.optimization_barrier(
        (there, hid_l, gg_l, ug_l, hid_r, gg_r, ug_r)
    )
    n_all, u_all = [normed_two, n_c, n_y, n_yc], [upstream, up_c, up_y, up_yc]
    near, away = (hid_l, gg_l, ug_l), (hid_r, gg_r, ug_r)
    if far == 1:
        parts = weight_grads(slot_of, n_all, u_all, near, away, height, wide)
    else:

        def over_tokens(left, right):
            return jnp.einsum(
                "gtd,gtf->df", left, right, preferred_element_type=WIDE
            ).astype(LOW)

        def by_rows(w):
            w = jnp.pad(w, ((0, 0), (0, half - units)))
            return w.reshape(far, 2, HEADS, 2 * rows, half).transpose(2, 0, 1, 3, 4)

        n_all, u_all = jnp.stack(n_all), jnp.stack(u_all)
        hid, gg, ug = (jnp.concatenate(pieces, axis=0) for pieces in zip(near, away))
        gu = jnp.concatenate(
            [by_rows(over_tokens(n_all, gg)), by_rows(over_tokens(n_all, ug))], axis=-1
        ).reshape(HEADS, far, 4 * rows, wide)
        down = over_tokens(hid, u_all).reshape(far, HEADS, share, D).transpose(1, 0, 2, 3)
        down = jnp.pad(down, ((0, 0), (0, 0), (0, 0), (0, wide - D)))
        parts = jnp.concatenate([gu, down], axis=2)
        parts = jnp.take(parts.reshape(HEADS, far * height, wide), chips, axis=0)

    out_l, out_r, _ = lax.optimization_barrier((out_l, out_r, parts))
    output = mid
    for part in (out_l[0], swap(out_l[1], "c"), swap(to_away(out_r), "dl")):
        output = output + part.astype(WIDE)
    output = output.astype(LOW)

    sums = [dn_l[0], swap(dn_l[1], "c"), swap(there, "dl")]
    sums[2], parts = lax.optimization_barrier((sums[2], parts))
    mid_grad, branch, att_grad = mid_block(mid, *sums, upstream, gain_two, out_w)
    ups = exchange(att_grad)

    def plus(block, arrived, start):
        size = arrived.shape[0]
        total = block[start : start + size].astype(WIDE) + arrived.astype(WIDE)
        pieces = [block[:start], total, block[start + size :]]
        pieces = [piece.astype(LOW) for piece in pieces if piece.shape[0]]
        return jnp.concatenate(pieces, axis=0)

    def ring_first(blocks, split):
        middle = blocks[HEADS // 2]
        return (
            plus(blocks[HEADS // 2 + 1], turn(middle[:split].astype(LOW), 1), 0),
            plus(blocks[HEADS // 2 - 1], turn(middle[split:].astype(LOW), -1), split),
        )

    def ring_next(blocks, forth, back, step):
        return (
            plus(blocks[HEADS // 2 + step], turn(forth, 1), 0),
            plus(blocks[HEADS // 2 - step], turn(back, -1), 0),
        )

    def ring_last(blocks, forth, back):
        return blocks[0].astype(WIDE) + forth.astype(WIDE) + back.astype(WIDE)

    def over_owner(w, width):
        w = w.reshape(far, 2, HEADS, 2, rows, width)
        kept = pick(core, w[:, :, :, 0], w[:, :, :, 1])
        came = swap(pick(core, w[:, :, :, 1], w[:, :, :, 0]), "c")
        w = kept.astype(WIDE) + came.astype(WIDE)
        kept = pick(pair, w[:, 0], w[:, 1])
        came = swap(pick(pair, w[:, 1], w[:, 0]).astype(LOW), "dl")
        w = (kept + came.astype(WIDE)).astype(LOW)
        if far > 1:
            w = lax.psum_scatter(w, "dh", scatter_dimension=0, tiled=True)
        return w[0]

    out_part = over_owner(
        jnp.einsum("td,te->de", attended, branch, preferred_element_type=WIDE).astype(LOW), D
    )
    strip = wide - D
    upper = 4 * rows if far == 1 else parts.shape[1] // 2
    blocks = [parts[slot].astype(WIDE) for slot in range(HEADS)]
    if far == 1:
        strips = out_strips(where, out_part, strip)
        below = share - strips.shape[1]
        for slot in range(HEADS):
            if slot != HEADS // 2:
                blocks[slot] = blocks[slot] + jnp.pad(
                    strips[slot].astype(WIDE), ((4 * rows, below), (D, 0))
                )
        out_far = turn(strips[HEADS // 2], HEADS // 2)
    else:
        out_far = exchange(out_part)
    forth, back = ring_first(blocks, upper)
    ups, forth, back = lax.optimization_barrier((ups, forth, back))
    forth, back = ring_next(blocks, forth, back, 2)

    dq, d_own, d_oth = attend_back(
        tab, queries, ups, attention, lse, own, other, memory, seg_thin, seg_own_row, seg_oth_row
    )
    d_got = swap(d_oth, "c")
    dq, forth, back = lax.optimization_barrier((dq, forth, back))
    dx, dw = qkv_back(
        chips_at(range(HEADS)), dq, d_own, d_got, loc, base, normed_one, w_qkv
    )
    arrived_forth, arrived_back = turn(forth, 1), turn(back, -1)
    dx, arrived_forth, arrived_back = lax.optimization_barrier((dx, arrived_forth, arrived_back))
    dx_forth, dx_back = ring_first(dx, split)
    dw, dx_forth, dx_back, arrived_forth, arrived_back = lax.optimization_barrier(
        (dw, dx_forth, dx_back, arrived_forth, arrived_back)
    )
    forth = plus(blocks[HEADS - 1], arrived_forth, 0)
    back = plus(blocks[1], arrived_back, 0)

    dw = over_owner(dw, 3 * HEAD_DIM)
    dx_forth, dx_back = ring_next(dx, dx_forth, dx_back, 2)
    dw, dx_forth, dx_back = lax.optimization_barrier((dw, dx_forth, dx_back))
    qkv_grads = exchange(dw).astype(WIDE)
    dx_forth, dx_back = ring_next(dx, dx_forth, dx_back, 3)
    normed_one_grad = ring_last(dx, turn(dx_forth, 1), turn(dx_back, -1))

    summed = ring_last(blocks, turn(forth, 1), turn(back, -1)).astype(LOW)
    if far > 1:
        summed = lax.psum_scatter(summed, "dh", scatter_dimension=0, tiled=True)
    down_w_grad = summed[4 * rows : 4 * rows + share, :D].astype(WIDE)
    if far == 1:
        out_w_grad = summed[4 * rows : 4 * rows + strips.shape[1], D:].astype(WIDE)
        out_w_grad = out_w_grad + out_far.astype(WIDE)
        out_w_grad = out_w_grad.reshape(D // strip, rows, strip).transpose(1, 0, 2).reshape(rows, D)
    else:
        out_w_grad = jnp.sum(out_far.astype(WIDE), axis=0)
    gu = summed[: 4 * rows].reshape(2, 2, rows, wide)
    kept = pick(core, gu[:, 0], gu[:, 1])
    came = swap(pick(core, gu[:, 1], gu[:, 0]), "c")
    gu = pick(core, jnp.stack([kept, came], 1), jnp.stack([came, kept], 1))
    kept = pick(pair, gu[0], gu[1])
    came = swap(pick(pair, gu[1], gu[0]), "dl")
    gu = pick(pair, jnp.stack([kept, came]), jnp.stack([came, kept]))
    gu = jnp.stack([gu[..., :units], gu[..., half : half + units]])
    gu = (
        gu.reshape(2, 2, 2, rows, far, HEADS, share)
        .transpose(0, 3, 4, 1, 5, 2, 6)
        .reshape(2, rows, FF)
        .astype(WIDE)
    )
    gate_w_grad, up_w_grad = gu[0], gu[1]

    wide_x = x.astype(WIDE)
    r = lax.rsqrt(jnp.mean(wide_x * wide_x, axis=-1, keepdims=True) + EPSILON)
    scaled = normed_one_grad * gain_one.astype(WIDE)
    inner = jnp.mean(scaled * wide_x, axis=-1, keepdims=True)
    input_grad = mid_grad + r * scaled - wide_x * (r * r * r * inner)

    q_w_grad, k_w_grad, v_w_grad = (
        qkv_grads[:, :, i * HEAD_DIM : (i + 1) * HEAD_DIM].transpose(1, 0, 2).reshape(rows, D)
        for i in range(3)
    )

    def gain_grad(gain, pairs):
        total = 0.0
        for grad, weight in pairs:
            total = total + jnp.sum(grad * weight.astype(WIDE), axis=1)
        return total / gain.astype(WIDE)

    first_gain_grad = gain_grad(
        first_gain,
        ((q_w_grad, query_weight), (k_w_grad, key_weight), (v_w_grad, value_weight)),
    )
    second_gain_grad = gain_grad(
        second_gain, ((gate_w_grad, gate_weight), (up_w_grad, up_weight))
    )
    return (
        output[None],
        input_grad[None],
        first_gain_grad,
        q_w_grad,
        k_w_grad,
        v_w_grad,
        out_w_grad,
        second_gain_grad,
        gate_w_grad,
        up_w_grad,
        down_w_grad,
    )


def solution(mesh):
    far = mesh.shape["dp"] // 2
    cores = mesh.shape["seq"] // HEADS
    fine = Mesh(mesh.devices.reshape(far, 2, HEADS, cores), ("dh", "dl", "h", "c"))
    dp, seq, every = ("dh", "dl"), ("h", "c"), ("dh", "dl", "h", "c")
    rows = P(every, None)
    return jax.shard_map(
        functools.partial(local, far),
        mesh=fine,
        in_specs=(
            P(dp, seq, None),
            P(dp, seq),
            P(dp, None),
            P(dp, seq, None, None),
            P(dp, None, None, None),
            P(dp, None, None, None),
            P(every),
            rows,
            rows,
            rows,
            rows,
            P(every),
            rows,
            rows,
            rows,
            P(dp, seq, None),
        ),
        out_specs=(
            P(dp, seq, None),
            P(dp, seq, None),
            P(every),
            rows,
            rows,
            rows,
            rows,
            P(every),
            rows,
            rows,
            rows,
        ),
        check_vma=False,
    )
```

```python
import functools
import math

import jax
import jax.numpy as jnp
import numpy as np
from jax import lax
from jax.experimental import pallas as pl
from jax.experimental.pallas import tpu as pltpu
from jax.sharding import Mesh
from jax.sharding import PartitionSpec as P

D = 1024
FF = 2816
HEADS = 8
HEAD_DIM = 128
QUERY_BLOCK = 128
MEM_ROWS = 256
EPSILON = 1e-05
NEGATIVE = -1e30
SCALE = 1.0 / math.sqrt(HEAD_DIM)
LOG2 = SCALE * math.log2(math.e)
LOW = jnp.bfloat16
WIDE = jnp.float32

RING = [2 * i for i in range(HEADS // 2)] + [2 * i + 1 for i in reversed(range(HEADS // 2))]
PLACE = [RING.index(i) for i in range(HEADS)]


def dot_nn(a, b):
    return lax.dot_general(a, b, (((1,), (0,)), ((), ())), preferred_element_type=WIDE)


def dot_nt(a, b):
    return lax.dot_general(a, b, (((1,), (1,)), ((), ())), preferred_element_type=WIDE)


def dot_tn(a, b):
    return lax.dot_general(a, b, (((0,), (0,)), ((), ())), preferred_element_type=WIDE)


def swap(block, axis):
    return lax.ppermute(block, axis, [(0, 1), (1, 0)])


def turn(block, distance):
    route = [(RING[i], RING[(i + distance) % HEADS]) for i in range(HEADS)]
    return lax.ppermute(block, "h", route)


def at_place(place):
    place = lax.rem(place + 2 * HEADS, HEADS)
    return jnp.where(place < HEADS // 2, 2 * place, 2 * (HEADS - 1 - place) + 1)


def exchange(blocks):
    return lax.all_to_all(blocks, "h", 0, 0)


def pick(flag, first, second):
    return jnp.where(flag == 0, first, second)


def smem():
    return pl.BlockSpec(memory_space=pltpu.SMEM)


def vmem():
    return pl.BlockSpec(memory_space=pltpu.VMEM)


def turn_tables(count):
    half = HEAD_DIM // 2
    freqs = 10000.0 ** (-np.arange(half, dtype=np.float64) * 2.0 / HEAD_DIM)
    freqs = np.concatenate([freqs, freqs])

    def table(positions):
        angles = positions[:, None] * freqs
        return np.stack([np.cos(angles), np.sin(angles)]).astype(np.float32)

    return table(np.arange(count)), table(np.arange(2 * HEADS) * count).transpose(1, 0, 2)


def turning(loc_ref, base_ref):
    cl, sl = loc_ref[0], loc_ref[1]
    cb, sb = base_ref[0, 0:1, :], base_ref[0, 1:2, :]
    sine = sl * cb + cl * sb
    lane = lax.broadcasted_iota(jnp.int32, sine.shape, 1)
    return cl * cb - sl * sb, jnp.where(lane < HEAD_DIM // 2, -sine, sine)


def qkv_kernel(parts, tab, *refs):
    xs, (gain_ref, w_ref, loc_ref, base_ref) = refs[: sum(parts)], refs[sum(parts) : sum(parts) + 4]
    q_ref, kv_ref, n_ref, x_ref = refs[-4:]
    i = pl.program_id(0)
    first = 0
    for step, number in enumerate(parts):

        @pl.when(i == step)
        def _(blocks=xs[first : first + number]):
            row = 0
            for block in blocks:
                size = block.shape[0]
                x_ref[row : row + size, :] = block[...]
                row += size

        first += number
    x = x_ref[...].astype(WIDE)
    r = lax.rsqrt(jnp.mean(x * x, axis=-1, keepdims=True) + EPSILON)
    normed = (x * r * gain_ref[...].astype(WIDE)).astype(LOW)
    n_ref[0] = normed
    out = dot_nn(normed, w_ref[...])
    c, s = turning(loc_ref, base_ref)

    def rot(v):
        return v * c + pltpu.roll(v, HEAD_DIM // 2, 1) * s

    q_ref[0] = rot(out[:, :HEAD_DIM]).astype(LOW)
    kv_ref[0, 0] = rot(out[:, HEAD_DIM : 2 * HEAD_DIM]).astype(LOW)
    kv_ref[1, 0] = out[:, 2 * HEAD_DIM :].astype(LOW)


def qkv_blocks(chips, xs, gain, w, loc, base, held):
    count = loc.shape[1]
    steps = len(xs)
    flat = [piece for block in xs for piece, _ in block]
    read = [size for block in xs for _, size in block]

    def whole(shape):
        return pl.BlockSpec(shape, lambda i, t: (0, 0))

    def block(*shape):
        return pl.BlockSpec((1, *shape), lambda i, t: (t[i], 0, 0))

    spec = pltpu.PrefetchScalarGridSpec(
        num_scalar_prefetch=1,
        grid=(len(xs),),
        in_specs=[whole((size, D)) for size in read]
        + [
            whole((1, D)),
            whole((D, 3 * HEAD_DIM)),
            pl.BlockSpec((2, count, HEAD_DIM), lambda i, t: (0, 0, 0)),
            pl.BlockSpec((1, 2, HEAD_DIM), lambda i, t: (2 * t[i] + t[steps], 0, 0)),
        ]
        + [pl.BlockSpec(memory_space=pl.ANY)] * len(held),
        out_specs=[
            block(count, HEAD_DIM),
            pl.BlockSpec((2, 1, count, HEAD_DIM), lambda i, t: (0, t[i], 0, 0)),
            block(count, D),
        ],
        scratch_shapes=[pltpu.VMEM((count, D), LOW)],
    )
    return pl.pallas_call(
        functools.partial(qkv_kernel, [len(block) for block in xs]),
        grid_spec=spec,
        out_shape=[
            jax.ShapeDtypeStruct((HEADS, count, HEAD_DIM), LOW),
            jax.ShapeDtypeStruct((2, HEADS, count, HEAD_DIM), LOW),
            jax.ShapeDtypeStruct((HEADS, count, D), LOW),
        ],
        input_output_aliases={len(flat) + 5 + i: i for i in range(len(held))},
        cost_estimate=pl.CostEstimate(
            flops=len(xs) * count * D, bytes_accessed=len(xs) * count, transcendentals=0
        ),
        name=f"qkv{len(xs)}",
    )(chips, *flat, gain, w, loc, base, *held)


def causal(count):
    rows = lax.broadcasted_iota(jnp.int32, (count, count), 0)
    return lax.broadcasted_iota(jnp.int32, (count, count), 1) <= rows


def attend_kernel(
    tab, q_ref, own_ref, oth_ref, segq_ref, sego_ref, segt_ref, idx_ref, ck_ref, cv_ref,
    o_ref, low_ref, lse_ref, mem_ref,
):
    i = pl.program_id(0)
    parity = tab[40]
    count = q_ref.shape[1]
    q = q_ref[0]
    segq = segq_ref[0]

    s1 = dot_nt(q, own_ref[0, i]) * LOG2
    s2 = dot_nt(q, oth_ref[0, i]) * LOG2
    s1 = jnp.where((sego_ref[i] == segq) & causal(count), s1, NEGATIVE)
    s2 = jnp.where(segt_ref[i] == segq + 64 * (1 - parity), s2, NEGATIVE)
    memory = []
    for b in range(count // QUERY_BLOCK):
        rows = slice(b * QUERY_BLOCK, (b + 1) * QUERY_BLOCK)
        doc = tab[2 * i + b]
        mate = tab[16 + 2 * i + b]
        idx = idx_ref[0, rows, :]
        lane = lax.broadcasted_iota(jnp.int32, (QUERY_BLOCK, MEM_ROWS), 1)
        first = jnp.where(idx == lane, 1.0, 0.0).astype(LOW)
        second = jnp.where(idx == lane + MEM_ROWS, 1.0, 0.0).astype(LOW)
        here = pl.ds(pl.multiple_of(doc * MEM_ROWS, MEM_ROWS), MEM_ROWS)
        there = pl.ds(pl.multiple_of(mate * MEM_ROWS, MEM_ROWS), MEM_ROWS)
        mk = (dot_nn(first, ck_ref[here, :]) + dot_nn(second, ck_ref[there, :])).astype(LOW)
        mv = (dot_nn(first, cv_ref[here, :]) + dot_nn(second, cv_ref[there, :])).astype(LOW)
        mem_ref[0, 0, rows, :] = mk
        mem_ref[1, 0, rows, :] = mv
        s = jnp.where(segq[rows] == doc, dot_nt(q[rows], mk) * LOG2, NEGATIVE)
        memory.append((s, mv))
    sm = jnp.concatenate([s for s, _ in memory], axis=0)
    top = jnp.maximum(
        jnp.max(jnp.maximum(s1, s2), axis=-1, keepdims=True), jnp.max(sm, axis=-1, keepdims=True)
    )
    p1 = jnp.exp2(s1 - top)
    p2 = jnp.exp2(s2 - top)
    pm = jnp.exp2(sm - top)
    total = jnp.sum(p1 + p2, axis=-1, keepdims=True) + jnp.sum(pm, axis=-1, keepdims=True)
    pm = pm.astype(LOW)
    acc = jnp.concatenate(
        [
            dot_nn(pm[b * QUERY_BLOCK : (b + 1) * QUERY_BLOCK], mv)
            for b, (_, mv) in enumerate(memory)
        ],
        axis=0,
    )
    acc = acc + dot_nn(p1.astype(LOW), own_ref[1, i]) + dot_nn(p2.astype(LOW), oth_ref[1, i])

    def body(j, state):
        top, total, acc = state
        s1 = dot_nt(q, own_ref[0, j]) * LOG2
        s2 = dot_nt(q, oth_ref[0, j]) * LOG2
        s1 = jnp.where(sego_ref[j] == segq, s1, NEGATIVE)
        s2 = jnp.where(segt_ref[j] == segq, s2, NEGATIVE)
        fresh = jnp.maximum(top, jnp.max(jnp.maximum(s1, s2), axis=-1, keepdims=True))
        p1 = jnp.exp2(s1 - fresh)
        p2 = jnp.exp2(s2 - fresh)
        decay = jnp.exp2(top - fresh)
        total = total * decay + jnp.sum(p1 + p2, axis=-1, keepdims=True)
        acc = (
            acc * decay
            + dot_nn(p1.astype(LOW), own_ref[1, j])
            + dot_nn(p2.astype(LOW), oth_ref[1, j])
        )
        return fresh, total, acc

    top, total, acc = lax.fori_loop(tab[32 + i], i, body, (top, total, acc))
    out = acc / total
    o_ref[0] = out
    low_ref[0] = out.astype(LOW)
    lse_ref[0] = top + jnp.log2(total)


def attend(tab, q, own, oth, segq, sego, segt, idx, ck, cv):
    count = q.shape[1]
    block = pl.BlockSpec((1, count, HEAD_DIM), lambda i, t: (i, 0, 0))
    thin = pl.BlockSpec((1, count, 1), lambda i, t: (i, 0, 0))
    whole = pl.BlockSpec((2, HEADS, count, HEAD_DIM), lambda i, t: (0, 0, 0, 0))
    segs = pl.BlockSpec((HEADS, 1, count), lambda i, t: (0, 0, 0))
    cache = pl.BlockSpec((ck.shape[0], HEAD_DIM), lambda i, t: (0, t[41]))
    mem = pl.BlockSpec((2, 1, count, HEAD_DIM), lambda i, t: (0, i, 0, 0))
    return pl.pallas_call(
        attend_kernel,
        grid_spec=pltpu.PrefetchScalarGridSpec(
            num_scalar_prefetch=1,
            grid=(HEADS,),
            in_specs=[block, whole, whole, thin, segs, segs, thin, cache, cache],
            out_specs=[block, block, thin, mem],
        ),
        out_shape=[
            jax.ShapeDtypeStruct((HEADS, count, HEAD_DIM), WIDE),
            jax.ShapeDtypeStruct((HEADS, count, HEAD_DIM), LOW),
            jax.ShapeDtypeStruct((HEADS, count, 1), WIDE),
            jax.ShapeDtypeStruct((2, HEADS, count, HEAD_DIM), LOW),
        ],
        cost_estimate=pl.CostEstimate(
            flops=25 * 10**9, bytes_accessed=6 * 2**20, transcendentals=3 * 10**6
        ),
        name="attend",
    )(tab, q, own, oth, segq, sego, segt, idx, ck, cv)


def attend_back_kernel(
    tab, q_ref, up_ref, o_ref, lse_ref, own_ref, oth_ref, mem_ref, segq_ref, sego_ref, segt_ref,
    dq_ref, down_ref, doth_ref, sum_ref,
):
    i = pl.program_id(0)

    @pl.when(i == 0)
    def _():
        sum_ref[...] = jnp.zeros_like(sum_ref)

    parity = tab[40]
    count = q_ref.shape[1]
    q = q_ref[0]
    up = up_ref[0]
    lse = lse_ref[0]
    segq = segq_ref[0]
    delta = jnp.sum(up.astype(WIDE) * o_ref[0], axis=-1, keepdims=True)
    partial = []
    for b in range(count // QUERY_BLOCK):
        rows = slice(b * QUERY_BLOCK, (b + 1) * QUERY_BLOCK)
        mk = mem_ref[0, 0, rows, :]
        mv = mem_ref[1, 0, rows, :]
        ok = segq[rows] == tab[2 * i + b]
        p = jnp.exp2(jnp.where(ok, dot_nt(q[rows], mk) * LOG2 - lse[rows], NEGATIVE))
        ds = (p * (dot_nt(up[rows], mv) - delta[rows])).astype(LOW)
        partial.append(dot_nn(ds, mk))

    def tile(side, ref, j, ok, dq):
        k = ref[0, j]
        v = ref[1, j]
        p = jnp.exp2(jnp.where(ok, dot_nt(q, k) * LOG2 - lse, NEGATIVE))
        ds = (p * (dot_nt(up, v) - delta)).astype(LOW)
        sum_ref[side, 0, j] += dot_tn(ds, q)
        sum_ref[side, 1, j] += dot_tn(p.astype(LOW), up)
        return dq + dot_nn(ds, k)

    dq = jnp.concatenate(partial, axis=0)
    dq = tile(0, own_ref, i, (sego_ref[i] == segq) & causal(count), dq)
    dq = tile(1, oth_ref, i, segt_ref[i] == segq + 64 * (1 - parity), dq)

    def body(j, dq):
        dq = tile(0, own_ref, j, sego_ref[j] == segq, dq)
        return tile(1, oth_ref, j, segt_ref[j] == segq, dq)

    dq_ref[0] = lax.fori_loop(tab[32 + i], i, body, dq)

    @pl.when(i == HEADS - 1)
    def _():
        down_ref[...] = sum_ref[0]
        doth_ref[...] = sum_ref[1].astype(LOW)


def attend_back(tab, q, up, o, lse, own, oth, mem, segq, sego, segt):
    count = q.shape[1]
    block = pl.BlockSpec((1, count, HEAD_DIM), lambda i, t: (i, 0, 0))
    thin = pl.BlockSpec((1, count, 1), lambda i, t: (i, 0, 0))
    whole = pl.BlockSpec((2, HEADS, count, HEAD_DIM), lambda i, t: (0, 0, 0, 0))
    segs = pl.BlockSpec((HEADS, 1, count), lambda i, t: (0, 0, 0))
    memory = pl.BlockSpec((2, 1, count, HEAD_DIM), lambda i, t: (0, i, 0, 0))
    return pl.pallas_call(
        attend_back_kernel,
        grid_spec=pltpu.PrefetchScalarGridSpec(
            num_scalar_prefetch=1,
            grid=(HEADS,),
            in_specs=[block, block, block, thin, whole, whole, memory, thin, segs, segs],
            out_specs=[block, whole, whole],
            scratch_shapes=[pltpu.VMEM((2, 2, HEADS, count, HEAD_DIM), WIDE)],
        ),
        out_shape=[
            jax.ShapeDtypeStruct((HEADS, count, HEAD_DIM), WIDE),
            jax.ShapeDtypeStruct((2, HEADS, count, HEAD_DIM), WIDE),
            jax.ShapeDtypeStruct((2, HEADS, count, HEAD_DIM), LOW),
        ],
        cost_estimate=pl.CostEstimate(
            flops=30 * 10**9, bytes_accessed=10 * 2**20, transcendentals=3 * 10**6
        ),
        name="attend_back",
    )(tab, q, up, o, lse, own, oth, mem, segq, sego, segt)


def place_rows(tab, sources, w_ref):
    rows = sources[0].shape[1]
    for k, source in enumerate(sources):
        pair = tab[8] if k < 2 else 1 - tab[8]
        core = tab[9] if k % 2 == 0 else 1 - tab[9]
        for slot in range(HEADS):
            start = ((pair * HEADS + tab[slot]) * 2 + core) * rows
            w_ref[pl.ds(pl.multiple_of(start, rows), rows), :] = source[slot]


def out_kernel(tab, heads_ref, *refs):
    sources, (x_ref, gain_ref, att_ref, mid_ref, n_ref, w_ref) = refs[:-6], refs[-6:]
    if len(sources) == 1:
        w_ref[...] = sources[0][...]
    else:
        place_rows(tab, sources, w_ref)
    for h in range(HEADS):
        att_ref[:, h * HEAD_DIM : (h + 1) * HEAD_DIM] = heads_ref[h]
    mid = x_ref[...].astype(WIDE) + dot_nn(att_ref[...], w_ref[...])
    mid_ref[...] = mid
    r = lax.rsqrt(jnp.mean(mid * mid, axis=-1, keepdims=True) + EPSILON)
    n_ref[...] = (mid * r * gain_ref[...].astype(WIDE)).astype(LOW)


def out_block(tab, heads, sources, x, gain):
    count = x.shape[0]
    return pl.pallas_call(
        out_kernel,
        in_specs=[smem()] + [vmem()] * (3 + len(sources)),
        out_specs=[vmem()] * 4,
        out_shape=[
            jax.ShapeDtypeStruct((count, D), LOW),
            jax.ShapeDtypeStruct((count, D), WIDE),
            jax.ShapeDtypeStruct((count, D), LOW),
            jax.ShapeDtypeStruct((D, D), LOW),
        ],
        cost_estimate=pl.CostEstimate(
            flops=2 * count * D * D, bytes_accessed=6 * 2**20, transcendentals=0
        ),
        name="out_block",
    )(tab, heads, *sources, x, gain)


def fold(block, deep):
    half, rest = D // 2, block.shape[0] - deep
    middle = jnp.concatenate([block[deep:, :half], block[: deep - rest, half:]], axis=0)
    last = block[deep - rest :, half:]
    last = jnp.concatenate([last, jnp.zeros((deep - last.shape[0], half), last.dtype)], axis=0)
    return block[:deep, :half], middle, last


def unfolded(block, share):
    deep, half = block.shape[0], D // 2
    rest = share - deep
    return [
        (0, deep, 0, block[:, :half]),
        (deep, rest, 0, block[:rest, half:D]),
        (0, deep - rest, half, block[rest:, half:D]),
        (deep - rest, share - deep + rest, half, block[: share - deep + rest, D:]),
    ]


def weights_kernel(tab, *refs):
    blocks, (gate_ref, up_ref, down_ref, acc_ref) = refs[:-4], refs[-4:]
    units = gate_ref.shape[1]
    height, wide = blocks[0].shape
    half = wide // 2
    share = units // HEADS
    rows = D // (2 * HEADS)
    middle = blocks[HEADS // 2].shape[0]
    for slot in range(HEADS):
        chip = tab[slot]
        if slot == HEADS // 2:
            pieces = [(0, blocks[slot]), (middle, blocks[slot + 1])]
        else:
            pieces = [(0, blocks[slot if slot < HEADS // 2 else slot + 1])]
        for start, ref in pieces:
            stop = start + ref.shape[0]
            for pair in range(2):
                first, last = max(start, pair * rows), min(stop, (pair + 1) * rows)
                if first < last:
                    size = last - first
                    here = (pair * HEADS + chip) * rows + first - pair * rows
                    here = pl.ds(pl.multiple_of(here, math.gcd(rows, first)), size)
                    gate_ref[here, :] = ref[first - start : last - start, :units]
                    up_ref[here, :] = ref[first - start : last - start, half : half + units]
        lower = ref[2 * rows - start :, :].astype(WIDE)
        for row, size, column, piece in unfolded(lower, share):
            here = pl.ds(pl.multiple_of(chip * share + row, 8), size)
            acc_ref[here, column : column + D // 2] = piece
    down_ref[...] = acc_ref[...].astype(LOW)


def weights(chips, blocks, units):
    return pl.pallas_call(
        weights_kernel,
        in_specs=[smem()] + [vmem()] * len(blocks),
        out_specs=[vmem()] * 3,
        out_shape=[
            jax.ShapeDtypeStruct((D, units), LOW),
            jax.ShapeDtypeStruct((D, units), LOW),
            jax.ShapeDtypeStruct((units, D), LOW),
        ],
        scratch_shapes=[pltpu.VMEM((units, D), WIDE)],
        cost_estimate=pl.CostEstimate(
            flops=0, bytes_accessed=12 * D * units, transcendentals=0
        ),
        name="weights",
    )(chips, *blocks)


def ffn_kernel(na, nb, ga, gb, g_ref, u_ref, d_ref, hid_ref, gg_ref, ug_ref, dn_ref, out_ref, n_ref, c_ref):
    for step, (tokens, cotangent) in enumerate(((na, ga), (nb, gb))):

        @pl.when(pl.program_id(0) == step)
        def _(tokens=tokens, cotangent=cotangent):
            n_ref[...] = tokens[...]
            c_ref[...] = cotangent[...]

    n = n_ref[...]
    gate = dot_nn(n, g_ref[...])
    upper = dot_nn(n, u_ref[...])
    sigma = jax.nn.sigmoid(gate)
    silu = gate * sigma
    hid = (silu * upper).astype(LOW)
    hid_ref[0] = hid
    hg = dot_nt(c_ref[...], d_ref[...])
    gg = (hg * upper * sigma * (1.0 + gate * (1.0 - sigma))).astype(LOW)
    ug = (hg * silu).astype(LOW)
    gg_ref[0] = gg
    ug_ref[0] = ug
    dn_ref[0] = (dot_nt(gg, g_ref[...]) + dot_nt(ug, u_ref[...])).astype(LOW)
    out_ref[0] = dot_nn(hid, d_ref[...]).astype(LOW)


def ffn(na, nb, ga, gb, g, u, d):
    count = na.shape[0]
    units = g.shape[1]

    def whole(rows, columns):
        return pl.BlockSpec((rows, columns), lambda i: (0, 0))

    def block(columns):
        return pl.BlockSpec((1, count, columns), lambda i: (i, 0, 0))

    return pl.pallas_call(
        ffn_kernel,
        grid=(2,),
        in_specs=[whole(count, D)] * 4 + [whole(D, units)] * 2 + [whole(units, D)],
        out_specs=[block(units)] * 3 + [block(D)] * 2,
        scratch_shapes=[pltpu.VMEM((count, D), LOW)] * 2,
        out_shape=[jax.ShapeDtypeStruct((2, count, units), LOW)] * 3
        + [jax.ShapeDtypeStruct((2, count, D), LOW)] * 2,
        cost_estimate=pl.CostEstimate(
            flops=24 * count * D * units,
            bytes_accessed=6 * D * units + 16 * count * D,
            transcendentals=2 * count * units,
        ),
        name="ffn",
    )(na, nb, ga, gb, g, u, d)


def grads_kernel(tab, *refs):
    ns, ups, (hid_l, gg_l, ug_l, hid_r, gg_r, ug_r, parts_ref) = (
        refs[:4], refs[4:8], refs[8:],
    )
    wide = parts_ref.shape[2]
    half = wide // 2
    units = hid_l.shape[2]
    share = units // HEADS
    rows = ns[0].shape[1] // (2 * HEADS)
    edge = units - units % HEAD_DIM

    def tokens(near, away):
        return jnp.concatenate([near[0], near[1], away[0], away[1]], axis=0)

    n = jnp.concatenate([v[...] for v in ns], axis=0)
    up = jnp.concatenate([v[...] for v in ups], axis=0)
    for near, away, start in ((gg_l, gg_r, 0), (ug_l, ug_r, half)):
        total = dot_tn(n, tokens(near, away)).astype(LOW)
        for h in range(HEADS):
            slot = tab[h]
            for pair in range(2):
                first = (pair * HEADS + h) * rows
                here = slice(pair * rows, (pair + 1) * rows)
                parts_ref[slot, here, start + edge : start + half] = jnp.zeros(
                    (rows, half - edge), LOW
                )
                parts_ref[slot, here, start : start + units] = total[first : first + rows]
    total = dot_tn(tokens(hid_l, hid_r), up)
    strip = wide - D
    for h in range(HEADS):
        slot = tab[h]
        piece = total[h * share : (h + 1) * share].astype(LOW)
        parts_ref[slot, 2 * rows : 2 * rows + share, :D] = piece
        parts_ref[slot, 2 * rows : 2 * rows + share, D:] = jnp.zeros((share, strip), LOW)


def weight_grads(slot_of, ns, ups, near, away, height, wide):
    count = ns[0].shape[0]
    units = near[0].shape[2]
    return pl.pallas_call(
        grads_kernel,
        in_specs=[smem()] + [vmem()] * 14,
        out_specs=vmem(),
        out_shape=jax.ShapeDtypeStruct((HEADS, height, wide), LOW),
        cost_estimate=pl.CostEstimate(
            flops=24 * count * D * units, bytes_accessed=14 * 2**20, transcendentals=0
        ),
        name="weight_grads",
    )(slot_of, *ns, *ups, *near, *away)


def strips_kernel(tab, out_ref, strips_ref):
    rows, strip = out_ref.shape[1], strips_ref.shape[2]
    for slot in range(HEADS):
        for i in range(D // strip):
            strips_ref[slot, i * rows : (i + 1) * rows, :] = out_ref[
                tab[slot], :, i * strip : (i + 1) * strip
            ]


def out_strips(chips, out, strip):
    return pl.pallas_call(
        strips_kernel,
        in_specs=[smem(), vmem()],
        out_specs=vmem(),
        out_shape=jax.ShapeDtypeStruct((HEADS, out.shape[1] * D // strip, strip), LOW),
        cost_estimate=pl.CostEstimate(
            flops=0, bytes_accessed=4 * HEADS * out.shape[1] * D, transcendentals=0
        ),
        name="out_strips",
    )(chips, out)


def mid_kernel(mid_ref, pa, pb, pc, up_ref, gain_ref, w_ref, mg_ref, bg_ref, ag_ref):
    mid = mid_ref[...]
    scaled = (pa[...].astype(WIDE) + pb[...].astype(WIDE) + pc[...].astype(WIDE)) * gain_ref[
        ...
    ].astype(WIDE)
    r = lax.rsqrt(jnp.mean(mid * mid, axis=-1, keepdims=True) + EPSILON)
    inner = jnp.mean(scaled * mid, axis=-1, keepdims=True)
    mid_grad = up_ref[...].astype(WIDE) + r * scaled - mid * (r * r * r * inner)
    mg_ref[...] = mid_grad
    branch = mid_grad.astype(LOW)
    bg_ref[...] = branch
    att = dot_nt(branch, w_ref[...]).astype(LOW)
    for h in range(HEADS):
        ag_ref[h] = att[:, h * HEAD_DIM : (h + 1) * HEAD_DIM]


def mid_block(mid, pa, pb, pc, up, gain, w):
    count = mid.shape[0]
    return pl.pallas_call(
        mid_kernel,
        in_specs=[vmem()] * 7,
        out_specs=[vmem()] * 3,
        out_shape=[
            jax.ShapeDtypeStruct((count, D), WIDE),
            jax.ShapeDtypeStruct((count, D), LOW),
            jax.ShapeDtypeStruct((HEADS, count, HEAD_DIM), LOW),
        ],
        cost_estimate=pl.CostEstimate(
            flops=2 * count * D * D, bytes_accessed=6 * 2**20, transcendentals=0
        ),
        name="mid_block",
    )(mid, pa, pb, pc, up, gain, w)


def qkv_back_kernel(
    tab, dq_ref, own_ref, got_ref, loc_ref, base_ref, n_ref, w_ref, dx_ref, dw_ref, sum_ref
):
    i = pl.program_id(0)
    c, s = turning(loc_ref, base_ref)

    def rot(v):
        return v * c - pltpu.roll(v, HEAD_DIM // 2, 1) * s

    dq = rot(dq_ref[0] * SCALE).astype(LOW)
    dk = rot((own_ref[0, 0] + got_ref[0, 0].astype(WIDE)) * SCALE).astype(LOW)
    dv = (own_ref[1, 0] + got_ref[1, 0].astype(WIDE)).astype(LOW)
    grads = jnp.concatenate([dq, dk, dv], axis=1)
    dx_ref[0] = dot_nt(grads, w_ref[...]).astype(LOW)
    part = dot_tn(n_ref[0], grads)

    @pl.when(i == 0)
    def _():
        sum_ref[...] = part

    @pl.when(i > 0)
    def _():
        sum_ref[...] += part

    @pl.when(i == HEADS - 1)
    def _():
        dw_ref[...] = sum_ref[...].astype(LOW)


def qkv_back(chips, dq, own, got, loc, base, normed, w):
    count = dq.shape[1]
    block = pl.BlockSpec((1, count, HEAD_DIM), lambda i, t: (t[i], 0, 0))
    pair = pl.BlockSpec((2, 1, count, HEAD_DIM), lambda i, t: (0, t[i], 0, 0))
    weight = pl.BlockSpec((D, 3 * HEAD_DIM), lambda i, t: (0, 0))
    return pl.pallas_call(
        qkv_back_kernel,
        grid_spec=pltpu.PrefetchScalarGridSpec(
            num_scalar_prefetch=1,
            grid=(HEADS,),
            in_specs=[
                block, pair, pair,
                pl.BlockSpec((2, count, HEAD_DIM), lambda i, t: (0, 0, 0)),
                pl.BlockSpec((1, 2, HEAD_DIM), lambda i, t: (2 * t[i] + t[HEADS], 0, 0)),
                pl.BlockSpec((1, count, D), lambda i, t: (t[i], 0, 0)),
                weight,
            ],
            out_specs=[pl.BlockSpec((1, count, D), lambda i, t: (i, 0, 0)), weight],
            scratch_shapes=[pltpu.VMEM((D, 3 * HEAD_DIM), WIDE)],
        ),
        out_shape=[
            jax.ShapeDtypeStruct((HEADS, count, D), LOW),
            jax.ShapeDtypeStruct((D, 3 * HEAD_DIM), LOW),
        ],
        cost_estimate=pl.CostEstimate(
            flops=4 * HEADS * count * D * 3 * HEAD_DIM,
            bytes_accessed=6 * HEADS * count * D,
            transcendentals=0,
        ),
        name="qkv_back",
    )(chips, dq, own, got, loc, base, normed, w)


def local(
    far,
    tokens,
    segment_ids,
    second_doc,
    memory_index,
    cache_keys,
    cache_values,
    first_gain,
    query_weight,
    key_weight,
    value_weight,
    out_weight,
    second_gain,
    gate_weight,
    up_weight,
    down_weight,
    cotangent,
):
    x = tokens[0]
    upstream = cotangent[0]
    count = x.shape[0]
    blocks = count // QUERY_BLOCK
    rows = query_weight.shape[0]
    share = down_weight.shape[0]
    units = far * HEADS * share
    chip, core, pair = lax.axis_index("h"), lax.axis_index("c"), lax.axis_index("dl")
    mine = jnp.where(chip % 2 == 0, chip // 2, HEADS - 1 - chip // 2)
    slots = jnp.arange(HEADS, dtype=jnp.int32)
    chips = at_place(mine - slots)

    def by_head(w):
        return w.reshape(rows, HEADS, HEAD_DIM).transpose(1, 0, 2)

    picked = memory_index[0].transpose(1, 0, 2)
    seg_rows = jnp.broadcast_to(
        segment_ids[0].astype(LOW).reshape(1, blocks, QUERY_BLOCK), (HEADS, blocks, QUERY_BLOCK)
    )
    gains = jnp.concatenate([first_gain, second_gain])
    gain_rows = jnp.broadcast_to(
        jnp.pad(gains, (0, HEAD_DIM - 2 * rows)).reshape(1, 1, HEAD_DIM), (HEADS, 1, HEAD_DIM)
    )
    pack = jnp.concatenate(
        [
            by_head(query_weight),
            by_head(key_weight),
            by_head(value_weight),
            seg_rows,
            (picked // MEM_ROWS).astype(LOW),
            (picked % MEM_ROWS).astype(LOW),
            gain_rows,
        ],
        axis=1,
    )
    height = pack.shape[1]
    pack = jnp.pad(pack, ((0, 0), (0, -height % 16), (0, 0)))

    block = jnp.concatenate([x, out_weight], axis=0)
    split = count // 2
    got = exchange(pack)
    up_c = swap(upstream, "c")
    up_y = swap(upstream, "dl")
    up_yc = swap(up_y, "c")
    got, x_forth, x_back = lax.optimization_barrier((got, turn(block, 1), turn(block, -1)))
    forth, back = [block, x_forth, turn(x_forth, 1)], [block, x_back, turn(x_back, -1)]
    got_c = swap(got, "c")
    got_y = swap(got, "dl")
    got_yc = swap(got_y, "c")
    near = pick(core, jnp.stack([got, got_c]), jnp.stack([got_c, got]))
    away = pick(core, jnp.stack([got_y, got_yc]), jnp.stack([got_yc, got_y]))
    every = pick(pair, jnp.stack([near, away]), jnp.stack([away, near]))
    every = every.transpose(2, 0, 1, 3, 4)
    if far > 1:
        every = lax.all_gather(every, "dh", axis=0)
    else:
        every = every[None]
    every = every.transpose(0, 2, 1, 3, 4, 5)
    w_qkv = jnp.concatenate(
        [every[..., i * rows : (i + 1) * rows, :].reshape(D, HEAD_DIM) for i in range(3)], axis=1
    )
    gain_all = every[..., 3 * rows + 3 * blocks, : 2 * rows].reshape(-1, 2, rows)
    gain_one = gain_all[:, 0].reshape(1, D)
    gain_two = gain_all[:, 1].reshape(1, D)

    def seg_of(blocks_of):
        return (
            blocks_of[:, 3 * rows : 3 * rows + blocks]
            .astype(WIDE)
            .astype(jnp.int32)
            .reshape(HEADS, count)
        )

    seg_own = seg_of(got)
    seg_oth = seg_of(got_c)
    idx = (
        got[:, 3 * rows + blocks : 3 * rows + 2 * blocks].astype(WIDE) * MEM_ROWS
        + got[:, 3 * rows + 2 * blocks : 3 * rows + 3 * blocks].astype(WIDE)
    ).astype(jnp.int32)
    idx = idx.reshape(HEADS, count, 1)

    block_docs = seg_own[:, ::QUERY_BLOCK]
    docs = second_doc.shape[1]
    doc_ids = jnp.arange(docs, dtype=jnp.int32)
    mates = jnp.sum(
        jnp.where(block_docs[:, :, None] == doc_ids, second_doc[0][None, None, :], 0), axis=-1
    )
    seg_all = jnp.concatenate([seg_own, seg_oth], axis=0)
    before = jnp.sum(
        (seg_all.reshape(1, -1) < block_docs[:, :1]).astype(jnp.int32), axis=1
    )
    tab = jnp.concatenate(
        [
            block_docs.reshape(-1),
            mates.reshape(-1),
            before // (2 * count),
            jnp.stack([core, chip]),
        ]
    ).astype(jnp.int32)

    loc, base = (jnp.asarray(table) for table in turn_tables(count))

    seg_thin = seg_own.reshape(HEADS, count, 1)
    early = (w_qkv, gain_one, tab, up_c, up_y, up_yc)
    early, gate_late, up_late, forth[2], back[2] = lax.optimization_barrier(
        (early, gate_weight, up_weight, forth[2], back[2])
    )
    w_qkv, gain_one, tab, up_c, up_y, up_yc = early
    forth.append(turn(forth[2], 1))
    back.append(turn(back[2], -1))
    at_near, at_far = [0, 1, 7, 2, 6], [3, 5, 4]

    def chips_at(order):
        places = at_place(mine - jnp.asarray(list(order), jnp.int32))
        return jnp.concatenate([places, core[None]]).astype(jnp.int32)

    near_slots = [forth[0], forth[1], back[1], forth[2], back[2]]
    held = qkv_blocks(
        chips_at(at_near), [((v, count),) for v in near_slots], gain_one, w_qkv, loc, base, ()
    )
    half = units + -units % HEAD_DIM
    wide = 2 * half

    def by_owner(w):
        w = w.reshape(rows, far, 2, HEADS, 2, share).transpose(2, 4, 0, 1, 3, 5)
        return jnp.pad(w.reshape(2, 2, rows, units), ((0, 0),) * 3 + ((0, half - units),))

    gu = jnp.concatenate([by_owner(gate_late), by_owner(up_late)], axis=-1)
    kept = pick(core, gu[:, 0], gu[:, 1])
    came = swap(pick(core, gu[:, 1], gu[:, 0]), "c")
    gu = pick(core, jnp.stack([kept, came], 1), jnp.stack([came, kept], 1))
    kept = pick(pair, gu[0], gu[1])
    came = swap(pick(pair, gu[1], gu[0]), "dl")
    gu = pick(pair, jnp.stack([kept, came]), jnp.stack([came, kept])).reshape(4 * rows, wide)
    if far == 1:
        deep = 2 * rows
        lower = jnp.concatenate(fold(down_weight, deep), axis=1)
    else:
        deep = share
        lower = jnp.pad(down_weight, ((0, 0), (0, wide - D)))
    bundle = jnp.concatenate([gu, lower], axis=0)
    height = 4 * rows + share
    if far > 1:
        bundle = lax.all_gather(bundle, "dh", axis=0, tiled=True)
    upper = bundle.shape[0] // 2
    *held, bundle, forth[3], back[3] = lax.optimization_barrier(
        (*held, bundle, forth[3], back[3])
    )
    far_first, far_last = turn(forth[3][:split], 1), turn(back[3][split:], -1)
    bundle, *_ = lax.optimization_barrier((bundle, far_first, far_last))
    w_forth, w_back = [bundle, turn(bundle, 1)], [bundle, turn(bundle, -1)]

    far_slots = [
        ((forth[3], count),),
        ((back[3], count),),
        ((far_first, split), (far_last, count - split)),
    ]
    queries, own, normed_one = qkv_blocks(
        chips_at(at_far), far_slots, gain_one, w_qkv, loc, base, tuple(held)
    )
    outs = jnp.stack([v[-rows:] for v in (*forth, far_last, *back[:0:-1])])
    queries, own, outs, w_forth[1], w_back[1] = lax.optimization_barrier(
        (queries, own, outs, w_forth[1], w_back[1])
    )
    other = swap(own, "c")
    outs_c = swap(outs, "c")
    outs_y = swap(outs, "dl")
    seg_own_row = seg_own.reshape(HEADS, 1, count)
    seg_oth_row = seg_oth.reshape(HEADS, 1, count)
    cached = [cache[0].reshape(-1, D) for cache in (cache_keys, cache_values)]
    attention, attention_low, lse, memory = attend(
        tab, queries, own, other, seg_thin, seg_own_row, seg_oth_row, idx, *cached
    )
    w_forth.append(turn(w_forth[1], 1))
    w_back.append(turn(w_back[1], -1))
    attention_low, outs_y, w_forth[2], w_back[2] = lax.optimization_barrier(
        (attention_low, outs_y, w_forth[2], w_back[2])
    )

    heads = exchange(attention_low)
    w_forth.append(turn(w_forth[2], 1))
    w_back.append(turn(w_back[2], -1))
    outs_yc = swap(outs_y, "c")
    heads, w_forth[3], w_back[3] = lax.optimization_barrier((heads, w_forth[3], w_back[3]))
    w_first, w_last = turn(w_forth[3][:upper], 1), turn(w_back[3][upper:], -1)
    slot_of = lax.rem(mine - jnp.asarray(PLACE, jnp.int32) + HEADS, HEADS).astype(jnp.int32)
    if far == 1:
        sources = [outs, outs_c, outs_y, outs_yc]
    else:
        near = pick(core, jnp.stack([outs, outs_c], 1), jnp.stack([outs_c, outs], 1))
        away = pick(core, jnp.stack([outs_y, outs_yc], 1), jnp.stack([outs_yc, outs_y], 1))
        sources = pick(pair, jnp.stack([near, away]), jnp.stack([away, near]))
        sources = lax.all_gather(jnp.take(sources, slot_of, axis=1), "dh", axis=0)
        sources = [sources.reshape(D, D)]
    where = jnp.concatenate([chips, jnp.stack([pair, core])]).astype(jnp.int32)
    attended, mid, normed_two, out_w = out_block(where, heads, sources, x, gain_two)
    normed_two, w_first, w_last = lax.optimization_barrier((normed_two, w_first, w_last))
    w_slots = w_forth + [w_first, w_last] + w_back[:0:-1]

    if far == 1:
        gate_w, up_w, down_w = weights(where, w_slots, units)
    else:
        middle = jnp.concatenate(w_slots[HEADS // 2 : HEADS // 2 + 2], axis=0)
        every = jnp.stack(w_slots[: HEADS // 2] + [middle] + w_slots[HEADS // 2 + 2 :])
        every = jnp.take(every, slot_of, axis=0).reshape(HEADS, far, height, wide)
        gu = every[:, :, : 4 * rows].reshape(HEADS, far, 2, 2 * rows, wide)
        gu = gu.transpose(1, 2, 0, 3, 4).reshape(D, wide)
        gate_w, up_w = gu[:, :units], gu[:, half : half + units]
        down_w = every[:, :, 4 * rows :, :D].transpose(1, 0, 2, 3).reshape(units, D)

    n_c = swap(normed_two, "c")
    n_y = swap(normed_two, "dl")
    hid_l, gg_l, ug_l, dn_l, out_l = ffn(normed_two, n_c, upstream, up_c, gate_w, up_w, down_w)
    n_y, dn_l = lax.optimization_barrier((n_y, dn_l))
    n_yc = swap(n_y, "c")
    hid_r, gg_r, ug_r, dn_r, out_r = ffn(n_y, n_yc, up_y, up_yc, gate_w, up_w, down_w)

    def to_away(away):
        return (away[0].astype(WIDE) + swap(away[1], "c").astype(WIDE)).astype(LOW)

    there = to_away(dn_r)
    there, hid_l, gg_l, ug_l, hid_r, gg_r, ug_r = lax.optimization_barrier(
        (there, hid_l, gg_l, ug_l, hid_r, gg_r, ug_r)
    )
    n_all, u_all = [normed_two, n_c, n_y, n_yc], [upstream, up_c, up_y, up_yc]
    near, away = (hid_l, gg_l, ug_l), (hid_r, gg_r, ug_r)
    if far == 1:
        parts = weight_grads(slot_of, n_all, u_all, near, away, height, wide)
    else:

        def over_tokens(left, right):
            return jnp.einsum(
                "gtd,gtf->df", left, right, preferred_element_type=WIDE
            ).astype(LOW)

        def by_rows(w):
            w = jnp.pad(w, ((0, 0), (0, half - units)))
            return w.reshape(far, 2, HEADS, 2 * rows, half).transpose(2, 0, 1, 3, 4)

        n_all, u_all = jnp.stack(n_all), jnp.stack(u_all)
        hid, gg, ug = (jnp.concatenate(pieces, axis=0) for pieces in zip(near, away))
        gu = jnp.concatenate(
            [by_rows(over_tokens(n_all, gg)), by_rows(over_tokens(n_all, ug))], axis=-1
        ).reshape(HEADS, far, 4 * rows, wide)
        down = over_tokens(hid, u_all).reshape(far, HEADS, share, D).transpose(1, 0, 2, 3)
        down = jnp.pad(down, ((0, 0), (0, 0), (0, 0), (0, wide - D)))
        parts = jnp.concatenate([gu, down], axis=2)
        parts = jnp.take(parts.reshape(HEADS, far * height, wide), chips, axis=0)

    out_l, out_r, _ = lax.optimization_barrier((out_l, out_r, parts))
    output = mid
    for part in (out_l[0], swap(out_l[1], "c"), swap(to_away(out_r), "dl")):
        output = output + part.astype(WIDE)
    output = output.astype(LOW)

    sums = [dn_l[0], swap(dn_l[1], "c"), swap(there, "dl")]
    sums[2], parts = lax.optimization_barrier((sums[2], parts))
    mid_grad, branch, att_grad = mid_block(mid, *sums, upstream, gain_two, out_w)
    ups = exchange(att_grad)

    def plus(block, arrived, start):
        size = arrived.shape[0]
        total = block[start : start + size].astype(WIDE) + arrived.astype(WIDE)
        pieces = [block[:start], total, block[start + size :]]
        pieces = [piece.astype(LOW) for piece in pieces if piece.shape[0]]
        return jnp.concatenate(pieces, axis=0)

    def ring_first(blocks, split):
        middle = blocks[HEADS // 2]
        return (
            plus(blocks[HEADS // 2 + 1], turn(middle[:split].astype(LOW), 1), 0),
            plus(blocks[HEADS // 2 - 1], turn(middle[split:].astype(LOW), -1), split),
        )

    def ring_next(blocks, forth, back, step):
        return (
            plus(blocks[HEADS // 2 + step], turn(forth, 1), 0),
            plus(blocks[HEADS // 2 - step], turn(back, -1), 0),
        )

    def ring_last(blocks, forth, back):
        return blocks[0].astype(WIDE) + forth.astype(WIDE) + back.astype(WIDE)

    def over_owner(w, width):
        w = w.reshape(far, 2, HEADS, 2, rows, width)
        kept = pick(core, w[:, :, :, 0], w[:, :, :, 1])
        came = swap(pick(core, w[:, :, :, 1], w[:, :, :, 0]), "c")
        w = kept.astype(WIDE) + came.astype(WIDE)
        kept = pick(pair, w[:, 0], w[:, 1])
        came = swap(pick(pair, w[:, 1], w[:, 0]).astype(LOW), "dl")
        w = (kept + came.astype(WIDE)).astype(LOW)
        if far > 1:
            w = lax.psum_scatter(w, "dh", scatter_dimension=0, tiled=True)
        return w[0]

    out_part = over_owner(
        jnp.einsum("td,te->de", attended, branch, preferred_element_type=WIDE).astype(LOW), D
    )
    strip = wide - D
    upper = 4 * rows if far == 1 else parts.shape[1] // 2
    blocks = [parts[slot].astype(WIDE) for slot in range(HEADS)]
    if far == 1:
        strips = out_strips(where, out_part, strip)
        below = share - strips.shape[1]
        for slot in range(HEADS):
            if slot != HEADS // 2:
                blocks[slot] = blocks[slot] + jnp.pad(
                    strips[slot].astype(WIDE), ((4 * rows, below), (D, 0))
                )
        out_far = turn(strips[HEADS // 2], HEADS // 2)
    else:
        out_far = exchange(out_part)
    forth, back = ring_first(blocks, upper)
    ups, forth, back = lax.optimization_barrier((ups, forth, back))
    forth, back = ring_next(blocks, forth, back, 2)

    dq, d_own, d_oth = attend_back(
        tab, queries, ups, attention, lse, own, other, memory, seg_thin, seg_own_row, seg_oth_row
    )
    d_got = swap(d_oth, "c")
    dq, forth, back = lax.optimization_barrier((dq, forth, back))
    dx, dw = qkv_back(
        chips_at(range(HEADS)), dq, d_own, d_got, loc, base, normed_one, w_qkv
    )
    arrived_forth, arrived_back = turn(forth, 1), turn(back, -1)
    dx, arrived_forth, arrived_back = lax.optimization_barrier((dx, arrived_forth, arrived_back))
    dx_forth, dx_back = ring_first(dx, split)
    dw, dx_forth, dx_back, arrived_forth, arrived_back = lax.optimization_barrier(
        (dw, dx_forth, dx_back, arrived_forth, arrived_back)
    )
    forth = plus(blocks[HEADS - 1], arrived_forth, 0)
    back = plus(blocks[1], arrived_back, 0)

    dw = over_owner(dw, 3 * HEAD_DIM)
    dx_forth, dx_back = ring_next(dx, dx_forth, dx_back, 2)
    qkv_grads = exchange(dw).astype(WIDE)
    got_forth, got_back = turn(dx_forth, 1), turn(dx_back, -1)
    qkv_grads, got_forth, got_back = lax.optimization_barrier((qkv_grads, got_forth, got_back))
    dx_forth, dx_back = plus(dx[HEADS - 1], got_forth, 0), plus(dx[1], got_back, 0)
    normed_one_grad = ring_last(dx, turn(dx_forth, 1), turn(dx_back, -1))

    summed = ring_last(blocks, turn(forth, 1), turn(back, -1)).astype(LOW)
    if far > 1:
        summed = lax.psum_scatter(summed, "dh", scatter_dimension=0, tiled=True)
    down_w_grad = summed[4 * rows : 4 * rows + share, :D].astype(WIDE)
    if far == 1:
        out_w_grad = summed[4 * rows : 4 * rows + strips.shape[1], D:].astype(WIDE)
        out_w_grad = out_w_grad + out_far.astype(WIDE)
        out_w_grad = out_w_grad.reshape(D // strip, rows, strip).transpose(1, 0, 2).reshape(rows, D)
    else:
        out_w_grad = jnp.sum(out_far.astype(WIDE), axis=0)
    gu = summed[: 4 * rows].reshape(2, 2, rows, wide)
    kept = pick(core, gu[:, 0], gu[:, 1])
    came = swap(pick(core, gu[:, 1], gu[:, 0]), "c")
    gu = pick(core, jnp.stack([kept, came], 1), jnp.stack([came, kept], 1))
    kept = pick(pair, gu[0], gu[1])
    came = swap(pick(pair, gu[1], gu[0]), "dl")
    gu = pick(pair, jnp.stack([kept, came]), jnp.stack([came, kept]))
    gu = jnp.stack([gu[..., :units], gu[..., half : half + units]])
    gu = (
        gu.reshape(2, 2, 2, rows, far, HEADS, share)
        .transpose(0, 3, 4, 1, 5, 2, 6)
        .reshape(2, rows, FF)
        .astype(WIDE)
    )
    gate_w_grad, up_w_grad = gu[0], gu[1]

    wide_x = x.astype(WIDE)
    r = lax.rsqrt(jnp.mean(wide_x * wide_x, axis=-1, keepdims=True) + EPSILON)
    scaled = normed_one_grad * gain_one.astype(WIDE)
    inner = jnp.mean(scaled * wide_x, axis=-1, keepdims=True)
    input_grad = mid_grad + r * scaled - wide_x * (r * r * r * inner)

    q_w_grad, k_w_grad, v_w_grad = (
        qkv_grads[:, :, i * HEAD_DIM : (i + 1) * HEAD_DIM].transpose(1, 0, 2).reshape(rows, D)
        for i in range(3)
    )

    def gain_grad(gain, pairs):
        total = 0.0
        for grad, weight in pairs:
            total = total + jnp.sum(grad * weight.astype(WIDE), axis=1)
        return total / gain.astype(WIDE)

    first_gain_grad = gain_grad(
        first_gain,
        ((q_w_grad, query_weight), (k_w_grad, key_weight), (v_w_grad, value_weight)),
    )
    second_gain_grad = gain_grad(
        second_gain, ((gate_w_grad, gate_weight), (up_w_grad, up_weight))
    )
    return (
        output[None],
        input_grad[None],
        first_gain_grad,
        q_w_grad,
        k_w_grad,
        v_w_grad,
        out_w_grad,
        second_gain_grad,
        gate_w_grad,
        up_w_grad,
        down_w_grad,
    )


def solution(mesh):
    far = mesh.shape["dp"] // 2
    cores = mesh.shape["seq"] // HEADS
    fine = Mesh(mesh.devices.reshape(far, 2, HEADS, cores), ("dh", "dl", "h", "c"))
    dp, seq, every = ("dh", "dl"), ("h", "c"), ("dh", "dl", "h", "c")
    rows = P(every, None)
    return jax.shard_map(
        functools.partial(local, far),
        mesh=fine,
        in_specs=(
            P(dp, seq, None),
            P(dp, seq),
            P(dp, None),
            P(dp, seq, None, None),
            P(dp, None, None, None),
            P(dp, None, None, None),
            P(every),
            rows,
            rows,
            rows,
            rows,
            P(every),
            rows,
            rows,
            rows,
            P(dp, seq, None),
        ),
        out_specs=(
            P(dp, seq, None),
            P(dp, seq, None),
            P(every),
            rows,
            rows,
            rows,
            rows,
            P(every),
            rows,
            rows,
            rows,
        ),
        check_vma=False,
    )
```

```python
import functools
import math

import jax
import jax.numpy as jnp
import numpy as np
from jax import lax
from jax.experimental import pallas as pl
from jax.experimental.pallas import tpu as pltpu
from jax.sharding import Mesh
from jax.sharding import PartitionSpec as P

D = 1024
FF = 2816
HEADS = 8
HEAD_DIM = 128
QUERY_BLOCK = 128
MEM_ROWS = 256
EPSILON = 1e-05
NEGATIVE = -1e30
SCALE = 1.0 / math.sqrt(HEAD_DIM)
LOG2 = SCALE * math.log2(math.e)
LOW = jnp.bfloat16
WIDE = jnp.float32

RING = [2 * i for i in range(HEADS // 2)] + [2 * i + 1 for i in reversed(range(HEADS // 2))]
PLACE = [RING.index(i) for i in range(HEADS)]


def dot_nn(a, b):
    return lax.dot_general(a, b, (((1,), (0,)), ((), ())), preferred_element_type=WIDE)


def dot_nt(a, b):
    return lax.dot_general(a, b, (((1,), (1,)), ((), ())), preferred_element_type=WIDE)


def dot_tn(a, b):
    return lax.dot_general(a, b, (((0,), (0,)), ((), ())), preferred_element_type=WIDE)


def swap(block, axis):
    return lax.ppermute(block, axis, [(0, 1), (1, 0)])


def turn(block, distance):
    route = [(RING[i], RING[(i + distance) % HEADS]) for i in range(HEADS)]
    return lax.ppermute(block, "h", route)


def at_place(place):
    place = lax.rem(place + 2 * HEADS, HEADS)
    return jnp.where(place < HEADS // 2, 2 * place, 2 * (HEADS - 1 - place) + 1)


def exchange(blocks):
    return lax.all_to_all(blocks, "h", 0, 0)


def pick(flag, first, second):
    return jnp.where(flag == 0, first, second)


def smem():
    return pl.BlockSpec(memory_space=pltpu.SMEM)


def vmem():
    return pl.BlockSpec(memory_space=pltpu.VMEM)


def turn_tables(count):
    half = HEAD_DIM // 2
    freqs = 10000.0 ** (-np.arange(half, dtype=np.float64) * 2.0 / HEAD_DIM)
    freqs = np.concatenate([freqs, freqs])

    def table(positions):
        angles = positions[:, None] * freqs
        return np.stack([np.cos(angles), np.sin(angles)]).astype(np.float32)

    return table(np.arange(count)), table(np.arange(2 * HEADS) * count).transpose(1, 0, 2)


def turning(loc_ref, base_ref):
    cl, sl = loc_ref[0], loc_ref[1]
    cb, sb = base_ref[0, 0:1, :], base_ref[0, 1:2, :]
    sine = sl * cb + cl * sb
    lane = lax.broadcasted_iota(jnp.int32, sine.shape, 1)
    return cl * cb - sl * sb, jnp.where(lane < HEAD_DIM // 2, -sine, sine)


def qkv_kernel(parts, tab, *refs):
    xs, (gain_ref, w_ref, loc_ref, base_ref) = refs[: sum(parts)], refs[sum(parts) : sum(parts) + 4]
    q_ref, kv_ref, n_ref, x_ref = refs[-4:]
    i = pl.program_id(0)
    first = 0
    for step, number in enumerate(parts):

        @pl.when(i == step)
        def _(blocks=xs[first : first + number]):
            row = 0
            for block in blocks:
                size = block.shape[0]
                x_ref[row : row + size, :] = block[...]
                row += size

        first += number
    x = x_ref[...].astype(WIDE)
    r = lax.rsqrt(jnp.mean(x * x, axis=-1, keepdims=True) + EPSILON)
    normed = (x * r * gain_ref[...].astype(WIDE)).astype(LOW)
    n_ref[0] = normed
    out = dot_nn(normed, w_ref[...])
    c, s = turning(loc_ref, base_ref)

    def rot(v):
        return v * c + pltpu.roll(v, HEAD_DIM // 2, 1) * s

    q_ref[0] = rot(out[:, :HEAD_DIM]).astype(LOW)
    kv_ref[0, 0] = rot(out[:, HEAD_DIM : 2 * HEAD_DIM]).astype(LOW)
    kv_ref[1, 0] = out[:, 2 * HEAD_DIM :].astype(LOW)


def qkv_blocks(chips, xs, gain, w, loc, base, held):
    count = loc.shape[1]
    steps = len(xs)
    flat = [piece for block in xs for piece, _ in block]
    read = [size for block in xs for _, size in block]

    def whole(shape):
        return pl.BlockSpec(shape, lambda i, t: (0, 0))

    def block(*shape):
        return pl.BlockSpec((1, *shape), lambda i, t: (t[i], 0, 0))

    spec = pltpu.PrefetchScalarGridSpec(
        num_scalar_prefetch=1,
        grid=(len(xs),),
        in_specs=[whole((size, D)) for size in read]
        + [
            whole((1, D)),
            whole((D, 3 * HEAD_DIM)),
            pl.BlockSpec((2, count, HEAD_DIM), lambda i, t: (0, 0, 0)),
            pl.BlockSpec((1, 2, HEAD_DIM), lambda i, t: (2 * t[i] + t[steps], 0, 0)),
        ]
        + [pl.BlockSpec(memory_space=pl.ANY)] * len(held),
        out_specs=[
            block(count, HEAD_DIM),
            pl.BlockSpec((2, 1, count, HEAD_DIM), lambda i, t: (0, t[i], 0, 0)),
            block(count, D),
        ],
        scratch_shapes=[pltpu.VMEM((count, D), LOW)],
    )
    return pl.pallas_call(
        functools.partial(qkv_kernel, [len(block) for block in xs]),
        grid_spec=spec,
        out_shape=[
            jax.ShapeDtypeStruct((HEADS, count, HEAD_DIM), LOW),
            jax.ShapeDtypeStruct((2, HEADS, count, HEAD_DIM), LOW),
            jax.ShapeDtypeStruct((HEADS, count, D), LOW),
        ],
        input_output_aliases={len(flat) + 5 + i: i for i in range(len(held))},
        cost_estimate=pl.CostEstimate(
            flops=len(xs) * count * D, bytes_accessed=len(xs) * count, transcendentals=0
        ),
        name=f"qkv{len(xs)}",
    )(chips, *flat, gain, w, loc, base, *held)


def causal(count):
    rows = lax.broadcasted_iota(jnp.int32, (count, count), 0)
    return lax.broadcasted_iota(jnp.int32, (count, count), 1) <= rows


def attend_kernel(
    tab, q_ref, own_ref, oth_ref, segq_ref, sego_ref, segt_ref, idx_ref, ck_ref, cv_ref,
    o_ref, low_ref, lse_ref, mem_ref,
):
    i = pl.program_id(0)
    parity = tab[40]
    count = q_ref.shape[1]
    q = q_ref[0]
    segq = segq_ref[0]

    s1 = dot_nt(q, own_ref[0, i]) * LOG2
    s2 = dot_nt(q, oth_ref[0, i]) * LOG2
    s1 = jnp.where((sego_ref[i] == segq) & causal(count), s1, NEGATIVE)
    s2 = jnp.where(segt_ref[i] == segq + 64 * (1 - parity), s2, NEGATIVE)
    memory = []
    for b in range(count // QUERY_BLOCK):
        rows = slice(b * QUERY_BLOCK, (b + 1) * QUERY_BLOCK)
        doc = tab[2 * i + b]
        mate = tab[16 + 2 * i + b]
        idx = idx_ref[0, rows, :]
        lane = lax.broadcasted_iota(jnp.int32, (QUERY_BLOCK, MEM_ROWS), 1)
        first = jnp.where(idx == lane, 1.0, 0.0).astype(LOW)
        second = jnp.where(idx == lane + MEM_ROWS, 1.0, 0.0).astype(LOW)
        here = pl.ds(pl.multiple_of(doc * MEM_ROWS, MEM_ROWS), MEM_ROWS)
        there = pl.ds(pl.multiple_of(mate * MEM_ROWS, MEM_ROWS), MEM_ROWS)
        mk = (dot_nn(first, ck_ref[here, :]) + dot_nn(second, ck_ref[there, :])).astype(LOW)
        mv = (dot_nn(first, cv_ref[here, :]) + dot_nn(second, cv_ref[there, :])).astype(LOW)
        mem_ref[0, 0, rows, :] = mk
        mem_ref[1, 0, rows, :] = mv
        s = jnp.where(segq[rows] == doc, dot_nt(q[rows], mk) * LOG2, NEGATIVE)
        memory.append((s, mv))
    sm = jnp.concatenate([s for s, _ in memory], axis=0)
    top = jnp.maximum(
        jnp.max(jnp.maximum(s1, s2), axis=-1, keepdims=True), jnp.max(sm, axis=-1, keepdims=True)
    )
    p1 = jnp.exp2(s1 - top)
    p2 = jnp.exp2(s2 - top)
    pm = jnp.exp2(sm - top)
    total = jnp.sum(p1 + p2, axis=-1, keepdims=True) + jnp.sum(pm, axis=-1, keepdims=True)
    pm = pm.astype(LOW)
    acc = jnp.concatenate(
        [
            dot_nn(pm[b * QUERY_BLOCK : (b + 1) * QUERY_BLOCK], mv)
            for b, (_, mv) in enumerate(memory)
        ],
        axis=0,
    )
    acc = acc + dot_nn(p1.astype(LOW), own_ref[1, i]) + dot_nn(p2.astype(LOW), oth_ref[1, i])

    def body(j, state):
        top, total, acc = state
        s1 = dot_nt(q, own_ref[0, j]) * LOG2
        s2 = dot_nt(q, oth_ref[0, j]) * LOG2
        s1 = jnp.where(sego_ref[j] == segq, s1, NEGATIVE)
        s2 = jnp.where(segt_ref[j] == segq, s2, NEGATIVE)
        fresh = jnp.maximum(top, jnp.max(jnp.maximum(s1, s2), axis=-1, keepdims=True))
        p1 = jnp.exp2(s1 - fresh)
        p2 = jnp.exp2(s2 - fresh)
        decay = jnp.exp2(top - fresh)
        total = total * decay + jnp.sum(p1 + p2, axis=-1, keepdims=True)
        acc = (
            acc * decay
            + dot_nn(p1.astype(LOW), own_ref[1, j])
            + dot_nn(p2.astype(LOW), oth_ref[1, j])
        )
        return fresh, total, acc

    top, total, acc = lax.fori_loop(tab[32 + i], i, body, (top, total, acc))
    out = acc / total
    o_ref[0] = out
    low_ref[0] = out.astype(LOW)
    lse_ref[0] = top + jnp.log2(total)


def attend(tab, q, own, oth, segq, sego, segt, idx, ck, cv):
    count = q.shape[1]
    block = pl.BlockSpec((1, count, HEAD_DIM), lambda i, t: (i, 0, 0))
    thin = pl.BlockSpec((1, count, 1), lambda i, t: (i, 0, 0))
    whole = pl.BlockSpec((2, HEADS, count, HEAD_DIM), lambda i, t: (0, 0, 0, 0))
    segs = pl.BlockSpec((HEADS, 1, count), lambda i, t: (0, 0, 0))
    cache = pl.BlockSpec((ck.shape[0], HEAD_DIM), lambda i, t: (0, t[41]))
    mem = pl.BlockSpec((2, 1, count, HEAD_DIM), lambda i, t: (0, i, 0, 0))
    return pl.pallas_call(
        attend_kernel,
        grid_spec=pltpu.PrefetchScalarGridSpec(
            num_scalar_prefetch=1,
            grid=(HEADS,),
            in_specs=[block, whole, whole, thin, segs, segs, thin, cache, cache],
            out_specs=[block, block, thin, mem],
        ),
        out_shape=[
            jax.ShapeDtypeStruct((HEADS, count, HEAD_DIM), WIDE),
            jax.ShapeDtypeStruct((HEADS, count, HEAD_DIM), LOW),
            jax.ShapeDtypeStruct((HEADS, count, 1), WIDE),
            jax.ShapeDtypeStruct((2, HEADS, count, HEAD_DIM), LOW),
        ],
        cost_estimate=pl.CostEstimate(
            flops=25 * 10**9, bytes_accessed=6 * 2**20, transcendentals=3 * 10**6
        ),
        name="attend",
    )(tab, q, own, oth, segq, sego, segt, idx, ck, cv)


def attend_back_kernel(
    tab, q_ref, up_ref, o_ref, lse_ref, own_ref, oth_ref, mem_ref, segq_ref, sego_ref, segt_ref,
    dq_ref, down_ref, doth_ref, sum_ref,
):
    i = pl.program_id(0)

    @pl.when(i == 0)
    def _():
        sum_ref[...] = jnp.zeros_like(sum_ref)

    parity = tab[40]
    count = q_ref.shape[1]
    q = q_ref[0]
    up = up_ref[0]
    lse = lse_ref[0]
    segq = segq_ref[0]
    delta = jnp.sum(up.astype(WIDE) * o_ref[0], axis=-1, keepdims=True)
    partial = []
    for b in range(count // QUERY_BLOCK):
        rows = slice(b * QUERY_BLOCK, (b + 1) * QUERY_BLOCK)
        mk = mem_ref[0, 0, rows, :]
        mv = mem_ref[1, 0, rows, :]
        ok = segq[rows] == tab[2 * i + b]
        p = jnp.exp2(jnp.where(ok, dot_nt(q[rows], mk) * LOG2 - lse[rows], NEGATIVE))
        ds = (p * (dot_nt(up[rows], mv) - delta[rows])).astype(LOW)
        partial.append(dot_nn(ds, mk))

    def tile(side, ref, j, ok, dq):
        k = ref[0, j]
        v = ref[1, j]
        p = jnp.exp2(jnp.where(ok, dot_nt(q, k) * LOG2 - lse, NEGATIVE))
        ds = (p * (dot_nt(up, v) - delta)).astype(LOW)
        sum_ref[side, 0, j] += dot_tn(ds, q)
        sum_ref[side, 1, j] += dot_tn(p.astype(LOW), up)
        return dq + dot_nn(ds, k)

    dq = jnp.concatenate(partial, axis=0)
    dq = tile(0, own_ref, i, (sego_ref[i] == segq) & causal(count), dq)
    dq = tile(1, oth_ref, i, segt_ref[i] == segq + 64 * (1 - parity), dq)

    def body(j, dq):
        dq = tile(0, own_ref, j, sego_ref[j] == segq, dq)
        return tile(1, oth_ref, j, segt_ref[j] == segq, dq)

    dq_ref[0] = lax.fori_loop(tab[32 + i], i, body, dq)

    @pl.when(i == HEADS - 1)
    def _():
        down_ref[...] = sum_ref[0]
        doth_ref[...] = sum_ref[1].astype(LOW)


def attend_back(tab, q, up, o, lse, own, oth, mem, segq, sego, segt):
    count = q.shape[1]
    block = pl.BlockSpec((1, count, HEAD_DIM), lambda i, t: (i, 0, 0))
    thin = pl.BlockSpec((1, count, 1), lambda i, t: (i, 0, 0))
    whole = pl.BlockSpec((2, HEADS, count, HEAD_DIM), lambda i, t: (0, 0, 0, 0))
    segs = pl.BlockSpec((HEADS, 1, count), lambda i, t: (0, 0, 0))
    memory = pl.BlockSpec((2, 1, count, HEAD_DIM), lambda i, t: (0, i, 0, 0))
    return pl.pallas_call(
        attend_back_kernel,
        grid_spec=pltpu.PrefetchScalarGridSpec(
            num_scalar_prefetch=1,
            grid=(HEADS,),
            in_specs=[block, block, block, thin, whole, whole, memory, thin, segs, segs],
            out_specs=[block, whole, whole],
            scratch_shapes=[pltpu.VMEM((2, 2, HEADS, count, HEAD_DIM), WIDE)],
        ),
        out_shape=[
            jax.ShapeDtypeStruct((HEADS, count, HEAD_DIM), WIDE),
            jax.ShapeDtypeStruct((2, HEADS, count, HEAD_DIM), WIDE),
            jax.ShapeDtypeStruct((2, HEADS, count, HEAD_DIM), LOW),
        ],
        cost_estimate=pl.CostEstimate(
            flops=30 * 10**9, bytes_accessed=10 * 2**20, transcendentals=3 * 10**6
        ),
        name="attend_back",
    )(tab, q, up, o, lse, own, oth, mem, segq, sego, segt)


def place_rows(tab, sources, w_ref):
    rows = sources[0].shape[1]
    for k, source in enumerate(sources):
        pair = tab[8] if k < 2 else 1 - tab[8]
        core = tab[9] if k % 2 == 0 else 1 - tab[9]
        for slot in range(HEADS):
            start = ((pair * HEADS + tab[slot]) * 2 + core) * rows
            w_ref[pl.ds(pl.multiple_of(start, rows), rows), :] = source[slot]


def out_kernel(tab, heads_ref, *refs):
    sources, (x_ref, gain_ref, att_ref, mid_ref, n_ref, w_ref) = refs[:-6], refs[-6:]
    if len(sources) == 1:
        w_ref[...] = sources[0][...]
    else:
        place_rows(tab, sources, w_ref)
    for h in range(HEADS):
        att_ref[:, h * HEAD_DIM : (h + 1) * HEAD_DIM] = heads_ref[h]
    mid = x_ref[...].astype(WIDE) + dot_nn(att_ref[...], w_ref[...])
    mid_ref[...] = mid
    r = lax.rsqrt(jnp.mean(mid * mid, axis=-1, keepdims=True) + EPSILON)
    n_ref[...] = (mid * r * gain_ref[...].astype(WIDE)).astype(LOW)


def out_block(tab, heads, sources, x, gain):
    count = x.shape[0]
    return pl.pallas_call(
        out_kernel,
        in_specs=[smem()] + [vmem()] * (3 + len(sources)),
        out_specs=[vmem()] * 4,
        out_shape=[
            jax.ShapeDtypeStruct((count, D), LOW),
            jax.ShapeDtypeStruct((count, D), WIDE),
            jax.ShapeDtypeStruct((count, D), LOW),
            jax.ShapeDtypeStruct((D, D), LOW),
        ],
        cost_estimate=pl.CostEstimate(
            flops=2 * count * D * D, bytes_accessed=6 * 2**20, transcendentals=0
        ),
        name="out_block",
    )(tab, heads, *sources, x, gain)


def fold(block, deep):
    half, rest = D // 2, block.shape[0] - deep
    middle = jnp.concatenate([block[deep:, :half], block[: deep - rest, half:]], axis=0)
    last = block[deep - rest :, half:]
    last = jnp.concatenate([last, jnp.zeros((deep - last.shape[0], half), last.dtype)], axis=0)
    return block[:deep, :half], middle, last


def unfolded(block, share):
    deep, half = block.shape[0], D // 2
    rest = share - deep
    return [
        (0, deep, 0, block[:, :half]),
        (deep, rest, 0, block[:rest, half:D]),
        (0, deep - rest, half, block[rest:, half:D]),
        (deep - rest, share - deep + rest, half, block[: share - deep + rest, D:]),
    ]


def weights_kernel(tab, *refs):
    blocks, (gate_ref, up_ref, down_ref, acc_ref) = refs[:-4], refs[-4:]
    units = gate_ref.shape[1]
    height, wide = blocks[0].shape
    half = wide // 2
    share = units // HEADS
    rows = D // (2 * HEADS)
    middle = blocks[HEADS // 2].shape[0]
    for slot in range(HEADS):
        chip = tab[slot]
        if slot == HEADS // 2:
            pieces = [(0, blocks[slot]), (middle, blocks[slot + 1])]
        else:
            pieces = [(0, blocks[slot if slot < HEADS // 2 else slot + 1])]
        for start, ref in pieces:
            stop = start + ref.shape[0]
            for pair in range(2):
                first, last = max(start, pair * rows), min(stop, (pair + 1) * rows)
                if first < last:
                    size = last - first
                    here = (pair * HEADS + chip) * rows + first - pair * rows
                    here = pl.ds(pl.multiple_of(here, math.gcd(rows, first)), size)
                    gate_ref[here, :] = ref[first - start : last - start, :units]
                    up_ref[here, :] = ref[first - start : last - start, half : half + units]
        lower = ref[2 * rows - start :, :].astype(WIDE)
        for row, size, column, piece in unfolded(lower, share):
            here = pl.ds(pl.multiple_of(chip * share + row, 8), size)
            acc_ref[here, column : column + D // 2] = piece
    down_ref[...] = acc_ref[...].astype(LOW)


def weights(chips, blocks, units):
    return pl.pallas_call(
        weights_kernel,
        in_specs=[smem()] + [vmem()] * len(blocks),
        out_specs=[vmem()] * 3,
        out_shape=[
            jax.ShapeDtypeStruct((D, units), LOW),
            jax.ShapeDtypeStruct((D, units), LOW),
            jax.ShapeDtypeStruct((units, D), LOW),
        ],
        scratch_shapes=[pltpu.VMEM((units, D), WIDE)],
        cost_estimate=pl.CostEstimate(
            flops=0, bytes_accessed=12 * D * units, transcendentals=0
        ),
        name="weights",
    )(chips, *blocks)


def ffn_kernel(na, nb, ga, gb, g_ref, u_ref, d_ref, hid_ref, gg_ref, ug_ref, dn_ref, out_ref, n_ref, c_ref):
    for step, (tokens, cotangent) in enumerate(((na, ga), (nb, gb))):

        @pl.when(pl.program_id(0) == step)
        def _(tokens=tokens, cotangent=cotangent):
            n_ref[...] = tokens[...]
            c_ref[...] = cotangent[...]

    n = n_ref[...]
    gate = dot_nn(n, g_ref[...])
    upper = dot_nn(n, u_ref[...])
    sigma = jax.nn.sigmoid(gate)
    silu = gate * sigma
    hid = (silu * upper).astype(LOW)
    hid_ref[0] = hid
    hg = dot_nt(c_ref[...], d_ref[...])
    gg = (hg * upper * sigma * (1.0 + gate * (1.0 - sigma))).astype(LOW)
    ug = (hg * silu).astype(LOW)
    gg_ref[0] = gg
    ug_ref[0] = ug
    dn_ref[0] = (dot_nt(gg, g_ref[...]) + dot_nt(ug, u_ref[...])).astype(LOW)
    out_ref[0] = dot_nn(hid, d_ref[...]).astype(LOW)


def ffn(na, nb, ga, gb, g, u, d):
    count = na.shape[0]
    units = g.shape[1]

    def whole(rows, columns):
        return pl.BlockSpec((rows, columns), lambda i: (0, 0))

    def block(columns):
        return pl.BlockSpec((1, count, columns), lambda i: (i, 0, 0))

    return pl.pallas_call(
        ffn_kernel,
        grid=(2,),
        in_specs=[whole(count, D)] * 4 + [whole(D, units)] * 2 + [whole(units, D)],
        out_specs=[block(units)] * 3 + [block(D)] * 2,
        scratch_shapes=[pltpu.VMEM((count, D), LOW)] * 2,
        out_shape=[jax.ShapeDtypeStruct((2, count, units), LOW)] * 3
        + [jax.ShapeDtypeStruct((2, count, D), LOW)] * 2,
        cost_estimate=pl.CostEstimate(
            flops=24 * count * D * units,
            bytes_accessed=6 * D * units + 16 * count * D,
            transcendentals=2 * count * units,
        ),
        name="ffn",
    )(na, nb, ga, gb, g, u, d)


def grads_kernel(tab, *refs):
    ns, ups, (hid_l, gg_l, ug_l, hid_r, gg_r, ug_r, parts_ref) = (
        refs[:4], refs[4:8], refs[8:],
    )
    wide = parts_ref.shape[2]
    half = wide // 2
    units = hid_l.shape[2]
    share = units // HEADS
    rows = ns[0].shape[1] // (2 * HEADS)
    edge = units - units % HEAD_DIM

    def tokens(near, away):
        return jnp.concatenate([near[0], near[1], away[0], away[1]], axis=0)

    n = jnp.concatenate([v[...] for v in ns], axis=0)
    up = jnp.concatenate([v[...] for v in ups], axis=0)
    for near, away, start in ((gg_l, gg_r, 0), (ug_l, ug_r, half)):
        total = dot_tn(n, tokens(near, away)).astype(LOW)
        for h in range(HEADS):
            slot = tab[h]
            for pair in range(2):
                first = (pair * HEADS + h) * rows
                here = slice(pair * rows, (pair + 1) * rows)
                parts_ref[slot, here, start + edge : start + half] = jnp.zeros(
                    (rows, half - edge), LOW
                )
                parts_ref[slot, here, start : start + units] = total[first : first + rows]
    total = dot_tn(tokens(hid_l, hid_r), up)
    strip = wide - D
    for h in range(HEADS):
        slot = tab[h]
        piece = total[h * share : (h + 1) * share].astype(LOW)
        parts_ref[slot, 2 * rows : 2 * rows + share, :D] = piece
        parts_ref[slot, 2 * rows : 2 * rows + share, D:] = jnp.zeros((share, strip), LOW)


def weight_grads(slot_of, ns, ups, near, away, height, wide):
    count = ns[0].shape[0]
    units = near[0].shape[2]
    return pl.pallas_call(
        grads_kernel,
        in_specs=[smem()] + [vmem()] * 14,
        out_specs=vmem(),
        out_shape=jax.ShapeDtypeStruct((HEADS, height, wide), LOW),
        cost_estimate=pl.CostEstimate(
            flops=24 * count * D * units, bytes_accessed=14 * 2**20, transcendentals=0
        ),
        name="weight_grads",
    )(slot_of, *ns, *ups, *near, *away)


def strips_kernel(tab, out_ref, strips_ref):
    rows, strip = out_ref.shape[1], strips_ref.shape[2]
    for slot in range(HEADS):
        for i in range(D // strip):
            strips_ref[slot, i * rows : (i + 1) * rows, :] = out_ref[
                tab[slot], :, i * strip : (i + 1) * strip
            ]


def out_strips(chips, out, strip):
    return pl.pallas_call(
        strips_kernel,
        in_specs=[smem(), vmem()],
        out_specs=vmem(),
        out_shape=jax.ShapeDtypeStruct((HEADS, out.shape[1] * D // strip, strip), LOW),
        cost_estimate=pl.CostEstimate(
            flops=0, bytes_accessed=4 * HEADS * out.shape[1] * D, transcendentals=0
        ),
        name="out_strips",
    )(chips, out)


def mid_kernel(mid_ref, pa, pb, pc, up_ref, gain_ref, w_ref, mg_ref, bg_ref, ag_ref):
    mid = mid_ref[...]
    scaled = (pa[...].astype(WIDE) + pb[...].astype(WIDE) + pc[...].astype(WIDE)) * gain_ref[
        ...
    ].astype(WIDE)
    r = lax.rsqrt(jnp.mean(mid * mid, axis=-1, keepdims=True) + EPSILON)
    inner = jnp.mean(scaled * mid, axis=-1, keepdims=True)
    mid_grad = up_ref[...].astype(WIDE) + r * scaled - mid * (r * r * r * inner)
    mg_ref[...] = mid_grad
    branch = mid_grad.astype(LOW)
    bg_ref[...] = branch
    att = dot_nt(branch, w_ref[...]).astype(LOW)
    for h in range(HEADS):
        ag_ref[h] = att[:, h * HEAD_DIM : (h + 1) * HEAD_DIM]


def mid_block(mid, pa, pb, pc, up, gain, w):
    count = mid.shape[0]
    return pl.pallas_call(
        mid_kernel,
        in_specs=[vmem()] * 7,
        out_specs=[vmem()] * 3,
        out_shape=[
            jax.ShapeDtypeStruct((count, D), WIDE),
            jax.ShapeDtypeStruct((count, D), LOW),
            jax.ShapeDtypeStruct((HEADS, count, HEAD_DIM), LOW),
        ],
        cost_estimate=pl.CostEstimate(
            flops=2 * count * D * D, bytes_accessed=6 * 2**20, transcendentals=0
        ),
        name="mid_block",
    )(mid, pa, pb, pc, up, gain, w)


def qkv_back_kernel(
    tab, dq_ref, own_ref, got_ref, loc_ref, base_ref, n_ref, w_ref, dx_ref, dw_ref, sum_ref
):
    i = pl.program_id(0)
    c, s = turning(loc_ref, base_ref)

    def rot(v):
        return v * c - pltpu.roll(v, HEAD_DIM // 2, 1) * s

    dq = rot(dq_ref[0] * SCALE).astype(LOW)
    dk = rot((own_ref[0, 0] + got_ref[0, 0].astype(WIDE)) * SCALE).astype(LOW)
    dv = (own_ref[1, 0] + got_ref[1, 0].astype(WIDE)).astype(LOW)
    grads = jnp.concatenate([dq, dk, dv], axis=1)
    dx_ref[0] = dot_nt(grads, w_ref[...]).astype(LOW)
    part = dot_tn(n_ref[0], grads)

    @pl.when(i == 0)
    def _():
        sum_ref[...] = part

    @pl.when(i > 0)
    def _():
        sum_ref[...] += part

    @pl.when(i == HEADS - 1)
    def _():
        dw_ref[...] = sum_ref[...].astype(LOW)


def qkv_back(chips, dq, own, got, loc, base, normed, w):
    count = dq.shape[1]
    block = pl.BlockSpec((1, count, HEAD_DIM), lambda i, t: (t[i], 0, 0))
    pair = pl.BlockSpec((2, 1, count, HEAD_DIM), lambda i, t: (0, t[i], 0, 0))
    weight = pl.BlockSpec((D, 3 * HEAD_DIM), lambda i, t: (0, 0))
    return pl.pallas_call(
        qkv_back_kernel,
        grid_spec=pltpu.PrefetchScalarGridSpec(
            num_scalar_prefetch=1,
            grid=(HEADS,),
            in_specs=[
                block, pair, pair,
                pl.BlockSpec((2, count, HEAD_DIM), lambda i, t: (0, 0, 0)),
                pl.BlockSpec((1, 2, HEAD_DIM), lambda i, t: (2 * t[i] + t[HEADS], 0, 0)),
                pl.BlockSpec((1, count, D), lambda i, t: (t[i], 0, 0)),
                weight,
            ],
            out_specs=[pl.BlockSpec((1, count, D), lambda i, t: (i, 0, 0)), weight],
            scratch_shapes=[pltpu.VMEM((D, 3 * HEAD_DIM), WIDE)],
        ),
        out_shape=[
            jax.ShapeDtypeStruct((HEADS, count, D), LOW),
            jax.ShapeDtypeStruct((D, 3 * HEAD_DIM), LOW),
        ],
        cost_estimate=pl.CostEstimate(
            flops=4 * HEADS * count * D * 3 * HEAD_DIM,
            bytes_accessed=6 * HEADS * count * D,
            transcendentals=0,
        ),
        name="qkv_back",
    )(chips, dq, own, got, loc, base, normed, w)


def local(
    far,
    tokens,
    segment_ids,
    second_doc,
    memory_index,
    cache_keys,
    cache_values,
    first_gain,
    query_weight,
    key_weight,
    value_weight,
    out_weight,
    second_gain,
    gate_weight,
    up_weight,
    down_weight,
    cotangent,
):
    x = tokens[0]
    upstream = cotangent[0]
    count = x.shape[0]
    blocks = count // QUERY_BLOCK
    rows = query_weight.shape[0]
    share = down_weight.shape[0]
    units = far * HEADS * share
    chip, core, pair = lax.axis_index("h"), lax.axis_index("c"), lax.axis_index("dl")
    mine = jnp.where(chip % 2 == 0, chip // 2, HEADS - 1 - chip // 2)
    slots = jnp.arange(HEADS, dtype=jnp.int32)
    chips = at_place(mine - slots)

    def by_head(w):
        return w.reshape(rows, HEADS, HEAD_DIM).transpose(1, 0, 2)

    picked = memory_index[0].transpose(1, 0, 2)
    seg_rows = jnp.broadcast_to(
        segment_ids[0].astype(LOW).reshape(1, blocks, QUERY_BLOCK), (HEADS, blocks, QUERY_BLOCK)
    )
    gains = jnp.concatenate([first_gain, second_gain])
    gain_rows = jnp.broadcast_to(
        jnp.pad(gains, (0, HEAD_DIM - 2 * rows)).reshape(1, 1, HEAD_DIM), (HEADS, 1, HEAD_DIM)
    )
    pack = jnp.concatenate(
        [
            by_head(query_weight),
            by_head(key_weight),
            by_head(value_weight),
            seg_rows,
            (picked // MEM_ROWS).astype(LOW),
            (picked % MEM_ROWS).astype(LOW),
            gain_rows,
        ],
        axis=1,
    )
    height = pack.shape[1]
    pack = jnp.pad(pack, ((0, 0), (0, -height % 16), (0, 0)))

    block = jnp.concatenate([x, out_weight], axis=0)
    split = count // 2
    got = exchange(pack)
    up_c = swap(upstream, "c")
    up_y = swap(upstream, "dl")
    up_yc = swap(up_y, "c")
    got, x_forth, x_back = lax.optimization_barrier((got, turn(block, 1), turn(block, -1)))
    forth, back = [block, x_forth, turn(x_forth, 1)], [block, x_back, turn(x_back, -1)]
    got_c = swap(got, "c")
    got_y = swap(got, "dl")
    got_yc = swap(got_y, "c")
    near = pick(core, jnp.stack([got, got_c]), jnp.stack([got_c, got]))
    away = pick(core, jnp.stack([got_y, got_yc]), jnp.stack([got_yc, got_y]))
    every = pick(pair, jnp.stack([near, away]), jnp.stack([away, near]))
    every = every.transpose(2, 0, 1, 3, 4)
    if far > 1:
        every = lax.all_gather(every, "dh", axis=0)
    else:
        every = every[None]
    every = every.transpose(0, 2, 1, 3, 4, 5)
    w_qkv = jnp.concatenate(
        [every[..., i * rows : (i + 1) * rows, :].reshape(D, HEAD_DIM) for i in range(3)], axis=1
    )
    gain_all = every[..., 3 * rows + 3 * blocks, : 2 * rows].reshape(-1, 2, rows)
    gain_one = gain_all[:, 0].reshape(1, D)
    gain_two = gain_all[:, 1].reshape(1, D)

    def seg_of(blocks_of):
        return (
            blocks_of[:, 3 * rows : 3 * rows + blocks]
            .astype(WIDE)
            .astype(jnp.int32)
            .reshape(HEADS, count)
        )

    seg_own = seg_of(got)
    seg_oth = seg_of(got_c)
    idx = (
        got[:, 3 * rows + blocks : 3 * rows + 2 * blocks].astype(WIDE) * MEM_ROWS
        + got[:, 3 * rows + 2 * blocks : 3 * rows + 3 * blocks].astype(WIDE)
    ).astype(jnp.int32)
    idx = idx.reshape(HEADS, count, 1)

    block_docs = seg_own[:, ::QUERY_BLOCK]
    docs = second_doc.shape[1]
    doc_ids = jnp.arange(docs, dtype=jnp.int32)
    mates = jnp.sum(
        jnp.where(block_docs[:, :, None] == doc_ids, second_doc[0][None, None, :], 0), axis=-1
    )
    seg_all = jnp.concatenate([seg_own, seg_oth], axis=0)
    before = jnp.sum(
        (seg_all.reshape(1, -1) < block_docs[:, :1]).astype(jnp.int32), axis=1
    )
    tab = jnp.concatenate(
        [
            block_docs.reshape(-1),
            mates.reshape(-1),
            before // (2 * count),
            jnp.stack([core, chip]),
        ]
    ).astype(jnp.int32)

    loc, base = (jnp.asarray(table) for table in turn_tables(count))

    seg_thin = seg_own.reshape(HEADS, count, 1)
    early = (w_qkv, gain_one, tab, up_c, up_y, up_yc)
    early, gate_late, up_late, forth[2], back[2] = lax.optimization_barrier(
        (early, gate_weight, up_weight, forth[2], back[2])
    )
    w_qkv, gain_one, tab, up_c, up_y, up_yc = early
    forth.append(turn(forth[2], 1))
    back.append(turn(back[2], -1))
    at_near, at_far = [0, 1, 7, 2, 6], [3, 5, 4]

    def chips_at(order):
        places = at_place(mine - jnp.asarray(list(order), jnp.int32))
        return jnp.concatenate([places, core[None]]).astype(jnp.int32)

    near_slots = [forth[0], forth[1], back[1], forth[2], back[2]]
    held = qkv_blocks(
        chips_at(at_near), [((v, count),) for v in near_slots], gain_one, w_qkv, loc, base, ()
    )
    half = units + -units % HEAD_DIM
    wide = 2 * half

    def by_owner(w):
        w = w.reshape(rows, far, 2, HEADS, 2, share).transpose(2, 4, 0, 1, 3, 5)
        return jnp.pad(w.reshape(2, 2, rows, units), ((0, 0),) * 3 + ((0, half - units),))

    gu = jnp.concatenate([by_owner(gate_late), by_owner(up_late)], axis=-1)
    kept = pick(core, gu[:, 0], gu[:, 1])
    came = swap(pick(core, gu[:, 1], gu[:, 0]), "c")
    gu = pick(core, jnp.stack([kept, came], 1), jnp.stack([came, kept], 1))
    kept = pick(pair, gu[0], gu[1])
    came = swap(pick(pair, gu[1], gu[0]), "dl")
    gu = pick(pair, jnp.stack([kept, came]), jnp.stack([came, kept])).reshape(4 * rows, wide)
    if far == 1:
        deep = 2 * rows
        lower = jnp.concatenate(fold(down_weight, deep), axis=1)
    else:
        deep = share
        lower = jnp.pad(down_weight, ((0, 0), (0, wide - D)))
    bundle = jnp.concatenate([gu, lower], axis=0)
    height = 4 * rows + share
    if far > 1:
        bundle = lax.all_gather(bundle, "dh", axis=0, tiled=True)
    upper = bundle.shape[0] // 2
    *held, bundle, forth[3], back[3] = lax.optimization_barrier(
        (*held, bundle, forth[3], back[3])
    )
    far_first, far_last = turn(forth[3][:split], 1), turn(back[3][split:], -1)
    bundle, *_ = lax.optimization_barrier((bundle, far_first, far_last))
    w_forth, w_back = [bundle, turn(bundle, 1)], [bundle, turn(bundle, -1)]

    far_slots = [
        ((forth[3], count),),
        ((back[3], count),),
        ((far_first, split), (far_last, count - split)),
    ]
    queries, own, normed_one = qkv_blocks(
        chips_at(at_far), far_slots, gain_one, w_qkv, loc, base, tuple(held)
    )
    outs = jnp.stack([v[-rows:] for v in (*forth, far_last, *back[:0:-1])])
    queries, own, outs, w_forth[1], w_back[1] = lax.optimization_barrier(
        (queries, own, outs, w_forth[1], w_back[1])
    )
    other = swap(own, "c")
    outs_c = swap(outs, "c")
    outs_y = swap(outs, "dl")
    seg_own_row = seg_own.reshape(HEADS, 1, count)
    seg_oth_row = seg_oth.reshape(HEADS, 1, count)
    cached = [cache[0].reshape(-1, D) for cache in (cache_keys, cache_values)]
    attention, attention_low, lse, memory = attend(
        tab, queries, own, other, seg_thin, seg_own_row, seg_oth_row, idx, *cached
    )
    w_forth.append(turn(w_forth[1], 1))
    w_back.append(turn(w_back[1], -1))
    attention_low, outs_y, w_forth[2], w_back[2] = lax.optimization_barrier(
        (attention_low, outs_y, w_forth[2], w_back[2])
    )

    heads = exchange(attention_low)
    w_forth.append(turn(w_forth[2], 1))
    w_back.append(turn(w_back[2], -1))
    outs_yc = swap(outs_y, "c")
    heads, w_forth[3], w_back[3] = lax.optimization_barrier((heads, w_forth[3], w_back[3]))
    w_first, w_last = turn(w_forth[3][:upper], 1), turn(w_back[3][upper:], -1)
    slot_of = lax.rem(mine - jnp.asarray(PLACE, jnp.int32) + HEADS, HEADS).astype(jnp.int32)
    if far == 1:
        sources = [outs, outs_c, outs_y, outs_yc]
    else:
        near = pick(core, jnp.stack([outs, outs_c], 1), jnp.stack([outs_c, outs], 1))
        away = pick(core, jnp.stack([outs_y, outs_yc], 1), jnp.stack([outs_yc, outs_y], 1))
        sources = pick(pair, jnp.stack([near, away]), jnp.stack([away, near]))
        sources = lax.all_gather(jnp.take(sources, slot_of, axis=1), "dh", axis=0)
        sources = [sources.reshape(D, D)]
    where = jnp.concatenate([chips, jnp.stack([pair, core])]).astype(jnp.int32)
    attended, mid, normed_two, out_w = out_block(where, heads, sources, x, gain_two)
    normed_two, w_first, w_last = lax.optimization_barrier((normed_two, w_first, w_last))
    w_slots = w_forth + [w_first, w_last] + w_back[:0:-1]

    if far == 1:
        gate_w, up_w, down_w = weights(where, w_slots, units)
    else:
        middle = jnp.concatenate(w_slots[HEADS // 2 : HEADS // 2 + 2], axis=0)
        every = jnp.stack(w_slots[: HEADS // 2] + [middle] + w_slots[HEADS // 2 + 2 :])
        every = jnp.take(every, slot_of, axis=0).reshape(HEADS, far, height, wide)
        gu = every[:, :, : 4 * rows].reshape(HEADS, far, 2, 2 * rows, wide)
        gu = gu.transpose(1, 2, 0, 3, 4).reshape(D, wide)
        gate_w, up_w = gu[:, :units], gu[:, half : half + units]
        down_w = every[:, :, 4 * rows :, :D].transpose(1, 0, 2, 3).reshape(units, D)

    n_c = swap(normed_two, "c")
    n_y = swap(normed_two, "dl")
    hid_l, gg_l, ug_l, dn_l, out_l = ffn(normed_two, n_c, upstream, up_c, gate_w, up_w, down_w)
    n_y, dn_l = lax.optimization_barrier((n_y, dn_l))
    n_yc = swap(n_y, "c")
    hid_r, gg_r, ug_r, dn_r, out_r = ffn(n_y, n_yc, up_y, up_yc, gate_w, up_w, down_w)

    def to_away(away):
        return (away[0].astype(WIDE) + swap(away[1], "c").astype(WIDE)).astype(LOW)

    there = to_away(dn_r)
    there, hid_l, gg_l, ug_l, hid_r, gg_r, ug_r = lax.optimization_barrier(
        (there, hid_l, gg_l, ug_l, hid_r, gg_r, ug_r)
    )
    n_all, u_all = [normed_two, n_c, n_y, n_yc], [upstream, up_c, up_y, up_yc]
    near, away = (hid_l, gg_l, ug_l), (hid_r, gg_r, ug_r)
    if far == 1:
        parts = weight_grads(slot_of, n_all, u_all, near, away, height, wide)
    else:

        def over_tokens(left, right):
            return jnp.einsum(
                "gtd,gtf->df", left, right, preferred_element_type=WIDE
            ).astype(LOW)

        def by_rows(w):
            w = jnp.pad(w, ((0, 0), (0, half - units)))
            return w.reshape(far, 2, HEADS, 2 * rows, half).transpose(2, 0, 1, 3, 4)

        n_all, u_all = jnp.stack(n_all), jnp.stack(u_all)
        hid, gg, ug = (jnp.concatenate(pieces, axis=0) for pieces in zip(near, away))
        gu = jnp.concatenate(
            [by_rows(over_tokens(n_all, gg)), by_rows(over_tokens(n_all, ug))], axis=-1
        ).reshape(HEADS, far, 4 * rows, wide)
        down = over_tokens(hid, u_all).reshape(far, HEADS, share, D).transpose(1, 0, 2, 3)
        down = jnp.pad(down, ((0, 0), (0, 0), (0, 0), (0, wide - D)))
        parts = jnp.concatenate([gu, down], axis=2)
        parts = jnp.take(parts.reshape(HEADS, far * height, wide), chips, axis=0)

    out_l, out_r, _ = lax.optimization_barrier((out_l, out_r, parts))
    output = mid
    for part in (out_l[0], swap(out_l[1], "c"), swap(to_away(out_r), "dl")):
        output = output + part.astype(WIDE)
    output = output.astype(LOW)

    sums = [dn_l[0], swap(dn_l[1], "c"), swap(there, "dl")]
    sums[2], parts = lax.optimization_barrier((sums[2], parts))
    mid_grad, branch, att_grad = mid_block(mid, *sums, upstream, gain_two, out_w)
    ups = exchange(att_grad)

    def plus(block, arrived, start):
        size = arrived.shape[0]
        total = block[start : start + size].astype(WIDE) + arrived.astype(WIDE)
        pieces = [block[:start], total, block[start + size :]]
        pieces = [piece.astype(LOW) for piece in pieces if piece.shape[0]]
        return jnp.concatenate(pieces, axis=0)

    def ring_first(blocks, split):
        middle = blocks[HEADS // 2]
        return (
            plus(blocks[HEADS // 2 + 1], turn(middle[:split].astype(LOW), 1), 0),
            plus(blocks[HEADS // 2 - 1], turn(middle[split:].astype(LOW), -1), split),
        )

    def ring_next(blocks, forth, back, step):
        return (
            plus(blocks[HEADS // 2 + step], turn(forth, 1), 0),
            plus(blocks[HEADS // 2 - step], turn(back, -1), 0),
        )

    def ring_last(blocks, forth, back):
        return blocks[0].astype(WIDE) + forth.astype(WIDE) + back.astype(WIDE)

    def over_owner(w, width):
        w = w.reshape(far, 2, HEADS, 2, rows, width)
        kept = pick(core, w[:, :, :, 0], w[:, :, :, 1])
        came = swap(pick(core, w[:, :, :, 1], w[:, :, :, 0]), "c")
        w = kept.astype(WIDE) + came.astype(WIDE)
        kept = pick(pair, w[:, 0], w[:, 1])
        came = swap(pick(pair, w[:, 1], w[:, 0]).astype(LOW), "dl")
        w = (kept + came.astype(WIDE)).astype(LOW)
        if far > 1:
            w = lax.psum_scatter(w, "dh", scatter_dimension=0, tiled=True)
        return w[0]

    out_part = over_owner(
        jnp.einsum("td,te->de", attended, branch, preferred_element_type=WIDE).astype(LOW), D
    )
    strip = wide - D
    upper = 4 * rows if far == 1 else parts.shape[1] // 2
    blocks = [parts[slot].astype(WIDE) for slot in range(HEADS)]
    if far == 1:
        strips = out_strips(where, out_part, strip)
        below = share - strips.shape[1]
        for slot in range(HEADS):
            if slot != HEADS // 2:
                blocks[slot] = blocks[slot] + jnp.pad(
                    strips[slot].astype(WIDE), ((4 * rows, below), (D, 0))
                )
        out_far = turn(strips[HEADS // 2], HEADS // 2)
    else:
        out_far = exchange(out_part)
    forth, back = ring_first(blocks, upper)
    ups, forth, back = lax.optimization_barrier((ups, forth, back))
    forth, back = ring_next(blocks, forth, back, 2)

    dq, d_own, d_oth = attend_back(
        tab, queries, ups, attention, lse, own, other, memory, seg_thin, seg_own_row, seg_oth_row
    )
    d_got = swap(d_oth, "c")
    dq, forth, back = lax.optimization_barrier((dq, forth, back))
    dx, dw = qkv_back(
        chips_at(range(HEADS)), dq, d_own, d_got, loc, base, normed_one, w_qkv
    )
    arrived_forth, arrived_back = turn(forth, 1), turn(back, -1)
    dx, arrived_forth, arrived_back = lax.optimization_barrier((dx, arrived_forth, arrived_back))
    dx_forth, dx_back = ring_first(dx, split)
    dw, dx_forth, dx_back = lax.optimization_barrier((dw, dx_forth, dx_back))
    forth = plus(blocks[HEADS - 1], arrived_forth, 0)
    back = plus(blocks[1], arrived_back, 0)

    dw = over_owner(dw, 3 * HEAD_DIM)
    dx_forth, dx_back = ring_next(dx, dx_forth, dx_back, 2)
    qkv_grads = exchange(dw).astype(WIDE)
    got_forth, got_back = turn(dx_forth, 1), turn(dx_back, -1)
    qkv_grads, got_forth, got_back = lax.optimization_barrier((qkv_grads, got_forth, got_back))
    dx_forth, dx_back = plus(dx[HEADS - 1], got_forth, 0), plus(dx[1], got_back, 0)
    normed_one_grad = ring_last(dx, turn(dx_forth, 1), turn(dx_back, -1))

    summed = ring_last(blocks, turn(forth, 1), turn(back, -1)).astype(LOW)
    if far > 1:
        summed = lax.psum_scatter(summed, "dh", scatter_dimension=0, tiled=True)
    down_w_grad = summed[4 * rows : 4 * rows + share, :D].astype(WIDE)
    if far == 1:
        out_w_grad = summed[4 * rows : 4 * rows + strips.shape[1], D:].astype(WIDE)
        out_w_grad = out_w_grad + out_far.astype(WIDE)
        out_w_grad = out_w_grad.reshape(D // strip, rows, strip).transpose(1, 0, 2).reshape(rows, D)
    else:
        out_w_grad = jnp.sum(out_far.astype(WIDE), axis=0)
    gu = summed[: 4 * rows].reshape(2, 2, rows, wide)
    kept = pick(core, gu[:, 0], gu[:, 1])
    came = swap(pick(core, gu[:, 1], gu[:, 0]), "c")
    gu = pick(core, jnp.stack([kept, came], 1), jnp.stack([came, kept], 1))
    kept = pick(pair, gu[0], gu[1])
    came = swap(pick(pair, gu[1], gu[0]), "dl")
    gu = pick(pair, jnp.stack([kept, came]), jnp.stack([came, kept]))
    gu = jnp.stack([gu[..., :units], gu[..., half : half + units]])
    gu = (
        gu.reshape(2, 2, 2, rows, far, HEADS, share)
        .transpose(0, 3, 4, 1, 5, 2, 6)
        .reshape(2, rows, FF)
        .astype(WIDE)
    )
    gate_w_grad, up_w_grad = gu[0], gu[1]

    wide_x = x.astype(WIDE)
    r = lax.rsqrt(jnp.mean(wide_x * wide_x, axis=-1, keepdims=True) + EPSILON)
    scaled = normed_one_grad * gain_one.astype(WIDE)
    inner = jnp.mean(scaled * wide_x, axis=-1, keepdims=True)
    input_grad = mid_grad + r * scaled - wide_x * (r * r * r * inner)

    q_w_grad, k_w_grad, v_w_grad = (
        qkv_grads[:, :, i * HEAD_DIM : (i + 1) * HEAD_DIM].transpose(1, 0, 2).reshape(rows, D)
        for i in range(3)
    )

    def gain_grad(gain, pairs):
        total = 0.0
        for grad, weight in pairs:
            total = total + jnp.sum(grad * weight.astype(WIDE), axis=1)
        return total / gain.astype(WIDE)

    first_gain_grad = gain_grad(
        first_gain,
        ((q_w_grad, query_weight), (k_w_grad, key_weight), (v_w_grad, value_weight)),
    )
    second_gain_grad = gain_grad(
        second_gain, ((gate_w_grad, gate_weight), (up_w_grad, up_weight))
    )
    return (
        output[None],
        input_grad[None],
        first_gain_grad,
        q_w_grad,
        k_w_grad,
        v_w_grad,
        out_w_grad,
        second_gain_grad,
        gate_w_grad,
        up_w_grad,
        down_w_grad,
    )


def solution(mesh):
    far = mesh.shape["dp"] // 2
    cores = mesh.shape["seq"] // HEADS
    fine = Mesh(mesh.devices.reshape(far, 2, HEADS, cores), ("dh", "dl", "h", "c"))
    dp, seq, every = ("dh", "dl"), ("h", "c"), ("dh", "dl", "h", "c")
    rows = P(every, None)
    return jax.shard_map(
        functools.partial(local, far),
        mesh=fine,
        in_specs=(
            P(dp, seq, None),
            P(dp, seq),
            P(dp, None),
            P(dp, seq, None, None),
            P(dp, None, None, None),
            P(dp, None, None, None),
            P(every),
            rows,
            rows,
            rows,
            rows,
            P(every),
            rows,
            rows,
            rows,
            P(dp, seq, None),
        ),
        out_specs=(
            P(dp, seq, None),
            P(dp, seq, None),
            P(every),
            rows,
            rows,
            rows,
            rows,
            P(every),
            rows,
            rows,
            rows,
        ),
        check_vma=False,
    )
```
